32 devices in a mesh: dp: 4 (over y, core), fsdp: 8 (over z, x).
Axes of the slice: x: 2, y: 2, z: 4, core: 2. Of those that a mesh axis runs over, the one named last changes fastest.
Arguments:
- frames: bfloat16 [16384, 2, 1024], P(('dp', 'fsdp')), may hold values from -6 to 6
- cotangent: bfloat16 [16384, 2, 1024], P(('dp', 'fsdp')), may hold values from -12 to 12
- segment_ids: int32 [16384], replicated, may hold values from 0 to 1023, never falling along the last dimension, each value on 1 to 256 neighbouring positions
- qkv_weight: float32 [2, 1024, 3072], P(None, 'fsdp'), may hold values from -0.1875 to 0.1875
- mix_weight: float32 [2, 1024, 1024], P(None, 'fsdp'), may hold values from -0.25 to 0.25
- inner_weight: float32 [2, 1024, 5632], P(None, 'fsdp'), may hold values from -0.1875 to 0.1875
- down_weight: float32 [2, 2816, 1024], P(None, 'fsdp'), may hold values from -0.109375 to 0.109375
- norm_gains: float32 [2, 1024], P(None, 'fsdp'), may hold values from 0.5 to 1.5
- qkv_moment: float32 [2, 1024, 3072], P(None, 'fsdp'), may hold values from -448 to 448
- mix_moment: float32 [2, 1024, 1024], P(None, 'fsdp'), may hold values from -448 to 448
- inner_moment: float32 [2, 1024, 5632], P(None, 'fsdp'), may hold values from -224 to 224
- down_moment: float32 [2, 2816, 1024], P(None, 'fsdp'), may hold values from -448 to 448
- gains_moment: float32 [2, 1024], P(None, 'fsdp'), may hold values from -1024 to 1024
- qkv_average: float32 [2, 1024, 3072], P(None, 'fsdp'), may hold values from -0.1875 to 0.1875
- mix_average: float32 [2, 1024, 1024], P(None, 'fsdp'), may hold values from -0.25 to 0.25
- inner_average: float32 [2, 1024, 5632], P(None, 'fsdp'), may hold values from -0.1875 to 0.1875
- down_average: float32 [2, 2816, 1024], P(None, 'fsdp'), may hold values from -0.109375 to 0.109375
- gains_average: float32 [2, 1024], P(None, 'fsdp'), may hold values from 0.1 to 1.9
Outputs:
- layer_out: bfloat16 [16384, 2, 1024], P(('dp', 'fsdp'))
- frames_grad: bfloat16 [16384, 2, 1024], P(('dp', 'fsdp'))
- qkv_grad: float32 [2, 1024, 3072], P(None, 'fsdp')
- mix_grad: float32 [2, 1024, 1024], P(None, 'fsdp')
- inner_grad: float32 [2, 1024, 5632], P(None, 'fsdp')
- down_grad: float32 [2, 2816, 1024], P(None, 'fsdp')
- gains_grad: float32 [2, 1024], P(None, 'fsdp')
- qkv_moment_new: float32 [2, 1024, 3072], P(None, 'fsdp')
- mix_moment_new: float32 [2, 1024, 1024], P(None, 'fsdp')
- inner_moment_new: float32 [2, 1024, 5632], P(None, 'fsdp')
- down_moment_new: float32 [2, 2816, 1024], P(None, 'fsdp')
- gains_moment_new: float32 [2, 1024], P(None, 'fsdp')
- qkv_average_new: float32 [2, 1024, 3072], P(None, 'fsdp')
- mix_average_new: float32 [2, 1024, 1024], P(None, 'fsdp')
- inner_average_new: float32 [2, 1024, 5632], P(None, 'fsdp')
- down_average_new: float32 [2, 2816, 1024], P(None, 'fsdp')
- gains_average_new: float32 [2, 1024], P(None, 'fsdp')
- qkv_weight_new: float32 [2, 1024, 3072], P(None, 'fsdp')
- mix_weight_new: float32 [2, 1024, 1024], P(None, 'fsdp')
- inner_weight_new: float32 [2, 1024, 5632], P(None, 'fsdp')
- down_weight_new: float32 [2, 2816, 1024], P(None, 'fsdp')
- gains_new: float32 [2, 1024], P(None, 'fsdp')
The draws below stay inside these ranges and needn't reach their ends.
Inputs may be any that keep to these rules, and one draw needn't show every extreme that they name: `segment_ids`: ids never fall along the frames and rise by at most 1 from a frame to the next.
All inputs are finite; a program needn't handle non-finite values.
Results may differ from the reference program's by a relative error of at most 0.017.
Values may be sent and summed in bfloat16 or wider, within the bound.
A program may use at most 384 MiB of HBM per device.

```python
import math
import jax
import jax.numpy as jnp
import numpy as np
from jax import lax

D = 1024
HEADS = 16
FF = 2816
HEAD_DIM = 64
POS = 2
FRAMES = 16384


def spiked(drawn, key, source, target, shards_of, factor):
    owner, partner = [(jnp.arange(drawn.shape[dim]) // (drawn.shape[dim] // shards_of)).reshape([-1 if axis == dim else 1 for axis in range(drawn.ndim)]) for dim in (source, target)]
    chosen = jax.random.permutation(key, shards_of)[partner]
    strong = (owner == chosen) | (owner == (partner + shards_of // 2) % shards_of)
    return jnp.where(strong, factor * drawn, drawn)


def block_scale(rng, dims, cuts, least, largest):
    loudness, own = 1.0, jax.random.fold_in(rng, 6)
    for dim, blocks in cuts:
        draws = jnp.exp(jax.random.uniform(jax.random.fold_in(own, dim), (blocks,), jnp.float32, least / len(cuts), largest / len(cuts)))
        loudness = loudness * jnp.repeat(draws, dims[dim] // blocks).reshape([-1 if axis == dim else 1 for axis in range(len(dims))])
    return loudness


def length_profile(number_of, total, most, slope):
    weights = [(1 << 20) // math.isqrt(grade ** slope) + 1 for grade in range(2, number_of + 1)]
    spare, holding = total - most - (number_of - 1), [1] * (number_of - 1)
    while spare > 0:
        free = [i for i in range(number_of - 1) if holding[i] < most]
        mass, left = sum([weights[i] for i in free]), spare
        for i in free:
            addition = min(most - holding[i], max(1, left * weights[i] // mass), spare)
            holding[i] = holding[i] + addition
            spare = spare - addition
    return np.array([most] + holding)


def ragged(stream_key, count, total, most, slope):
    if count == 2:
        one = jax.random.randint(stream_key, (), max(1, total - most), min(most, total - 1) + 1)
        return jnp.stack([one, total - one])
    lengths = jnp.asarray(length_profile(count, total, most, slope), jnp.int32)
    twos = (count - 1) // 2
    source_of, sink = lengths[1:1 + 2 * twos:2], lengths[2:2 + 2 * twos:2]
    room = jnp.minimum(source_of - 1, most - sink)
    moved = jax.random.randint(jax.random.fold_in(stream_key, 1), (twos,), 0, 1 << 20) % (room + 1)
    lengths = lengths.at[1:1 + 2 * twos:2].set(source_of - moved).at[2:2 + 2 * twos:2].set(sink + moved)
    return lengths[jax.random.permutation(jax.random.fold_in(stream_key, 2), count)]


def gaussian(key, shape, scale, most, split=(), kind=jnp.bfloat16):
    array = scale * jax.random.normal(key, shape, jnp.float32)
    if split:
        array = array * block_scale(key, shape, split, -0.22, 0.18)
    return jnp.clip(array, -most, most).astype(kind)


def gaussian_with(own_key, dims, deviation, limit, split, heavy, dtype=jnp.bfloat16):
    drawn = deviation * jax.random.normal(own_key, dims, jnp.float32)
    if split:
        drawn = drawn * block_scale(own_key, dims, split, -0.22, 0.18)
    return jnp.clip(spiked(drawn, jax.random.fold_in(own_key, 3), *heavy), -limit, limit).astype(dtype)


def setup_inputs(seed: int = 0) -> dict:
    arg_keys = jax.random.split(jax.random.key(seed), 19)
    return {
        "frames": gaussian(arg_keys[0], (FRAMES, POS, D), 1.0, 6.0, ((0, 32),)),
        "cotangent": gaussian_with(arg_keys[1], (FRAMES, POS, D), 1.0, 12.0, ((0, 32),), (0, 2, 32, 2.75)),
        "segment_ids": jnp.searchsorted(jnp.cumsum(ragged(arg_keys[2], FRAMES // 16, FRAMES, min(256, FRAMES // 4), 1)), jnp.arange(FRAMES), side="right").astype(jnp.int32),
        "qkv_weight": gaussian(arg_keys[3], (POS, D, 3 * D), D ** -0.5, 0.1875, ((1, 8),), jnp.float32),
        "mix_weight": gaussian(arg_keys[4], (POS, D, D), (D // 2) ** -0.5, 0.25, ((1, 8),), jnp.float32),
        "inner_weight": gaussian(arg_keys[5], (POS, D, 2 * FF), D ** -0.5, 0.1875, ((1, 8),), jnp.float32),
        "down_weight": gaussian(arg_keys[6], (POS, FF, D), FF ** -0.5, 0.109375, ((1, 8),), jnp.float32),
        "norm_gains": jnp.clip(1.0 + 0.1 * jax.random.normal(arg_keys[7], (2, D), jnp.float32), 0.5, 1.5),
        "qkv_moment": gaussian(arg_keys[8], (POS, D, 3 * D), (0.6 * FRAMES ** 0.5), 448.0, ((1, 8),), jnp.float32),
        "mix_moment": gaussian(arg_keys[9], (POS, D, D), (0.6 * FRAMES ** 0.5), 448.0, ((1, 8),), jnp.float32),
        "inner_moment": gaussian(arg_keys[10], (POS, D, 2 * FF), (0.3 * FRAMES ** 0.5), 224.0, ((1, 8),), jnp.float32),
        "down_moment": gaussian(arg_keys[11], (POS, FF, D), (0.6 * FRAMES ** 0.5), 448.0, ((1, 8),), jnp.float32),
        "gains_moment": gaussian(arg_keys[12], (2, D), ((FRAMES * POS) ** 0.5), 1024.0, ((1, 8),), jnp.float32),
        "qkv_average": gaussian(arg_keys[13], (POS, D, 3 * D), D ** -0.5, 0.1875, ((1, 8),), jnp.float32),
        "mix_average": gaussian(arg_keys[14], (POS, D, D), (D // 2) ** -0.5, 0.25, ((1, 8),), jnp.float32),
        "inner_average": gaussian(arg_keys[15], (POS, D, 2 * FF), D ** -0.5, 0.1875, ((1, 8),), jnp.float32),
        "down_average": gaussian(arg_keys[16], (POS, FF, D), FF ** -0.5, 0.109375, ((1, 8),), jnp.float32),
        "gains_average": jnp.clip(1.0 + 0.18 * jax.random.normal(arg_keys[17], (2, D), jnp.float32), 0.1, 1.9),
    }


@jax.custom_vjp
def low(v):
    return lax.optimization_barrier(v.astype(jnp.bfloat16)).astype(jnp.float32)

@jax.custom_vjp
def low_back(v):
    return v

def low_keep(v):
    return (low(v), None)

def low_pass(kept, grad):
    return (grad,)

def back_keep(v):
    return (v, None)

def back_low(kept, grad):
    return (low(grad),)
low.defvjp(low_keep, low_pass)
low_back.defvjp(back_keep, back_low)
highest = lax.Precision.HIGHEST
norm_eps = 1e-05
momentum_rate = 0.5
average_rate = 0.5
step_rate = 0.05

def scale_rows(values):
    return lax.rsqrt(lax.optimization_barrier(jnp.mean(values * values, axis=-1, keepdims=True)) + norm_eps)

def attend(queries, key_here, value_here, carried):
    frame_count = queries.shape[0]
    zero_frame = jnp.zeros_like(key_here[:1])
    key_before = jnp.concatenate([zero_frame, key_here[:-1]], axis=0)
    value_before = jnp.concatenate([zero_frame, value_here[:-1]], axis=0)
    key_rows = jnp.concatenate([key_before, key_here], axis=1)
    value_rows = jnp.concatenate([value_before, value_here], axis=1)
    scores = jnp.einsum('fphe,fqhe->fhpq', queries, key_rows, precision=highest) / math.sqrt(HEAD_DIM)
    scores = low_back(scores)
    places = jnp.arange(POS)
    causal = places[None, :] <= places[:, None]
    allowed = jnp.concatenate([jnp.broadcast_to(carried[:, None, None, None] > 0, (frame_count, 1, POS, POS)), jnp.broadcast_to(causal[None, None], (frame_count, 1, POS, POS))], axis=-1)
    masked = jnp.where(allowed, scores, -1e+30)
    row_max = lax.optimization_barrier(jnp.max(masked, axis=-1, keepdims=True))
    exponent = jnp.where(allowed, jnp.exp(masked - row_max), 0.0)
    attn_probs = exponent / lax.optimization_barrier(jnp.sum(exponent, axis=-1, keepdims=True))
    probs_low = low(attn_probs)
    return jnp.einsum('fhpq,fqhe->fphe', probs_low, value_rows, precision=highest)

def layer(frames_f32, qkv_w, mix_w, inner_w, down_w, gains, carried):
    qkv_low = low(qkv_w)
    mix_low = low(mix_w)
    inner_low = low(inner_w)
    down_low = low(down_w)
    gains_low = low(gains)
    first_scale = scale_rows(frames_f32)
    inputs_one = low(frames_f32 * first_scale * gains_low[0])
    qkv_rows = jnp.einsum('fpd,pde->fpe', inputs_one, qkv_low, precision=highest)
    qkv_rows = low(low_back(qkv_rows))
    qkv_heads = qkv_rows.reshape(FRAMES, POS, 3, HEADS, HEAD_DIM)
    mixed = attend(qkv_heads[:, :, 0], qkv_heads[:, :, 1], qkv_heads[:, :, 2], carried)
    mixed_low = low(low_back(mixed.reshape(FRAMES, POS, D)))
    residual = frames_f32 + low_back(jnp.einsum('fpd,pde->fpe', mixed_low, mix_low, precision=highest))
    block_rows = math.gcd(FRAMES, 2048)

    def inner_block(resid_block):
        second_scale = scale_rows(resid_block)
        inputs_two = low(resid_block * second_scale * gains_low[1])
        gate_up = low_back(jnp.einsum('fpd,pde->fpe', inputs_two, inner_low, precision=highest))
        hidden = low(jax.nn.silu(gate_up[..., :FF]) * gate_up[..., FF:])
        return jnp.einsum('fpk,pkd->fpd', hidden, down_low, precision=highest)
    branch = lax.map(jax.checkpoint(inner_block), residual.reshape(FRAMES // block_rows, block_rows, POS, D))
    return residual + branch.reshape(residual.shape)

def update(weight, gradient, moment, average, step_size):
    moment_new = momentum_rate * moment + gradient
    weight_new = weight - step_size * (gradient + momentum_rate * moment_new)
    average_new = average_rate * average + (1.0 - average_rate) * weight_new
    return (moment_new, average_new, weight_new)

def reference(frames, cotangent, segment_ids, qkv_weight, mix_weight, inner_weight, down_weight, norm_gains, qkv_moment, mix_moment, inner_moment, down_moment, gains_moment, qkv_average, mix_average, inner_average, down_average, gains_average):
    carried = jnp.concatenate([jnp.zeros((1,), jnp.int32), (segment_ids[1:] == segment_ids[:-1]).astype(jnp.int32)])

    def forward(frames_f32, qkv_w, mix_w, inner_w, down_w, gains):
        return layer(frames_f32, qkv_w, mix_w, inner_w, down_w, gains, carried)
    frames_f32 = frames.astype(jnp.float32)
    layer_f32, pullback = jax.vjp(forward, frames_f32, qkv_weight, mix_weight, inner_weight, down_weight, norm_gains)
    frames_back, qkv_grad, mix_grad, inner_grad, down_grad, gains_grad = pullback(cotangent.astype(jnp.float32))
    step_size = step_rate / math.sqrt(FRAMES)
    qkv_new = update(qkv_weight, qkv_grad, qkv_moment, qkv_average, step_size)
    mix_new = update(mix_weight, mix_grad, mix_moment, mix_average, step_size)
    inner_new = update(inner_weight, inner_grad, inner_moment, inner_average, step_size)
    down_new = update(down_weight, down_grad, down_moment, down_average, step_size)
    gains_new = update(norm_gains, gains_grad, gains_moment, gains_average, step_size)
    return (layer_f32.astype(jnp.bfloat16), frames_back.astype(jnp.bfloat16), qkv_grad, mix_grad, inner_grad, down_grad, gains_grad, qkv_new[0], mix_new[0], inner_new[0], down_new[0], gains_new[0], qkv_new[1], mix_new[1], inner_new[1], down_new[1], gains_new[1], qkv_new[2], mix_new[2], inner_new[2], down_new[2], gains_new[2])
```

```python
import functools
import math

import jax
import jax.numpy as jnp
from jax import lax
from jax.experimental import pallas as pl
from jax.experimental.pallas import tpu as pltpu
from jax.sharding import PartitionSpec as P

HEADS = 16
Z = 4
MESH = pl.DeviceIdType.MESH
ANY = pl.BlockSpec(memory_space=pl.ANY)
BF = jnp.bfloat16
F32 = jnp.float32

norm_eps = 1e-05
momentum_rate = 0.5
average_rate = 0.5
step_rate = 0.05
VMEM_BYTES = 60 * 1024 * 1024


def nn(a, b):
    return lax.dot_general(a, b, (((1,), (0,)), ((), ())), preferred_element_type=F32)


def nt(a, b):
    return lax.dot_general(a, b, (((1,), (1,)), ((), ())), preferred_element_type=F32)


def tn(a, b):
    return lax.dot_general(a, b, (((0,), (0,)), ((), ())), preferred_element_type=F32)


def scale_rows(values):
    return lax.rsqrt(jnp.mean(values * values, axis=-1, keepdims=True) + norm_eps)


def norm_back(grad_in, normed, gain_row, inverse):
    scaled = grad_in * gain_row
    return inverse * (scaled - normed * jnp.mean(scaled * normed, axis=-1, keepdims=True))


def owner_update(weight, gradient, moment, average, step_size):
    moment_new = momentum_rate * moment + gradient
    weight_new = weight - step_size * (gradient + momentum_rate * moment_new)
    average_new = average_rate * average + (1.0 - average_rate) * weight_new
    return (moment_new, average_new, weight_new)


def gather_kernel(
    inner_peers, attn_own, inner_own, down_own, gains_own, attn, inner, down, gains,
    local_sem, send_z, recv_z, send_x, recv_x, send_c, recv_c, send_y, recv_y, send_r, recv_r,
):
    X = inner_peers
    dp = lax.axis_index("dp")
    fs = lax.axis_index("fsdp")
    y, core = dp // 2, dp % 2
    z, x = fs // X, fs % X
    other_core = (y * 2 + 1 - core, fs)
    other_y = ((1 - y) * 2 + core, fs)

    def z_peer(k):
        return (dp, lax.rem(z + k, Z) * X + x)

    def x_peer(i):
        return (dp, z * X + lax.rem(x + i, X))

    owns = (attn_own, inner_own, down_own, gains_own)
    rows = [o.shape[-2] for o in owns]

    def place(array, source, part=None):
        if array == 0:
            return attn.at[dp if part is None else part, :, pl.ds(source * rows[0], rows[0]), :]
        if array == 1:
            return inner.at[core, pl.ds(source * rows[1], rows[1]), :]
        if array == 2:
            return down.at[core, pl.ds(source * rows[2], rows[2]), :]
        return gains.at[source]

    barrier = pltpu.get_barrier_semaphore()
    peers = [z_peer(k) for k in range(1, Z)] + [x_peer(i) for i in range(1, X)]
    peers += [other_core, other_y]
    for peer in peers:
        pl.semaphore_signal(barrier, inc=1, device_id=peer, device_id_type=MESH)
    pl.semaphore_wait(barrier, len(peers))

    started = []

    def remote(src, dst, ss, rs, peer):
        copy = pltpu.make_async_remote_copy(
            src_ref=src, dst_ref=dst, send_sem=ss, recv_sem=rs, device_id=peer, device_id_type=MESH
        )
        copy.start()
        started.append(copy)
        return copy

    local = []
    for n, own in enumerate(owns):
        copy = pltpu.make_async_copy(own, place(n, fs), local_sem.at[n])
        copy.start()
        local.append(copy)

    def chunk_source(k, i):
        return lax.rem(z - k + Z, Z) * X + lax.rem(x - i + X, X)

    def start_array(n):
        for k in range(1, Z):
            remote(owns[n], place(n, fs), send_z.at[n, k], recv_z.at[n, k], z_peer(k))
        for i in range(1, X):
            remote(owns[n], place(n, fs), send_x.at[n, 0, i], recv_x.at[n, 0, i], x_peer(i))

    def share(n, k, i):
        if n == 3:
            return
        source = chunk_source(k, i)
        src = owns[n] if (k == 0 and i == 0) else place(n, source)
        if n == 0:
            remote(src, place(0, source), send_y.at[k, i], recv_y.at[k, i], other_y)
        remote(src, place(n, source), send_c.at[n, k, i], recv_c.at[n, k, i], other_core)

    def wait_recv(dst, rs, ss):
        pltpu.make_async_remote_copy(
            src_ref=dst, dst_ref=dst, send_sem=ss, recv_sem=rs, device_id=other_core, device_id_type=MESH
        ).wait_recv()

    def pass_on(n):
        share(n, 0, 0)
        for i in range(1, X):
            wait_recv(place(n, chunk_source(0, i)), recv_x.at[n, 0, i], send_x.at[n, 0, i])
            share(n, 0, i)
        for k in range(1, Z):
            source = chunk_source(k, 0)
            wait_recv(place(n, source), recv_z.at[n, k], send_z.at[n, k])
            for i in range(1, X):
                remote(place(n, source), place(n, source), send_x.at[n, k, i], recv_x.at[n, k, i], x_peer(i))
            share(n, k, 0)
        for k in range(1, Z):
            for i in range(1, X):
                wait_recv(place(n, chunk_source(k, i)), recv_x.at[n, k, i], send_x.at[n, k, i])
                share(n, k, i)

    start_array(3)
    start_array(0)
    start_array(1)
    start_array(2)
    pass_on(0)
    pass_on(3)
    pass_on(1)
    pass_on(2)
    part = (1 - y) * 2 + core
    for k in range(Z):
        for i in range(X):
            source = chunk_source(k, i)
            wait_recv(place(0, source, part), recv_y.at[k, i], send_y.at[k, i])
            remote(place(0, source, part), place(0, source, part), send_r.at[k, i], recv_r.at[k, i], other_core)
    for k in range(Z):
        for i in range(X):
            source = chunk_source(k, i)
            wait_recv(place(0, source, (1 - y) * 2 + 1 - core), recv_r.at[k, i], send_r.at[k, i])
            for n in range(3):
                half = y * 2 + 1 - core if n == 0 else None
                dst = place(0, source, half) if n == 0 else (
                    inner.at[1 - core, pl.ds(source * rows[1], rows[1]), :] if n == 1
                    else down.at[1 - core, pl.ds(source * rows[2], rows[2]), :]
                )
                wait_recv(dst, recv_c.at[n, k, i], send_c.at[n, k, i])
    for copy in started:
        copy.wait_send()
    for copy in local:
        copy.wait()


def gather_weights(attn_own, inner_own, down_own, gains_own, fsdp_count):
    X = fsdp_count // Z
    _, rows, width = attn_own.shape
    dma = pltpu.SemaphoreType.DMA
    return pl.pallas_call(
        functools.partial(gather_kernel, X),
        out_shape=(
            jax.ShapeDtypeStruct((4, 2, rows * fsdp_count, width), BF),
            jax.ShapeDtypeStruct((2, inner_own.shape[0] * fsdp_count, inner_own.shape[1]), BF),
            jax.ShapeDtypeStruct((2, down_own.shape[0] * fsdp_count, down_own.shape[1]), BF),
            jax.ShapeDtypeStruct((fsdp_count,) + gains_own.shape, F32),
        ),
        in_specs=[ANY] * 4,
        out_specs=(ANY,) * 4,
        scratch_shapes=[
            dma((4,)), dma((4, Z)), dma((4, Z)), dma((4, Z, X)), dma((4, Z, X)),
            dma((3, Z, X)), dma((3, Z, X)), dma((Z, X)), dma((Z, X)), dma((Z, X)), dma((Z, X)),
        ],
        compiler_params=pltpu.CompilerParams(collective_id=0, has_side_effects=True),
        name="gather_weights",
    )(attn_own, inner_own, down_own, gains_own)


def head_ones(lanes, head_size):
    row = lax.broadcasted_iota(jnp.int32, (lanes, lanes), 0) // head_size
    column = lax.broadcasted_iota(jnp.int32, (lanes, lanes), 1) // head_size
    return (row == column).astype(BF)


KEYS = ((0, 1, 2), (0, 1, 2, 3))


def load_heads(q, k, v, edge):
    frames = q.shape[1]
    first = lax.broadcasted_iota(jnp.int32, (frames, q.shape[2]), 0) == 0
    queries = [q[p].astype(F32) for p in range(2)]
    here_k = [k[p].astype(F32) for p in range(2)]
    here_v = [v[p].astype(F32) for p in range(2)]
    before_k = [jnp.where(first, edge[p : p + 1, :], pltpu.roll(here_k[p], 1, 0)) for p in range(2)]
    before_v = [jnp.where(first, edge[2 + p : 3 + p, :], pltpu.roll(here_v[p], 1, 0)) for p in range(2)]
    return queries, before_k + here_k, before_v + here_v


def head_probs(queries, keys, p, allowed, ones, root_size):
    scores = []
    for n in KEYS[p]:
        s = nn((queries[p] * keys[n]).astype(BF), ones) * (1.0 / root_size)
        scores.append(jnp.where(allowed, s, -1e30) if n < 2 else s)
    top = functools.reduce(jnp.maximum, scores)
    exps = [jnp.exp(s - top) for s in scores]
    exps = [jnp.where(allowed, e, 0.0) if n < 2 else e for n, e in zip(KEYS[p], exps)]
    inverse = 1.0 / functools.reduce(jnp.add, exps)
    return [e * inverse for e in exps]


def attend_kernel(head_size, carried, q, k, v, edge, out):
    ones = head_ones(q.shape[2], head_size)
    allowed = jnp.broadcast_to(carried[...], q.shape[1:]) > 0.5
    queries, keys, values = load_heads(q, k, v, edge)
    for p in range(2):
        probs = head_probs(queries, keys, p, allowed, ones, math.sqrt(head_size))
        mixed = [pr.astype(BF).astype(F32) * values[n] for n, pr in zip(KEYS[p], probs)]
        out[p] = functools.reduce(jnp.add, mixed).astype(BF)


def attend_back_kernel(head_size, carried, q, k, v, edge, mixed_grad, dq, dk, dv, edge_out):
    frames = q.shape[1]
    ones = head_ones(q.shape[2], head_size)
    allowed = jnp.broadcast_to(carried[...], q.shape[1:]) > 0.5
    queries, keys, values = load_heads(q, k, v, edge)
    scale = 1.0 / math.sqrt(head_size)
    key_grads = [0.0] * 4
    value_grads = [0.0] * 4
    for p in range(2):
        probs = head_probs(queries, keys, p, allowed, ones, math.sqrt(head_size))
        grad = mixed_grad[p].astype(F32)
        dprobs = [nn((grad * values[n]).astype(BF), ones) for n in KEYS[p]]
        mean = functools.reduce(jnp.add, [a * b for a, b in zip(probs, dprobs)])
        query_grad = 0.0
        for n, pr, dp in zip(KEYS[p], probs, dprobs):
            ds = (pr * (dp - mean)).astype(BF).astype(F32)
            query_grad = query_grad + ds * keys[n]
            key_grads[n] = key_grads[n] + ds * queries[p]
            value_grads[n] = value_grads[n] + pr.astype(BF).astype(F32) * grad
        dq[p] = (query_grad * scale).astype(BF)
    last = lax.broadcasted_iota(jnp.int32, q.shape[1:], 0) == frames - 1
    for kind, (grads, out, factor) in enumerate(((key_grads, dk, scale), (value_grads, dv, 1.0))):
        for p in range(2):
            before = grads[p] * factor
            total = grads[2 + p] * factor + jnp.where(last, 0.0, pltpu.roll(before, frames - 1, 0))
            out[p] = total.astype(BF)
            row = 2 * kind + p
            edge_out[row : row + 1, :] = before[0:1, :]
            edge_out[4 + row : 5 + row, :] = total[frames - 1 : frames, :]


def attention_specs(frames, width, lanes):
    rows = pl.BlockSpec((2, frames, lanes), lambda j: (0, 0, j))
    edge = pl.BlockSpec((8, lanes), lambda j: (0, j))
    mask = pl.BlockSpec((frames, 1), lambda j: (0, 0))
    return rows, edge, mask


def attend(carried, q, k, v, edge, head_size):
    _, frames, width = q.shape
    lanes = 256
    rows, edge_spec, mask = attention_specs(frames, width, lanes)
    return pl.pallas_call(
        functools.partial(attend_kernel, head_size),
        grid=(width // lanes,),
        out_shape=jax.ShapeDtypeStruct(q.shape, BF),
        in_specs=[mask, rows, rows, rows, edge_spec],
        out_specs=rows,
        compiler_params=pltpu.CompilerParams(vmem_limit_bytes=VMEM_BYTES),
        name="attend",
    )(carried, q, k, v, edge)


def attend_back(carried, q, k, v, edge, mixed_grad, head_size):
    _, frames, width = q.shape
    lanes = 256
    rows, edge_spec, mask = attention_specs(frames, width, lanes)
    return pl.pallas_call(
        functools.partial(attend_back_kernel, head_size),
        grid=(width // lanes,),
        out_shape=(jax.ShapeDtypeStruct(q.shape, BF),) * 3 + (jax.ShapeDtypeStruct((8, width), F32),),
        in_specs=[mask, rows, rows, rows, edge_spec, rows],
        out_specs=(rows, rows, rows, edge_spec),
        compiler_params=pltpu.CompilerParams(vmem_limit_bytes=VMEM_BYTES),
        name="attend_back",
    )(carried, q, k, v, edge, mixed_grad)


def feed_forward_kernel(b, c, inner, down, out, back, inner_grad, down_grad):
    half = down.shape[2]

    @pl.when(pl.program_id(0) == 0)
    def _():
        out[...] = jnp.zeros_like(out)
        back[...] = jnp.zeros_like(back)

    rows, cot = b[...], c[...]
    gate = nn(rows, inner[0])
    up = nn(rows, inner[1])
    squashed = jax.nn.sigmoid(gate)
    active = gate * squashed
    hidden = (active * up).astype(BF)
    hidden_grad = nt(cot[:, :half], down[0]) + nt(cot[:, half:], down[1])
    gate_grad = (hidden_grad * up * (squashed * (1.0 + gate * (1.0 - squashed)))).astype(BF)
    up_grad = (hidden_grad * active).astype(BF)
    for n in range(2):
        part = slice(n * half, (n + 1) * half)
        down_grad[n] = tn(hidden, cot[:, part]).astype(BF)
        out[:, part] += nn(hidden, down[n])
    inner_grad[0] = tn(rows, gate_grad).astype(BF)
    inner_grad[1] = tn(rows, up_grad).astype(BF)
    back[...] += nt(gate_grad, inner[0]) + nt(up_grad, inner[1])


def feed_forward(b, c, inner, down):
    rows, width = b.shape
    _, _, hidden = inner.shape
    step = 256
    whole = pl.BlockSpec((rows, width), lambda j: (0, 0))
    inner_spec = pl.BlockSpec((2, width, step), lambda j: (0, 0, j))
    down_spec = pl.BlockSpec((2, step, down.shape[2]), lambda j: (0, j, 0))
    return pl.pallas_call(
        feed_forward_kernel,
        grid=(hidden // step,),
        out_shape=(
            jax.ShapeDtypeStruct((rows, width), F32),
            jax.ShapeDtypeStruct((rows, width), F32),
            jax.ShapeDtypeStruct(inner.shape, BF),
            jax.ShapeDtypeStruct(down.shape, BF),
        ),
        in_specs=[whole, whole, inner_spec, down_spec],
        out_specs=(whole, whole, inner_spec, down_spec),
        compiler_params=pltpu.CompilerParams(vmem_limit_bytes=VMEM_BYTES),
        cost_estimate=pl.CostEstimate(flops=18 * rows * width * hidden, bytes_accessed=60 * 2**20, transcendentals=0),
        name="feed_forward",
    )(b, c, inner, down)


def per_device(
    frames, cotangent, segment_ids,
    qkv_weight, mix_weight, inner_weight, down_weight, norm_gains,
    qkv_moment, mix_moment, inner_moment, down_moment, gains_moment,
    qkv_average, mix_average, inner_average, down_average, gains_average,
):
    frame_count, positions, width = frames.shape
    head_size = width // HEADS
    hidden = inner_weight.shape[2] // 2
    dp_count, fsdp_count = lax.axis_size("dp"), lax.axis_size("fsdp")
    X = fsdp_count // Z
    devices = dp_count * fsdp_count
    total_frames = frame_count * devices
    dp, fs = lax.axis_index("dp"), lax.axis_index("fsdp")
    y, core = dp // 2, dp % 2
    z, x = fs // X, fs % X
    axes = ("dp", "fsdp")

    def permute(value, target):
        pairs = []
        for d in range(dp_count):
            for f in range(fsdp_count):
                to = target(d, f)
                if to is not None:
                    pairs.append((d * fsdp_count + f, to[0] * fsdp_count + to[1]))
        return lax.ppermute(value, axes, pairs)

    def to_core(value):
        return permute(value, lambda d, f: (d ^ 1, f))

    def to_y(value):
        return permute(value, lambda d, f: (d ^ 2, f))

    def to_x(value, i):
        return permute(value, lambda d, f: (d, (f // X) * X + (f % X + i) % X))

    def to_z(value, k):
        return permute(value, lambda d, f: (d, ((f // X + k) % Z) * X + f % X))

    def shifted(value, steps):
        def target(d, f):
            to = d * fsdp_count + f + steps
            return divmod(to, fsdp_count) if 0 <= to < devices else None

        return permute(value, target)

    device = dp * fsdp_count + fs
    padded_ids = jnp.concatenate([jnp.full((1,), -1, jnp.int32), segment_ids])
    window = lax.dynamic_slice_in_dim(padded_ids, device * frame_count, frame_count + 1)
    carried = (window[1:] == window[:-1]).astype(F32)[:, None]

    attn_own = lax.select_n(
        dp, qkv_weight[:, :, :width], qkv_weight[:, :, width : 2 * width], qkv_weight[:, :, 2 * width :], mix_weight
    ).astype(BF)
    inner_own = lax.dynamic_slice(
        inner_weight, (y, 0, core * hidden), (1, inner_weight.shape[1], hidden)
    )[0].astype(BF)
    half_width = width // 2
    down_own = lax.dynamic_slice(
        down_weight, (y, 0, core * half_width), (1, down_weight.shape[1], half_width)
    )[0].astype(BF)
    own_gains = norm_gains.astype(BF).astype(F32)
    gains_own = jnp.zeros((8, 128), F32).at[: own_gains.shape[0], : own_gains.shape[1]].set(own_gains)
    attn, inner, down, gains_all = gather_weights(attn_own, inner_own, down_own, gains_own, fsdp_count)
    gains = gains_all[:, :2, : own_gains.shape[1]].transpose(1, 0, 2).reshape(2, width)

    xf = frames.transpose(1, 0, 2).astype(F32)
    cot = cotangent.transpose(1, 0, 2)
    cot_there = to_y(lax.dynamic_index_in_dim(cot, 1 - y, 0, keepdims=False))
    r1 = scale_rows(xf)
    n1 = xf * r1
    a = (n1 * gains[0]).astype(BF)

    def each(left, right):
        return jnp.einsum("pfd,pde->pfe", left, right, preferred_element_type=F32)

    q, k, v = (each(a, attn[t]).astype(BF) for t in range(3))
    edge_rows = shifted(jnp.concatenate([k[:, -1], v[:, -1]], axis=0), 1)
    edge = jnp.pad(edge_rows.astype(F32), ((0, 4), (0, 0)))
    mixed = attend(carried, q, k, v, edge, head_size)
    hres = xf + each(mixed, attn[3])
    r2 = scale_rows(hres)
    n2 = hres * r2
    b = (n2 * gains[1]).astype(BF)

    b_there = to_y(lax.dynamic_index_in_dim(b, 1 - y, 0, keepdims=False))
    b_rows = jnp.concatenate([lax.dynamic_index_in_dim(b, y, 0, keepdims=False), b_there], axis=0)
    c_rows = jnp.concatenate([lax.dynamic_index_in_dim(cot, y, 0, keepdims=False), cot_there], axis=0)
    out, back, inner_part, down_part = feed_forward(b_rows, c_rows, inner, down)
    both = to_y(jnp.stack([out[frame_count:], back[frame_count:]]).astype(BF)).astype(F32)

    def by_position(mine, theirs):
        return jnp.where(y == 0, jnp.stack([mine, theirs]), jnp.stack([theirs, mine]))

    layer_out = (hres + by_position(out[:frame_count], both[0])).astype(BF).transpose(1, 0, 2)
    db = by_position(back[:frame_count], both[1])

    e2 = jnp.sum(db * n2, axis=(0, 1))
    dh = cot.astype(F32) + norm_back(db, n2, gains[1], r2)
    dhb = dh.astype(BF)

    def back_each(left, right):
        return jnp.einsum("pfe,pde->pfd", left, right, preferred_element_type=F32)

    def grad_each(left, right):
        return jnp.einsum("pfd,pfe->pde", left, right, preferred_element_type=F32).astype(BF)

    mixed_grad = back_each(dhb, attn[3]).astype(BF)
    dq, dk, dv, edges = attend_back(carried, q, k, v, edge, mixed_grad, head_size)
    edge_back = shifted(edges[:4], -1)
    last = (edges[4:] + edge_back).astype(BF)
    dk = lax.dynamic_update_slice(dk, last[:2, None], (0, frame_count - 1, 0))
    dv = lax.dynamic_update_slice(dv, last[2:, None], (0, frame_count - 1, 0))
    attn_part = [grad_each(a, dq), grad_each(a, dk), grad_each(a, dv), grad_each(mixed, dhb)]
    da = back_each(dq, attn[0]) + back_each(dk, attn[1]) + back_each(dv, attn[2])
    e1 = jnp.sum(da * n1, axis=(0, 1))
    frames_grad = (dh + norm_back(da, n1, gains[0], r1)).astype(BF).transpose(1, 0, 2)

    def add(left, right):
        return (left.astype(F32) + right.astype(F32)).astype(BF)

    def at(value, index):
        return lax.dynamic_index_in_dim(value, index, 0, keepdims=False)

    def over_fsdp(value):
        grid = value.reshape((Z, X) + value.shape[1:])
        column = lax.dynamic_index_in_dim(grid, x, 1, keepdims=False)
        for i in range(1, X):
            column = add(column, to_x(lax.dynamic_index_in_dim(grid, lax.rem(x + i, X), 1, keepdims=False), i))
        total = at(column, z).astype(F32)
        for k in range(1, Z):
            total = total + to_z(at(column, lax.rem(z + k, Z)), k).astype(F32)
        return total

    def over_fsdp_rows(value):
        return over_fsdp(value.reshape((fsdp_count, value.shape[0] // fsdp_count) + value.shape[1:]))

    down_half = add(at(down_part, core), to_core(at(down_part, 1 - core)))
    inner_half = add(at(inner_part, core), to_core(at(inner_part, 1 - core)))
    down_mine = over_fsdp_rows(down_half).astype(BF)
    inner_mine = over_fsdp_rows(inner_half).astype(BF)

    parts = jnp.stack(attn_part).reshape(2, 2, 2 * width, width)
    pair = add(
        lax.dynamic_index_in_dim(parts, core, 1, keepdims=False),
        to_core(lax.dynamic_index_in_dim(parts, 1 - core, 1, keepdims=False)),
    )
    quarter = add(at(pair, y), to_y(at(pair, 1 - y)))
    quarter = quarter.reshape(2, fsdp_count, width // fsdp_count, width)
    attn_mine = jnp.stack(
        [over_fsdp(quarter[p]) for p in range(2)]
    ).astype(BF)

    def share_y(value):
        theirs = to_y(value)
        mine = jnp.where(y == 0, jnp.stack([value, theirs]), jnp.stack([theirs, value]))
        return mine

    def share_all(value):
        pair_y = share_y(value)
        others = to_core(pair_y)
        return jnp.where(core == 0, jnp.stack([pair_y, others], 1), jnp.stack([others, pair_y], 1))

    down_all = share_all(down_mine).astype(F32)
    inner_all = share_all(inner_mine).astype(F32)
    attn_all = share_all(attn_mine).astype(F32)
    down_grad = jnp.concatenate([down_all[:, 0], down_all[:, 1]], axis=-1)
    inner_grad = jnp.concatenate([inner_all[:, 0], inner_all[:, 1]], axis=-1)
    qkv_grad = jnp.concatenate([attn_all[0, 0], attn_all[0, 1], attn_all[1, 0]], axis=-1)
    mix_grad = attn_all[1, 1]

    gains_part = jnp.stack([e1, e2])
    gains_part = gains_part + to_core(gains_part)
    gains_part = gains_part + to_y(gains_part)
    gains_grid = gains_part.reshape(2, Z, X, -1).transpose(1, 2, 0, 3)
    column = lax.dynamic_index_in_dim(gains_grid, x, 1, keepdims=False)
    for i in range(1, X):
        column = column + to_x(lax.dynamic_index_in_dim(gains_grid, lax.rem(x + i, X), 1, keepdims=False), i)
    gains_grad = at(column, z)
    for kk in range(1, Z):
        gains_grad = gains_grad + to_z(at(column, lax.rem(z + kk, Z)), kk)

    step_size = step_rate / math.sqrt(total_frames)
    grads = (qkv_grad, mix_grad, inner_grad, down_grad, gains_grad)
    new = [
        owner_update(w, g, m, av, step_size)
        for w, g, m, av in zip(
            (qkv_weight, mix_weight, inner_weight, down_weight, norm_gains),
            grads,
            (qkv_moment, mix_moment, inner_moment, down_moment, gains_moment),
            (qkv_average, mix_average, inner_average, down_average, gains_average),
        )
    ]
    return (
        (layer_out, frames_grad) + grads
        + tuple(n[0] for n in new) + tuple(n[1] for n in new) + tuple(n[2] for n in new)
    )


def solution(mesh):
    rows = P(("dp", "fsdp"), None, None)
    weight = P(None, "fsdp", None)
    gains = P(None, "fsdp")
    weights = (weight,) * 4 + (gains,)
    return jax.shard_map(
        per_device,
        mesh=mesh,
        in_specs=(rows, rows, P()) + weights * 3,
        out_specs=(rows, rows) + weights * 4,
        check_vma=False,
    )
```

```python
import functools
import math

import jax
import jax.numpy as jnp
from jax import lax
from jax.experimental import pallas as pl
from jax.experimental.pallas import tpu as pltpu
from jax.sharding import PartitionSpec as P

HEADS = 16
Z = 4
MESH = pl.DeviceIdType.MESH
ANY = pl.BlockSpec(memory_space=pl.ANY)
BF = jnp.bfloat16
F32 = jnp.float32

norm_eps = 1e-05
momentum_rate = 0.5
average_rate = 0.5
step_rate = 0.05
VMEM_BYTES = 60 * 1024 * 1024


def nn(a, b):
    return lax.dot_general(a, b, (((1,), (0,)), ((), ())), preferred_element_type=F32)


def nt(a, b):
    return lax.dot_general(a, b, (((1,), (1,)), ((), ())), preferred_element_type=F32)


def tn(a, b):
    return lax.dot_general(a, b, (((0,), (0,)), ((), ())), preferred_element_type=F32)


def scale_rows(values):
    return lax.rsqrt(jnp.mean(values * values, axis=-1, keepdims=True) + norm_eps)


def norm_back(grad_in, normed, gain_row, inverse):
    scaled = grad_in * gain_row
    return inverse * (scaled - normed * jnp.mean(scaled * normed, axis=-1, keepdims=True))


def owner_update(weight, gradient, moment, average, step_size):
    moment_new = momentum_rate * moment + gradient
    weight_new = weight - step_size * (gradient + momentum_rate * moment_new)
    average_new = average_rate * average + (1.0 - average_rate) * weight_new
    return (moment_new, average_new, weight_new)


def gather_kernel(
    inner_peers, attn_own, inner_own, down_own, gains_own, attn, inner, down, gains,
    local_sem, send_z, recv_z, send_x, recv_x, send_c, recv_c, send_y, recv_y, send_r, recv_r,
):
    X = inner_peers
    dp = lax.axis_index("dp")
    fs = lax.axis_index("fsdp")
    y, core = dp // 2, dp % 2
    z, x = fs // X, fs % X
    other_core = (y * 2 + 1 - core, fs)
    other_y = ((1 - y) * 2 + core, fs)

    def z_peer(k):
        return (dp, lax.rem(z + k, Z) * X + x)

    def x_peer(i):
        return (dp, z * X + lax.rem(x + i, X))

    owns = (attn_own, inner_own, down_own, gains_own)
    rows = [o.shape[-2] for o in owns]

    def place(array, source, part=None):
        if array == 0:
            return attn.at[dp if part is None else part, :, pl.ds(source * rows[0], rows[0]), :]
        if array == 1:
            return inner.at[core, pl.ds(source * rows[1], rows[1]), :]
        if array == 2:
            return down.at[core, pl.ds(source * rows[2], rows[2]), :]
        return gains.at[source]

    barrier = pltpu.get_barrier_semaphore()
    peers = [z_peer(k) for k in range(1, Z)] + [x_peer(i) for i in range(1, X)]
    peers += [other_core, other_y]
    for peer in peers:
        pl.semaphore_signal(barrier, inc=1, device_id=peer, device_id_type=MESH)
    pl.semaphore_wait(barrier, len(peers))

    started = []

    def remote(src, dst, ss, rs, peer):
        copy = pltpu.make_async_remote_copy(
            src_ref=src, dst_ref=dst, send_sem=ss, recv_sem=rs, device_id=peer, device_id_type=MESH
        )
        copy.start()
        started.append(copy)
        return copy

    local = []
    for n, own in enumerate(owns):
        copy = pltpu.make_async_copy(own, place(n, fs), local_sem.at[n])
        copy.start()
        local.append(copy)

    def chunk_source(k, i):
        return lax.rem(z - k + Z, Z) * X + lax.rem(x - i + X, X)

    def start_array(n):
        for k in range(1, Z):
            remote(owns[n], place(n, fs), send_z.at[n, k], recv_z.at[n, k], z_peer(k))
        for i in range(1, X):
            remote(owns[n], place(n, fs), send_x.at[n, 0, i], recv_x.at[n, 0, i], x_peer(i))

    def share(n, k, i):
        if n == 3:
            return
        source = chunk_source(k, i)
        src = owns[n] if (k == 0 and i == 0) else place(n, source)
        if n == 0:
            remote(src, place(0, source), send_y.at[k, i], recv_y.at[k, i], other_y)
        remote(src, place(n, source), send_c.at[n, k, i], recv_c.at[n, k, i], other_core)

    def wait_recv(dst, rs, ss):
        pltpu.make_async_remote_copy(
            src_ref=dst, dst_ref=dst, send_sem=ss, recv_sem=rs, device_id=other_core, device_id_type=MESH
        ).wait_recv()

    def pass_on(n):
        share(n, 0, 0)
        for i in range(1, X):
            wait_recv(place(n, chunk_source(0, i)), recv_x.at[n, 0, i], send_x.at[n, 0, i])
            share(n, 0, i)
        for k in range(1, Z):
            source = chunk_source(k, 0)
            wait_recv(place(n, source), recv_z.at[n, k], send_z.at[n, k])
            for i in range(1, X):
                remote(place(n, source), place(n, source), send_x.at[n, k, i], recv_x.at[n, k, i], x_peer(i))
            share(n, k, 0)
        for k in range(1, Z):
            for i in range(1, X):
                wait_recv(place(n, chunk_source(k, i)), recv_x.at[n, k, i], send_x.at[n, k, i])
                share(n, k, i)

    start_array(3)
    start_array(0)
    start_array(1)
    start_array(2)
    pass_on(0)
    pass_on(3)
    pass_on(1)
    pass_on(2)
    part = (1 - y) * 2 + core
    for k in range(Z):
        for i in range(X):
            source = chunk_source(k, i)
            wait_recv(place(0, source, part), recv_y.at[k, i], send_y.at[k, i])
            remote(place(0, source, part), place(0, source, part), send_r.at[k, i], recv_r.at[k, i], other_core)
    for k in range(Z):
        for i in range(X):
            source = chunk_source(k, i)
            wait_recv(place(0, source, (1 - y) * 2 + 1 - core), recv_r.at[k, i], send_r.at[k, i])
            for n in range(3):
                half = y * 2 + 1 - core if n == 0 else None
                dst = place(0, source, half) if n == 0 else (
                    inner.at[1 - core, pl.ds(source * rows[1], rows[1]), :] if n == 1
                    else down.at[1 - core, pl.ds(source * rows[2], rows[2]), :]
                )
                wait_recv(dst, recv_c.at[n, k, i], send_c.at[n, k, i])
    for copy in started:
        copy.wait_send()
    for copy in local:
        copy.wait()


def gather_weights(attn_own, inner_own, down_own, gains_own, fsdp_count):
    X = fsdp_count // Z
    _, rows, width = attn_own.shape
    dma = pltpu.SemaphoreType.DMA
    return pl.pallas_call(
        functools.partial(gather_kernel, X),
        out_shape=(
            jax.ShapeDtypeStruct((4, 2, rows * fsdp_count, width), BF),
            jax.ShapeDtypeStruct((2, inner_own.shape[0] * fsdp_count, inner_own.shape[1]), BF),
            jax.ShapeDtypeStruct((2, down_own.shape[0] * fsdp_count, down_own.shape[1]), BF),
            jax.ShapeDtypeStruct((fsdp_count,) + gains_own.shape, F32),
        ),
        in_specs=[ANY] * 4,
        out_specs=(ANY,) * 4,
        scratch_shapes=[
            dma((4,)), dma((4, Z)), dma((4, Z)), dma((4, Z, X)), dma((4, Z, X)),
            dma((3, Z, X)), dma((3, Z, X)), dma((Z, X)), dma((Z, X)), dma((Z, X)), dma((Z, X)),
        ],
        compiler_params=pltpu.CompilerParams(collective_id=0, has_side_effects=True),
        name="gather_weights",
    )(attn_own, inner_own, down_own, gains_own)


def head_ones(lanes, head_size):
    row = lax.broadcasted_iota(jnp.int32, (lanes, lanes), 0) // head_size
    column = lax.broadcasted_iota(jnp.int32, (lanes, lanes), 1) // head_size
    return (row == column).astype(BF)


KEYS = ((0, 1, 2), (0, 1, 2, 3))


def load_heads(q, k, v, edge):
    frames = q.shape[1]
    first = lax.broadcasted_iota(jnp.int32, (frames, q.shape[2]), 0) == 0
    queries = [q[p].astype(F32) for p in range(2)]
    here_k = [k[p].astype(F32) for p in range(2)]
    here_v = [v[p].astype(F32) for p in range(2)]
    before_k = [jnp.where(first, edge[p : p + 1, :], pltpu.roll(here_k[p], 1, 0)) for p in range(2)]
    before_v = [jnp.where(first, edge[2 + p : 3 + p, :], pltpu.roll(here_v[p], 1, 0)) for p in range(2)]
    return queries, before_k + here_k, before_v + here_v


def head_probs(queries, keys, p, allowed, ones, root_size):
    scores = []
    for n in KEYS[p]:
        s = nn((queries[p] * keys[n]).astype(BF), ones) * (1.0 / root_size)
        scores.append(jnp.where(allowed, s, -1e30) if n < 2 else s)
    top = functools.reduce(jnp.maximum, scores)
    exps = [jnp.exp(s - top) for s in scores]
    exps = [jnp.where(allowed, e, 0.0) if n < 2 else e for n, e in zip(KEYS[p], exps)]
    inverse = 1.0 / functools.reduce(jnp.add, exps)
    return [e * inverse for e in exps]


def attend_kernel(head_size, carried, q, k, v, edge, out):
    ones = head_ones(q.shape[2], head_size)
    allowed = jnp.broadcast_to(carried[...], q.shape[1:]) > 0.5
    queries, keys, values = load_heads(q, k, v, edge)
    for p in range(2):
        probs = head_probs(queries, keys, p, allowed, ones, math.sqrt(head_size))
        mixed = [pr.astype(BF).astype(F32) * values[n] for n, pr in zip(KEYS[p], probs)]
        out[p] = functools.reduce(jnp.add, mixed).astype(BF)


def attention_specs(frames, width, lanes):
    rows = pl.BlockSpec((2, frames, lanes), lambda j: (0, 0, j))
    edge = pl.BlockSpec((8, lanes), lambda j: (0, j))
    mask = pl.BlockSpec((frames, 1), lambda j: (0, 0))
    return rows, edge, mask


def attend(carried, q, k, v, edge, head_size):
    _, frames, width = q.shape
    lanes = 256
    rows, edge_spec, mask = attention_specs(frames, width, lanes)
    return pl.pallas_call(
        functools.partial(attend_kernel, head_size),
        grid=(width // lanes,),
        out_shape=jax.ShapeDtypeStruct(q.shape, BF),
        in_specs=[mask, rows, rows, rows, edge_spec],
        out_specs=rows,
        compiler_params=pltpu.CompilerParams(vmem_limit_bytes=VMEM_BYTES),
        name="attend",
    )(carried, q, k, v, edge)


def remote_copy(src, dst, send_sem, recv_sem, peer):
    return pltpu.make_async_remote_copy(
        src_ref=src, dst_ref=dst, send_sem=send_sem, recv_sem=recv_sem, device_id=peer, device_id_type=MESH
    )


def feed_forward_kernel(
    X, J, b, c, inner, down, out_mine, back_mine, out_theirs, back_recv, inner_all, down_sum,
    out, back, down_here, down_there, down_from_core, mine, other, from_core, summed, from_x, column, from_z, final, staged,
    s1, r1, s2, r2, s3, r3, s5, r5, s6, r6, s7, r7, local_sem,
):
    j = pl.program_id(0)
    half = down.shape[2]
    rows_here = out_mine.shape[0]
    R, step = final.shape[1:]
    dp, fs = lax.axis_index("dp"), lax.axis_index("fsdp")
    y, core = dp // 2, dp % 2
    z, x = fs // X, fs % X
    core_peer = (y * 2 + 1 - core, fs)
    y_peer = ((1 - y) * 2 + core, fs)

    def z_peer(k):
        return (dp, lax.rem(z + k, Z) * X + x)

    def x_peer(i):
        return (dp, z * X + lax.rem(x + i, X))

    def dp_peer(d):
        return (((y + d // 2) % 2) * 2 + (core + d % 2) % 2, fs)

    def to_core(n):
        return remote_copy(other.at[n % 2], from_core.at[n], s1.at[n % 2], r1.at[n], core_peer)

    def to_x(n, i):
        return remote_copy(
            summed.at[n % 2, :, lax.rem(x + i, X)], from_x.at[n, i - 1], s2.at[n % 2, i - 1], r2.at[n, i - 1], x_peer(i)
        )

    def to_z(n, k):
        return remote_copy(
            column.at[n % 2, lax.rem(z + k, Z)], from_z.at[n, k - 1], s3.at[n % 2, k - 1], r3.at[n, k - 1], z_peer(k)
        )

    def place(n, owner):
        return inner_all.at[owner, :, pl.ds(pl.multiple_of(n * step, step), step)]

    def share(n, d):
        return remote_copy(final.at[n], place(n, dp), s5.at[n, d - 1], r5.at[n, d - 1], dp_peer(d))

    def keep(n):
        return pltpu.make_async_copy(final.at[n], place(n, dp), local_sem.at[n])

    exchange = remote_copy(staged, back_recv, s6, r6, y_peer)

    def down_to_core(n):
        return remote_copy(down_there.at[n % 2], down_from_core.at[n], s7.at[n % 2], r7.at[n], core_peer)

    @pl.when(j == 0)
    def _():
        barrier = pltpu.get_barrier_semaphore()
        peers = [z_peer(k) for k in range(1, Z)] + [x_peer(i) for i in range(1, X)]
        peers += [dp_peer(d) for d in range(1, 4)]
        for peer in peers:
            pl.semaphore_signal(barrier, inc=1, device_id=peer, device_id_type=MESH)
        pl.semaphore_wait(barrier, len(peers))
        out[...] = jnp.zeros_like(out)
        back[...] = jnp.zeros_like(back)

    @pl.when((j >= 1) & (j < J + 1))
    def _():
        n = j - 1
        to_core(n).wait_recv()

        @pl.when(n >= 2)
        def _():
            for i in range(1, X):
                to_x(n - 2, i).wait_send()

        down_to_core(n).wait_recv()
        down_sum[...] = (down_here[n % 2].astype(F32) + down_from_core[n].astype(F32)).astype(BF)
        total = (mine[n % 2].astype(F32) + from_core[n].astype(F32)).astype(BF)
        summed[n % 2] = total.reshape(summed.shape[1:])
        for i in range(1, X):
            to_x(n, i).start()

    @pl.when((j >= 2) & (j < J + 2))
    def _():
        n = j - 2
        for i in range(1, X):
            to_x(n, i).wait_recv()

        @pl.when(n >= 2)
        def _():
            for k in range(1, Z):
                to_z(n - 2, k).wait_send()

        total = summed[n % 2, :, x].astype(F32)
        for i in range(1, X):
            total = total + from_x[n, i - 1].astype(F32)
        column[n % 2] = total.astype(BF)
        for k in range(1, Z):
            to_z(n, k).start()

    @pl.when(j >= 3)
    def _():
        n = j - 3
        for k in range(1, Z):
            to_z(n, k).wait_recv()
        total = column[n % 2, z].astype(F32)
        for k in range(1, Z):
            total = total + from_z[n, k - 1].astype(F32)
        final[n] = total.astype(BF)
        keep(n).start()
        for d in range(1, 4):
            share(n, d).start()

    @pl.when(j < J)
    def _():
        rows, cot = b[...], c[...]
        gate = nn(rows, inner[0])
        up = nn(rows, inner[1])
        squashed = jax.nn.sigmoid(gate)
        active = gate * squashed
        hidden = (active * up).astype(BF)
        hidden_grad = nt(cot[:, :half], down[0]) + nt(cot[:, half:], down[1])
        gate_grad = (hidden_grad * up * (squashed * (1.0 + gate * (1.0 - squashed)))).astype(BF)
        up_grad = (hidden_grad * active).astype(BF)
        gate_term = tn(rows, gate_grad).astype(BF)
        up_term = tn(rows, up_grad).astype(BF)

        @pl.when(j >= 2)
        def _():
            to_core(j - 2).wait_send()
            down_to_core(j - 2).wait_send()

        mine[j % 2] = jnp.where(core == 0, gate_term, up_term)
        other[j % 2] = jnp.where(core == 0, up_term, gate_term)
        to_core(j).start()
        down_term = tn(hidden, cot).astype(BF)
        down_here[j % 2] = jnp.where(core == 0, down_term[:, :half], down_term[:, half:])
        down_there[j % 2] = jnp.where(core == 0, down_term[:, half:], down_term[:, :half])
        down_to_core(j).start()
        for n in range(2):
            part = slice(n * half, (n + 1) * half)
            out[:, part] += nn(hidden, down[n])
        back[...] += nt(gate_grad, inner[0]) + nt(up_grad, inner[1])

    @pl.when(j == J - 1)
    def _():
        staged[...] = back[rows_here:, :].astype(BF)
        exchange.start()
        out_theirs[...] = out[rows_here:, :].astype(BF)
        out_mine[...] = out[:rows_here, :]
        back_mine[...] = back[:rows_here, :]

    @pl.when(j == J + 2)
    def _():
        for n in (J - 2, J - 1):
            to_core(n).wait_send()
            down_to_core(n).wait_send()
            for i in range(1, X):
                to_x(n, i).wait_send()
            for k in range(1, Z):
                to_z(n, k).wait_send()

        def finish(n, carry):
            keep(n).wait()
            for d in range(1, 4):
                share(n, d).wait()
            return carry

        lax.fori_loop(0, J, finish, 0)
        exchange.wait()


def feed_forward(b, c, inner, down, fsdp_count):
    rows, width = b.shape
    _, _, hidden = inner.shape
    half = down.shape[2]
    step = 256
    J = hidden // step
    X = fsdp_count // Z
    R = width // fsdp_count
    whole = pl.BlockSpec((rows, width), lambda j: (0, 0), pipeline_mode=pl.Buffered(1))
    part = pl.BlockSpec((rows // 2, width), lambda j: (0, 0), pipeline_mode=pl.Buffered(1))
    inner_spec = pl.BlockSpec((2, width, step), lambda j: (0, 0, jnp.minimum(j, J - 1)))
    down_spec = pl.BlockSpec((2, step, half), lambda j: (0, jnp.minimum(j, J - 1), 0))
    sum_spec = pl.BlockSpec((step, half), lambda j: (jnp.clip(j - 1, 0, J - 1), 0))
    dma, vmem = pltpu.SemaphoreType.DMA, pltpu.VMEM
    return pl.pallas_call(
        functools.partial(feed_forward_kernel, X, J),
        grid=(J + 3,),
        out_shape=(
            jax.ShapeDtypeStruct((rows // 2, width), F32),
            jax.ShapeDtypeStruct((rows // 2, width), F32),
            jax.ShapeDtypeStruct((rows // 2, width), BF),
            jax.ShapeDtypeStruct((rows // 2, width), BF),
            jax.ShapeDtypeStruct((4, R, hidden), BF),
            jax.ShapeDtypeStruct((hidden, half), BF),
        ),
        in_specs=[whole, whole, inner_spec, down_spec],
        out_specs=(part, part, part, ANY, ANY, sum_spec),
        scratch_shapes=[
            vmem((rows, width), F32), vmem((rows, width), F32),
            vmem((2, step, half), BF), vmem((2, step, half), BF), vmem((J, step, half), BF),
            vmem((2, width, step), BF), vmem((2, width, step), BF), vmem((J, width, step), BF),
            vmem((2, Z, X, R, step), BF), vmem((J, X - 1, Z, R, step), BF),
            vmem((2, Z, R, step), BF), vmem((J, Z - 1, R, step), BF),
            vmem((J, R, step), BF), vmem((rows // 2, width), BF),
            dma((2,)), dma((J,)), dma((2, X - 1)), dma((J, X - 1)), dma((2, Z - 1)), dma((J, Z - 1)),
            dma((J, 3)), dma((J, 3)), dma, dma, dma((2,)), dma((J,)), dma((J,)),
        ],
        compiler_params=pltpu.CompilerParams(
            vmem_limit_bytes=VMEM_BYTES, collective_id=1, has_side_effects=True
        ),
        cost_estimate=pl.CostEstimate(flops=18 * rows * width * hidden, bytes_accessed=60 * 2**20, transcendentals=0),
        name="feed_forward",
    )(b, c, inner, down)


PAIRS = ((0, 0), (0, 1), (0, 2), (1, 0), (1, 1), (1, 2), (1, 3))
CHUNK = 32


def total_of(values):
    return functools.reduce(jnp.add, values)


def attention_back_kernel(
    X, groups, head_size, carried, q, k, v, edge, mix, dhb, mixed, inputs, proj, down_sum, out_send,
    da, attn_all, down_all, out_recv,
    mixed_grad, before, terms_before, terms_here, tails, grads, edge_send, edge_recv,
    mine, other, from_core, keep_y, send_y, from_y, summed, from_x, column, from_z, final, plane, from_plane, final_plane,
    down_column, down_from_x, down_from_z, down_final,
    s_edge, r_edge, s1, r1, sy, ry, sxa, rxa, sxb, rxb, sz, rz, sf, rf, sp, rp, sc, rc, local_sem,
    sdx, rdx, sdz, rdz, sdf, rdf, down_sem, s_out, r_out, free,
):
    i = pl.program_id(0)
    frames, step = q.shape[1:]
    R = final.shape[1]
    dp, fs = lax.axis_index("dp"), lax.axis_index("fsdp")
    F = Z * X
    y, core = dp // 2, dp % 2
    z, x = fs // X, fs % X
    me = dp * F + fs
    devices = 4 * F
    core_peer = (y * 2 + 1 - core, fs)
    y_peer = ((1 - y) * 2 + core, fs)
    before_me = ((me - 1 + devices) % devices // F, (me - 1 + devices) % devices % F)
    after_me = ((me + 1) % devices // F, (me + 1) % devices % F)

    def z_peer(n):
        return (dp, lax.rem(z + n, Z) * X + x)

    def x_peer(n):
        return (dp, z * X + lax.rem(x + n, X))

    def dp_peer(d):
        return (((y + d // 2) % 2) * 2 + (core + d % 2) % 2, fs)

    def to_before(n):
        return remote_copy(edge_send.at[n % 2], edge_recv.at[n], s_edge.at[n % 2], r_edge.at[n], before_me)

    def to_core(n):
        return remote_copy(other, from_core.at[n % 2], s1, r1.at[n % 2], core_peer)

    def to_y(n):
        return remote_copy(send_y.at[n % 2], from_y.at[n], sy.at[n % 2], ry.at[n], y_peer)

    def to_x_early(n, j):
        return remote_copy(
            summed.at[n % 2, pl.ds(1, 2), :, lax.rem(x + j, X)], from_x.at[n, j - 1, pl.ds(1, 2)],
            sxa.at[n % 2, j - 1], rxa.at[n, j - 1], x_peer(j),
        )

    def to_x_late(n, j):
        return remote_copy(
            summed.at[n % 2, 0, :, lax.rem(x + j, X)], from_x.at[n, j - 1, 0],
            sxb.at[n % 2, j - 1], rxb.at[n, j - 1], x_peer(j),
        )

    def to_z(n, j):
        return remote_copy(
            column.at[n % 2, :, lax.rem(z + j, Z)], from_z.at[n, j - 1], sz.at[n % 2, j - 1], rz.at[n, j - 1], z_peer(j)
        )

    def place(n, t):
        return attn_all.at[t, core, :, pl.ds(pl.multiple_of(n * step, step), step)]

    def share(n, d):
        return remote_copy(final.at[n], place(n, y), sf.at[n, d - 1], rf.at[n, d - 1], dp_peer(d))

    def to_plane(n):
        return remote_copy(plane.at[n], from_plane.at[n], sp.at[n], rp.at[n], y_peer)

    def share_core(n, t):
        return remote_copy(final_plane.at[n, t], place(n, 2 + t), sc.at[n, t], rc.at[n, t], core_peer)

    def keep(n, t):
        src = final.at[n] if t == 0 else final_plane.at[n, t - 1]
        return pltpu.make_async_copy(src, place(n, y if t == 0 else 1 + t), local_sem.at[n, t])

    def down_to_x(j):
        return remote_copy(
            down_sum.at[:, lax.rem(x + j, X)], down_from_x.at[j - 1], sdx.at[j - 1], rdx.at[j - 1], x_peer(j)
        )

    def down_to_z(j):
        return remote_copy(
            down_column.at[lax.rem(z + j, Z)], down_from_z.at[j - 1], sdz.at[j - 1], rdz.at[j - 1], z_peer(j)
        )

    def down_share(d):
        return remote_copy(down_final, down_all.at[dp], sdf.at[d - 1], rdf.at[d - 1], dp_peer(d))

    down_mine = pltpu.make_async_copy(down_sum.at[:, x], down_column, down_sem.at[0])
    down_keep = pltpu.make_async_copy(down_final, down_all.at[dp], down_sem.at[1])
    out_copy = remote_copy(out_send, out_recv, s_out, r_out, y_peer)

    @pl.when(i == 0)
    def _():
        barrier = pltpu.get_barrier_semaphore()
        peers = [z_peer(n) for n in range(1, Z)] + [x_peer(n) for n in range(1, X)]
        peers += [dp_peer(d) for d in range(1, 4)] + [before_me, after_me]
        for peer in peers:
            pl.semaphore_signal(barrier, inc=1, device_id=peer, device_id_type=MESH)
        pl.semaphore_wait(barrier, len(peers))
        out_copy.start()
        for j in range(1, X):
            down_to_x(j).start()
        down_mine.start()
        da[...] = jnp.zeros_like(da)

        @pl.when(me == devices - 1)
        def _():
            edge_recv[...] = jnp.zeros_like(edge_recv)

    def active(first):
        return (i >= first) & (i < first + groups)

    @pl.when(active(6))
    def _():
        n = i - 6
        to_plane(n).wait_recv()
        final_plane[n] = (plane[n].astype(F32) + from_plane[n].astype(F32)).astype(BF)
        for t in range(2):
            keep(n, t + 1).start()
            share_core(n, t).start()

    @pl.when(active(5))
    def _():
        n = i - 5
        for j in range(1, Z):
            to_z(n, j).wait_recv()
        total = column[n % 2, :, z].astype(F32) + total_of([from_z[n, j].astype(F32) for j in range(Z - 1)])
        total = total.astype(BF)
        final[n] = total[0]
        plane[n] = total[1:]
        to_plane(n).start()
        keep(n, 0).start()
        for d in range(1, 4):
            share(n, d).start()

    @pl.when(active(4))
    def _():
        n = i - 4
        for j in range(1, X):
            to_x_early(n, j).wait_recv()
            to_x_late(n, j).wait_recv()

        @pl.when(n >= 2)
        def _():
            for j in range(1, Z):
                to_z(n - 2, j).wait_send()

        total = summed[n % 2, :, :, x].astype(F32) + total_of([from_x[n, j].astype(F32) for j in range(X - 1)])
        column[n % 2] = total.astype(BF)
        for j in range(1, Z):
            to_z(n, j).start()

    @pl.when(active(3))
    def _():
        n = i - 3
        to_y(n).wait_recv()

        @pl.when(n >= 2)
        def _():
            for j in range(1, X):
                to_x_late(n - 2, j).wait_send()

        total = (keep_y[n % 2].astype(F32) + from_y[n].astype(F32)).astype(BF)
        summed[n % 2, 0] = total.reshape(summed.shape[2:])
        for j in range(1, X):
            to_x_late(n, j).start()

    @pl.when(active(2))
    def _():
        n = i - 2
        to_core(n).wait_recv()

        @pl.when(n >= 2)
        def _():
            to_y(n - 2).wait_send()
            for j in range(1, X):
                to_x_early(n - 2, j).wait_send()

        def both(t):
            return (mine[t].astype(F32) + from_core[n % 2, t].astype(F32)).astype(BF)

        send_y[n % 2] = both(1 - y)
        to_y(n).start()
        for t in range(2):
            summed[n % 2, 1 + t] = both(2 + t).reshape(summed.shape[2:])
        for j in range(1, X):
            to_x_early(n, j).start()
        keep_y[n % 2] = both(y)

        @pl.when(n < groups - 2)
        def _():
            pl.semaphore_signal(free, inc=1, device_id=core_peer, device_id_type=MESH)

    @pl.when(i == 2)
    def _():
        down_mine.wait()
        for j in range(1, X):
            down_to_x(j).wait_recv()
        for row in range(Z):
            total = down_column[row].astype(F32) + total_of([down_from_x[j, row].astype(F32) for j in range(X - 1)])
            down_column[row] = total.astype(BF)
        for j in range(1, Z):
            down_to_z(j).start()

    @pl.when(i == 4)
    def _():
        for j in range(1, Z):
            down_to_z(j).wait_recv()
        total = down_column[z].astype(F32) + total_of([down_from_z[j].astype(F32) for j in range(Z - 1)])
        down_final[...] = total.astype(BF)
        down_keep.start()
        for d in range(1, 4):
            down_share(d).start()

    @pl.when(i < groups)
    def _():
        slot = i % 2
        ones = head_ones(step, head_size)
        scale = 1.0 / math.sqrt(head_size)
        first = lax.broadcasted_iota(jnp.int32, (frames, step), 0) == 0
        last = lax.broadcasted_iota(jnp.int32, (frames, step), 0) == frames - 1
        for p in range(2):
            mixed_grad[p] = nt(dhb[p], mix[0, p]).astype(BF)
            before[p] = jnp.where(first, edge[p : p + 1, :], pltpu.roll(k[p].astype(F32), 1, 0))
            before[2 + p] = jnp.where(first, edge[2 + p : 3 + p, :], pltpu.roll(v[p].astype(F32), 1, 0))

        def chunk(c, carry):
            rows = pl.ds(pl.multiple_of(c * CHUNK, CHUNK), CHUNK)
            allowed = jnp.broadcast_to(carried[rows, :], (CHUNK, step)) > 0.5
            queries = [q[p, rows, :].astype(F32) for p in range(2)]
            cots = [mixed_grad[p, rows, :].astype(F32) for p in range(2)]
            keys = [before[p, rows, :] for p in range(2)] + [k[p, rows, :].astype(F32) for p in range(2)]
            values = [before[2 + p, rows, :] for p in range(2)] + [v[p, rows, :].astype(F32) for p in range(2)]

            def per_head(left, right):
                products = [(left[p] * right[n]).astype(BF) for p, n in PAIRS]
                sums = nn(jnp.concatenate(products, axis=0), ones)
                return [sums[m * CHUNK : (m + 1) * CHUNK] for m in range(len(PAIRS))]

            scores = per_head(queries, keys)
            dprobs = per_head(cots, values)
            key_grads, value_grads = [[] for _ in range(4)], [[] for _ in range(4)]
            for p, span in ((0, range(0, 3)), (1, range(3, 7))):
                s = [jnp.where(allowed, scores[m] * scale, -1e30) if PAIRS[m][1] < 2 else scores[m] * scale for m in span]
                top = functools.reduce(jnp.maximum, s)
                e = [jnp.exp(value - top) for value in s]
                e = [jnp.where(allowed, value, 0.0) if PAIRS[m][1] < 2 else value for m, value in zip(span, e)]
                inverse = 1.0 / total_of(e)
                probs = [value * inverse for value in e]
                mean = total_of([pr * dprobs[m] for m, pr in zip(span, probs)])
                query_grad = []
                for m, pr in zip(span, probs):
                    n = PAIRS[m][1]
                    ds = (pr * (dprobs[m] - mean)).astype(BF).astype(F32) * scale
                    query_grad.append(ds * keys[n])
                    key_grads[n].append(ds * queries[p])
                    value_grads[n].append(pr.astype(BF).astype(F32) * cots[p])
                grads[slot, 0, p, rows, :] = total_of(query_grad).astype(BF)
            for p in range(2):
                terms_before[p, rows, :] = total_of(key_grads[p])
                terms_before[2 + p, rows, :] = total_of(value_grads[p])
                terms_here[p, rows, :] = total_of(key_grads[2 + p])
                terms_here[2 + p, rows, :] = total_of(value_grads[2 + p])
            return carry

        lax.fori_loop(0, frames // CHUNK, chunk, 0)

        @pl.when((i >= 2) & (me > 0))
        def _():
            to_before(i - 2).wait_send()

        for m in range(4):
            kind, p = m // 2, m % 2
            later = terms_before[m]
            edge_send[slot, m : m + 1, :] = later[0:1, :]
            total = terms_here[m] + jnp.where(last, 0.0, pltpu.roll(later, frames - 1, 0))
            grads[slot, 1 + kind, p] = total.astype(BF)
            tails[slot, m] = total[frames - 16 :, :]

        @pl.when(me > 0)
        def _():
            to_before(i).start()

    @pl.when(active(1))
    def _():
        n = i - 1
        slot = n % 2

        @pl.when(me < devices - 1)
        def _():
            to_before(n).wait_recv()

        bottom = lax.broadcasted_iota(jnp.int32, (16, step), 0) == 15
        for m in range(4):
            fixed = tails[slot, m] + jnp.where(bottom, edge_recv[n, m : m + 1, :], 0.0)
            grads[slot, 1 + m // 2, m % 2, frames - 16 :, :] = fixed.astype(BF)

        @pl.when(n >= 1)
        def _():
            to_core(n - 1).wait_send()

        for t in range(4):
            pair = []
            for p in range(2):
                if t < 3:
                    pair.append(tn(inputs[p], grads[slot, t, p]).astype(BF))
                else:
                    pair.append(tn(mixed[p], dhb[p, :, pl.ds(pl.multiple_of(n * step, step), step)]).astype(BF))
            mine[t] = jnp.where(core == 0, pair[0], pair[1])
            other[t] = jnp.where(core == 0, pair[1], pair[0])

        @pl.when(n >= 2)
        def _():
            pl.semaphore_wait(free, 1)

        to_core(n).start()
        for p in range(2):
            da[p] += total_of([nt(grads[slot, t, p], proj[t, p]) for t in range(3)])

    @pl.when(i == groups + 5)
    def _():
        to_core(groups - 1).wait_send()
        for n in (groups - 2, groups - 1):
            @pl.when(me > 0)
            def _():
                to_before(n).wait_send()

            to_y(n).wait_send()
            for j in range(1, X):
                to_x_early(n, j).wait_send()
                to_x_late(n, j).wait_send()
            for j in range(1, Z):
                to_z(n, j).wait_send()

        def finish(n, carry):
            to_plane(n).wait_send()
            keep(n, 0).wait()
            for d in range(1, 4):
                share(n, d).wait()
            for t in range(2):
                keep(n, t + 1).wait()
                share_core(n, t).wait()
            return carry

        lax.fori_loop(0, groups, finish, 0)
        for j in range(1, X):
            down_to_x(j).wait_send()
        for j in range(1, Z):
            down_to_z(j).wait_send()
        down_keep.wait()
        for d in range(1, 4):
            down_share(d).wait()
        out_copy.wait()


def attention_back(carried, q, k, v, edge, attn, dhb, mixed, inputs, down_sum, out_send, head_size, fsdp_count):
    _, frames, width = q.shape
    step = 256
    groups = width // step
    X = fsdp_count // Z
    R = width // fsdp_count
    R2, half = down_sum.shape[2:]

    def early(i):
        return jnp.minimum(i, groups - 1)

    rows = pl.BlockSpec((2, frames, step), lambda i: (0, 0, early(i)))
    edge_spec = pl.BlockSpec((8, step), lambda i: (0, early(i)))
    mask = pl.BlockSpec((frames, 1), lambda i: (0, 0), pipeline_mode=pl.Buffered(1))
    whole = pl.BlockSpec((2, frames, width), lambda i: (0, 0, 0), pipeline_mode=pl.Buffered(1))
    mix_spec = pl.BlockSpec((1, 2, step, width), lambda i: (3, 0, early(i), 0))
    proj_spec = pl.BlockSpec((3, 2, width, step), lambda i: (0, 0, 0, jnp.clip(i - 1, 0, groups - 1)))
    dma, vmem = pltpu.SemaphoreType.DMA, pltpu.VMEM
    n = groups
    return pl.pallas_call(
        functools.partial(attention_back_kernel, X, groups, head_size),
        grid=(groups + 6,),
        out_shape=(
            jax.ShapeDtypeStruct((2, frames, width), F32),
            jax.ShapeDtypeStruct((4, 2, R, width), BF),
            jax.ShapeDtypeStruct((4, R2, half), BF),
            jax.ShapeDtypeStruct(out_send.shape, BF),
        ),
        in_specs=[mask, rows, rows, rows, edge_spec, mix_spec, whole, whole, whole, proj_spec, ANY, ANY],
        out_specs=(whole, ANY, ANY, ANY),
        scratch_shapes=[
            vmem((2, frames, step), BF), vmem((4, frames, step), F32), vmem((4, frames, step), F32),
            vmem((4, frames, step), F32), vmem((2, 4, 16, step), F32), vmem((2, 3, 2, frames, step), BF),
            vmem((2, 8, step), F32), vmem((n, 8, step), F32),
            vmem((4, width, step), BF), vmem((4, width, step), BF), vmem((2, 4, width, step), BF),
            vmem((2, width, step), BF), vmem((2, width, step), BF), vmem((n, width, step), BF),
            vmem((2, 3, Z, X, R, step), BF), vmem((n, X - 1, 3, Z, R, step), BF),
            vmem((2, 3, Z, R, step), BF), vmem((n, Z - 1, 3, R, step), BF),
            vmem((n, R, step), BF), vmem((n, 2, R, step), BF), vmem((n, 2, R, step), BF), vmem((n, 2, R, step), BF),
            vmem((Z, R2, half), BF), vmem((X - 1, Z, R2, half), BF), vmem((Z - 1, R2, half), BF), vmem((R2, half), BF),
            dma((2,)), dma((n,)), dma, dma((2,)), dma((2,)), dma((n,)),
            dma((2, X - 1)), dma((n, X - 1)), dma((2, X - 1)), dma((n, X - 1)),
            dma((2, Z - 1)), dma((n, Z - 1)), dma((n, 3)), dma((n, 3)), dma((n,)), dma((n,)),
            dma((n, 2)), dma((n, 2)), dma((n, 3)),
            dma((X - 1,)), dma((X - 1,)), dma((Z - 1,)), dma((Z - 1,)), dma((3,)), dma((3,)), dma((2,)),
            dma, dma, pltpu.SemaphoreType.REGULAR,
        ],
        compiler_params=pltpu.CompilerParams(vmem_limit_bytes=63 * 2**20, collective_id=2, has_side_effects=True),
        name="attention_back",
    )(carried, q, k, v, edge, attn, dhb, mixed, inputs, attn, down_sum, out_send)


def per_device(
    frames, cotangent, segment_ids,
    qkv_weight, mix_weight, inner_weight, down_weight, norm_gains,
    qkv_moment, mix_moment, inner_moment, down_moment, gains_moment,
    qkv_average, mix_average, inner_average, down_average, gains_average,
):
    frame_count, positions, width = frames.shape
    head_size = width // HEADS
    hidden = inner_weight.shape[2] // 2
    dp_count, fsdp_count = lax.axis_size("dp"), lax.axis_size("fsdp")
    X = fsdp_count // Z
    devices = dp_count * fsdp_count
    total_frames = frame_count * devices
    dp, fs = lax.axis_index("dp"), lax.axis_index("fsdp")
    y, core = dp // 2, dp % 2
    z, x = fs // X, fs % X
    axes = ("dp", "fsdp")

    def permute(value, target):
        pairs = []
        for d in range(dp_count):
            for f in range(fsdp_count):
                to = target(d, f)
                if to is not None:
                    pairs.append((d * fsdp_count + f, to[0] * fsdp_count + to[1]))
        return lax.ppermute(value, axes, pairs)

    def to_core(value):
        return permute(value, lambda d, f: (d ^ 1, f))

    def to_y(value):
        return permute(value, lambda d, f: (d ^ 2, f))

    def to_x(value, i):
        return permute(value, lambda d, f: (d, (f // X) * X + (f % X + i) % X))

    def to_z(value, k):
        return permute(value, lambda d, f: (d, ((f // X + k) % Z) * X + f % X))

    def shifted(value, steps):
        def target(d, f):
            to = d * fsdp_count + f + steps
            return divmod(to, fsdp_count) if 0 <= to < devices else None

        return permute(value, target)

    device = dp * fsdp_count + fs
    padded_ids = jnp.concatenate([jnp.full((1,), -1, jnp.int32), segment_ids])
    window = lax.dynamic_slice_in_dim(padded_ids, device * frame_count, frame_count + 1)
    carried = (window[1:] == window[:-1]).astype(F32)[:, None]

    attn_own = lax.select_n(
        dp, qkv_weight[:, :, :width], qkv_weight[:, :, width : 2 * width], qkv_weight[:, :, 2 * width :], mix_weight
    ).astype(BF)
    inner_own = lax.dynamic_slice(
        inner_weight, (y, 0, core * hidden), (1, inner_weight.shape[1], hidden)
    )[0].astype(BF)
    half_width = width // 2
    down_own = lax.dynamic_slice(
        down_weight, (y, 0, core * half_width), (1, down_weight.shape[1], half_width)
    )[0].astype(BF)
    own_gains = norm_gains.astype(BF).astype(F32)
    gains_own = jnp.zeros((8, 128), F32).at[: own_gains.shape[0], : own_gains.shape[1]].set(own_gains)
    attn, inner, down, gains_all = gather_weights(attn_own, inner_own, down_own, gains_own, fsdp_count)
    gains = gains_all[:, :2, : own_gains.shape[1]].transpose(1, 0, 2).reshape(2, width)

    xf = frames.transpose(1, 0, 2).astype(F32)
    cot = cotangent.transpose(1, 0, 2)
    cot_there = to_y(lax.dynamic_index_in_dim(cot, 1 - y, 0, keepdims=False))
    r1 = scale_rows(xf)
    n1 = xf * r1
    a = (n1 * gains[0]).astype(BF)

    def each(left, right):
        return jnp.einsum("pfd,pde->pfe", left, right, preferred_element_type=F32)

    q, k, v = (each(a, attn[t]).astype(BF) for t in range(3))
    edge_rows = shifted(jnp.concatenate([k[:, -1], v[:, -1]], axis=0), 1)
    edge = jnp.pad(edge_rows.astype(F32), ((0, 4), (0, 0)))
    mixed = attend(carried, q, k, v, edge, head_size)
    hres = xf + each(mixed, attn[3])
    r2 = scale_rows(hres)
    n2 = hres * r2
    b = (n2 * gains[1]).astype(BF)

    b_there = to_y(lax.dynamic_index_in_dim(b, 1 - y, 0, keepdims=False))
    b_rows = jnp.concatenate([lax.dynamic_index_in_dim(b, y, 0, keepdims=False), b_there], axis=0)
    c_rows = jnp.concatenate([lax.dynamic_index_in_dim(cot, y, 0, keepdims=False), cot_there], axis=0)
    out, back, out_there, back_there, inner_shares, down_sum = feed_forward(b_rows, c_rows, inner, down, fsdp_count)

    def by_position(mine, theirs):
        return jnp.where(y == 0, jnp.stack([mine, theirs]), jnp.stack([theirs, mine]))

    db = by_position(back, back_there.astype(F32))

    e2 = jnp.sum(db * n2, axis=(0, 1))
    dh = cot.astype(F32) + norm_back(db, n2, gains[1], r2)
    dhb = dh.astype(BF)
    down_sum = down_sum.reshape(Z, X, -1, half_width)
    da, attn_shares, down_shares, out_here = attention_back(
        carried, q, k, v, edge, attn, dhb, mixed, a, down_sum, out_there, head_size, fsdp_count
    )
    layer_out = (hres + by_position(out, out_here.astype(F32))).astype(BF).transpose(1, 0, 2)
    e1 = jnp.sum(da * n1, axis=(0, 1))
    frames_grad = (dh + norm_back(da, n1, gains[0], r1)).astype(BF).transpose(1, 0, 2)

    inner_grad = inner_shares.reshape((2, 2) + inner_shares.shape[1:])
    inner_grad = jnp.concatenate([inner_grad[:, 0], inner_grad[:, 1]], axis=-1).astype(F32)
    down_grad = down_shares.reshape((2, 2) + down_shares.shape[1:])
    down_grad = jnp.concatenate([down_grad[:, 0], down_grad[:, 1]], axis=-1).astype(F32)
    qkv_grad = jnp.concatenate([attn_shares[0], attn_shares[1], attn_shares[2]], axis=-1).astype(F32)
    mix_grad = attn_shares[3].astype(F32)

    gains_part = jnp.stack([e1, e2])
    gains_part = gains_part + to_core(gains_part)
    gains_part = gains_part + to_y(gains_part)
    gains_grid = gains_part.reshape(2, Z, X, -1).transpose(1, 2, 0, 3)
    column = lax.dynamic_index_in_dim(gains_grid, x, 1, keepdims=False)
    for i in range(1, X):
        column = column + to_x(lax.dynamic_index_in_dim(gains_grid, lax.rem(x + i, X), 1, keepdims=False), i)
    gains_grad = lax.dynamic_index_in_dim(column, z, 0, keepdims=False)
    for kk in range(1, Z):
        gains_grad = gains_grad + to_z(lax.dynamic_index_in_dim(column, lax.rem(z + kk, Z), 0, keepdims=False), kk)

    step_size = step_rate / math.sqrt(total_frames)
    grads = (qkv_grad, mix_grad, inner_grad, down_grad, gains_grad)
    new = [
        owner_update(w, g, m, av, step_size)
        for w, g, m, av in zip(
            (qkv_weight, mix_weight, inner_weight, down_weight, norm_gains),
            grads,
            (qkv_moment, mix_moment, inner_moment, down_moment, gains_moment),
            (qkv_average, mix_average, inner_average, down_average, gains_average),
        )
    ]
    return (
        (layer_out, frames_grad) + grads
        + tuple(n[0] for n in new) + tuple(n[1] for n in new) + tuple(n[2] for n in new)
    )


def solution(mesh):
    rows = P(("dp", "fsdp"), None, None)
    weight = P(None, "fsdp", None)
    gains = P(None, "fsdp")
    weights = (weight,) * 4 + (gains,)
    return jax.shard_map(
        per_device,
        mesh=mesh,
        in_specs=(rows, rows, P()) + weights * 3,
        out_specs=(rows, rows) + weights * 4,
        check_vma=False,
    )
```

```python
import functools
import math

import jax
import jax.numpy as jnp
from jax import lax
from jax.experimental import pallas as pl
from jax.experimental.pallas import tpu as pltpu
from jax.sharding import PartitionSpec as P

HEADS = 16
Z = 4
MESH = pl.DeviceIdType.MESH
ANY = pl.BlockSpec(memory_space=pl.ANY)
BF = jnp.bfloat16
F32 = jnp.float32

norm_eps = 1e-05
momentum_rate = 0.5
average_rate = 0.5
step_rate = 0.05
VMEM_BYTES = 60 * 1024 * 1024


def nn(a, b):
    return lax.dot_general(a, b, (((1,), (0,)), ((), ())), preferred_element_type=F32)


def nt(a, b):
    return lax.dot_general(a, b, (((1,), (1,)), ((), ())), preferred_element_type=F32)


def tn(a, b):
    return lax.dot_general(a, b, (((0,), (0,)), ((), ())), preferred_element_type=F32)


def scale_rows(values):
    square = jnp.mean(values * values, axis=-1, keepdims=True) + norm_eps
    inverse = lax.rsqrt(square)
    return inverse * (1.5 - 0.5 * square * inverse * inverse)


def norm_back(grad_in, normed, gain_row, inverse):
    scaled = grad_in * gain_row
    return inverse * (scaled - normed * jnp.mean(scaled * normed, axis=-1, keepdims=True))


def owner_update(weight, gradient, moment, average, step_size):
    moment_new = momentum_rate * moment + gradient
    weight_new = weight - step_size * (gradient + momentum_rate * moment_new)
    average_new = average_rate * average + (1.0 - average_rate) * weight_new
    return (moment_new, average_new, weight_new)


PAIRS = ((0, 0), (0, 1), (0, 2), (1, 0), (1, 1), (1, 2), (1, 3))
SPANS = ((0, range(0, 3)), (1, range(3, 7)))
CHUNK = 128
STEP = 256


def total_of(values):
    return functools.reduce(jnp.add, values)


def remote_copy(src, dst, send_sem, recv_sem, peer):
    return pltpu.make_async_remote_copy(
        src_ref=src, dst_ref=dst, send_sem=send_sem, recv_sem=recv_sem, device_id=peer, device_id_type=MESH
    )


def head_ones(lanes, head_size):
    row = lax.broadcasted_iota(jnp.int32, (lanes, lanes), 0) // head_size
    column = lax.broadcasted_iota(jnp.int32, (lanes, lanes), 1) // head_size
    return (row == column).astype(BF)


def per_head(left, right, ones):
    rows = left[0].shape[0]
    products = [(left[p] * right[n]).astype(BF) for p, n in PAIRS]
    sums = nn(jnp.concatenate(products, axis=0), ones)
    return [sums[m * rows : (m + 1) * rows] for m in range(len(PAIRS))]


def head_probs(scores, span, allowed, scale):
    s = [jnp.where(allowed, scores[m] * scale, -1e30) if PAIRS[m][1] < 2 else scores[m] * scale for m in span]
    top = functools.reduce(jnp.maximum, s)
    e = [jnp.exp(value - top) for value in s]
    e = [jnp.where(allowed, value, 0.0) if PAIRS[m][1] < 2 else value for m, value in zip(span, e)]
    inverse = 1.0 / total_of(e)
    return [value * inverse for value in e]


def forward_kernel(
    X, groups, head_size, frames, carried, cot, attn_own, inner_own, down_own, gains_own,
    attn, inner, down, gains_out, inputs_out, rows_out, mixed_out, edge_out, hres_out, b_rows, c_rows,
    gains, inputs, rows_in, mixed, before, hres, b, proj, mix, edge_send, edge_recv,
    send_up, recv_up, send_down, recv_down, send_x, recv_x, send_y, recv_y, send_c, recv_c, send_r, recv_r,
    send_g, recv_g, send_e, recv_e, send_b, recv_b, send_q, recv_q, local_sem, out_sem,
):
    dp, fs = lax.axis_index("dp"), lax.axis_index("fsdp")
    F = Z * X
    y, core = dp // 2, dp % 2
    z, x = fs // X, fs % X
    me = dp * F + fs
    devices = 4 * F
    count = frames.shape[1]
    core_peer = (y * 2 + 1 - core, fs)
    y_peer = ((1 - y) * 2 + core, fs)
    up_peer = (dp, lax.rem(z + 1, Z) * X + x)
    down_peer = (dp, lax.rem(z + Z - 1, Z) * X + x)
    before_me = ((me - 1 + devices) % devices // F, (me - 1 + devices) % devices % F)
    after_me = ((me + 1) % devices // F, (me + 1) % devices % F)

    def z_peer(k):
        return (dp, lax.rem(z + k, Z) * X + x)

    def x_peer(i):
        return (dp, z * X + lax.rem(x + i, X))

    UNITS = unit_list(groups, inner_own.shape[1], down_own.shape[1])

    def own(u):
        kind, n, columns = UNITS[u]
        if kind in ("quarter", "low", "high"):
            return attn_own.at[n if kind != "high" else n + 1]
        return (down_own if kind == "down" else inner_own).at[:, columns]

    def part_of(u, core_index, plane):
        kind = UNITS[u][0]
        if kind == "quarter":
            return plane * 2 + core_index
        return 2 + core_index if kind == "high" else core_index

    def whole(u, part):
        kind, n, columns = UNITS[u]
        if kind == "down":
            return down.at[part, :, columns]
        if kind == "inner":
            return inner.at[part, :, columns]
        return attn.at[n, part]

    def place(u, source, part=None):
        kind, n, columns = UNITS[u]
        part = part_of(u, core, y) if part is None else part
        if kind == "down":
            R = down_own.shape[0]
            return down.at[part, pl.ds(source * R, R), columns]
        if kind == "inner":
            R = inner_own.shape[0]
            return inner.at[part, pl.ds(source * R, R), columns]
        R = attn_own.shape[2]
        return attn.at[n, part, :, pl.ds(source * R, R), :]

    barrier = pltpu.get_barrier_semaphore()
    peers = [z_peer(k) for k in range(1, Z)] + [x_peer(i) for i in range(1, X)]
    peers += [core_peer, y_peer, before_me, after_me]
    for peer in peers:
        pl.semaphore_signal(barrier, inc=1, device_id=peer, device_id_type=MESH)
    pl.semaphore_wait(barrier, len(peers))

    sent, local = [], []

    def send(condition, make):
        remote_copy(*make()).start()
        sent.append((condition, make))

    def wait_send(condition, make):
        def action():
            remote_copy(*make()).wait_send()

        if condition is None:
            action()
        else:
            pl.when(condition())(action)

    def wait_recv(dst, recv_sem, send_sem):
        remote_copy(dst, dst, send_sem, recv_sem, core_peer).wait_recv()

    def store(src, dst):
        copy = pltpu.make_async_copy(src, dst, out_sem.at[len(local)])
        copy.start()
        local.append(copy)

    def spread(u, row, mine, condition):
        def src():
            return own(u) if mine else place(u, row() * X + x)

        for i in range(1, X):
            send(
                condition,
                lambda i=i: (
                    src(), place(u, row() * X + x), send_x.at[u, row(), i], recv_x.at[u, row(), i], x_peer(i)
                ),
            )
        to_plane(u, lambda: row() * X + x, src, condition)

    def to_plane(u, source, src, condition):
        if UNITS[u][0] == "quarter":
            send(
                condition,
                lambda: (src(), place(u, source()), send_y.at[u, source()], recv_y.at[u, source()], y_peer),
            )

    def start_unit(u):
        def below_top():
            return z < Z - 1

        def above_bottom():
            return z > 0

        def upward():
            return (own(u), place(u, fs), send_up.at[u, 1], recv_up.at[u, 1], up_peer)

        def downward():
            return (own(u), place(u, fs), send_down.at[u, 1], recv_down.at[u, 1], down_peer)

        pl.when(below_top())(lambda: send(below_top, upward))
        pl.when(above_bottom())(lambda: send(above_bottom, downward))
        spread(u, lambda: z, True, None)
        store(own(u), place(u, fs))

    def hop(u, k):
        def side(reached, row, further, send_sem, recv_sem, peer):
            def here():
                return place(u, row() * X + x)

            def both():
                return reached() & further()

            def action():
                wait_recv(here(), recv_sem.at[u, k], send_sem.at[u, k])
                if k < Z - 1:
                    pl.when(further())(
                        lambda: send(
                            both, lambda: (here(), here(), send_sem.at[u, k + 1], recv_sem.at[u, k + 1], peer)
                        )
                    )
                spread(u, row, False, reached)

            pl.when(reached())(action)

        side(lambda: z >= k, lambda: z - k, lambda: z < Z - 1, send_up, recv_up, up_peer)
        side(lambda: z + k < Z, lambda: z + k, lambda: z > 0, send_down, recv_down, down_peer)

    def arrivals(u):
        for row in range(Z):
            for i in range(1, X):
                column = lax.rem(x - i + X, X)
                source = row * X + column
                wait_recv(place(u, source), recv_x.at[u, row, i], send_x.at[u, row, i])
                to_plane(u, lambda source=source: source, lambda source=source: place(u, source), None)
        local[own_store[u]].wait()
        mine = whole(u, part_of(u, core, y))
        send(None, lambda: (mine, mine, send_c.at[u], recv_c.at[u], core_peer))

    def relay(u):
        if UNITS[u][0] != "quarter":
            return
        part = (1 - y) * 2 + core
        for source in range(F):
            wait_recv(place(u, source, part), recv_y.at[u, source], send_y.at[u, source])
        theirs = whole(u, part)
        send(None, lambda: (theirs, theirs, send_r.at[u], recv_r.at[u], core_peer))

    def complete(u):
        wait_recv(whole(u, part_of(u, 1 - core, y)), recv_c.at[u], send_c.at[u])
        if UNITS[u][0] == "quarter":
            wait_recv(whole(u, (1 - y) * 2 + 1 - core), recv_r.at[u], send_r.at[u])

    scale = 1.0 / math.sqrt(head_size)

    def gather_gains():
        keep = pltpu.make_async_copy(gains_own, gains.at[fs], local_sem.at[0])
        keep.start()
        for k in range(1, Z):
            send(None, lambda k=k: (gains_own, gains.at[fs], send_g.at[0, k], recv_g.at[0, k], z_peer(k)))
        for i in range(1, X):
            send(None, lambda i=i: (gains_own, gains.at[fs], send_g.at[i, 0], recv_g.at[i, 0], x_peer(i)))
        keep.wait()

    def chunk_source(k, i):
        return lax.rem(z - k + Z, Z) * X + lax.rem(x - i + X, X)

    def pass_gains():
        for k in range(1, Z):
            here = gains.at[chunk_source(k, 0)]
            wait_recv(here, recv_g.at[0, k], send_g.at[0, k])
            for i in range(1, X):
                send(
                    None,
                    lambda here=here, i=i, k=k: (here, here, send_g.at[i, k], recv_g.at[i, k], x_peer(i)),
                )

    def take_gains():
        for k in range(Z):
            for i in range(1, X):
                wait_recv(gains.at[chunk_source(k, i)], recv_g.at[i, k], send_g.at[i, k])
        total = gains[0]
        for source in range(1, F):
            total = total + gains[source]
        gains_out[...] = total

    def norm_rows():
        def chunk(c, carry):
            rows = pl.ds(pl.multiple_of(c * CHUNK, CHUNK), CHUNK)
            for p in range(2):
                value = frames[p, rows, :].astype(F32)
                inputs[p, rows, :] = (value * scale_rows(value) * gains_out[0:1, :]).astype(BF)
            return carry

        lax.fori_loop(0, count // CHUNK, chunk, 0)
        store(inputs, inputs_out)

    def heads(m):
        columns = slice(m * STEP, (m + 1) * STEP)
        load = pltpu.make_async_copy(attn.at[m, pl.ds(0, 3)], proj, local_sem.at[0])
        load.start()
        load.wait()
        for t in (1, 2, 0):
            for p in range(2):
                rows_in[t, p, :, columns] = nn(inputs[p], proj[t, p]).astype(BF)
                if t > 0:
                    tail = rows_in[t, p, count - 16 :, columns].astype(F32)
                    row = 2 * (t - 1) + p
                    edge_send[m, row : row + 1, :] = tail[15:16, :]
            if t == 2:
                to_after = remote_copy(edge_send.at[m], edge_recv.at[m], send_e.at[m], recv_e.at[m], after_me)
                pl.when(me < devices - 1)(to_after.start)
        pl.when(me > 0)(to_after.wait_recv)
        first = lax.broadcasted_iota(jnp.int32, (count, STEP), 0) == 0
        for t in range(2):
            for p in range(2):
                n = 2 * t + p
                shifted = pltpu.roll(rows_in[1 + t, p, :, columns].astype(F32), 1, 0)
                before[n] = jnp.where(first, edge_recv[m, n : n + 1, :], shifted)
        ones = head_ones(STEP, head_size)

        def chunk(c, carry):
            rows = pl.ds(pl.multiple_of(c * CHUNK, CHUNK), CHUNK)
            allowed = jnp.broadcast_to(carried[rows, :], (CHUNK, STEP)) > 0.5
            queries, here_k, here_v = (
                [rows_in[t, p, rows, columns].astype(F32) for p in range(2)] for t in range(3)
            )
            keys = [before[p, rows, :] for p in range(2)] + here_k
            values = [before[2 + p, rows, :] for p in range(2)] + here_v
            scores = per_head(queries, keys, ones)
            for p, span in SPANS:
                probs = head_probs(scores, span, allowed, scale)
                terms = [pr.astype(BF).astype(F32) * values[PAIRS[n][1]] for n, pr in zip(span, probs)]
                mixed[p, rows, columns] = total_of(terms).astype(BF)
            return carry

        lax.fori_loop(0, count // CHUNK, chunk, 0)

    def load_mix():
        return pltpu.make_async_copy(attn.at[:, 3], mix, local_sem.at[1])

    def finish_rows():
        load_mix().wait()
        for turn in range(2):
            p = 1 - y if turn == 0 else y
            for m in range(groups):
                columns = slice(m * STEP, (m + 1) * STEP)
                hres[p, :, columns] = frames[p, :, columns].astype(F32) + nn(mixed[p], mix[m, p])

            def chunk(c, carry):
                rows = pl.ds(pl.multiple_of(c * CHUNK, CHUNK), CHUNK)
                value = hres[p, rows, :]
                b[turn, rows, :] = (value * scale_rows(value) * gains_out[1:2, :]).astype(BF)
                return carry

            lax.fori_loop(0, count // CHUNK, chunk, 0)
            if turn == 0:
                send(None, lambda: (b.at[0], b_rows.at[1], send_b, recv_b, y_peer))
            else:
                store(b.at[1], b_rows.at[0])
        store(hres, hres_out)

    @pl.when(me == 0)
    def _():
        edge_recv[...] = jnp.zeros_like(edge_recv)

    own_store = {}
    last_of = {kind_n[1]: u for u, kind_n in enumerate(UNITS) if kind_n[0] in ("quarter", "low", "high")}
    last_plane = max(u for u, kind_n in enumerate(UNITS) if kind_n[0] == "quarter")
    store(cot.at[y], c_rows.at[0])
    gather_gains()
    for tick in range(len(UNITS) + Z + 2):
        if tick < len(UNITS):
            own_store[tick] = len(local)
            start_unit(tick)
        for k in range(1, Z):
            if 0 <= tick - k < len(UNITS):
                hop(tick - k, k)
        if tick == 1:
            pass_gains()
        if tick == 2:
            take_gains()
            norm_rows()
        u = tick - Z
        if 0 <= u < len(UNITS):
            arrivals(u)
            if u == last_plane:
                send(None, lambda: (cot.at[1 - y], c_rows.at[1], send_q, recv_q, y_peer))
        u = tick - Z - 1
        if 0 <= u < len(UNITS):
            relay(u)
            complete(u)
            for m in range(groups):
                if last_of[m] == u:
                    if m == groups - 1:
                        load_mix().start()
                    heads(m)
                    if m == groups - 1:
                        store(rows_in, rows_out)
                        store(mixed, mixed_out)
                        store(edge_recv, edge_out)
                        finish_rows()
    wait_recv(b_rows.at[1], recv_b, send_b)
    wait_recv(c_rows.at[1], recv_q, send_q)
    for condition, make in sent:
        wait_send(condition, make)
    for n, copy in enumerate(local):
        if n not in own_store.values():
            copy.wait()

    @pl.when(me < devices - 1)
    def _():
        for m in range(groups):
            remote_copy(edge_send.at[m], edge_recv.at[m], send_e.at[m], recv_e.at[m], after_me).wait_send()


def unit_list(groups, inner_width, down_width):
    units = [("quarter", n, None) for n in range(groups - 1)]
    units += [("low", groups - 1, None), ("high", groups - 1, None)]
    units += [("down", 0, slice(0, down_width // 2)), ("down", 0, slice(down_width // 2, down_width))]
    tiles = inner_width // 128
    cuts = [128 * (tiles * n // 4) for n in range(5)]
    return units + [("inner", 0, slice(lo, hi)) for lo, hi in zip(cuts, cuts[1:])]


def forward(frames, carried, cot, attn_own, inner_own, down_own, gains_own, head_size, fsdp_count):
    X = fsdp_count // Z
    _, count, width = frames.shape
    _, _, R, _ = attn_own.shape
    groups = width // STEP
    units = len(unit_list(groups, inner_own.shape[1], down_own.shape[1]))
    dma, vmem = pltpu.SemaphoreType.DMA, pltpu.VMEM
    whole = pl.BlockSpec(memory_space=pltpu.VMEM)
    act = jax.ShapeDtypeStruct((2, count, width), BF)
    return pl.pallas_call(
        functools.partial(forward_kernel, X, groups, head_size),
        out_shape=(
            jax.ShapeDtypeStruct((groups, 4, 2, R * fsdp_count, STEP), BF),
            jax.ShapeDtypeStruct((2, inner_own.shape[0] * fsdp_count, inner_own.shape[1]), BF),
            jax.ShapeDtypeStruct((2, down_own.shape[0] * fsdp_count, down_own.shape[1]), BF),
            jax.ShapeDtypeStruct(gains_own.shape, F32),
            act,
            jax.ShapeDtypeStruct((3, 2, count, width), BF),
            act,
            jax.ShapeDtypeStruct((groups, 8, STEP), F32),
            jax.ShapeDtypeStruct((2, count, width), F32),
            act,
            act,
        ),
        in_specs=[whole] * 7,
        out_specs=(ANY,) * 3 + (whole,) + (ANY,) * 7,
        scratch_shapes=[
            vmem((fsdp_count,) + gains_own.shape, F32),
            vmem((2, count, width), BF), vmem((3, 2, count, width), BF), vmem((2, count, width), BF),
            vmem((4, count, STEP), F32), vmem((2, count, width), F32), vmem((2, count, width), BF),
            vmem((3, 2, width, STEP), BF), vmem((groups, 2, width, STEP), BF),
            vmem((groups, 8, STEP), F32), vmem((groups, 8, STEP), F32),
            dma((units, Z)), dma((units, Z)), dma((units, Z)), dma((units, Z)),
            dma((units, Z, X)), dma((units, Z, X)), dma((groups, fsdp_count)), dma((groups, fsdp_count)),
            dma((units,)), dma((units,)), dma((groups,)), dma((groups,)),
            dma((X, Z)), dma((X, Z)), dma((groups,)), dma((groups,)), dma, dma, dma, dma,
            dma((2,)), dma((units + 8,)),
        ],
        compiler_params=pltpu.CompilerParams(
            vmem_limit_bytes=VMEM_BYTES, collective_id=0, has_side_effects=True
        ),
        name="attention_forward",
    )(frames, carried, cot, attn_own, inner_own, down_own, gains_own)


def feed_forward_kernel(
    X, J, b, c, inner, down, out_mine, back_mine, out_theirs, back_recv, inner_all, down_sum,
    out, back, down_here, down_there, down_from_core, mine, other, from_core, summed, from_x, column, from_z, final, staged,
    s1, r1, s2, r2, s3, r3, s5, r5, s6, r6, s7, r7, local_sem,
):
    j = pl.program_id(0)
    half = down.shape[2]
    rows_here = out_mine.shape[0]
    R, step = final.shape[1:]
    dp, fs = lax.axis_index("dp"), lax.axis_index("fsdp")
    y, core = dp // 2, dp % 2
    z, x = fs // X, fs % X
    core_peer = (y * 2 + 1 - core, fs)
    y_peer = ((1 - y) * 2 + core, fs)

    def z_peer(k):
        return (dp, lax.rem(z + k, Z) * X + x)

    def x_peer(i):
        return (dp, z * X + lax.rem(x + i, X))

    def dp_peer(d):
        return (((y + d // 2) % 2) * 2 + (core + d % 2) % 2, fs)

    def to_core(n):
        return remote_copy(other.at[n % 2], from_core.at[n], s1.at[n % 2], r1.at[n], core_peer)

    def to_x(n, i):
        return remote_copy(
            summed.at[n % 2, :, lax.rem(x + i, X)], from_x.at[n, i - 1], s2.at[n % 2, i - 1], r2.at[n, i - 1], x_peer(i)
        )

    def to_z(n, k):
        return remote_copy(
            column.at[n % 2, lax.rem(z + k, Z)], from_z.at[n, k - 1], s3.at[n % 2, k - 1], r3.at[n, k - 1], z_peer(k)
        )

    def place(n, owner):
        return inner_all.at[owner, :, pl.ds(pl.multiple_of(n * step, step), step)]

    def share(n, d):
        return remote_copy(final.at[n], place(n, dp), s5.at[n, d - 1], r5.at[n, d - 1], dp_peer(d))

    def keep(n):
        return pltpu.make_async_copy(final.at[n], place(n, dp), local_sem.at[n])

    exchange = remote_copy(staged, back_recv, s6, r6, y_peer)

    def down_to_core(n):
        return remote_copy(down_there.at[n % 2], down_from_core.at[n], s7.at[n % 2], r7.at[n], core_peer)

    @pl.when(j == 0)
    def _():
        barrier = pltpu.get_barrier_semaphore()
        peers = [z_peer(k) for k in range(1, Z)] + [x_peer(i) for i in range(1, X)]
        peers += [dp_peer(d) for d in range(1, 4)]
        for peer in peers:
            pl.semaphore_signal(barrier, inc=1, device_id=peer, device_id_type=MESH)
        pl.semaphore_wait(barrier, len(peers))
        out[...] = jnp.zeros_like(out)
        back[...] = jnp.zeros_like(back)

    @pl.when((j >= 1) & (j < J + 1))
    def _():
        n = j - 1
        to_core(n).wait_recv()

        @pl.when(n >= 2)
        def _():
            for i in range(1, X):
                to_x(n - 2, i).wait_send()

        down_to_core(n).wait_recv()
        down_sum[...] = (down_here[n % 2].astype(F32) + down_from_core[n].astype(F32)).astype(BF)
        total = (mine[n % 2].astype(F32) + from_core[n].astype(F32)).astype(BF)
        summed[n % 2] = total.reshape(summed.shape[1:])
        for i in range(1, X):
            to_x(n, i).start()

    @pl.when((j >= 2) & (j < J + 2))
    def _():
        n = j - 2
        for i in range(1, X):
            to_x(n, i).wait_recv()

        @pl.when(n >= 2)
        def _():
            for k in range(1, Z):
                to_z(n - 2, k).wait_send()

        total = summed[n % 2, :, x].astype(F32)
        for i in range(1, X):
            total = total + from_x[n, i - 1].astype(F32)
        column[n % 2] = total.astype(BF)
        for k in range(1, Z):
            to_z(n, k).start()

    @pl.when(j >= 3)
    def _():
        n = j - 3
        for k in range(1, Z):
            to_z(n, k).wait_recv()
        total = column[n % 2, z].astype(F32)
        for k in range(1, Z):
            total = total + from_z[n, k - 1].astype(F32)
        final[n] = total.astype(BF)
        keep(n).start()
        for d in range(1, 4):
            share(n, d).start()

    @pl.when(j < J)
    def _():
        rows, cot = b[...], c[...]
        gate = nn(rows, inner[0])
        up = nn(rows, inner[1])
        squashed = jax.nn.sigmoid(gate)
        active = gate * squashed
        hidden = (active * up).astype(BF)
        hidden_grad = nt(cot[:, :half], down[0]) + nt(cot[:, half:], down[1])
        gate_grad = (hidden_grad * up * (squashed * (1.0 + gate * (1.0 - squashed)))).astype(BF)
        up_grad = (hidden_grad * active).astype(BF)
        gate_term = tn(rows, gate_grad).astype(BF)
        up_term = tn(rows, up_grad).astype(BF)

        @pl.when(j >= 2)
        def _():
            to_core(j - 2).wait_send()
            down_to_core(j - 2).wait_send()

        mine[j % 2] = jnp.where(core == 0, gate_term, up_term)
        other[j % 2] = jnp.where(core == 0, up_term, gate_term)
        to_core(j).start()
        down_term = tn(hidden, cot).astype(BF)
        down_here[j % 2] = jnp.where(core == 0, down_term[:, :half], down_term[:, half:])
        down_there[j % 2] = jnp.where(core == 0, down_term[:, half:], down_term[:, :half])
        down_to_core(j).start()
        for n in range(2):
            part = slice(n * half, (n + 1) * half)
            out[:, part] += nn(hidden, down[n])
        back[...] += nt(gate_grad, inner[0]) + nt(up_grad, inner[1])

    @pl.when(j == J - 1)
    def _():
        staged[...] = back[rows_here:, :].astype(BF)
        exchange.start()
        out_theirs[...] = out[rows_here:, :].astype(BF)
        out_mine[...] = out[:rows_here, :]
        back_mine[...] = back[:rows_here, :]

    @pl.when(j == J + 2)
    def _():
        for n in (J - 2, J - 1):
            to_core(n).wait_send()
            down_to_core(n).wait_send()
            for i in range(1, X):
                to_x(n, i).wait_send()
            for k in range(1, Z):
                to_z(n, k).wait_send()

        def finish(n, carry):
            keep(n).wait()
            for d in range(1, 4):
                share(n, d).wait()
            return carry

        lax.fori_loop(0, J, finish, 0)
        exchange.wait()


def feed_forward(b, c, inner, down, fsdp_count):
    rows, width = b.shape
    _, _, hidden = inner.shape
    half = down.shape[2]
    step = 256
    J = hidden // step
    X = fsdp_count // Z
    R = width // fsdp_count
    whole = pl.BlockSpec((rows, width), lambda j: (0, 0), pipeline_mode=pl.Buffered(1))
    part = pl.BlockSpec((rows // 2, width), lambda j: (0, 0), pipeline_mode=pl.Buffered(1))
    inner_spec = pl.BlockSpec((2, width, step), lambda j: (0, 0, jnp.minimum(j, J - 1)))
    down_spec = pl.BlockSpec((2, step, half), lambda j: (0, jnp.minimum(j, J - 1), 0))
    sum_spec = pl.BlockSpec((step, half), lambda j: (jnp.clip(j - 1, 0, J - 1), 0))
    dma, vmem = pltpu.SemaphoreType.DMA, pltpu.VMEM
    return pl.pallas_call(
        functools.partial(feed_forward_kernel, X, J),
        grid=(J + 3,),
        out_shape=(
            jax.ShapeDtypeStruct((rows // 2, width), F32),
            jax.ShapeDtypeStruct((rows // 2, width), F32),
            jax.ShapeDtypeStruct((rows // 2, width), BF),
            jax.ShapeDtypeStruct((rows // 2, width), BF),
            jax.ShapeDtypeStruct((4, R, hidden), BF),
            jax.ShapeDtypeStruct((hidden, half), BF),
        ),
        in_specs=[whole, whole, inner_spec, down_spec],
        out_specs=(part, part, part, ANY, ANY, sum_spec),
        scratch_shapes=[
            vmem((rows, width), F32), vmem((rows, width), F32),
            vmem((2, step, half), BF), vmem((2, step, half), BF), vmem((J, step, half), BF),
            vmem((2, width, step), BF), vmem((2, width, step), BF), vmem((J, width, step), BF),
            vmem((2, Z, X, R, step), BF), vmem((J, X - 1, Z, R, step), BF),
            vmem((2, Z, R, step), BF), vmem((J, Z - 1, R, step), BF),
            vmem((J, R, step), BF), vmem((rows // 2, width), BF),
            dma((2,)), dma((J,)), dma((2, X - 1)), dma((J, X - 1)), dma((2, Z - 1)), dma((J, Z - 1)),
            dma((J, 3)), dma((J, 3)), dma, dma, dma((2,)), dma((J,)), dma((J,)),
        ],
        compiler_params=pltpu.CompilerParams(
            vmem_limit_bytes=VMEM_BYTES, collective_id=1, has_side_effects=True
        ),
        cost_estimate=pl.CostEstimate(flops=18 * rows * width * hidden, bytes_accessed=60 * 2**20, transcendentals=0),
        name="feed_forward",
    )(b, c, inner, down)


def total_of(values):
    return functools.reduce(jnp.add, values)


def attention_back_kernel(
    X, groups, head_size, carried, q, k, v, edge, mix, dhb, mixed, inputs, proj, down_sum, out_send,
    da, attn_all, down_all, out_recv,
    mixed_grad, before, terms_before, terms_here, tails, grads, edge_send, edge_recv,
    mine, other, from_core, keep_y, send_y, from_y, summed, from_x, column, from_z, final, plane, from_plane, final_plane,
    down_column, down_from_x, down_from_z, down_final,
    s_edge, r_edge, s1, r1, sy, ry, sxa, rxa, sxb, rxb, sz, rz, sf, rf, sp, rp, sc, rc, local_sem,
    sdx, rdx, sdz, rdz, sdf, rdf, down_sem, s_out, r_out, free,
):
    i = pl.program_id(0)
    frames, step = q.shape[2:]
    R = final.shape[1]
    dp, fs = lax.axis_index("dp"), lax.axis_index("fsdp")
    F = Z * X
    y, core = dp // 2, dp % 2
    z, x = fs // X, fs % X
    me = dp * F + fs
    devices = 4 * F
    core_peer = (y * 2 + 1 - core, fs)
    y_peer = ((1 - y) * 2 + core, fs)
    before_me = ((me - 1 + devices) % devices // F, (me - 1 + devices) % devices % F)
    after_me = ((me + 1) % devices // F, (me + 1) % devices % F)

    def z_peer(n):
        return (dp, lax.rem(z + n, Z) * X + x)

    def x_peer(n):
        return (dp, z * X + lax.rem(x + n, X))

    def dp_peer(d):
        return (((y + d // 2) % 2) * 2 + (core + d % 2) % 2, fs)

    def to_before(n):
        return remote_copy(edge_send.at[n % 2], edge_recv.at[n], s_edge.at[n % 2], r_edge.at[n], before_me)

    def to_core(n):
        return remote_copy(other, from_core.at[n % 2], s1, r1.at[n % 2], core_peer)

    def to_y(n):
        return remote_copy(send_y.at[n % 2], from_y.at[n], sy.at[n % 2], ry.at[n], y_peer)

    def to_x_early(n, j):
        return remote_copy(
            summed.at[n % 2, pl.ds(1, 2), :, lax.rem(x + j, X)], from_x.at[n, j - 1, pl.ds(1, 2)],
            sxa.at[n % 2, j - 1], rxa.at[n, j - 1], x_peer(j),
        )

    def to_x_late(n, j):
        return remote_copy(
            summed.at[n % 2, 0, :, lax.rem(x + j, X)], from_x.at[n, j - 1, 0],
            sxb.at[n % 2, j - 1], rxb.at[n, j - 1], x_peer(j),
        )

    def to_z(n, j):
        return remote_copy(
            column.at[n % 2, :, lax.rem(z + j, Z)], from_z.at[n, j - 1], sz.at[n % 2, j - 1], rz.at[n, j - 1], z_peer(j)
        )

    def place(n, t):
        return attn_all.at[t, core, :, pl.ds(pl.multiple_of(n * step, step), step)]

    def share(n, d):
        return remote_copy(final.at[n], place(n, y), sf.at[n, d - 1], rf.at[n, d - 1], dp_peer(d))

    def to_plane(n):
        return remote_copy(plane.at[n], from_plane.at[n], sp.at[n], rp.at[n], y_peer)

    def share_core(n, t):
        return remote_copy(final_plane.at[n, t], place(n, 2 + t), sc.at[n, t], rc.at[n, t], core_peer)

    def keep(n, t):
        src = final.at[n] if t == 0 else final_plane.at[n, t - 1]
        return pltpu.make_async_copy(src, place(n, y if t == 0 else 1 + t), local_sem.at[n, t])

    def down_to_x(j):
        return remote_copy(
            down_sum.at[:, lax.rem(x + j, X)], down_from_x.at[j - 1], sdx.at[j - 1], rdx.at[j - 1], x_peer(j)
        )

    def down_to_z(j):
        return remote_copy(
            down_column.at[lax.rem(z + j, Z)], down_from_z.at[j - 1], sdz.at[j - 1], rdz.at[j - 1], z_peer(j)
        )

    def down_share(d):
        return remote_copy(down_final, down_all.at[dp], sdf.at[d - 1], rdf.at[d - 1], dp_peer(d))

    down_mine = pltpu.make_async_copy(down_sum.at[:, x], down_column, down_sem.at[0])
    down_keep = pltpu.make_async_copy(down_final, down_all.at[dp], down_sem.at[1])
    out_copy = remote_copy(out_send, out_recv, s_out, r_out, y_peer)

    @pl.when(i == 0)
    def _():
        barrier = pltpu.get_barrier_semaphore()
        peers = [z_peer(n) for n in range(1, Z)] + [x_peer(n) for n in range(1, X)]
        peers += [dp_peer(d) for d in range(1, 4)] + [before_me, after_me]
        for peer in peers:
            pl.semaphore_signal(barrier, inc=1, device_id=peer, device_id_type=MESH)
        pl.semaphore_wait(barrier, len(peers))
        out_copy.start()
        for j in range(1, X):
            down_to_x(j).start()
        down_mine.start()
        da[...] = jnp.zeros_like(da)

        @pl.when(me == devices - 1)
        def _():
            edge_recv[...] = jnp.zeros_like(edge_recv)

    def active(first):
        return (i >= first) & (i < first + groups)

    @pl.when(active(6))
    def _():
        n = i - 6
        to_plane(n).wait_recv()
        final_plane[n] = (plane[n].astype(F32) + from_plane[n].astype(F32)).astype(BF)
        for t in range(2):
            keep(n, t + 1).start()
            share_core(n, t).start()

    @pl.when(active(5))
    def _():
        n = i - 5
        for j in range(1, Z):
            to_z(n, j).wait_recv()
        total = column[n % 2, :, z].astype(F32) + total_of([from_z[n, j].astype(F32) for j in range(Z - 1)])
        total = total.astype(BF)
        final[n] = total[0]
        plane[n] = total[1:]
        to_plane(n).start()
        keep(n, 0).start()
        for d in range(1, 4):
            share(n, d).start()

    @pl.when(active(4))
    def _():
        n = i - 4
        for j in range(1, X):
            to_x_early(n, j).wait_recv()
            to_x_late(n, j).wait_recv()

        @pl.when(n >= 2)
        def _():
            for j in range(1, Z):
                to_z(n - 2, j).wait_send()

        total = summed[n % 2, :, :, x].astype(F32) + total_of([from_x[n, j].astype(F32) for j in range(X - 1)])
        column[n % 2] = total.astype(BF)
        for j in range(1, Z):
            to_z(n, j).start()

    @pl.when(active(3))
    def _():
        n = i - 3
        to_y(n).wait_recv()

        @pl.when(n >= 2)
        def _():
            for j in range(1, X):
                to_x_late(n - 2, j).wait_send()

        total = (keep_y[n % 2].astype(F32) + from_y[n].astype(F32)).astype(BF)
        summed[n % 2, 0] = total.reshape(summed.shape[2:])
        for j in range(1, X):
            to_x_late(n, j).start()

    @pl.when(active(2))
    def _():
        n = i - 2
        to_core(n).wait_recv()

        @pl.when(n >= 2)
        def _():
            to_y(n - 2).wait_send()
            for j in range(1, X):
                to_x_early(n - 2, j).wait_send()

        def both(t):
            return (mine[t].astype(F32) + from_core[n % 2, t].astype(F32)).astype(BF)

        send_y[n % 2] = both(1 - y)
        to_y(n).start()
        for t in range(2):
            summed[n % 2, 1 + t] = both(2 + t).reshape(summed.shape[2:])
        for j in range(1, X):
            to_x_early(n, j).start()
        keep_y[n % 2] = both(y)

        @pl.when(n < groups - 2)
        def _():
            pl.semaphore_signal(free, inc=1, device_id=core_peer, device_id_type=MESH)

    @pl.when(i == 2)
    def _():
        down_mine.wait()
        for j in range(1, X):
            down_to_x(j).wait_recv()
        for row in range(Z):
            total = down_column[row].astype(F32) + total_of([down_from_x[j, row].astype(F32) for j in range(X - 1)])
            down_column[row] = total.astype(BF)
        for j in range(1, Z):
            down_to_z(j).start()

    @pl.when(i == 4)
    def _():
        for j in range(1, Z):
            down_to_z(j).wait_recv()
        total = down_column[z].astype(F32) + total_of([down_from_z[j].astype(F32) for j in range(Z - 1)])
        down_final[...] = total.astype(BF)
        down_keep.start()
        for d in range(1, 4):
            down_share(d).start()

    @pl.when(i < groups)
    def _():
        slot = i % 2
        ones = head_ones(step, head_size)
        scale = 1.0 / math.sqrt(head_size)
        first = lax.broadcasted_iota(jnp.int32, (frames, step), 0) == 0
        last = lax.broadcasted_iota(jnp.int32, (frames, step), 0) == frames - 1
        for p in range(2):
            mixed_grad[p] = total_of(
                [nt(dhb[p, :, g * step : (g + 1) * step], mix[g, 0, p]) for g in range(groups)]
            ).astype(BF)
            before[p] = jnp.where(first, edge[0, p : p + 1, :], pltpu.roll(k[0, p].astype(F32), 1, 0))
            before[2 + p] = jnp.where(first, edge[0, 2 + p : 3 + p, :], pltpu.roll(v[0, p].astype(F32), 1, 0))

        def chunk(c, carry):
            rows = pl.ds(pl.multiple_of(c * CHUNK, CHUNK), CHUNK)
            allowed = jnp.broadcast_to(carried[rows, :], (CHUNK, step)) > 0.5
            queries = [q[0, p, rows, :].astype(F32) for p in range(2)]
            cots = [mixed_grad[p, rows, :].astype(F32) for p in range(2)]
            keys = [before[p, rows, :] for p in range(2)] + [k[0, p, rows, :].astype(F32) for p in range(2)]
            values = [before[2 + p, rows, :] for p in range(2)] + [v[0, p, rows, :].astype(F32) for p in range(2)]

            scores = per_head(queries, keys, ones)
            dprobs = per_head(cots, values, ones)
            key_grads, value_grads = [[] for _ in range(4)], [[] for _ in range(4)]
            for p, span in SPANS:
                probs = head_probs(scores, span, allowed, scale)
                mean = total_of([pr * dprobs[m] for m, pr in zip(span, probs)])
                query_grad = []
                for m, pr in zip(span, probs):
                    n = PAIRS[m][1]
                    ds = (pr * (dprobs[m] - mean)).astype(BF).astype(F32) * scale
                    query_grad.append(ds * keys[n])
                    key_grads[n].append(ds * queries[p])
                    value_grads[n].append(pr.astype(BF).astype(F32) * cots[p])
                grads[slot, 0, p, rows, :] = total_of(query_grad).astype(BF)
            for p in range(2):
                terms_before[p, rows, :] = total_of(key_grads[p])
                terms_before[2 + p, rows, :] = total_of(value_grads[p])
                terms_here[p, rows, :] = total_of(key_grads[2 + p])
                terms_here[2 + p, rows, :] = total_of(value_grads[2 + p])
            return carry

        lax.fori_loop(0, frames // CHUNK, chunk, 0)

        @pl.when((i >= 2) & (me > 0))
        def _():
            to_before(i - 2).wait_send()

        for m in range(4):
            kind, p = m // 2, m % 2
            later = terms_before[m]
            edge_send[slot, m : m + 1, :] = later[0:1, :]
            total = terms_here[m] + jnp.where(last, 0.0, pltpu.roll(later, frames - 1, 0))
            grads[slot, 1 + kind, p] = total.astype(BF)
            tails[slot, m] = total[frames - 16 :, :]

        @pl.when(me > 0)
        def _():
            to_before(i).start()

    @pl.when(active(1))
    def _():
        n = i - 1
        slot = n % 2

        @pl.when(me < devices - 1)
        def _():
            to_before(n).wait_recv()

        bottom = lax.broadcasted_iota(jnp.int32, (16, step), 0) == 15
        for m in range(4):
            fixed = tails[slot, m] + jnp.where(bottom, edge_recv[n, m : m + 1, :], 0.0)
            grads[slot, 1 + m // 2, m % 2, frames - 16 :, :] = fixed.astype(BF)

        @pl.when(n >= 1)
        def _():
            to_core(n - 1).wait_send()

        for t in range(4):
            pair = []
            for p in range(2):
                if t < 3:
                    pair.append(tn(inputs[p], grads[slot, t, p]).astype(BF))
                else:
                    pair.append(tn(mixed[p], dhb[p, :, pl.ds(pl.multiple_of(n * step, step), step)]).astype(BF))
            mine[t] = jnp.where(core == 0, pair[0], pair[1])
            other[t] = jnp.where(core == 0, pair[1], pair[0])

        @pl.when(n >= 2)
        def _():
            pl.semaphore_wait(free, 1)

        to_core(n).start()
        for p in range(2):
            da[p] += total_of([nt(grads[slot, t, p], proj[0, t, p]) for t in range(3)])

    @pl.when(i == groups + 5)
    def _():
        to_core(groups - 1).wait_send()
        for n in (groups - 2, groups - 1):
            @pl.when(me > 0)
            def _():
                to_before(n).wait_send()

            to_y(n).wait_send()
            for j in range(1, X):
                to_x_early(n, j).wait_send()
                to_x_late(n, j).wait_send()
            for j in range(1, Z):
                to_z(n, j).wait_send()

        def finish(n, carry):
            to_plane(n).wait_send()
            keep(n, 0).wait()
            for d in range(1, 4):
                share(n, d).wait()
            for t in range(2):
                keep(n, t + 1).wait()
                share_core(n, t).wait()
            return carry

        lax.fori_loop(0, groups, finish, 0)
        for j in range(1, X):
            down_to_x(j).wait_send()
        for j in range(1, Z):
            down_to_z(j).wait_send()
        down_keep.wait()
        for d in range(1, 4):
            down_share(d).wait()
        out_copy.wait()


def attention_back(carried, qkv_rows, edge, attn, dhb, mixed, inputs, down_sum, out_send, head_size, fsdp_count):
    _, frames, width = dhb.shape
    step = STEP
    groups = width // step
    X = fsdp_count // Z
    R = width // fsdp_count
    R2, half = down_sum.shape[2:]

    def early(i):
        return jnp.minimum(i, groups - 1)

    rows = [pl.BlockSpec((1, 2, frames, step), lambda i, t=t: (t, 0, 0, early(i))) for t in range(3)]
    edge_spec = pl.BlockSpec((1, 8, step), lambda i: (early(i), 0, 0))
    mask = pl.BlockSpec((frames, 1), lambda i: (0, 0), pipeline_mode=pl.Buffered(1))
    whole = pl.BlockSpec((2, frames, width), lambda i: (0, 0, 0), pipeline_mode=pl.Buffered(1))
    mix_spec = pl.BlockSpec((groups, 1, 2, step, step), lambda i: (0, 3, 0, early(i), 0))
    proj_spec = pl.BlockSpec((1, 3, 2, width, step), lambda i: (jnp.clip(i - 1, 0, groups - 1), 0, 0, 0, 0))
    dma, vmem = pltpu.SemaphoreType.DMA, pltpu.VMEM
    n = groups
    return pl.pallas_call(
        functools.partial(attention_back_kernel, X, groups, head_size),
        grid=(groups + 6,),
        out_shape=(
            jax.ShapeDtypeStruct((2, frames, width), F32),
            jax.ShapeDtypeStruct((4, 2, R, width), BF),
            jax.ShapeDtypeStruct((4, R2, half), BF),
            jax.ShapeDtypeStruct(out_send.shape, BF),
        ),
        in_specs=[mask, *rows, edge_spec, mix_spec, whole, whole, whole, proj_spec, ANY, ANY],
        out_specs=(whole, ANY, ANY, ANY),
        scratch_shapes=[
            vmem((2, frames, step), BF), vmem((4, frames, step), F32), vmem((4, frames, step), F32),
            vmem((4, frames, step), F32), vmem((2, 4, 16, step), F32), vmem((2, 3, 2, frames, step), BF),
            vmem((2, 8, step), F32), vmem((n, 8, step), F32),
            vmem((4, width, step), BF), vmem((4, width, step), BF), vmem((2, 4, width, step), BF),
            vmem((2, width, step), BF), vmem((2, width, step), BF), vmem((n, width, step), BF),
            vmem((2, 3, Z, X, R, step), BF), vmem((n, X - 1, 3, Z, R, step), BF),
            vmem((2, 3, Z, R, step), BF), vmem((n, Z - 1, 3, R, step), BF),
            vmem((n, R, step), BF), vmem((n, 2, R, step), BF), vmem((n, 2, R, step), BF), vmem((n, 2, R, step), BF),
            vmem((Z, R2, half), BF), vmem((X - 1, Z, R2, half), BF), vmem((Z - 1, R2, half), BF), vmem((R2, half), BF),
            dma((2,)), dma((n,)), dma, dma((2,)), dma((2,)), dma((n,)),
            dma((2, X - 1)), dma((n, X - 1)), dma((2, X - 1)), dma((n, X - 1)),
            dma((2, Z - 1)), dma((n, Z - 1)), dma((n, 3)), dma((n, 3)), dma((n,)), dma((n,)),
            dma((n, 2)), dma((n, 2)), dma((n, 3)),
            dma((X - 1,)), dma((X - 1,)), dma((Z - 1,)), dma((Z - 1,)), dma((3,)), dma((3,)), dma((2,)),
            dma, dma, pltpu.SemaphoreType.REGULAR,
        ],
        compiler_params=pltpu.CompilerParams(vmem_limit_bytes=63 * 2**20, collective_id=2, has_side_effects=True),
        name="attention_back",
    )(carried, qkv_rows, qkv_rows, qkv_rows, edge, attn, dhb, mixed, inputs, attn, down_sum, out_send)


def per_device(
    frames, cotangent, segment_ids,
    qkv_weight, mix_weight, inner_weight, down_weight, norm_gains,
    qkv_moment, mix_moment, inner_moment, down_moment, gains_moment,
    qkv_average, mix_average, inner_average, down_average, gains_average,
):
    frame_count, positions, width = frames.shape
    head_size = width // HEADS
    hidden = inner_weight.shape[2] // 2
    dp_count, fsdp_count = lax.axis_size("dp"), lax.axis_size("fsdp")
    X = fsdp_count // Z
    devices = dp_count * fsdp_count
    total_frames = frame_count * devices
    dp, fs = lax.axis_index("dp"), lax.axis_index("fsdp")
    y, core = dp // 2, dp % 2
    z, x = fs // X, fs % X
    axes = ("dp", "fsdp")

    def permute(value, target):
        pairs = []
        for d in range(dp_count):
            for f in range(fsdp_count):
                to = target(d, f)
                if to is not None:
                    pairs.append((d * fsdp_count + f, to[0] * fsdp_count + to[1]))
        return lax.ppermute(value, axes, pairs)

    def to_core(value):
        return permute(value, lambda d, f: (d ^ 1, f))

    def to_y(value):
        return permute(value, lambda d, f: (d ^ 2, f))

    def to_x(value, i):
        return permute(value, lambda d, f: (d, (f // X) * X + (f % X + i) % X))

    def to_z(value, k):
        return permute(value, lambda d, f: (d, ((f // X + k) % Z) * X + f % X))

    device = dp * fsdp_count + fs
    padded_ids = jnp.concatenate([jnp.full((1,), -1, jnp.int32), segment_ids])
    window = lax.dynamic_slice_in_dim(padded_ids, device * frame_count, frame_count + 1)
    carried = (window[1:] == window[:-1]).astype(F32)[:, None]

    quarters = (
        qkv_weight[:, :, :width], qkv_weight[:, :, width : 2 * width], qkv_weight[:, :, 2 * width :], mix_weight
    )
    last = width - STEP
    own_rows = jnp.concatenate(
        [
            lax.select_n(dp, *(m[:, :, :last] for m in quarters)),
            lax.select_n(core > 0, *(m[:, :, last:] for m in quarters[:2])),
            lax.select_n(core > 0, *(m[:, :, last:] for m in quarters[2:])),
        ],
        axis=-1,
    ).astype(BF)
    attn_own = own_rows.reshape(positions, -1, width // STEP + 1, STEP).transpose(2, 0, 1, 3)
    inner_own = lax.dynamic_slice(
        inner_weight, (y, 0, core * hidden), (1, inner_weight.shape[1], hidden)
    )[0].astype(BF)
    half_width = width // 2
    down_own = lax.dynamic_slice(
        down_weight, (y, 0, core * half_width), (1, down_weight.shape[1], half_width)
    )[0].astype(BF)
    own_gains = norm_gains.astype(BF).astype(F32)
    gains_own = lax.dynamic_update_slice(jnp.zeros((8, width), F32), own_gains, (0, fs * own_gains.shape[1]))
    frames_by = frames.transpose(1, 0, 2)
    cot = cotangent.transpose(1, 0, 2)
    attn, inner, down, gains, a, qkv_rows, mixed, edge, hres, b_rows, c_rows = forward(
        frames_by, carried, cot, attn_own, inner_own, down_own, gains_own, head_size, fsdp_count
    )
    xf = frames_by.astype(F32)
    r1 = scale_rows(xf)
    n1 = xf * r1
    r2 = scale_rows(hres)
    n2 = hres * r2
    b_rows = b_rows.reshape(2 * frame_count, width)
    c_rows = c_rows.reshape(2 * frame_count, width)
    out, back, out_there, back_there, inner_shares, down_sum = feed_forward(b_rows, c_rows, inner, down, fsdp_count)

    def by_position(mine, theirs):
        return jnp.where(y == 0, jnp.stack([mine, theirs]), jnp.stack([theirs, mine]))

    db = by_position(back, back_there.astype(F32))

    e2 = jnp.sum(db * n2, axis=(0, 1))
    dh = cot.astype(F32) + norm_back(db, n2, gains[1], r2)
    dhb = dh.astype(BF)
    down_sum = down_sum.reshape(Z, X, -1, half_width)
    da, attn_shares, down_shares, out_here = attention_back(
        carried, qkv_rows, edge, attn, dhb, mixed, a, down_sum, out_there, head_size, fsdp_count
    )
    layer_out = (hres + by_position(out, out_here.astype(F32))).astype(BF).transpose(1, 0, 2)
    e1 = jnp.sum(da * n1, axis=(0, 1))
    frames_grad = (dh + norm_back(da, n1, gains[0], r1)).astype(BF).transpose(1, 0, 2)

    inner_grad = inner_shares.reshape((2, 2) + inner_shares.shape[1:])
    inner_grad = jnp.concatenate([inner_grad[:, 0], inner_grad[:, 1]], axis=-1).astype(F32)
    down_grad = down_shares.reshape((2, 2) + down_shares.shape[1:])
    down_grad = jnp.concatenate([down_grad[:, 0], down_grad[:, 1]], axis=-1).astype(F32)
    qkv_grad = jnp.concatenate([attn_shares[0], attn_shares[1], attn_shares[2]], axis=-1).astype(F32)
    mix_grad = attn_shares[3].astype(F32)

    gains_part = jnp.stack([e1, e2])
    gains_part = gains_part + to_core(gains_part)
    gains_part = gains_part + to_y(gains_part)
    gains_grid = gains_part.reshape(2, Z, X, -1).transpose(1, 2, 0, 3)
    column = lax.dynamic_index_in_dim(gains_grid, x, 1, keepdims=False)
    for i in range(1, X):
        column = column + to_x(lax.dynamic_index_in_dim(gains_grid, lax.rem(x + i, X), 1, keepdims=False), i)
    gains_grad = lax.dynamic_index_in_dim(column, z, 0, keepdims=False)
    for kk in range(1, Z):
        gains_grad = gains_grad + to_z(lax.dynamic_index_in_dim(column, lax.rem(z + kk, Z), 0, keepdims=False), kk)

    step_size = step_rate / math.sqrt(total_frames)
    grads = (qkv_grad, mix_grad, inner_grad, down_grad, gains_grad)
    new = [
        owner_update(w, g, m, av, step_size)
        for w, g, m, av in zip(
            (qkv_weight, mix_weight, inner_weight, down_weight, norm_gains),
            grads,
            (qkv_moment, mix_moment, inner_moment, down_moment, gains_moment),
            (qkv_average, mix_average, inner_average, down_average, gains_average),
        )
    ]
    return (
        (layer_out, frames_grad) + grads
        + tuple(n[0] for n in new) + tuple(n[1] for n in new) + tuple(n[2] for n in new)
    )


def solution(mesh):
    rows = P(("dp", "fsdp"), None, None)
    weight = P(None, "fsdp", None)
    gains = P(None, "fsdp")
    weights = (weight,) * 4 + (gains,)
    return jax.shard_map(
        per_device,
        mesh=mesh,
        in_specs=(rows, rows, P()) + weights * 3,
        out_specs=(rows, rows) + weights * 4,
        check_vma=False,
    )
```

```python
import functools
import math

import jax
import jax.numpy as jnp
from jax import lax
from jax.experimental import pallas as pl
from jax.experimental.pallas import tpu as pltpu
from jax.sharding import PartitionSpec as P

HEADS = 16
Z = 4
MESH = pl.DeviceIdType.MESH
ANY = pl.BlockSpec(memory_space=pl.ANY)
BF = jnp.bfloat16
F32 = jnp.float32

norm_eps = 1e-05
momentum_rate = 0.5
average_rate = 0.5
step_rate = 0.05
VMEM_BYTES = 60 * 1024 * 1024


def nn(a, b):
    return lax.dot_general(a, b, (((1,), (0,)), ((), ())), preferred_element_type=F32)


def nt(a, b):
    return lax.dot_general(a, b, (((1,), (1,)), ((), ())), preferred_element_type=F32)


def tn(a, b):
    return lax.dot_general(a, b, (((0,), (0,)), ((), ())), preferred_element_type=F32)


def scale_rows(values):
    square = jnp.mean(values * values, axis=-1, keepdims=True) + norm_eps
    inverse = lax.rsqrt(square)
    return inverse * (1.5 - 0.5 * square * inverse * inverse)


def norm_back(grad_in, normed, gain_row, inverse):
    scaled = grad_in * gain_row
    return inverse * (scaled - normed * jnp.mean(scaled * normed, axis=-1, keepdims=True))


def owner_update(weight, gradient, moment, average, step_size):
    moment_new = momentum_rate * moment + gradient
    weight_new = weight - step_size * (gradient + momentum_rate * moment_new)
    average_new = average_rate * average + (1.0 - average_rate) * weight_new
    return (moment_new, average_new, weight_new)


PAIRS = ((0, 0), (0, 1), (0, 2), (1, 0), (1, 1), (1, 2), (1, 3))
SPANS = ((0, range(0, 3)), (1, range(3, 7)))
CHUNK = 128
STEP = 256


def total_of(values):
    return functools.reduce(jnp.add, values)


def remote_copy(src, dst, send_sem, recv_sem, peer):
    return pltpu.make_async_remote_copy(
        src_ref=src, dst_ref=dst, send_sem=send_sem, recv_sem=recv_sem, device_id=peer, device_id_type=MESH
    )


def head_ones(lanes, head_size):
    row = lax.broadcasted_iota(jnp.int32, (lanes, lanes), 0) // head_size
    column = lax.broadcasted_iota(jnp.int32, (lanes, lanes), 1) // head_size
    return (row == column).astype(BF)


def per_head(left, right, ones):
    rows = left[0].shape[0]
    products = [(left[p] * right[n]).astype(BF) for p, n in PAIRS]
    sums = nn(jnp.concatenate(products, axis=0), ones)
    return [sums[m * rows : (m + 1) * rows] for m in range(len(PAIRS))]


def head_probs(scores, span, allowed, scale):
    s = [jnp.where(allowed, scores[m] * scale, -1e30) if PAIRS[m][1] < 2 else scores[m] * scale for m in span]
    top = functools.reduce(jnp.maximum, s)
    e = [jnp.exp(value - top) for value in s]
    e = [jnp.where(allowed, value, 0.0) if PAIRS[m][1] < 2 else value for m, value in zip(span, e)]
    inverse = 1.0 / total_of(e)
    return [value * inverse for value in e]


def forward_kernel(
    X, groups, head_size, frames, carried, cot, attn_own, inner_own, down_own, gains_own,
    attn, inner, down, gains_out, inputs_out, rows_out, mixed_out, edge_out, hres_out, b_rows, c_rows,
    gains, inputs, rows_in, mixed, before, hres, b, proj, mix, edge_send, edge_recv,
    send_up, recv_up, send_down, recv_down, send_x, recv_x, send_y, recv_y, send_c, recv_c, send_r, recv_r,
    send_g, recv_g, send_e, recv_e, send_b, recv_b, send_q, recv_q, local_sem, out_sem,
):
    dp, fs = lax.axis_index("dp"), lax.axis_index("fsdp")
    F = Z * X
    y, core = dp // 2, dp % 2
    z, x = fs // X, fs % X
    me = dp * F + fs
    devices = 4 * F
    count = frames.shape[1]
    core_peer = (y * 2 + 1 - core, fs)
    y_peer = ((1 - y) * 2 + core, fs)
    up_peer = (dp, lax.rem(z + 1, Z) * X + x)
    down_peer = (dp, lax.rem(z + Z - 1, Z) * X + x)
    before_me = ((me - 1 + devices) % devices // F, (me - 1 + devices) % devices % F)
    after_me = ((me + 1) % devices // F, (me + 1) % devices % F)

    def z_peer(k):
        return (dp, lax.rem(z + k, Z) * X + x)

    def x_peer(i):
        return (dp, z * X + lax.rem(x + i, X))

    UNITS = unit_list(groups, inner_own.shape[1], down_own.shape[1])

    def own(u):
        kind, n, columns = UNITS[u]
        if kind in ("quarter", "low", "high"):
            return attn_own.at[n if kind != "high" else n + 1]
        return (down_own if kind == "down" else inner_own).at[:, columns]

    def part_of(u, core_index, plane):
        kind = UNITS[u][0]
        if kind == "quarter":
            return plane * 2 + core_index
        return 2 + core_index if kind == "high" else core_index

    def whole(u, part):
        kind, n, columns = UNITS[u]
        if kind == "down":
            return down.at[part, :, columns]
        if kind == "inner":
            return inner.at[part, :, columns]
        return attn.at[n, part]

    def place(u, source, part=None):
        kind, n, columns = UNITS[u]
        part = part_of(u, core, y) if part is None else part
        if kind == "down":
            R = down_own.shape[0]
            return down.at[part, pl.ds(source * R, R), columns]
        if kind == "inner":
            R = inner_own.shape[0]
            return inner.at[part, pl.ds(source * R, R), columns]
        R = attn_own.shape[2]
        return attn.at[n, part, :, pl.ds(source * R, R), :]

    barrier = pltpu.get_barrier_semaphore()
    peers = [z_peer(k) for k in range(1, Z)] + [x_peer(i) for i in range(1, X)]
    peers += [core_peer, y_peer, before_me, after_me]
    for peer in peers:
        pl.semaphore_signal(barrier, inc=1, device_id=peer, device_id_type=MESH)
    pl.semaphore_wait(barrier, len(peers))

    sent, local = [], []

    def send(condition, make):
        remote_copy(*make()).start()
        sent.append((condition, make))

    def wait_send(condition, make):
        def action():
            remote_copy(*make()).wait_send()

        if condition is None:
            action()
        else:
            pl.when(condition())(action)

    def wait_recv(dst, recv_sem, send_sem):
        remote_copy(dst, dst, send_sem, recv_sem, core_peer).wait_recv()

    def store(src, dst):
        copy = pltpu.make_async_copy(src, dst, out_sem.at[len(local)])
        copy.start()
        local.append(copy)

    def spread(u, row, mine, condition):
        def src():
            return own(u) if mine else place(u, row() * X + x)

        for i in range(1, X):
            send(
                condition,
                lambda i=i: (
                    src(), place(u, row() * X + x), send_x.at[u, row(), i], recv_x.at[u, row(), i], x_peer(i)
                ),
            )
        to_plane(u, lambda: row() * X + x, src, condition)

    def to_plane(u, source, src, condition):
        if UNITS[u][0] == "quarter":
            send(
                condition,
                lambda: (src(), place(u, source()), send_y.at[u, source()], recv_y.at[u, source()], y_peer),
            )

    def start_unit(u):
        def below_top():
            return z < Z - 1

        def above_bottom():
            return z > 0

        def upward():
            return (own(u), place(u, fs), send_up.at[u, 1], recv_up.at[u, 1], up_peer)

        def downward():
            return (own(u), place(u, fs), send_down.at[u, 1], recv_down.at[u, 1], down_peer)

        pl.when(below_top())(lambda: send(below_top, upward))
        pl.when(above_bottom())(lambda: send(above_bottom, downward))
        spread(u, lambda: z, True, None)
        store(own(u), place(u, fs))

    def hop(u, k):
        def side(reached, row, further, send_sem, recv_sem, peer):
            def here():
                return place(u, row() * X + x)

            def both():
                return reached() & further()

            def action():
                wait_recv(here(), recv_sem.at[u, k], send_sem.at[u, k])
                if k < Z - 1:
                    pl.when(further())(
                        lambda: send(
                            both, lambda: (here(), here(), send_sem.at[u, k + 1], recv_sem.at[u, k + 1], peer)
                        )
                    )
                spread(u, row, False, reached)

            pl.when(reached())(action)

        side(lambda: z >= k, lambda: z - k, lambda: z < Z - 1, send_up, recv_up, up_peer)
        side(lambda: z + k < Z, lambda: z + k, lambda: z > 0, send_down, recv_down, down_peer)

    def arrivals(u):
        for row in range(Z):
            for i in range(1, X):
                column = lax.rem(x - i + X, X)
                source = row * X + column
                wait_recv(place(u, source), recv_x.at[u, row, i], send_x.at[u, row, i])
                to_plane(u, lambda source=source: source, lambda source=source: place(u, source), None)
        local[own_store[u]].wait()
        mine = whole(u, part_of(u, core, y))
        send(None, lambda: (mine, mine, send_c.at[u], recv_c.at[u], core_peer))

    def relay(u):
        if UNITS[u][0] != "quarter":
            return
        part = (1 - y) * 2 + core
        for source in range(F):
            wait_recv(place(u, source, part), recv_y.at[u, source], send_y.at[u, source])
        theirs = whole(u, part)
        send(None, lambda: (theirs, theirs, send_r.at[u], recv_r.at[u], core_peer))

    def complete(u):
        wait_recv(whole(u, part_of(u, 1 - core, y)), recv_c.at[u], send_c.at[u])
        if UNITS[u][0] == "quarter":
            wait_recv(whole(u, (1 - y) * 2 + 1 - core), recv_r.at[u], send_r.at[u])

    scale = 1.0 / math.sqrt(head_size)

    def gather_gains():
        keep = pltpu.make_async_copy(gains_own, gains.at[fs], local_sem.at[0])
        keep.start()
        for k in range(1, Z):
            send(None, lambda k=k: (gains_own, gains.at[fs], send_g.at[0, k], recv_g.at[0, k], z_peer(k)))
        for i in range(1, X):
            send(None, lambda i=i: (gains_own, gains.at[fs], send_g.at[i, 0], recv_g.at[i, 0], x_peer(i)))
        keep.wait()

    def chunk_source(k, i):
        return lax.rem(z - k + Z, Z) * X + lax.rem(x - i + X, X)

    def pass_gains():
        for k in range(1, Z):
            here = gains.at[chunk_source(k, 0)]
            wait_recv(here, recv_g.at[0, k], send_g.at[0, k])
            for i in range(1, X):
                send(
                    None,
                    lambda here=here, i=i, k=k: (here, here, send_g.at[i, k], recv_g.at[i, k], x_peer(i)),
                )

    def take_gains():
        for k in range(Z):
            for i in range(1, X):
                wait_recv(gains.at[chunk_source(k, i)], recv_g.at[i, k], send_g.at[i, k])
        total = gains[0]
        for source in range(1, F):
            total = total + gains[source]
        gains_out[...] = total

    def norm_rows():
        def chunk(c, carry):
            rows = pl.ds(pl.multiple_of(c * CHUNK, CHUNK), CHUNK)
            for p in range(2):
                value = frames[p, rows, :].astype(F32)
                inputs[p, rows, :] = (value * scale_rows(value) * gains_out[0:1, :]).astype(BF)
            return carry

        lax.fori_loop(0, count // CHUNK, chunk, 0)
        store(inputs, inputs_out)

    def heads(m):
        columns = slice(m * STEP, (m + 1) * STEP)
        load = pltpu.make_async_copy(attn.at[m, pl.ds(0, 3)], proj, local_sem.at[0])
        load.start()
        load.wait()
        for t in (1, 2, 0):
            for p in range(2):
                rows_in[t, p, :, columns] = nn(inputs[p], proj[t, p]).astype(BF)
                if t > 0:
                    tail = rows_in[t, p, count - 16 :, columns].astype(F32)
                    row = 2 * (t - 1) + p
                    edge_send[m, row : row + 1, :] = tail[15:16, :]
            if t == 2:
                to_after = remote_copy(edge_send.at[m], edge_recv.at[m], send_e.at[m], recv_e.at[m], after_me)
                pl.when(me < devices - 1)(to_after.start)
        pl.when(me > 0)(to_after.wait_recv)
        first = lax.broadcasted_iota(jnp.int32, (count, STEP), 0) == 0
        for t in range(2):
            for p in range(2):
                n = 2 * t + p
                shifted = pltpu.roll(rows_in[1 + t, p, :, columns].astype(F32), 1, 0)
                before[n] = jnp.where(first, edge_recv[m, n : n + 1, :], shifted)
        ones = head_ones(STEP, head_size)

        def chunk(c, carry):
            rows = pl.ds(pl.multiple_of(c * CHUNK, CHUNK), CHUNK)
            allowed = jnp.broadcast_to(carried[rows, :], (CHUNK, STEP)) > 0.5
            queries, here_k, here_v = (
                [rows_in[t, p, rows, columns].astype(F32) for p in range(2)] for t in range(3)
            )
            keys = [before[p, rows, :] for p in range(2)] + here_k
            values = [before[2 + p, rows, :] for p in range(2)] + here_v
            scores = per_head(queries, keys, ones)
            for p, span in SPANS:
                probs = head_probs(scores, span, allowed, scale)
                terms = [pr.astype(BF).astype(F32) * values[PAIRS[n][1]] for n, pr in zip(span, probs)]
                mixed[p, rows, columns] = total_of(terms).astype(BF)
            return carry

        lax.fori_loop(0, count // CHUNK, chunk, 0)

    def load_mix():
        return pltpu.make_async_copy(attn.at[:, 3], mix, local_sem.at[1])

    def finish_rows():
        load_mix().wait()
        for turn in range(2):
            p = 1 - y if turn == 0 else y
            for m in range(groups):
                columns = slice(m * STEP, (m + 1) * STEP)
                hres[p, :, columns] = frames[p, :, columns].astype(F32) + nn(mixed[p], mix[m, p])

            def chunk(c, carry):
                rows = pl.ds(pl.multiple_of(c * CHUNK, CHUNK), CHUNK)
                value = hres[p, rows, :]
                b[turn, rows, :] = (value * scale_rows(value) * gains_out[1:2, :]).astype(BF)
                return carry

            lax.fori_loop(0, count // CHUNK, chunk, 0)
            if turn == 0:
                send(None, lambda: (b.at[0], b_rows.at[1], send_b, recv_b, y_peer))
            else:
                store(b.at[1], b_rows.at[0])
        store(hres, hres_out)

    @pl.when(me == 0)
    def _():
        edge_recv[...] = jnp.zeros_like(edge_recv)

    own_store = {}
    last_of = {kind_n[1]: u for u, kind_n in enumerate(UNITS) if kind_n[0] in ("quarter", "low", "high")}
    last_plane = max(u for u, kind_n in enumerate(UNITS) if kind_n[0] == "quarter")
    store(cot.at[y], c_rows.at[0])
    gather_gains()
    for tick in range(len(UNITS) + Z + 2):
        if tick < len(UNITS):
            own_store[tick] = len(local)
            start_unit(tick)
        for k in range(1, Z):
            if 0 <= tick - k < len(UNITS):
                hop(tick - k, k)
        if tick == 1:
            pass_gains()
        if tick == 2:
            take_gains()
            norm_rows()
        u = tick - Z
        if 0 <= u < len(UNITS):
            arrivals(u)
            if u == last_plane:
                send(None, lambda: (cot.at[1 - y], c_rows.at[1], send_q, recv_q, y_peer))
        u = tick - Z - 1
        if 0 <= u < len(UNITS):
            relay(u)
            complete(u)
            for m in range(groups):
                if last_of[m] == u:
                    if m == groups - 1:
                        load_mix().start()
                    heads(m)
                    if m == groups - 1:
                        store(rows_in, rows_out)
                        store(mixed, mixed_out)
                        store(edge_recv, edge_out)
                        finish_rows()
    wait_recv(b_rows.at[1], recv_b, send_b)
    wait_recv(c_rows.at[1], recv_q, send_q)
    for condition, make in sent:
        wait_send(condition, make)
    for n, copy in enumerate(local):
        if n not in own_store.values():
            copy.wait()

    @pl.when(me < devices - 1)
    def _():
        for m in range(groups):
            remote_copy(edge_send.at[m], edge_recv.at[m], send_e.at[m], recv_e.at[m], after_me).wait_send()


def unit_list(groups, inner_width, down_width):
    units = [("quarter", n, None) for n in range(groups - 1)]
    units += [("low", groups - 1, None), ("high", groups - 1, None)]
    units += [("down", 0, slice(0, down_width // 2)), ("down", 0, slice(down_width // 2, down_width))]
    tiles = inner_width // 128
    cuts = [128 * (tiles * n // 4) for n in range(5)]
    return units + [("inner", 0, slice(lo, hi)) for lo, hi in zip(cuts, cuts[1:])]


def forward(frames, carried, cot, attn_own, inner_own, down_own, gains_own, head_size, fsdp_count):
    X = fsdp_count // Z
    _, count, width = frames.shape
    _, _, R, _ = attn_own.shape
    groups = width // STEP
    units = len(unit_list(groups, inner_own.shape[1], down_own.shape[1]))
    dma, vmem = pltpu.SemaphoreType.DMA, pltpu.VMEM
    whole = pl.BlockSpec(memory_space=pltpu.VMEM)
    act = jax.ShapeDtypeStruct((2, count, width), BF)
    return pl.pallas_call(
        functools.partial(forward_kernel, X, groups, head_size),
        out_shape=(
            jax.ShapeDtypeStruct((groups, 4, 2, R * fsdp_count, STEP), BF),
            jax.ShapeDtypeStruct((2, inner_own.shape[0] * fsdp_count, inner_own.shape[1]), BF),
            jax.ShapeDtypeStruct((2, down_own.shape[0] * fsdp_count, down_own.shape[1]), BF),
            jax.ShapeDtypeStruct(gains_own.shape, F32),
            act,
            jax.ShapeDtypeStruct((3, 2, count, width), BF),
            act,
            jax.ShapeDtypeStruct((groups, 8, STEP), F32),
            jax.ShapeDtypeStruct((2, count, width), F32),
            act,
            act,
        ),
        in_specs=[whole] * 7,
        out_specs=(ANY,) * 3 + (whole,) + (ANY,) * 7,
        scratch_shapes=[
            vmem((fsdp_count,) + gains_own.shape, F32),
            vmem((2, count, width), BF), vmem((3, 2, count, width), BF), vmem((2, count, width), BF),
            vmem((4, count, STEP), F32), vmem((2, count, width), F32), vmem((2, count, width), BF),
            vmem((3, 2, width, STEP), BF), vmem((groups, 2, width, STEP), BF),
            vmem((groups, 8, STEP), F32), vmem((groups, 8, STEP), F32),
            dma((units, Z)), dma((units, Z)), dma((units, Z)), dma((units, Z)),
            dma((units, Z, X)), dma((units, Z, X)), dma((groups, fsdp_count)), dma((groups, fsdp_count)),
            dma((units,)), dma((units,)), dma((groups,)), dma((groups,)),
            dma((X, Z)), dma((X, Z)), dma((groups,)), dma((groups,)), dma, dma, dma, dma,
            dma((2,)), dma((units + 8,)),
        ],
        compiler_params=pltpu.CompilerParams(
            vmem_limit_bytes=VMEM_BYTES, collective_id=0, has_side_effects=True
        ),
        name="attention_forward",
    )(frames, carried, cot, attn_own, inner_own, down_own, gains_own)


def feed_forward_kernel(
    X, J, b, c, inner, down, out_mine, back_mine, out_theirs, back_recv, inner_all, down_columns, down_sum,
    out, back, down_here, down_there, down_from_core, down_stage, down_column, down_from_x, mine, other, from_core, summed, from_x, column, from_z, final, staged,
    s1, r1, s2, r2, s3, r3, s5, r5, s6, r6, s7, r7, local_sem,
    s_stage, s_own, sdx, rdx, s_column,
):
    j = pl.program_id(0)
    half = down.shape[2]
    rows_here = out_mine.shape[0]
    R, step = final.shape[1:]
    dp, fs = lax.axis_index("dp"), lax.axis_index("fsdp")
    y, core = dp // 2, dp % 2
    z, x = fs // X, fs % X
    core_peer = (y * 2 + 1 - core, fs)
    y_peer = ((1 - y) * 2 + core, fs)

    def z_peer(k):
        return (dp, lax.rem(z + k, Z) * X + x)

    def x_peer(i):
        return (dp, z * X + lax.rem(x + i, X))

    def dp_peer(d):
        return (((y + d // 2) % 2) * 2 + (core + d % 2) % 2, fs)

    def to_core(n):
        return remote_copy(other.at[n % 2], from_core.at[n], s1.at[n % 2], r1.at[n], core_peer)

    def to_x(n, i):
        return remote_copy(
            summed.at[n % 2, :, lax.rem(x + i, X)], from_x.at[n, i - 1], s2.at[n % 2, i - 1], r2.at[n, i - 1], x_peer(i)
        )

    def to_z(n, k):
        return remote_copy(
            column.at[n % 2, lax.rem(z + k, Z)], from_z.at[n, k - 1], s3.at[n % 2, k - 1], r3.at[n, k - 1], z_peer(k)
        )

    def place(n, owner):
        return inner_all.at[owner, :, pl.ds(pl.multiple_of(n * step, step), step)]

    def share(n, d):
        return remote_copy(final.at[n], place(n, dp), s5.at[n, d - 1], r5.at[n, d - 1], dp_peer(d))

    def keep(n):
        return pltpu.make_async_copy(final.at[n], place(n, dp), local_sem.at[n])

    exchange = remote_copy(staged, back_recv, s6, r6, y_peer)

    R2 = down_column.shape[1]
    ends = [-(-(g + 1) * X * R2 // step) - 1 for g in range(Z)]

    def down_rows(g, column):
        return down_sum.at[pl.ds((g * X + column) * R2, R2), :]

    def down_store(n):
        return pltpu.make_async_copy(
            down_stage.at[n % 2], down_sum.at[pl.ds(pl.multiple_of(n * step, step), step), :], s_stage.at[n % 2]
        )

    def down_load(g):
        return pltpu.make_async_copy(down_rows(g, x), down_column.at[g], s_own.at[g])

    def down_to_x(g, i):
        return remote_copy(
            down_rows(g, lax.rem(x + i, X)), down_from_x.at[g, i - 1], sdx.at[g, i - 1], rdx.at[g, i - 1], x_peer(i)
        )

    def down_keep(g):
        return pltpu.make_async_copy(down_column.at[g], down_columns.at[g], s_column.at[g])

    def down_to_core(n):
        return remote_copy(down_there.at[n % 2], down_from_core.at[n], s7.at[n % 2], r7.at[n], core_peer)

    @pl.when(j == 0)
    def _():
        barrier = pltpu.get_barrier_semaphore()
        peers = [z_peer(k) for k in range(1, Z)] + [x_peer(i) for i in range(1, X)]
        peers += [dp_peer(d) for d in range(1, 4)]
        for peer in peers:
            pl.semaphore_signal(barrier, inc=1, device_id=peer, device_id_type=MESH)
        pl.semaphore_wait(barrier, len(peers))
        out[...] = jnp.zeros_like(out)
        back[...] = jnp.zeros_like(back)

    @pl.when((j >= 2) & (j < J + 2))
    def _():
        down_store(j - 2).wait()

    for g in range(Z):
        @pl.when(j == ends[g] + 2)
        def _():
            for i in range(1, X):
                down_to_x(g, i).start()
            down_load(g).start()

    @pl.when((j >= 1) & (j < J + 1))
    def _():
        n = j - 1
        to_core(n).wait_recv()

        @pl.when(n >= 2)
        def _():
            for i in range(1, X):
                to_x(n - 2, i).wait_send()

        down_to_core(n).wait_recv()
        down_stage[n % 2] = (down_here[n % 2].astype(F32) + down_from_core[n].astype(F32)).astype(BF)
        down_store(n).start()
        total = (mine[n % 2].astype(F32) + from_core[n].astype(F32)).astype(BF)
        summed[n % 2] = total.reshape(summed.shape[1:])
        for i in range(1, X):
            to_x(n, i).start()

    @pl.when((j >= 2) & (j < J + 2))
    def _():
        n = j - 2
        for i in range(1, X):
            to_x(n, i).wait_recv()

        @pl.when(n >= 2)
        def _():
            for k in range(1, Z):
                to_z(n - 2, k).wait_send()

        total = summed[n % 2, :, x].astype(F32)
        for i in range(1, X):
            total = total + from_x[n, i - 1].astype(F32)
        column[n % 2] = total.astype(BF)
        for k in range(1, Z):
            to_z(n, k).start()

    for g in range(Z):
        @pl.when(j == ends[g] + 3)
        def _():
            down_load(g).wait()
            for i in range(1, X):
                down_to_x(g, i).wait_recv()
            total = down_column[g].astype(F32) + total_of([down_from_x[g, i].astype(F32) for i in range(X - 1)])
            down_column[g] = total.astype(BF)
            down_keep(g).start()

    @pl.when((j >= 3) & (j < J + 3))
    def _():
        n = j - 3
        for k in range(1, Z):
            to_z(n, k).wait_recv()
        total = column[n % 2, z].astype(F32)
        for k in range(1, Z):
            total = total + from_z[n, k - 1].astype(F32)
        final[n] = total.astype(BF)
        keep(n).start()
        for d in range(1, 4):
            share(n, d).start()

    @pl.when(j < J)
    def _():
        rows, cot = b[...], c[...]
        gate = nn(rows, inner[0])
        up = nn(rows, inner[1])
        squashed = jax.nn.sigmoid(gate)
        active = gate * squashed
        hidden = (active * up).astype(BF)
        hidden_grad = nt(cot[:, :half], down[0]) + nt(cot[:, half:], down[1])
        gate_grad = (hidden_grad * up * (squashed * (1.0 + gate * (1.0 - squashed)))).astype(BF)
        up_grad = (hidden_grad * active).astype(BF)
        gate_term = tn(rows, gate_grad).astype(BF)
        up_term = tn(rows, up_grad).astype(BF)

        @pl.when(j >= 2)
        def _():
            to_core(j - 2).wait_send()
            down_to_core(j - 2).wait_send()

        mine[j % 2] = jnp.where(core == 0, gate_term, up_term)
        other[j % 2] = jnp.where(core == 0, up_term, gate_term)
        to_core(j).start()
        down_term = tn(hidden, cot).astype(BF)
        down_here[j % 2] = jnp.where(core == 0, down_term[:, :half], down_term[:, half:])
        down_there[j % 2] = jnp.where(core == 0, down_term[:, half:], down_term[:, :half])
        down_to_core(j).start()
        for n in range(2):
            part = slice(n * half, (n + 1) * half)
            out[:, part] += nn(hidden, down[n])
        back[...] += nt(gate_grad, inner[0]) + nt(up_grad, inner[1])

    @pl.when(j == J - 1)
    def _():
        staged[...] = back[rows_here:, :].astype(BF)
        exchange.start()
        out_theirs[...] = out[rows_here:, :].astype(BF)
        out_mine[...] = out[:rows_here, :]
        back_mine[...] = back[:rows_here, :]

    @pl.when(j == J + 2)
    def _():
        for n in (J - 2, J - 1):
            to_core(n).wait_send()
            down_to_core(n).wait_send()
            for i in range(1, X):
                to_x(n, i).wait_send()
            for k in range(1, Z):
                to_z(n, k).wait_send()

        def finish(n, carry):
            keep(n).wait()
            for d in range(1, 4):
                share(n, d).wait()
            return carry

        lax.fori_loop(0, J, finish, 0)
        exchange.wait()
        for g in range(Z):
            down_keep(g).wait()
            for i in range(1, X):
                down_to_x(g, i).wait_send()


def feed_forward(b, c, inner, down, fsdp_count):
    rows, width = b.shape
    _, _, hidden = inner.shape
    half = down.shape[2]
    step = 256
    J = hidden // step
    X = fsdp_count // Z
    R, R2 = width // fsdp_count, hidden // fsdp_count
    whole = pl.BlockSpec((rows, width), lambda j: (0, 0), pipeline_mode=pl.Buffered(1))
    part = pl.BlockSpec((rows // 2, width), lambda j: (0, 0), pipeline_mode=pl.Buffered(1))
    inner_spec = pl.BlockSpec((2, width, step), lambda j: (0, 0, jnp.minimum(j, J - 1)))
    down_spec = pl.BlockSpec((2, step, half), lambda j: (0, jnp.minimum(j, J - 1), 0))
    dma, vmem = pltpu.SemaphoreType.DMA, pltpu.VMEM
    return pl.pallas_call(
        functools.partial(feed_forward_kernel, X, J),
        grid=(J + 3,),
        out_shape=(
            jax.ShapeDtypeStruct((rows // 2, width), F32),
            jax.ShapeDtypeStruct((rows // 2, width), F32),
            jax.ShapeDtypeStruct((rows // 2, width), BF),
            jax.ShapeDtypeStruct((rows // 2, width), BF),
            jax.ShapeDtypeStruct((4, R, hidden), BF),
            jax.ShapeDtypeStruct((Z, R2, half), BF),
            jax.ShapeDtypeStruct((hidden, half), BF),
        ),
        in_specs=[whole, whole, inner_spec, down_spec],
        out_specs=(part, part, part, ANY, ANY, ANY, ANY),
        scratch_shapes=[
            vmem((rows, width), F32), vmem((rows, width), F32),
            vmem((2, step, half), BF), vmem((2, step, half), BF), vmem((J, step, half), BF),
            vmem((2, step, half), BF), vmem((Z, R2, half), BF), vmem((Z, X - 1, R2, half), BF),
            vmem((2, width, step), BF), vmem((2, width, step), BF), vmem((J, width, step), BF),
            vmem((2, Z, X, R, step), BF), vmem((J, X - 1, Z, R, step), BF),
            vmem((2, Z, R, step), BF), vmem((J, Z - 1, R, step), BF),
            vmem((J, R, step), BF), vmem((rows // 2, width), BF),
            dma((2,)), dma((J,)), dma((2, X - 1)), dma((J, X - 1)), dma((2, Z - 1)), dma((J, Z - 1)),
            dma((J, 3)), dma((J, 3)), dma, dma, dma((2,)), dma((J,)), dma((J,)),
            dma((2,)), dma((Z,)), dma((Z, X - 1)), dma((Z, X - 1)), dma((Z,)),
        ],
        compiler_params=pltpu.CompilerParams(
            vmem_limit_bytes=VMEM_BYTES, collective_id=1, has_side_effects=True
        ),
        cost_estimate=pl.CostEstimate(flops=18 * rows * width * hidden, bytes_accessed=60 * 2**20, transcendentals=0),
        name="feed_forward",
    )(b, c, inner, down)


def total_of(values):
    return functools.reduce(jnp.add, values)


def attention_back_kernel(
    X, groups, head_size, carried, q, k, v, edge, mix, dhb, mixed, inputs, proj, gains, second_gain, frames_in, down_in, out_send,
    frames_grad, gains_sum, attn_all, down_all, out_recv,
    da, gain_terms, gain_from, mixed_grad, before, terms_before, terms_here, tails, grads, edge_send, edge_recv,
    mine, other, from_core, keep_y, send_y, from_y, summed, from_x, column, from_z, final, plane, from_plane, final_plane,
    down_mine, down_from_z, down_final,
    s_edge, r_edge, s1, r1, sy, ry, sxa, rxa, sxb, rxb, sz, rz, sf, rf, sp, rp, sc, rc, local_sem,
    s_out, r_out, sg, rg, frame_sem, sdz, rdz, sdf, rdf, down_sem, free,
):
    i = pl.program_id(0)
    frames, step = q.shape[2:]
    R, thin = final.shape[1:]
    subs = 2 * groups
    slots = from_core.shape[0]
    dp, fs = lax.axis_index("dp"), lax.axis_index("fsdp")
    F = Z * X
    y, core = dp // 2, dp % 2
    z, x = fs // X, fs % X
    me = dp * F + fs
    devices = 4 * F
    core_peer = (y * 2 + 1 - core, fs)
    y_peer = ((1 - y) * 2 + core, fs)
    before_me = ((me - 1 + devices) % devices // F, (me - 1 + devices) % devices % F)
    after_me = ((me + 1) % devices // F, (me + 1) % devices % F)

    def z_peer(n):
        return (dp, lax.rem(z + n, Z) * X + x)

    def x_peer(n):
        return (dp, z * X + lax.rem(x + n, X))

    def dp_peer(d):
        return (((y + d // 2) % 2) * 2 + (core + d % 2) % 2, fs)

    def to_before(n):
        return remote_copy(edge_send.at[n % 2], edge_recv.at[n], s_edge.at[n % 2], r_edge.at[n], before_me)

    def to_core(n):
        return remote_copy(other.at[n % 2], from_core.at[n % slots], s1.at[n % 2], r1.at[n % slots], core_peer)

    def to_y(n):
        return remote_copy(send_y.at[n % 2], from_y.at[n], sy.at[n % 2], ry.at[n], y_peer)

    def to_x_early(n, j):
        return remote_copy(
            summed.at[n % 3, pl.ds(1, 2), :, lax.rem(x + j, X)], from_x.at[n, j - 1, pl.ds(1, 2)],
            sxa.at[n % 3, j - 1], rxa.at[n, j - 1], x_peer(j),
        )

    def to_x_late(n, j):
        return remote_copy(
            summed.at[n % 3, 0, :, lax.rem(x + j, X)], from_x.at[n, j - 1, 0],
            sxb.at[n % 3, j - 1], rxb.at[n, j - 1], x_peer(j),
        )

    def to_z(n, j):
        return remote_copy(
            column.at[n % 2, :, lax.rem(z + j, Z)], from_z.at[n, j - 1], sz.at[n % 2, j - 1], rz.at[n, j - 1], z_peer(j)
        )

    def place(n, t):
        return attn_all.at[t, core, :, pl.ds(pl.multiple_of(n * thin, thin), thin)]

    def share(n, d):
        return remote_copy(final.at[n], place(n, y), sf.at[n, d - 1], rf.at[n, d - 1], dp_peer(d))

    def relay(n):
        return remote_copy(place(n, 1 - y), place(n, 1 - y), sf.at[n, 2], rf.at[n, 2], core_peer)

    def down_to_z(k):
        return remote_copy(
            down_in.at[lax.rem(z + k, Z)], down_from_z.at[k - 1], sdz.at[k - 1], rdz.at[k - 1], z_peer(k)
        )

    def down_share(d):
        return remote_copy(down_final, down_all.at[dp], sdf.at[d - 1], rdf.at[d - 1], dp_peer(d))

    def down_relay():
        part = down_all.at[(1 - y) * 2 + core]
        return remote_copy(part, part, sdf.at[2], rdf.at[2], core_peer)

    def to_plane(n):
        return remote_copy(plane.at[n], from_plane.at[n], sp.at[n], rp.at[n], y_peer)

    def share_core(n, t):
        return remote_copy(final_plane.at[n, t], place(n, 2 + t), sc.at[n, t], rc.at[n, t], core_peer)

    def keep(n, t):
        src = final.at[n] if t == 0 else final_plane.at[n, t - 1]
        return pltpu.make_async_copy(src, place(n, y if t == 0 else 1 + t), local_sem.at[n, t])

    def load_frames(g):
        dst = grads.at[g] if g < 3 else mixed_grad
        return pltpu.make_async_copy(frames_in.at[:, :, pl.ds(g * step, step)], dst, frame_sem.at[g])

    def gain_copy(level, n):
        peer = (core_peer, y_peer, x_peer(n + 1), z_peer(n + 1))[level]
        return remote_copy(gain_terms.at[level], gain_from.at[level, n], sg.at[level, n], rg.at[level, n], peer)

    down_load = pltpu.make_async_copy(down_in.at[z], down_mine, down_sem.at[0])
    down_keep = pltpu.make_async_copy(down_final, down_all.at[dp], down_sem.at[1])
    out_copy = remote_copy(out_send, out_recv, s_out, r_out, y_peer)

    @pl.when(i == 0)
    def _():
        barrier = pltpu.get_barrier_semaphore()
        peers = [z_peer(n) for n in range(1, Z)] + [x_peer(n) for n in range(1, X)]
        peers += [dp_peer(d) for d in range(1, 4)] + [before_me, after_me]
        for peer in peers:
            pl.semaphore_signal(barrier, inc=1, device_id=peer, device_id_type=MESH)
        pl.semaphore_wait(barrier, len(peers))
        out_copy.start()
        for k in range(1, Z):
            down_to_z(k).start()
        down_load.start()
        da[...] = jnp.zeros_like(da)

        @pl.when(me == devices - 1)
        def _():
            edge_recv[...] = jnp.zeros_like(edge_recv)

    def active(first):
        return (i >= first) & (i < first + subs)

    @pl.when(active(2))
    def _():
        n = i - 2
        to_core(n).wait_recv()

        @pl.when(n >= 2)
        def _():
            to_y(n - 2).wait_send()

        @pl.when(n >= 3)
        def _():
            for j in range(1, X):
                to_x_early(n - 3, j).wait_send()

        def both(t):
            return (mine[n % 2, t].astype(F32) + from_core[n % slots, t].astype(F32)).astype(BF)

        send_y[n % 2] = both(1 - y)
        to_y(n).start()
        for t in range(2):
            summed[n % 3, 1 + t] = both(2 + t).reshape(summed.shape[2:])
        for j in range(1, X):
            to_x_early(n, j).start()
        keep_y[n % 2] = both(y)

        @pl.when(n < subs - slots)
        def _():
            pl.semaphore_signal(free, inc=1, device_id=core_peer, device_id_type=MESH)

    @pl.when(active(3))
    def _():
        n = i - 3
        to_y(n).wait_recv()

        @pl.when(n >= 3)
        def _():
            for j in range(1, X):
                to_x_late(n - 3, j).wait_send()

        total = (keep_y[n % 2].astype(F32) + from_y[n].astype(F32)).astype(BF)
        summed[n % 3, 0] = total.reshape(summed.shape[2:])
        for j in range(1, X):
            to_x_late(n, j).start()

    @pl.when(active(4))
    def _():
        n = i - 4
        for j in range(1, X):
            to_x_early(n, j).wait_recv()
            to_x_late(n, j).wait_recv()

        @pl.when(n >= 2)
        def _():
            for j in range(1, Z):
                to_z(n - 2, j).wait_send()

        total = summed[n % 3, :, :, x].astype(F32) + total_of([from_x[n, j].astype(F32) for j in range(X - 1)])
        column[n % 2] = total.astype(BF)
        for j in range(1, Z):
            to_z(n, j).start()

    @pl.when(active(5))
    def _():
        n = i - 5
        for j in range(1, Z):
            to_z(n, j).wait_recv()
        total = column[n % 2, :, z].astype(F32) + total_of([from_z[n, j].astype(F32) for j in range(Z - 1)])
        total = total.astype(BF)
        final[n] = total[0]
        plane[n] = total[1:]
        to_plane(n).start()
        keep(n, 0).start()
        for d in range(1, 3):
            share(n, d).start()

    @pl.when(active(6))
    def _():
        n = i - 6
        to_plane(n).wait_recv()
        share(n, 2).wait_recv()
        relay(n).start()
        final_plane[n] = (plane[n].astype(F32) + from_plane[n].astype(F32)).astype(BF)
        for t in range(2):
            keep(n, t + 1).start()
            share_core(n, t).start()

    @pl.when(i == 4)
    def _():
        down_load.wait()
        for k in range(1, Z):
            down_to_z(k).wait_recv()
        total = down_mine[...].astype(F32) + total_of([down_from_z[k].astype(F32) for k in range(Z - 1)])
        down_final[...] = total.astype(BF)
        down_keep.start()
        for d in range(1, 3):
            down_share(d).start()

    @pl.when(i == 6)
    def _():
        down_share(2).wait_recv()
        down_relay().start()

    @pl.when((i < subs) & (i % 2 == 0))
    def _():
        m = i // 2
        slot = m % 2
        ones = head_ones(step, head_size)
        scale = 1.0 / math.sqrt(head_size)
        first = lax.broadcasted_iota(jnp.int32, (frames, step), 0) == 0
        last = lax.broadcasted_iota(jnp.int32, (frames, step), 0) == frames - 1
        for p in range(2):
            mixed_grad[p] = total_of(
                [nt(dhb[p, :, g * step : (g + 1) * step], mix[g, 0, p]) for g in range(groups)]
            ).astype(BF)
            before[p] = jnp.where(first, edge[0, p : p + 1, :], pltpu.roll(k[0, p].astype(F32), 1, 0))
            before[2 + p] = jnp.where(first, edge[0, 2 + p : 3 + p, :], pltpu.roll(v[0, p].astype(F32), 1, 0))

        def chunk(c, carry):
            rows = pl.ds(pl.multiple_of(c * CHUNK, CHUNK), CHUNK)
            allowed = jnp.broadcast_to(carried[rows, :], (CHUNK, step)) > 0.5
            queries = [q[0, p, rows, :].astype(F32) for p in range(2)]
            cots = [mixed_grad[p, rows, :].astype(F32) for p in range(2)]
            keys = [before[p, rows, :] for p in range(2)] + [k[0, p, rows, :].astype(F32) for p in range(2)]
            values = [before[2 + p, rows, :] for p in range(2)] + [v[0, p, rows, :].astype(F32) for p in range(2)]

            scores = per_head(queries, keys, ones)
            dprobs = per_head(cots, values, ones)
            key_grads, value_grads = [[] for _ in range(4)], [[] for _ in range(4)]
            for p, span in SPANS:
                probs = head_probs(scores, span, allowed, scale)
                mean = total_of([pr * dprobs[m] for m, pr in zip(span, probs)])
                query_grad = []
                for m, pr in zip(span, probs):
                    n = PAIRS[m][1]
                    ds = (pr * (dprobs[m] - mean)).astype(BF).astype(F32) * scale
                    query_grad.append(ds * keys[n])
                    key_grads[n].append(ds * queries[p])
                    value_grads[n].append(pr.astype(BF).astype(F32) * cots[p])
                grads[0, p, rows, :] = total_of(query_grad).astype(BF)
            for p in range(2):
                terms_before[p, rows, :] = total_of(key_grads[p])
                terms_before[2 + p, rows, :] = total_of(value_grads[p])
                terms_here[p, rows, :] = total_of(key_grads[2 + p])
                terms_here[2 + p, rows, :] = total_of(value_grads[2 + p])
            return carry

        lax.fori_loop(0, frames // CHUNK, chunk, 0)

        @pl.when((m >= 2) & (me > 0))
        def _():
            to_before(m - 2).wait_send()

        for row in range(4):
            edge_send[slot, row : row + 1, :] = terms_before[row, 0:1, :]

        @pl.when(me > 0)
        def _():
            to_before(m).start()

        for row in range(4):
            total = terms_here[row] + jnp.where(last, 0.0, pltpu.roll(terms_before[row], frames - 1, 0))
            grads[1 + row // 2, row % 2] = total.astype(BF)
            tails[row] = total[frames - 16 :, :]

    @pl.when((i < subs) & (i % 2 == 1))
    def _():
        m = i // 2

        @pl.when(me < devices - 1)
        def _():
            to_before(m).wait_recv()

        bottom = lax.broadcasted_iota(jnp.int32, (16, step), 0) == 15
        for row in range(4):
            fixed = tails[row] + jnp.where(bottom, edge_recv[m, row : row + 1, :], 0.0)
            grads[1 + row // 2, row % 2, frames - 16 :, :] = fixed.astype(BF)

        @pl.when(m >= 1)
        def _():
            for h in range(2):
                to_core(2 * m - 2 + h).wait_send()

        for t in range(4):
            pair = []
            for p in range(2):
                if t < 3:
                    pair.append(tn(inputs[p], grads[t, p]).astype(BF))
                else:
                    pair.append(tn(mixed[p], dhb[p, :, pl.ds(pl.multiple_of(m * step, step), step)]).astype(BF))
            here = jnp.where(core == 0, pair[0], pair[1])
            there = jnp.where(core == 0, pair[1], pair[0])
            for h in range(2):
                mine[h, t] = here[:, h * thin : (h + 1) * thin]
                other[h, t] = there[:, h * thin : (h + 1) * thin]

        @pl.when(m >= slots // 2)
        def _():
            pl.semaphore_wait(free, 2)

        for h in range(2):
            to_core(2 * m + h).start()
        for p in range(2):
            da[p] += total_of([nt(grads[t, p], proj[0, t, p]) for t in range(3)])

        @pl.when(m == groups - 1)
        def _():
            for g in range(groups):
                load_frames(g).start()

    @pl.when(i == subs)
    def _():
        for g in range(groups):
            load_frames(g).wait()

        def chunk(c, term):
            rows = pl.ds(pl.multiple_of(c * CHUNK, CHUNK), CHUNK)
            for p in range(2):
                pieces = [grads[g, p, rows, :] if g < 3 else mixed_grad[p, rows, :] for g in range(groups)]
                value = jnp.concatenate(pieces, axis=1).astype(F32)
                inverse = scale_rows(value)
                normed = value * inverse
                grad = da[p, rows, :]
                term = term + jnp.sum(grad * normed, axis=0, keepdims=True)
                total = dhb[p, rows, :].astype(F32) + norm_back(grad, normed, gains[0:1, :], inverse)
                frames_grad[p, rows, :] = total.astype(BF)
            return term

        term = lax.fori_loop(0, frames // CHUNK, chunk, jnp.zeros((1, da.shape[2]), F32))
        gain_terms[0] = second_gain[...]
        gain_terms[0, 0:1, :] = term
        gain_copy(0, 0).start()

    for level in range(1, 4):
        @pl.when(i == subs + level)
        def _():
            count = X - 1 if level == 3 else 1
            total = gain_terms[level - 1]
            for n in range(count):
                gain_copy(level - 1, n).wait()
                total = total + gain_from[level - 1, n]
            gain_terms[level] = total
            for n in range(Z - 1 if level == 3 else X - 1 if level == 2 else 1):
                gain_copy(level, n).start()

    @pl.when(i == subs + 4)
    def _():
        total = gain_terms[3]
        for n in range(Z - 1):
            gain_copy(3, n).wait()
            total = total + gain_from[3, n]
        gains_sum[...] = total

    @pl.when(i == subs + 5)
    def _():
        @pl.when(me > 0)
        def _():
            for n in (groups - 2, groups - 1):
                to_before(n).wait_send()

        for n in (subs - 3, subs - 2, subs - 1):
            for j in range(1, X):
                to_x_early(n, j).wait_send()
                to_x_late(n, j).wait_send()

        for n in (subs - 2, subs - 1):
            to_core(n).wait_send()
            to_y(n).wait_send()
            for j in range(1, Z):
                to_z(n, j).wait_send()

        def finish(n, carry):
            to_plane(n).wait_send()
            keep(n, 0).wait()
            share(n, 1).wait()
            share(n, 2).wait_send()
            relay(n).wait()
            for t in range(2):
                keep(n, t + 1).wait()
                share_core(n, t).wait()
            return carry

        lax.fori_loop(0, subs, finish, 0)
        out_copy.wait()
        for k in range(1, Z):
            down_to_z(k).wait_send()
        down_keep.wait()
        down_share(1).wait()
        down_share(2).wait_send()
        down_relay().wait()


def attention_back(
    carried, qkv_rows, edge, attn, dhb, mixed, inputs, gains, second_gain, frames_in, down_in, out_send, head_size, fsdp_count
):
    _, frames, width = dhb.shape
    step = STEP
    groups = width // step
    X = fsdp_count // Z
    R = width // fsdp_count

    def early(i):
        return jnp.minimum(i // 2, groups - 1)

    rows = [pl.BlockSpec((1, 2, frames, step), lambda i, t=t: (t, 0, 0, early(i))) for t in range(3)]
    edge_spec = pl.BlockSpec((1, 8, step), lambda i: (early(i), 0, 0))
    mask = pl.BlockSpec((frames, 1), lambda i: (0, 0), pipeline_mode=pl.Buffered(1))
    whole = pl.BlockSpec((2, frames, width), lambda i: (0, 0, 0), pipeline_mode=pl.Buffered(1))
    mix_spec = pl.BlockSpec((groups, 1, 2, step, step), lambda i: (0, 3, 0, early(i), 0))
    proj_spec = pl.BlockSpec((1, 3, 2, width, step), lambda i: (jnp.clip((i - 1) // 2, 0, groups - 1), 0, 0, 0, 0))
    line = pl.BlockSpec((8, width), lambda i: (0, 0), pipeline_mode=pl.Buffered(1))
    dma, vmem = pltpu.SemaphoreType.DMA, pltpu.VMEM
    thin = step // 2
    n, slots, peers = 2 * groups, 4, max(X, Z) - 1
    return pl.pallas_call(
        functools.partial(attention_back_kernel, X, groups, head_size),
        grid=(n + 6,),
        out_shape=(
            jax.ShapeDtypeStruct((2, frames, width), BF),
            jax.ShapeDtypeStruct((8, width), F32),
            jax.ShapeDtypeStruct((4, 2, R, width), BF),
            jax.ShapeDtypeStruct((4,) + down_in.shape[1:], BF),
            jax.ShapeDtypeStruct(out_send.shape, BF),
        ),
        in_specs=[mask, *rows, edge_spec, mix_spec, whole, whole, whole, proj_spec, line, line, ANY, ANY, ANY],
        out_specs=(whole, line, ANY, ANY, ANY),
        scratch_shapes=[
            vmem((2, frames, width), F32), vmem((4, 8, width), F32), vmem((4, peers, 8, width), F32),
            vmem((2, frames, step), BF), vmem((4, frames, step), F32), vmem((4, frames, step), F32),
            vmem((4, frames, step), F32), vmem((4, 16, step), F32), vmem((3, 2, frames, step), BF),
            vmem((2, 8, step), F32), vmem((groups, 8, step), F32),
            vmem((2, 4, width, thin), BF), vmem((2, 4, width, thin), BF), vmem((slots, 4, width, thin), BF),
            vmem((2, width, thin), BF), vmem((2, width, thin), BF), vmem((n, width, thin), BF),
            vmem((3, 3, Z, X, R, thin), BF), vmem((n, X - 1, 3, Z, R, thin), BF),
            vmem((2, 3, Z, R, thin), BF), vmem((n, Z - 1, 3, R, thin), BF),
            vmem((n, R, thin), BF), vmem((n, 2, R, thin), BF), vmem((n, 2, R, thin), BF), vmem((n, 2, R, thin), BF),
            vmem(down_in.shape[1:], BF), vmem((Z - 1,) + down_in.shape[1:], BF), vmem(down_in.shape[1:], BF),
            dma((2,)), dma((groups,)), dma((2,)), dma((slots,)), dma((2,)), dma((n,)),
            dma((3, X - 1)), dma((n, X - 1)), dma((3, X - 1)), dma((n, X - 1)),
            dma((2, Z - 1)), dma((n, Z - 1)), dma((n, 3)), dma((n, 3)), dma((n,)), dma((n,)),
            dma((n, 2)), dma((n, 2)), dma((n, 3)),
            dma, dma, dma((4, peers)), dma((4, peers)), dma((groups,)),
            dma((Z - 1,)), dma((Z - 1,)), dma((3,)), dma((3,)), dma((2,)), pltpu.SemaphoreType.REGULAR,
        ],
        compiler_params=pltpu.CompilerParams(vmem_limit_bytes=63 * 2**20, collective_id=2, has_side_effects=True),
        name="attention_back",
    )(
        carried, qkv_rows, qkv_rows, qkv_rows, edge, attn, dhb, mixed, inputs, attn,
        gains, second_gain, frames_in, down_in, out_send,
    )


def update_kernel(step_size, share, weight, moment, average, grad_out, moment_out, average_out, weight_out):
    gradient = share[...].reshape(weight.shape).astype(F32)
    moment_new, average_new, weight_new = owner_update(
        weight[...], gradient, moment[...], average[...], step_size
    )
    grad_out[...] = gradient
    moment_out[...] = moment_new
    average_out[...] = average_new
    weight_out[...] = weight_new


def update(shares, share_block, share_at, grid, block, at, weight, moment, average, step_size, name):
    share_spec = pl.BlockSpec(share_block, share_at)
    spec = pl.BlockSpec(block, at)
    return pl.pallas_call(
        functools.partial(update_kernel, step_size),
        grid=grid,
        out_shape=(jax.ShapeDtypeStruct(weight.shape, F32),) * 4,
        in_specs=[share_spec, spec, spec, spec],
        out_specs=(spec,) * 4,
        compiler_params=pltpu.CompilerParams(vmem_limit_bytes=VMEM_BYTES),
        name=name,
    )(shares, weight, moment, average)


def per_device(
    frames, cotangent, segment_ids,
    qkv_weight, mix_weight, inner_weight, down_weight, norm_gains,
    qkv_moment, mix_moment, inner_moment, down_moment, gains_moment,
    qkv_average, mix_average, inner_average, down_average, gains_average,
):
    frame_count, positions, width = frames.shape
    head_size = width // HEADS
    hidden = inner_weight.shape[2] // 2
    dp_count, fsdp_count = lax.axis_size("dp"), lax.axis_size("fsdp")
    X = fsdp_count // Z
    devices = dp_count * fsdp_count
    total_frames = frame_count * devices
    dp, fs = lax.axis_index("dp"), lax.axis_index("fsdp")
    y, core = dp // 2, dp % 2
    z, x = fs // X, fs % X
    axes = ("dp", "fsdp")

    device = dp * fsdp_count + fs
    padded_ids = jnp.concatenate([jnp.full((1,), -1, jnp.int32), segment_ids])
    window = lax.dynamic_slice_in_dim(padded_ids, device * frame_count, frame_count + 1)
    carried = (window[1:] == window[:-1]).astype(F32)[:, None]

    quarters = (
        qkv_weight[:, :, :width], qkv_weight[:, :, width : 2 * width], qkv_weight[:, :, 2 * width :], mix_weight
    )
    last = width - STEP
    own_rows = jnp.concatenate(
        [
            lax.select_n(dp, *(m[:, :, :last] for m in quarters)),
            lax.select_n(core > 0, *(m[:, :, last:] for m in quarters[:2])),
            lax.select_n(core > 0, *(m[:, :, last:] for m in quarters[2:])),
        ],
        axis=-1,
    ).astype(BF)
    attn_own = own_rows.reshape(positions, -1, width // STEP + 1, STEP).transpose(2, 0, 1, 3)
    inner_own = lax.dynamic_slice(
        inner_weight, (y, 0, core * hidden), (1, inner_weight.shape[1], hidden)
    )[0].astype(BF)
    half_width = width // 2
    down_own = lax.dynamic_slice(
        down_weight, (y, 0, core * half_width), (1, down_weight.shape[1], half_width)
    )[0].astype(BF)
    own_gains = norm_gains.astype(BF).astype(F32)
    gains_own = lax.dynamic_update_slice(jnp.zeros((8, width), F32), own_gains, (0, fs * own_gains.shape[1]))
    frames_by = frames.transpose(1, 0, 2)
    cot = cotangent.transpose(1, 0, 2)
    attn, inner, down, gains, a, qkv_rows, mixed, edge, hres, b_rows, c_rows = forward(
        frames_by, carried, cot, attn_own, inner_own, down_own, gains_own, head_size, fsdp_count
    )
    r2 = scale_rows(hres)
    n2 = hres * r2
    b_rows = b_rows.reshape(2 * frame_count, width)
    c_rows = c_rows.reshape(2 * frame_count, width)
    out, back, out_there, back_there, inner_shares, down_columns, _ = feed_forward(b_rows, c_rows, inner, down, fsdp_count)

    def by_position(mine, theirs):
        return jnp.where(y == 0, jnp.stack([mine, theirs]), jnp.stack([theirs, mine]))

    db = by_position(back, back_there.astype(F32))

    e2 = jnp.sum(db * n2, axis=(0, 1))
    dh = cot.astype(F32) + norm_back(db, n2, gains[1], r2)
    dhb = dh.astype(BF)
    second_gain = jnp.zeros((8, width), F32).at[1].set(e2)
    frames_grad, gains_sum, attn_shares, down_shares, out_here = attention_back(
        carried, qkv_rows, edge, attn, dhb, mixed, a, gains, second_gain, frames_by, down_columns, out_there, head_size, fsdp_count
    )
    frames_grad = frames_grad.transpose(1, 0, 2)
    layer_out = (hres + by_position(out, out_here.astype(F32))).astype(BF).transpose(1, 0, 2)

    step_size = step_rate / math.sqrt(total_frames)
    R, R2 = qkv_weight.shape[1], down_weight.shape[1]
    cut = min(R, 64)
    qkv_new = update(
        attn_shares, (1, 1, R, width), lambda p, t: (t, p, 0, 0), (2, 3), (1, R, width), lambda p, t: (p, 0, t),
        qkv_weight, qkv_moment, qkv_average, step_size, "update_qkv",
    )
    mix_new = update(
        attn_shares, (1, 1, R, width), lambda p: (3, p, 0, 0), (2,), (1, R, width), lambda p: (p, 0, 0),
        mix_weight, mix_moment, mix_average, step_size, "update_mix",
    )
    inner_new = update(
        inner_shares, (1, cut, hidden), lambda p, c, r: (2 * p + c, r, 0), (2, 2, R // cut),
        (1, cut, hidden), lambda p, c, r: (p, r, c), inner_weight, inner_moment, inner_average, step_size, "update_inner",
    )
    down_new = update(
        down_shares, (1, R2, half_width), lambda p, c: (2 * p + c, 0, 0), (2, 2),
        (1, R2, half_width), lambda p, c: (p, 0, c), down_weight, down_moment, down_average, step_size, "update_down",
    )
    own = norm_gains.shape[1]
    gains_grad = lax.dynamic_slice(gains_sum, (0, fs * own), (2, own))
    gains_new = (gains_grad,) + owner_update(norm_gains, gains_grad, gains_moment, gains_average, step_size)
    new = (qkv_new, mix_new, inner_new, down_new, gains_new)
    return (layer_out, frames_grad) + tuple(n[kind] for kind in range(4) for n in new)


def solution(mesh):
    rows = P(("dp", "fsdp"), None, None)
    weight = P(None, "fsdp", None)
    gains = P(None, "fsdp")
    weights = (weight,) * 4 + (gains,)
    return jax.shard_map(
        per_device,
        mesh=mesh,
        in_specs=(rows, rows, P()) + weights * 3,
        out_specs=(rows, rows) + weights * 4,
        check_vma=False,
    )
```

```python
import functools
import math

import jax
import jax.numpy as jnp
from jax import lax
from jax.experimental import pallas as pl
from jax.experimental.pallas import tpu as pltpu
from jax.sharding import PartitionSpec as P

HEADS = 16
Z = 4
MESH = pl.DeviceIdType.MESH
ANY = pl.BlockSpec(memory_space=pl.ANY)
BF = jnp.bfloat16
F32 = jnp.float32

norm_eps = 1e-05
momentum_rate = 0.5
average_rate = 0.5
step_rate = 0.05
VMEM_BYTES = 60 * 1024 * 1024


def nn(a, b):
    return lax.dot_general(a, b, (((1,), (0,)), ((), ())), preferred_element_type=F32)


def nt(a, b):
    return lax.dot_general(a, b, (((1,), (1,)), ((), ())), preferred_element_type=F32)


def tn(a, b):
    return lax.dot_general(a, b, (((0,), (0,)), ((), ())), preferred_element_type=F32)


def scale_rows(values):
    square = jnp.mean(values * values, axis=-1, keepdims=True) + norm_eps
    inverse = lax.rsqrt(square)
    return inverse * (1.5 - 0.5 * square * inverse * inverse)


def norm_back(grad_in, normed, gain_row, inverse):
    scaled = grad_in * gain_row
    return inverse * (scaled - normed * jnp.mean(scaled * normed, axis=-1, keepdims=True))


def owner_update(weight, gradient, moment, average, step_size):
    moment_new = momentum_rate * moment + gradient
    weight_new = weight - step_size * (gradient + momentum_rate * moment_new)
    average_new = average_rate * average + (1.0 - average_rate) * weight_new
    return (moment_new, average_new, weight_new)


PAIRS = ((0, 0), (0, 1), (0, 2), (1, 0), (1, 1), (1, 2), (1, 3))
SPANS = ((0, range(0, 3)), (1, range(3, 7)))
CHUNK = 128
STEP = 256


def total_of(values):
    return functools.reduce(jnp.add, values)


def remote_copy(src, dst, send_sem, recv_sem, peer):
    return pltpu.make_async_remote_copy(
        src_ref=src, dst_ref=dst, send_sem=send_sem, recv_sem=recv_sem, device_id=peer, device_id_type=MESH
    )


def head_ones(lanes, head_size):
    row = lax.broadcasted_iota(jnp.int32, (lanes, lanes), 0) // head_size
    column = lax.broadcasted_iota(jnp.int32, (lanes, lanes), 1) // head_size
    return (row == column).astype(BF)


def per_head(left, right, ones):
    rows = left[0].shape[0]
    products = [(left[p] * right[n]).astype(BF) for p, n in PAIRS]
    sums = nn(jnp.concatenate(products, axis=0), ones)
    return [sums[m * rows : (m + 1) * rows] for m in range(len(PAIRS))]


def head_probs(scores, span, allowed, scale):
    s = [jnp.where(allowed, scores[m] * scale, -1e30) if PAIRS[m][1] < 2 else scores[m] * scale for m in span]
    top = functools.reduce(jnp.maximum, s)
    e = [jnp.exp(value - top) for value in s]
    e = [jnp.where(allowed, value, 0.0) if PAIRS[m][1] < 2 else value for m, value in zip(span, e)]
    inverse = 1.0 / total_of(e)
    return [value * inverse for value in e]


def forward_kernel(
    X, groups, head_size, frames, carried, cot, gains_own, qkv_weight, mix_weight, inner_weight, down_weight,
    attn, inner, down, gains_out, inputs_out, rows_out, mixed_out, edge_out, hres_out, b_rows, c_rows,
    attn_wide, inner_wide, down_wide, attn_own, inner_own, down_own,
    gains, inputs, rows_in, mixed, before, hres, b, proj, mix, edge_send, edge_recv,
    send_up, recv_up, send_down, recv_down, send_x, recv_x, send_y, recv_y, send_c, recv_c, send_r, recv_r,
    send_g, recv_g, send_e, recv_e, send_b, recv_b, send_q, recv_q, local_sem, out_sem, wide_sem,
):
    dp, fs = lax.axis_index("dp"), lax.axis_index("fsdp")
    F = Z * X
    y, core = dp // 2, dp % 2
    z, x = fs // X, fs % X
    me = dp * F + fs
    devices = 4 * F
    count = frames.shape[1]
    core_peer = (y * 2 + 1 - core, fs)
    y_peer = ((1 - y) * 2 + core, fs)
    up_peer = (dp, lax.rem(z + 1, Z) * X + x)
    down_peer = (dp, lax.rem(z + Z - 1, Z) * X + x)
    before_me = ((me - 1 + devices) % devices // F, (me - 1 + devices) % devices % F)
    after_me = ((me + 1) % devices // F, (me + 1) % devices % F)

    def z_peer(k):
        return (dp, lax.rem(z + k, Z) * X + x)

    def x_peer(i):
        return (dp, z * X + lax.rem(x + i, X))

    UNITS = unit_list(groups, inner_own.shape[1], down_own.shape[1])

    width = frames.shape[2]

    def wide(slot):
        return (attn_wide.at[slot] if slot < groups + 1 else (inner_wide, down_wide)[slot - groups - 1])

    def fetch(slot, src, condition=None):
        copy = pltpu.make_async_copy(src, wide(slot), wide_sem.at[slot])
        if condition is None:
            copy.start()
        else:
            pl.when(condition)(copy.start)

    def columns_of(weight, part, block):
        return weight.at[:, :, pl.ds(pl.multiple_of(part * width + block * STEP, STEP), STEP)]

    def fetch_all():
        for n in range(groups - 1):
            fetch(n, columns_of(qkv_weight, jnp.minimum(dp, 2), n), dp < 3)
            fetch(n, columns_of(mix_weight, 0, n), dp == 3)
        fetch(groups - 1, columns_of(qkv_weight, core, groups - 1))
        fetch(groups, columns_of(qkv_weight, 2, groups - 1), core == 0)
        fetch(groups, columns_of(mix_weight, 0, groups - 1), core == 1)
        half, hidden = width // 2, inner_own.shape[1]
        fetch(groups + 1, inner_weight.at[y, :, pl.ds(pl.multiple_of(core * hidden, 128), hidden)])
        fetch(groups + 2, down_weight.at[y, :, pl.ds(pl.multiple_of(core * half, 128), half)])

    def take(slot):
        pltpu.make_async_copy(wide(slot), wide(slot), wide_sem.at[slot]).wait()
        if slot < groups + 1:
            attn_own[slot] = attn_wide[slot].astype(BF)
        elif slot == groups + 1:
            inner_own[...] = inner_wide[...].astype(BF)
        else:
            down_own[...] = down_wide[...].astype(BF)

    def own(u):
        kind, n, columns = UNITS[u][:3]
        if kind in ("quarter", "low", "high"):
            return attn_own.at[n if kind != "high" else n + 1]
        return (down_own if kind == "down" else inner_own).at[:, columns]

    def part_of(u, core_index, plane):
        kind = UNITS[u][0]
        if kind == "quarter":
            return plane * 2 + core_index
        return 2 + core_index if kind == "high" else core_index

    def whole(u, part):
        kind, n, columns = UNITS[u][:3]
        if kind == "down":
            return down.at[part, :, columns]
        if kind == "inner":
            return inner.at[part, :, columns]
        return attn.at[n, part]

    def place(u, source, part=None):
        kind, n, columns = UNITS[u][:3]
        part = part_of(u, core, y) if part is None else part
        if kind == "down":
            R = down_own.shape[0]
            return down.at[part, pl.ds(source * R, R), columns]
        if kind == "inner":
            R = inner_own.shape[0]
            return inner.at[part, pl.ds(source * R, R), columns]
        R = attn_own.shape[2]
        return attn.at[n, part, :, pl.ds(source * R, R), :]

    fetch_all()
    barrier = pltpu.get_barrier_semaphore()
    peers = [z_peer(k) for k in range(1, Z)] + [x_peer(i) for i in range(1, X)]
    peers += [core_peer, y_peer, before_me, after_me]
    for peer in peers:
        pl.semaphore_signal(barrier, inc=1, device_id=peer, device_id_type=MESH)
    pl.semaphore_wait(barrier, len(peers))

    sent, local = [], []

    def send(condition, make):
        remote_copy(*make()).start()
        sent.append((condition, make))

    def wait_send(condition, make):
        def action():
            remote_copy(*make()).wait_send()

        if condition is None:
            action()
        else:
            pl.when(condition())(action)

    def wait_recv(dst, recv_sem, send_sem):
        remote_copy(dst, dst, send_sem, recv_sem, core_peer).wait_recv()

    def store(src, dst):
        copy = pltpu.make_async_copy(src, dst, out_sem.at[len(local)])
        copy.start()
        local.append(copy)

    def spread(u, row, mine, condition):
        def src():
            return own(u) if mine else place(u, row() * X + x)

        for i in range(1, X):
            send(
                condition,
                lambda i=i: (
                    src(), place(u, row() * X + x), send_x.at[u, row(), i], recv_x.at[u, row(), i], x_peer(i)
                ),
            )
        to_plane(u, lambda: row() * X + x, src, condition)

    def to_plane(u, source, src, condition):
        if UNITS[u][0] == "quarter":
            send(
                condition,
                lambda: (src(), place(u, source()), send_y.at[u, source()], recv_y.at[u, source()], y_peer),
            )

    def crossed(u):
        return UNITS[u][3]

    def block(u, row):
        kind, n, columns = UNITS[u][:3]
        array, R = (down, down_own.shape[0]) if kind == "down" else (inner, inner_own.shape[0])
        return array.at[core, pl.ds(row * X * R, X * R), columns]

    def send_along(u, src, dst):
        def below_top():
            return z < Z - 1

        def above_bottom():
            return z > 0

        def upward():
            return (src(), dst(), send_up.at[u, 1], recv_up.at[u, 1], up_peer)

        def downward():
            return (src(), dst(), send_down.at[u, 1], recv_down.at[u, 1], down_peer)

        pl.when(below_top())(lambda: send(below_top, upward))
        pl.when(above_bottom())(lambda: send(above_bottom, downward))

    def start_unit(u):
        for slot in slots_of[u]:
            take(slot)
        if not crossed(u):
            send_along(u, lambda: own(u), lambda: place(u, fs))
        spread(u, lambda: z, True, None)
        store(own(u), place(u, fs))

    def turn(u):
        for i in range(1, X):
            column = lax.rem(x - i + X, X)
            wait_recv(place(u, z * X + column), recv_x.at[u, z, i], send_x.at[u, z, i])
        local[own_store[u]].wait()
        send_along(u, lambda: block(u, z), lambda: block(u, z))

    def hop(u, k):
        def side(reached, row, further, send_sem, recv_sem, peer):
            def here():
                return block(u, row()) if crossed(u) else place(u, row() * X + x)

            def both():
                return reached() & further()

            def action():
                wait_recv(here(), recv_sem.at[u, k], send_sem.at[u, k])
                if k < Z - 1:
                    pl.when(further())(
                        lambda: send(
                            both, lambda: (here(), here(), send_sem.at[u, k + 1], recv_sem.at[u, k + 1], peer)
                        )
                    )
                if not crossed(u):
                    spread(u, row, False, reached)

            pl.when(reached())(action)

        side(lambda: z >= k, lambda: z - k, lambda: z < Z - 1, send_up, recv_up, up_peer)
        side(lambda: z + k < Z, lambda: z + k, lambda: z > 0, send_down, recv_down, down_peer)

    def arrivals(u):
        for row in range(0 if crossed(u) else Z):
            for i in range(1, X):
                column = lax.rem(x - i + X, X)
                source = row * X + column
                wait_recv(place(u, source), recv_x.at[u, row, i], send_x.at[u, row, i])
                to_plane(u, lambda source=source: source, lambda source=source: place(u, source), None)
        if not crossed(u):
            local[own_store[u]].wait()
        mine = whole(u, part_of(u, core, y))
        send(None, lambda: (mine, mine, send_c.at[u], recv_c.at[u], core_peer))

    def relay(u):
        if UNITS[u][0] != "quarter":
            return
        part = (1 - y) * 2 + core
        for source in range(F):
            wait_recv(place(u, source, part), recv_y.at[u, source], send_y.at[u, source])
        theirs = whole(u, part)
        send(None, lambda: (theirs, theirs, send_r.at[u], recv_r.at[u], core_peer))

    def complete(u):
        wait_recv(whole(u, part_of(u, 1 - core, y)), recv_c.at[u], send_c.at[u])
        if UNITS[u][0] == "quarter":
            wait_recv(whole(u, (1 - y) * 2 + 1 - core), recv_r.at[u], send_r.at[u])

    scale = 1.0 / math.sqrt(head_size)

    def gather_gains():
        keep = pltpu.make_async_copy(gains_own, gains.at[fs], local_sem.at[0])
        keep.start()
        for k in range(1, Z):
            send(None, lambda k=k: (gains_own, gains.at[fs], send_g.at[0, k], recv_g.at[0, k], z_peer(k)))
        for i in range(1, X):
            send(None, lambda i=i: (gains_own, gains.at[fs], send_g.at[i, 0], recv_g.at[i, 0], x_peer(i)))
        keep.wait()

    def chunk_source(k, i):
        return lax.rem(z - k + Z, Z) * X + lax.rem(x - i + X, X)

    def pass_gains():
        for k in range(1, Z):
            here = gains.at[chunk_source(k, 0)]
            wait_recv(here, recv_g.at[0, k], send_g.at[0, k])
            for i in range(1, X):
                send(
                    None,
                    lambda here=here, i=i, k=k: (here, here, send_g.at[i, k], recv_g.at[i, k], x_peer(i)),
                )

    def take_gains():
        for k in range(Z):
            for i in range(1, X):
                wait_recv(gains.at[chunk_source(k, i)], recv_g.at[i, k], send_g.at[i, k])
        total = gains[0]
        for source in range(1, F):
            total = total + gains[source]
        gains_out[...] = total

    def norm_rows():
        def chunk(c, carry):
            rows = pl.ds(pl.multiple_of(c * CHUNK, CHUNK), CHUNK)
            for p in range(2):
                value = frames[p, rows, :].astype(F32)
                inputs[p, rows, :] = (value * scale_rows(value) * gains_out[0:1, :]).astype(BF)
            return carry

        lax.fori_loop(0, count // CHUNK, chunk, 0)
        store(inputs, inputs_out)

    def heads(m):
        columns = slice(m * STEP, (m + 1) * STEP)
        load = pltpu.make_async_copy(attn.at[m, pl.ds(0, 3)], proj, local_sem.at[0])
        load.start()
        load.wait()
        for t in (1, 2, 0):
            for p in range(2):
                rows_in[t, p, :, columns] = nn(inputs[p], proj[t, p]).astype(BF)
                if t > 0:
                    tail = rows_in[t, p, count - 16 :, columns].astype(F32)
                    row = 2 * (t - 1) + p
                    edge_send[m, row : row + 1, :] = tail[15:16, :]
            if t == 2:
                to_after = remote_copy(edge_send.at[m], edge_recv.at[m], send_e.at[m], recv_e.at[m], after_me)
                pl.when(me < devices - 1)(to_after.start)
        pl.when(me > 0)(to_after.wait_recv)
        first = lax.broadcasted_iota(jnp.int32, (count, STEP), 0) == 0
        for t in range(2):
            for p in range(2):
                n = 2 * t + p
                shifted = pltpu.roll(rows_in[1 + t, p, :, columns].astype(F32), 1, 0)
                before[n] = jnp.where(first, edge_recv[m, n : n + 1, :], shifted)
        ones = head_ones(STEP, head_size)

        def chunk(c, carry):
            rows = pl.ds(pl.multiple_of(c * CHUNK, CHUNK), CHUNK)
            allowed = jnp.broadcast_to(carried[rows, :], (CHUNK, STEP)) > 0.5
            queries, here_k, here_v = (
                [rows_in[t, p, rows, columns].astype(F32) for p in range(2)] for t in range(3)
            )
            keys = [before[p, rows, :] for p in range(2)] + here_k
            values = [before[2 + p, rows, :] for p in range(2)] + here_v
            scores = per_head(queries, keys, ones)
            for p, span in SPANS:
                probs = head_probs(scores, span, allowed, scale)
                terms = [pr.astype(BF).astype(F32) * values[PAIRS[n][1]] for n, pr in zip(span, probs)]
                mixed[p, rows, columns] = total_of(terms).astype(BF)
            return carry

        lax.fori_loop(0, count // CHUNK, chunk, 0)

    def load_mix():
        return pltpu.make_async_copy(attn.at[:, 3], mix, local_sem.at[1])

    def finish_rows():
        load_mix().wait()
        for turn in range(2):
            p = 1 - y if turn == 0 else y
            for m in range(groups):
                columns = slice(m * STEP, (m + 1) * STEP)
                hres[p, :, columns] = frames[p, :, columns].astype(F32) + nn(mixed[p], mix[m, p])

            def chunk(c, carry):
                rows = pl.ds(pl.multiple_of(c * CHUNK, CHUNK), CHUNK)
                value = hres[p, rows, :]
                b[turn, rows, :] = (value * scale_rows(value) * gains_out[1:2, :]).astype(BF)
                return carry

            lax.fori_loop(0, count // CHUNK, chunk, 0)
            if turn == 0:
                send(None, lambda: (b.at[0], b_rows.at[1], send_b, recv_b, y_peer))
            else:
                store(b.at[1], b_rows.at[0])
        store(hres, hres_out)

    @pl.when(me == 0)
    def _():
        edge_recv[...] = jnp.zeros_like(edge_recv)

    slots_of = [
        [n] if kind in ("quarter", "low") else [n + 1] if kind == "high" else [] for kind, n, *_ in UNITS
    ]
    slots_of[[u[0] for u in UNITS].index("inner")] = [groups + 1]
    slots_of[[u[0] for u in UNITS].index("down")] = [groups + 2]
    own_store = {}
    last_of = {kind_n[1]: u for u, kind_n in enumerate(UNITS) if kind_n[0] in ("quarter", "low", "high")}
    last_plane = max(u for u, kind_n in enumerate(UNITS) if kind_n[0] == "quarter")
    store(cot.at[y], c_rows.at[0])
    gather_gains()
    for tick in range(len(UNITS) + Z + 2):
        if tick < len(UNITS):
            own_store[tick] = len(local)
            start_unit(tick)
        if 0 <= tick - 1 < len(UNITS) and crossed(tick - 1):
            turn(tick - 1)
        for k in range(1, Z):
            u = tick - k
            if 0 <= u < len(UNITS) and not crossed(u):
                hop(u, k)
            u = tick - k - 1
            if 0 <= u < len(UNITS) and crossed(u):
                hop(u, k)
        if tick == 1:
            pass_gains()
        if tick == 2:
            take_gains()
            norm_rows()
        u = tick - Z
        if 0 <= u < len(UNITS):
            arrivals(u)
            if u == last_plane:
                send(None, lambda: (cot.at[1 - y], c_rows.at[1], send_q, recv_q, y_peer))
        u = tick - Z - 1
        if 0 <= u < len(UNITS):
            relay(u)
            complete(u)
            for m in range(groups):
                if last_of[m] == u:
                    if m == groups - 1:
                        load_mix().start()
                    heads(m)
                    if m == groups - 1:
                        store(rows_in, rows_out)
                        store(mixed, mixed_out)
                        store(edge_recv, edge_out)
                        finish_rows()
    wait_recv(b_rows.at[1], recv_b, send_b)
    wait_recv(c_rows.at[1], recv_q, send_q)
    for condition, make in sent:
        wait_send(condition, make)
    for n, copy in enumerate(local):
        if n not in own_store.values():
            copy.wait()

    @pl.when(me < devices - 1)
    def _():
        for m in range(groups):
            remote_copy(edge_send.at[m], edge_recv.at[m], send_e.at[m], recv_e.at[m], after_me).wait_send()


def unit_list(groups, inner_width, down_width):
    units = [("quarter", n, None, False) for n in range(groups - 1)]
    units += [("low", groups - 1, None, False), ("high", groups - 1, None, False)]
    units += [("down", 0, slice(0, down_width // 2), True), ("down", 0, slice(down_width // 2, down_width), False)]
    tiles = inner_width // 128
    cuts = [128 * (tiles * n // 4) for n in range(5)]
    return units + [("inner", 0, slice(lo, hi), n == 1) for n, (lo, hi) in enumerate(zip(cuts, cuts[1:]))]


def forward(
    frames, carried, cot, gains_own, qkv_weight, mix_weight, inner_weight, down_weight, head_size, fsdp_count
):
    X = fsdp_count // Z
    _, count, width = frames.shape
    R, R2 = qkv_weight.shape[1], down_weight.shape[1]
    hidden, half = inner_weight.shape[2] // 2, width // 2
    groups = width // STEP
    units = len(unit_list(groups, hidden, half))
    dma, vmem = pltpu.SemaphoreType.DMA, pltpu.VMEM
    whole = pl.BlockSpec(memory_space=pltpu.VMEM)
    act = jax.ShapeDtypeStruct((2, count, width), BF)
    return pl.pallas_call(
        functools.partial(forward_kernel, X, groups, head_size),
        out_shape=(
            jax.ShapeDtypeStruct((groups, 4, 2, R * fsdp_count, STEP), BF),
            jax.ShapeDtypeStruct((2, R * fsdp_count, hidden), BF),
            jax.ShapeDtypeStruct((2, R2 * fsdp_count, half), BF),
            jax.ShapeDtypeStruct(gains_own.shape, F32),
            act,
            jax.ShapeDtypeStruct((3, 2, count, width), BF),
            act,
            jax.ShapeDtypeStruct((groups, 8, STEP), F32),
            jax.ShapeDtypeStruct((2, count, width), F32),
            act,
            act,
        ),
        in_specs=[whole] * 4 + [ANY] * 4,
        out_specs=(ANY,) * 3 + (whole,) + (ANY,) * 7,
        scratch_shapes=[
            vmem((groups + 1, 2, R, STEP), F32), vmem((R, hidden), F32), vmem((R2, half), F32),
            vmem((groups + 1, 2, R, STEP), BF), vmem((R, hidden), BF), vmem((R2, half), BF),
            vmem((fsdp_count,) + gains_own.shape, F32),
            vmem((2, count, width), BF), vmem((3, 2, count, width), BF), vmem((2, count, width), BF),
            vmem((4, count, STEP), F32), vmem((2, count, width), F32), vmem((2, count, width), BF),
            vmem((3, 2, width, STEP), BF), vmem((groups, 2, width, STEP), BF),
            vmem((groups, 8, STEP), F32), vmem((groups, 8, STEP), F32),
            dma((units, Z)), dma((units, Z)), dma((units, Z)), dma((units, Z)),
            dma((units, Z, X)), dma((units, Z, X)), dma((groups, fsdp_count)), dma((groups, fsdp_count)),
            dma((units,)), dma((units,)), dma((groups,)), dma((groups,)),
            dma((X, Z)), dma((X, Z)), dma((groups,)), dma((groups,)), dma, dma, dma, dma,
            dma((2,)), dma((units + 8,)), dma((groups + 3,)),
        ],
        compiler_params=pltpu.CompilerParams(
            vmem_limit_bytes=VMEM_BYTES, collective_id=0, has_side_effects=True
        ),
        name="attention_forward",
    )(frames, carried, cot, gains_own, qkv_weight, mix_weight, inner_weight, down_weight)


def feed_forward_kernel(
    X, J, b, c, inner, down, out_mine, back_mine, out_theirs, back_recv, inner_all, down_columns, down_sum,
    out, back, down_here, down_there, down_from_core, down_stage, down_column, down_from_x, mine, other, from_core, summed, from_x, column, from_z, final, staged,
    s1, r1, s2, r2, s3, r3, s5, r5, s6, r6, s7, r7, local_sem,
    s_stage, s_own, sdx, rdx, s_column,
):
    j = pl.program_id(0)
    half = down.shape[2]
    rows_here = out_mine.shape[0]
    R, step = final.shape[1:]
    dp, fs = lax.axis_index("dp"), lax.axis_index("fsdp")
    y, core = dp // 2, dp % 2
    z, x = fs // X, fs % X
    core_peer = (y * 2 + 1 - core, fs)
    y_peer = ((1 - y) * 2 + core, fs)

    def z_peer(k):
        return (dp, lax.rem(z + k, Z) * X + x)

    def x_peer(i):
        return (dp, z * X + lax.rem(x + i, X))

    def dp_peer(d):
        return (((y + d // 2) % 2) * 2 + (core + d % 2) % 2, fs)

    def to_core(n):
        return remote_copy(other.at[n % 2], from_core.at[n], s1.at[n % 2], r1.at[n], core_peer)

    def to_x(n, i):
        return remote_copy(
            summed.at[n % 2, :, lax.rem(x + i, X)], from_x.at[n, i - 1], s2.at[n % 2, i - 1], r2.at[n, i - 1], x_peer(i)
        )

    def to_z(n, k):
        return remote_copy(
            column.at[n % 2, lax.rem(z + k, Z)], from_z.at[n, k - 1], s3.at[n % 2, k - 1], r3.at[n, k - 1], z_peer(k)
        )

    def place(n, owner):
        return inner_all.at[owner, :, pl.ds(pl.multiple_of(n * step, step), step)]

    def share(n, d):
        return remote_copy(final.at[n], place(n, dp), s5.at[n, d - 1], r5.at[n, d - 1], dp_peer(d))

    def keep(n):
        return pltpu.make_async_copy(final.at[n], place(n, dp), local_sem.at[n])

    exchange = remote_copy(staged, back_recv, s6, r6, y_peer)

    R2 = down_column.shape[1]
    ends = [-(-(g + 1) * X * R2 // step) - 1 for g in range(Z)]

    def down_rows(g, column):
        return down_sum.at[pl.ds((g * X + column) * R2, R2), :]

    def down_store(n):
        return pltpu.make_async_copy(
            down_stage.at[n % 2], down_sum.at[pl.ds(pl.multiple_of(n * step, step), step), :], s_stage.at[n % 2]
        )

    def down_load(g):
        return pltpu.make_async_copy(down_rows(g, x), down_column.at[g], s_own.at[g])

    def down_to_x(g, i):
        return remote_copy(
            down_rows(g, lax.rem(x + i, X)), down_from_x.at[g, i - 1], sdx.at[g, i - 1], rdx.at[g, i - 1], x_peer(i)
        )

    def down_keep(g):
        return pltpu.make_async_copy(down_column.at[g], down_columns.at[g], s_column.at[g])

    def down_to_core(n):
        return remote_copy(down_there.at[n % 2], down_from_core.at[n], s7.at[n % 2], r7.at[n], core_peer)

    @pl.when(j == 0)
    def _():
        barrier = pltpu.get_barrier_semaphore()
        peers = [z_peer(k) for k in range(1, Z)] + [x_peer(i) for i in range(1, X)]
        peers += [dp_peer(d) for d in range(1, 4)]
        for peer in peers:
            pl.semaphore_signal(barrier, inc=1, device_id=peer, device_id_type=MESH)
        pl.semaphore_wait(barrier, len(peers))
        out[...] = jnp.zeros_like(out)
        back[...] = jnp.zeros_like(back)

    @pl.when((j >= 2) & (j < J + 2))
    def _():
        down_store(j - 2).wait()

    for g in range(Z):
        @pl.when(j == ends[g] + 2)
        def _():
            for i in range(1, X):
                down_to_x(g, i).start()
            down_load(g).start()

    @pl.when((j >= 1) & (j < J + 1))
    def _():
        n = j - 1
        to_core(n).wait_recv()

        @pl.when(n >= 2)
        def _():
            for i in range(1, X):
                to_x(n - 2, i).wait_send()

        down_to_core(n).wait_recv()
        down_stage[n % 2] = (down_here[n % 2].astype(F32) + down_from_core[n].astype(F32)).astype(BF)
        down_store(n).start()
        total = (mine[n % 2].astype(F32) + from_core[n].astype(F32)).astype(BF)
        summed[n % 2] = total.reshape(summed.shape[1:])
        for i in range(1, X):
            to_x(n, i).start()

    @pl.when((j >= 2) & (j < J + 2))
    def _():
        n = j - 2
        for i in range(1, X):
            to_x(n, i).wait_recv()

        @pl.when(n >= 2)
        def _():
            for k in range(1, Z):
                to_z(n - 2, k).wait_send()

        total = summed[n % 2, :, x].astype(F32)
        for i in range(1, X):
            total = total + from_x[n, i - 1].astype(F32)
        column[n % 2] = total.astype(BF)
        for k in range(1, Z):
            to_z(n, k).start()

    for g in range(Z):
        @pl.when(j == min(ends[g] + 4, J + 2))
        def _():
            down_load(g).wait()
            for i in range(1, X):
                down_to_x(g, i).wait_recv()
            total = down_column[g].astype(F32) + total_of([down_from_x[g, i].astype(F32) for i in range(X - 1)])
            down_column[g] = total.astype(BF)
            down_keep(g).start()

    @pl.when((j >= 3) & (j < J + 3))
    def _():
        n = j - 3
        for k in range(1, Z):
            to_z(n, k).wait_recv()
        total = column[n % 2, z].astype(F32)
        for k in range(1, Z):
            total = total + from_z[n, k - 1].astype(F32)
        final[n] = total.astype(BF)
        keep(n).start()
        for d in range(1, 4):
            share(n, d).start()

    @pl.when(j < J)
    def _():
        rows, cot = b[...], c[...]
        gate = nn(rows, inner[0])
        up = nn(rows, inner[1])
        squashed = jax.nn.sigmoid(gate)
        active = gate * squashed
        hidden = (active * up).astype(BF)
        hidden_grad = nt(cot[:, :half], down[0]) + nt(cot[:, half:], down[1])
        gate_grad = (hidden_grad * up * (squashed * (1.0 + gate * (1.0 - squashed)))).astype(BF)
        up_grad = (hidden_grad * active).astype(BF)
        gate_term = tn(rows, gate_grad).astype(BF)
        up_term = tn(rows, up_grad).astype(BF)

        @pl.when(j >= 2)
        def _():
            to_core(j - 2).wait_send()
            down_to_core(j - 2).wait_send()

        mine[j % 2] = jnp.where(core == 0, gate_term, up_term)
        other[j % 2] = jnp.where(core == 0, up_term, gate_term)
        to_core(j).start()
        down_term = tn(hidden, cot).astype(BF)
        down_here[j % 2] = jnp.where(core == 0, down_term[:, :half], down_term[:, half:])
        down_there[j % 2] = jnp.where(core == 0, down_term[:, half:], down_term[:, :half])
        down_to_core(j).start()
        for n in range(2):
            part = slice(n * half, (n + 1) * half)
            out[:, part] += nn(hidden, down[n])
        back[...] += nt(gate_grad, inner[0]) + nt(up_grad, inner[1])

    @pl.when(j == J - 1)
    def _():
        staged[...] = back[rows_here:, :].astype(BF)
        exchange.start()
        out_theirs[...] = out[rows_here:, :].astype(BF)
        out_mine[...] = out[:rows_here, :]
        back_mine[...] = back[:rows_here, :]

    @pl.when(j == J + 2)
    def _():
        for n in (J - 2, J - 1):
            to_core(n).wait_send()
            down_to_core(n).wait_send()
            for i in range(1, X):
                to_x(n, i).wait_send()
            for k in range(1, Z):
                to_z(n, k).wait_send()

        def finish(n, carry):
            keep(n).wait()
            for d in range(1, 4):
                share(n, d).wait()
            return carry

        lax.fori_loop(0, J, finish, 0)
        exchange.wait()
        for g in range(Z):
            down_keep(g).wait()
            for i in range(1, X):
                down_to_x(g, i).wait_send()


def feed_forward(b, c, inner, down, fsdp_count):
    rows, width = b.shape
    _, _, hidden = inner.shape
    half = down.shape[2]
    step = 256
    J = hidden // step
    X = fsdp_count // Z
    R, R2 = width // fsdp_count, hidden // fsdp_count
    whole = pl.BlockSpec((rows, width), lambda j: (0, 0), pipeline_mode=pl.Buffered(1))
    part = pl.BlockSpec((rows // 2, width), lambda j: (0, 0), pipeline_mode=pl.Buffered(1))
    inner_spec = pl.BlockSpec((2, width, step), lambda j: (0, 0, jnp.minimum(j, J - 1)))
    down_spec = pl.BlockSpec((2, step, half), lambda j: (0, jnp.minimum(j, J - 1), 0))
    dma, vmem = pltpu.SemaphoreType.DMA, pltpu.VMEM
    return pl.pallas_call(
        functools.partial(feed_forward_kernel, X, J),
        grid=(J + 3,),
        out_shape=(
            jax.ShapeDtypeStruct((rows // 2, width), F32),
            jax.ShapeDtypeStruct((rows // 2, width), F32),
            jax.ShapeDtypeStruct((rows // 2, width), BF),
            jax.ShapeDtypeStruct((rows // 2, width), BF),
            jax.ShapeDtypeStruct((4, R, hidden), BF),
            jax.ShapeDtypeStruct((Z, R2, half), BF),
            jax.ShapeDtypeStruct((hidden, half), BF),
        ),
        in_specs=[whole, whole, inner_spec, down_spec],
        out_specs=(part, part, part, ANY, ANY, ANY, ANY),
        scratch_shapes=[
            vmem((rows, width), F32), vmem((rows, width), F32),
            vmem((2, step, half), BF), vmem((2, step, half), BF), vmem((J, step, half), BF),
            vmem((2, step, half), BF), vmem((Z, R2, half), BF), vmem((Z, X - 1, R2, half), BF),
            vmem((2, width, step), BF), vmem((2, width, step), BF), vmem((J, width, step), BF),
            vmem((2, Z, X, R, step), BF), vmem((J, X - 1, Z, R, step), BF),
            vmem((2, Z, R, step), BF), vmem((J, Z - 1, R, step), BF),
            vmem((J, R, step), BF), vmem((rows // 2, width), BF),
            dma((2,)), dma((J,)), dma((2, X - 1)), dma((J, X - 1)), dma((2, Z - 1)), dma((J, Z - 1)),
            dma((J, 3)), dma((J, 3)), dma, dma, dma((2,)), dma((J,)), dma((J,)),
            dma((2,)), dma((Z,)), dma((Z, X - 1)), dma((Z, X - 1)), dma((Z,)),
        ],
        compiler_params=pltpu.CompilerParams(
            vmem_limit_bytes=VMEM_BYTES, collective_id=1, has_side_effects=True
        ),
        cost_estimate=pl.CostEstimate(flops=18 * rows * width * hidden, bytes_accessed=60 * 2**20, transcendentals=0),
        name="feed_forward",
    )(b, c, inner, down)


def total_of(values):
    return functools.reduce(jnp.add, values)


def attention_back_kernel(
    X, groups, head_size, carried, q, k, v, edge, mix, dhb, mixed, inputs, proj, gains, second_gain, frames_in, down_in, out_send,
    frames_grad, gains_sum, attn_all, down_all, out_recv,
    da, gain_terms, gain_from, mixed_grad, before, terms_before, terms_here, tails, grads, edge_send, edge_recv,
    mine, other, from_core, keep_y, send_y, from_y, summed, from_x, column, from_z, final, plane, from_plane, final_plane,
    down_mine, down_from_z, down_final,
    s_edge, r_edge, s1, r1, sy, ry, sxa, rxa, sxb, rxb, sz, rz, sf, rf, sp, rp, sc, rc, local_sem,
    s_out, r_out, sg, rg, frame_sem, sdz, rdz, sdf, rdf, down_sem, free,
):
    i = pl.program_id(0)
    frames, step = q.shape[2:]
    R, thin = final.shape[1:]
    subs = 2 * groups
    slots = from_core.shape[0]
    dp, fs = lax.axis_index("dp"), lax.axis_index("fsdp")
    F = Z * X
    y, core = dp // 2, dp % 2
    z, x = fs // X, fs % X
    me = dp * F + fs
    devices = 4 * F
    core_peer = (y * 2 + 1 - core, fs)
    y_peer = ((1 - y) * 2 + core, fs)
    before_me = ((me - 1 + devices) % devices // F, (me - 1 + devices) % devices % F)
    after_me = ((me + 1) % devices // F, (me + 1) % devices % F)

    def z_peer(n):
        return (dp, lax.rem(z + n, Z) * X + x)

    def x_peer(n):
        return (dp, z * X + lax.rem(x + n, X))

    def dp_peer(d):
        return (((y + d // 2) % 2) * 2 + (core + d % 2) % 2, fs)

    def to_before(n):
        return remote_copy(edge_send.at[n % 2], edge_recv.at[n], s_edge.at[n % 2], r_edge.at[n], before_me)

    def to_core(n):
        return remote_copy(other.at[n % 2], from_core.at[n % slots], s1.at[n % 2], r1.at[n % slots], core_peer)

    def to_y(n):
        return remote_copy(send_y.at[n % 2], from_y.at[n], sy.at[n % 2], ry.at[n], y_peer)

    def to_x_early(n, j):
        return remote_copy(
            summed.at[n % 3, pl.ds(1, 2), :, lax.rem(x + j, X)], from_x.at[n, j - 1, pl.ds(1, 2)],
            sxa.at[n % 3, j - 1], rxa.at[n, j - 1], x_peer(j),
        )

    def to_x_late(n, j):
        return remote_copy(
            summed.at[n % 3, 0, :, lax.rem(x + j, X)], from_x.at[n, j - 1, 0],
            sxb.at[n % 3, j - 1], rxb.at[n, j - 1], x_peer(j),
        )

    def to_z(n, j):
        return remote_copy(
            column.at[n % 2, :, lax.rem(z + j, Z)], from_z.at[n, j - 1], sz.at[n % 2, j - 1], rz.at[n, j - 1], z_peer(j)
        )

    def place(n, t):
        return attn_all.at[t, core, :, pl.ds(pl.multiple_of(n * thin, thin), thin)]

    def share(n, d):
        return remote_copy(final.at[n], place(n, y), sf.at[n, d - 1], rf.at[n, d - 1], dp_peer(d))

    def relay(n):
        return remote_copy(place(n, 1 - y), place(n, 1 - y), sf.at[n, 2], rf.at[n, 2], core_peer)

    def down_to_z(k):
        return remote_copy(
            down_in.at[lax.rem(z + k, Z)], down_from_z.at[k - 1], sdz.at[k - 1], rdz.at[k - 1], z_peer(k)
        )

    def down_share(d):
        return remote_copy(down_final, down_all.at[dp], sdf.at[d - 1], rdf.at[d - 1], dp_peer(d))

    def down_relay():
        part = down_all.at[(1 - y) * 2 + core]
        return remote_copy(part, part, sdf.at[2], rdf.at[2], core_peer)

    def to_plane(n):
        return remote_copy(plane.at[n], from_plane.at[n], sp.at[n], rp.at[n], y_peer)

    def share_core(n, t):
        return remote_copy(final_plane.at[n, t], place(n, 2 + t), sc.at[n, t], rc.at[n, t], core_peer)

    def keep(n, t):
        src = final.at[n] if t == 0 else final_plane.at[n, t - 1]
        return pltpu.make_async_copy(src, place(n, y if t == 0 else 1 + t), local_sem.at[n, t])

    def load_frames(g):
        dst = grads.at[g] if g < 3 else mixed_grad
        return pltpu.make_async_copy(frames_in.at[:, :, pl.ds(g * step, step)], dst, frame_sem.at[g])

    def gain_copy(level, n):
        peer = (core_peer, y_peer, x_peer(n + 1), z_peer(n + 1))[level]
        return remote_copy(gain_terms.at[level], gain_from.at[level, n], sg.at[level, n], rg.at[level, n], peer)

    down_load = pltpu.make_async_copy(down_in.at[z], down_mine, down_sem.at[0])
    down_keep = pltpu.make_async_copy(down_final, down_all.at[dp], down_sem.at[1])
    out_copy = remote_copy(out_send, out_recv, s_out, r_out, y_peer)

    @pl.when(i == 0)
    def _():
        barrier = pltpu.get_barrier_semaphore()
        peers = [z_peer(n) for n in range(1, Z)] + [x_peer(n) for n in range(1, X)]
        peers += [dp_peer(d) for d in range(1, 4)] + [before_me, after_me]
        for peer in peers:
            pl.semaphore_signal(barrier, inc=1, device_id=peer, device_id_type=MESH)
        pl.semaphore_wait(barrier, len(peers))
        out_copy.start()
        for k in range(1, Z):
            down_to_z(k).start()
        down_load.start()
        da[...] = jnp.zeros_like(da)

        @pl.when(me == devices - 1)
        def _():
            edge_recv[...] = jnp.zeros_like(edge_recv)

    def active(first):
        return (i >= first) & (i < first + subs)

    @pl.when(active(2))
    def _():
        n = i - 2
        to_core(n).wait_recv()

        @pl.when(n >= 2)
        def _():
            to_y(n - 2).wait_send()

        @pl.when(n >= 3)
        def _():
            for j in range(1, X):
                to_x_early(n - 3, j).wait_send()

        def both(t):
            return (mine[n % 2, t].astype(F32) + from_core[n % slots, t].astype(F32)).astype(BF)

        send_y[n % 2] = both(1 - y)
        to_y(n).start()
        for t in range(2):
            summed[n % 3, 1 + t] = both(2 + t).reshape(summed.shape[2:])
        for j in range(1, X):
            to_x_early(n, j).start()
        keep_y[n % 2] = both(y)

        @pl.when(n < subs - slots)
        def _():
            pl.semaphore_signal(free, inc=1, device_id=core_peer, device_id_type=MESH)

    @pl.when(active(3))
    def _():
        n = i - 3
        to_y(n).wait_recv()

        @pl.when(n >= 3)
        def _():
            for j in range(1, X):
                to_x_late(n - 3, j).wait_send()

        total = (keep_y[n % 2].astype(F32) + from_y[n].astype(F32)).astype(BF)
        summed[n % 3, 0] = total.reshape(summed.shape[2:])
        for j in range(1, X):
            to_x_late(n, j).start()

    @pl.when(active(4))
    def _():
        n = i - 4
        for j in range(1, X):
            to_x_early(n, j).wait_recv()
            to_x_late(n, j).wait_recv()

        @pl.when(n >= 2)
        def _():
            for j in range(1, Z):
                to_z(n - 2, j).wait_send()

        total = summed[n % 3, :, :, x].astype(F32) + total_of([from_x[n, j].astype(F32) for j in range(X - 1)])
        column[n % 2] = total.astype(BF)
        for j in range(1, Z):
            to_z(n, j).start()

    @pl.when(active(5))
    def _():
        n = i - 5
        for j in range(1, Z):
            to_z(n, j).wait_recv()
        total = column[n % 2, :, z].astype(F32) + total_of([from_z[n, j].astype(F32) for j in range(Z - 1)])
        total = total.astype(BF)
        final[n] = total[0]
        plane[n] = total[1:]
        to_plane(n).start()
        keep(n, 0).start()
        for d in range(1, 3):
            share(n, d).start()

    @pl.when(active(6))
    def _():
        n = i - 6
        to_plane(n).wait_recv()
        share(n, 2).wait_recv()
        relay(n).start()
        final_plane[n] = (plane[n].astype(F32) + from_plane[n].astype(F32)).astype(BF)
        for t in range(2):
            keep(n, t + 1).start()
            share_core(n, t).start()

    @pl.when(i == 4)
    def _():
        down_load.wait()
        for k in range(1, Z):
            down_to_z(k).wait_recv()
        total = down_mine[...].astype(F32) + total_of([down_from_z[k].astype(F32) for k in range(Z - 1)])
        down_final[...] = total.astype(BF)
        down_keep.start()
        for d in range(1, 3):
            down_share(d).start()

    @pl.when(i == 6)
    def _():
        down_share(2).wait_recv()
        down_relay().start()

    @pl.when((i < subs) & (i % 2 == 0))
    def _():
        m = i // 2
        slot = m % 2
        ones = head_ones(step, head_size)
        scale = 1.0 / math.sqrt(head_size)
        first = lax.broadcasted_iota(jnp.int32, (frames, step), 0) == 0
        last = lax.broadcasted_iota(jnp.int32, (frames, step), 0) == frames - 1
        for p in range(2):
            mixed_grad[p] = total_of(
                [nt(dhb[p, :, g * step : (g + 1) * step], mix[g, 0, p]) for g in range(groups)]
            ).astype(BF)
            before[p] = jnp.where(first, edge[0, p : p + 1, :], pltpu.roll(k[0, p].astype(F32), 1, 0))
            before[2 + p] = jnp.where(first, edge[0, 2 + p : 3 + p, :], pltpu.roll(v[0, p].astype(F32), 1, 0))

        def chunk(c, carry):
            rows = pl.ds(pl.multiple_of(c * CHUNK, CHUNK), CHUNK)
            allowed = jnp.broadcast_to(carried[rows, :], (CHUNK, step)) > 0.5
            queries = [q[0, p, rows, :].astype(F32) for p in range(2)]
            cots = [mixed_grad[p, rows, :].astype(F32) for p in range(2)]
            keys = [before[p, rows, :] for p in range(2)] + [k[0, p, rows, :].astype(F32) for p in range(2)]
            values = [before[2 + p, rows, :] for p in range(2)] + [v[0, p, rows, :].astype(F32) for p in range(2)]

            scores = per_head(queries, keys, ones)
            dprobs = per_head(cots, values, ones)
            key_grads, value_grads = [[] for _ in range(4)], [[] for _ in range(4)]
            for p, span in SPANS:
                probs = head_probs(scores, span, allowed, scale)
                mean = total_of([pr * dprobs[m] for m, pr in zip(span, probs)])
                query_grad = []
                for m, pr in zip(span, probs):
                    n = PAIRS[m][1]
                    ds = (pr * (dprobs[m] - mean)).astype(BF).astype(F32) * scale
                    query_grad.append(ds * keys[n])
                    key_grads[n].append(ds * queries[p])
                    value_grads[n].append(pr.astype(BF).astype(F32) * cots[p])
                grads[0, p, rows, :] = total_of(query_grad).astype(BF)
            for p in range(2):
                terms_before[p, rows, :] = total_of(key_grads[p])
                terms_before[2 + p, rows, :] = total_of(value_grads[p])
                terms_here[p, rows, :] = total_of(key_grads[2 + p])
                terms_here[2 + p, rows, :] = total_of(value_grads[2 + p])
            return carry

        lax.fori_loop(0, frames // CHUNK, chunk, 0)

        @pl.when((m >= 2) & (me > 0))
        def _():
            to_before(m - 2).wait_send()

        for row in range(4):
            edge_send[slot, row : row + 1, :] = terms_before[row, 0:1, :]

        @pl.when(me > 0)
        def _():
            to_before(m).start()

        for row in range(4):
            total = terms_here[row] + jnp.where(last, 0.0, pltpu.roll(terms_before[row], frames - 1, 0))
            grads[1 + row // 2, row % 2] = total.astype(BF)
            tails[row] = total[frames - 16 :, :]

    @pl.when((i < subs) & (i % 2 == 1))
    def _():
        m = i // 2

        @pl.when(me < devices - 1)
        def _():
            to_before(m).wait_recv()

        bottom = lax.broadcasted_iota(jnp.int32, (16, step), 0) == 15
        for row in range(4):
            fixed = tails[row] + jnp.where(bottom, edge_recv[m, row : row + 1, :], 0.0)
            grads[1 + row // 2, row % 2, frames - 16 :, :] = fixed.astype(BF)

        @pl.when(m >= 1)
        def _():
            for h in range(2):
                to_core(2 * m - 2 + h).wait_send()

        for t in range(4):
            pair = []
            for p in range(2):
                if t < 3:
                    pair.append(tn(inputs[p], grads[t, p]).astype(BF))
                else:
                    pair.append(tn(mixed[p], dhb[p, :, pl.ds(pl.multiple_of(m * step, step), step)]).astype(BF))
            here = jnp.where(core == 0, pair[0], pair[1])
            there = jnp.where(core == 0, pair[1], pair[0])
            for h in range(2):
                mine[h, t] = here[:, h * thin : (h + 1) * thin]
                other[h, t] = there[:, h * thin : (h + 1) * thin]

        @pl.when(m >= slots // 2)
        def _():
            pl.semaphore_wait(free, 2)

        for h in range(2):
            to_core(2 * m + h).start()
        for p in range(2):
            da[p] += total_of([nt(grads[t, p], proj[0, t, p]) for t in range(3)])

        @pl.when(m == groups - 1)
        def _():
            for g in range(groups):
                load_frames(g).start()

    @pl.when(i == subs)
    def _():
        for g in range(groups):
            load_frames(g).wait()

        def chunk(c, term):
            rows = pl.ds(pl.multiple_of(c * CHUNK, CHUNK), CHUNK)
            for p in range(2):
                pieces = [grads[g, p, rows, :] if g < 3 else mixed_grad[p, rows, :] for g in range(groups)]
                value = jnp.concatenate(pieces, axis=1).astype(F32)
                inverse = scale_rows(value)
                normed = value * inverse
                grad = da[p, rows, :]
                term = term + jnp.sum(grad * normed, axis=0, keepdims=True)
                total = dhb[p, rows, :].astype(F32) + norm_back(grad, normed, gains[0:1, :], inverse)
                frames_grad[p, rows, :] = total.astype(BF)
            return term

        term = lax.fori_loop(0, frames // CHUNK, chunk, jnp.zeros((1, da.shape[2]), F32))
        gain_terms[0] = second_gain[...]
        gain_terms[0, 0:1, :] = term
        gain_copy(0, 0).start()

    for level in range(1, 4):
        @pl.when(i == subs + level)
        def _():
            count = X - 1 if level == 3 else 1
            total = gain_terms[level - 1]
            for n in range(count):
                gain_copy(level - 1, n).wait()
                total = total + gain_from[level - 1, n]
            gain_terms[level] = total
            for n in range(Z - 1 if level == 3 else X - 1 if level == 2 else 1):
                gain_copy(level, n).start()

    @pl.when(i == subs + 4)
    def _():
        total = gain_terms[3]
        for n in range(Z - 1):
            gain_copy(3, n).wait()
            total = total + gain_from[3, n]
        gains_sum[...] = total

    @pl.when(i == subs + 5)
    def _():
        @pl.when(me > 0)
        def _():
            for n in (groups - 2, groups - 1):
                to_before(n).wait_send()

        for n in (subs - 3, subs - 2, subs - 1):
            for j in range(1, X):
                to_x_early(n, j).wait_send()
                to_x_late(n, j).wait_send()

        for n in (subs - 2, subs - 1):
            to_core(n).wait_send()
            to_y(n).wait_send()
            for j in range(1, Z):
                to_z(n, j).wait_send()

        def finish(n, carry):
            to_plane(n).wait_send()
            keep(n, 0).wait()
            share(n, 1).wait()
            share(n, 2).wait_send()
            relay(n).wait()
            for t in range(2):
                keep(n, t + 1).wait()
                share_core(n, t).wait()
            return carry

        lax.fori_loop(0, subs, finish, 0)
        out_copy.wait()
        for k in range(1, Z):
            down_to_z(k).wait_send()
        down_keep.wait()
        down_share(1).wait()
        down_share(2).wait_send()
        down_relay().wait()


def attention_back(
    carried, qkv_rows, edge, attn, dhb, mixed, inputs, gains, second_gain, frames_in, down_in, out_send, head_size, fsdp_count
):
    _, frames, width = dhb.shape
    step = STEP
    groups = width // step
    X = fsdp_count // Z
    R = width // fsdp_count

    def early(i):
        return jnp.minimum(i // 2, groups - 1)

    rows = [pl.BlockSpec((1, 2, frames, step), lambda i, t=t: (t, 0, 0, early(i))) for t in range(3)]
    edge_spec = pl.BlockSpec((1, 8, step), lambda i: (early(i), 0, 0))
    mask = pl.BlockSpec((frames, 1), lambda i: (0, 0), pipeline_mode=pl.Buffered(1))
    whole = pl.BlockSpec((2, frames, width), lambda i: (0, 0, 0), pipeline_mode=pl.Buffered(1))
    mix_spec = pl.BlockSpec((groups, 1, 2, step, step), lambda i: (0, 3, 0, early(i), 0))
    proj_spec = pl.BlockSpec((1, 3, 2, width, step), lambda i: (jnp.clip((i - 1) // 2, 0, groups - 1), 0, 0, 0, 0))
    line = pl.BlockSpec((8, width), lambda i: (0, 0), pipeline_mode=pl.Buffered(1))
    dma, vmem = pltpu.SemaphoreType.DMA, pltpu.VMEM
    thin = step // 2
    n, slots, peers = 2 * groups, 4, max(X, Z) - 1
    return pl.pallas_call(
        functools.partial(attention_back_kernel, X, groups, head_size),
        grid=(n + 6,),
        out_shape=(
            jax.ShapeDtypeStruct((2, frames, width), BF),
            jax.ShapeDtypeStruct((8, width), F32),
            jax.ShapeDtypeStruct((4, 2, R, width), BF),
            jax.ShapeDtypeStruct((4,) + down_in.shape[1:], BF),
            jax.ShapeDtypeStruct(out_send.shape, BF),
        ),
        in_specs=[mask, *rows, edge_spec, mix_spec, whole, whole, whole, proj_spec, line, line, ANY, ANY, ANY],
        out_specs=(whole, line, ANY, ANY, ANY),
        scratch_shapes=[
            vmem((2, frames, width), F32), vmem((4, 8, width), F32), vmem((4, peers, 8, width), F32),
            vmem((2, frames, step), BF), vmem((4, frames, step), F32), vmem((4, frames, step), F32),
            vmem((4, frames, step), F32), vmem((4, 16, step), F32), vmem((3, 2, frames, step), BF),
            vmem((2, 8, step), F32), vmem((groups, 8, step), F32),
            vmem((2, 4, width, thin), BF), vmem((2, 4, width, thin), BF), vmem((slots, 4, width, thin), BF),
            vmem((2, width, thin), BF), vmem((2, width, thin), BF), vmem((n, width, thin), BF),
            vmem((3, 3, Z, X, R, thin), BF), vmem((n, X - 1, 3, Z, R, thin), BF),
            vmem((2, 3, Z, R, thin), BF), vmem((n, Z - 1, 3, R, thin), BF),
            vmem((n, R, thin), BF), vmem((n, 2, R, thin), BF), vmem((n, 2, R, thin), BF), vmem((n, 2, R, thin), BF),
            vmem(down_in.shape[1:], BF), vmem((Z - 1,) + down_in.shape[1:], BF), vmem(down_in.shape[1:], BF),
            dma((2,)), dma((groups,)), dma((2,)), dma((slots,)), dma((2,)), dma((n,)),
            dma((3, X - 1)), dma((n, X - 1)), dma((3, X - 1)), dma((n, X - 1)),
            dma((2, Z - 1)), dma((n, Z - 1)), dma((n, 3)), dma((n, 3)), dma((n,)), dma((n,)),
            dma((n, 2)), dma((n, 2)), dma((n, 3)),
            dma, dma, dma((4, peers)), dma((4, peers)), dma((groups,)),
            dma((Z - 1,)), dma((Z - 1,)), dma((3,)), dma((3,)), dma((2,)), pltpu.SemaphoreType.REGULAR,
        ],
        compiler_params=pltpu.CompilerParams(vmem_limit_bytes=63 * 2**20, collective_id=2, has_side_effects=True),
        name="attention_back",
    )(
        carried, qkv_rows, qkv_rows, qkv_rows, edge, attn, dhb, mixed, inputs, attn,
        gains, second_gain, frames_in, down_in, out_send,
    )


def update_kernel(step_size, share, weight, moment, average, grad_out, moment_out, average_out, weight_out):
    gradient = share[...].reshape(weight.shape).astype(F32)
    moment_new, average_new, weight_new = owner_update(
        weight[...], gradient, moment[...], average[...], step_size
    )
    grad_out[...] = gradient
    moment_out[...] = moment_new
    average_out[...] = average_new
    weight_out[...] = weight_new


def update(shares, share_block, share_at, grid, block, at, weight, moment, average, step_size, name):
    share_spec = pl.BlockSpec(share_block, share_at)
    spec = pl.BlockSpec(block, at)
    return pl.pallas_call(
        functools.partial(update_kernel, step_size),
        grid=grid,
        out_shape=(jax.ShapeDtypeStruct(weight.shape, F32),) * 4,
        in_specs=[share_spec, spec, spec, spec],
        out_specs=(spec,) * 4,
        compiler_params=pltpu.CompilerParams(vmem_limit_bytes=VMEM_BYTES),
        name=name,
    )(shares, weight, moment, average)


def per_device(
    frames, cotangent, segment_ids,
    qkv_weight, mix_weight, inner_weight, down_weight, norm_gains,
    qkv_moment, mix_moment, inner_moment, down_moment, gains_moment,
    qkv_average, mix_average, inner_average, down_average, gains_average,
):
    frame_count, positions, width = frames.shape
    head_size = width // HEADS
    hidden = inner_weight.shape[2] // 2
    dp_count, fsdp_count = lax.axis_size("dp"), lax.axis_size("fsdp")
    X = fsdp_count // Z
    devices = dp_count * fsdp_count
    total_frames = frame_count * devices
    dp, fs = lax.axis_index("dp"), lax.axis_index("fsdp")
    y, core = dp // 2, dp % 2
    z, x = fs // X, fs % X
    axes = ("dp", "fsdp")

    device = dp * fsdp_count + fs
    padded_ids = jnp.concatenate([jnp.full((1,), -1, jnp.int32), segment_ids])
    window = lax.dynamic_slice_in_dim(padded_ids, device * frame_count, frame_count + 1)
    carried = (window[1:] == window[:-1]).astype(F32)[:, None]

    half_width = width // 2
    own_gains = norm_gains.astype(BF).astype(F32)
    gains_own = lax.dynamic_update_slice(jnp.zeros((8, width), F32), own_gains, (0, fs * own_gains.shape[1]))
    frames_by = frames.transpose(1, 0, 2)
    cot = cotangent.transpose(1, 0, 2)
    attn, inner, down, gains, a, qkv_rows, mixed, edge, hres, b_rows, c_rows = forward(
        frames_by, carried, cot, gains_own, qkv_weight, mix_weight, inner_weight, down_weight, head_size, fsdp_count
    )
    r2 = scale_rows(hres)
    n2 = hres * r2
    b_rows = b_rows.reshape(2 * frame_count, width)
    c_rows = c_rows.reshape(2 * frame_count, width)
    out, back, out_there, back_there, inner_shares, down_columns, _ = feed_forward(b_rows, c_rows, inner, down, fsdp_count)

    def by_position(mine, theirs):
        return jnp.where(y == 0, jnp.stack([mine, theirs]), jnp.stack([theirs, mine]))

    db = by_position(back, back_there.astype(F32))

    e2 = jnp.sum(db * n2, axis=(0, 1))
    dh = cot.astype(F32) + norm_back(db, n2, gains[1], r2)
    dhb = dh.astype(BF)
    second_gain = jnp.zeros((8, width), F32).at[1].set(e2)
    frames_grad, gains_sum, attn_shares, down_shares, out_here = attention_back(
        carried, qkv_rows, edge, attn, dhb, mixed, a, gains, second_gain, frames_by, down_columns, out_there, head_size, fsdp_count
    )
    frames_grad = frames_grad.transpose(1, 0, 2)
    layer_out = (hres + by_position(out, out_here.astype(F32))).astype(BF).transpose(1, 0, 2)

    step_size = step_rate / math.sqrt(total_frames)
    R, R2 = qkv_weight.shape[1], down_weight.shape[1]
    cut = min(R, 64)
    qkv_new = update(
        attn_shares, (1, 1, R, width), lambda p, t: (t, p, 0, 0), (2, 3), (1, R, width), lambda p, t: (p, 0, t),
        qkv_weight, qkv_moment, qkv_average, step_size, "update_qkv",
    )
    mix_new = update(
        attn_shares, (1, 1, R, width), lambda p: (3, p, 0, 0), (2,), (1, R, width), lambda p: (p, 0, 0),
        mix_weight, mix_moment, mix_average, step_size, "update_mix",
    )
    inner_new = update(
        inner_shares, (1, cut, hidden), lambda p, c, r: (2 * p + c, r, 0), (2, 2, R // cut),
        (1, cut, hidden), lambda p, c, r: (p, r, c), inner_weight, inner_moment, inner_average, step_size, "update_inner",
    )
    down_new = update(
        down_shares, (1, R2, half_width), lambda p, c: (2 * p + c, 0, 0), (2, 2),
        (1, R2, half_width), lambda p, c: (p, 0, c), down_weight, down_moment, down_average, step_size, "update_down",
    )
    own = norm_gains.shape[1]
    gains_grad = lax.dynamic_slice(gains_sum, (0, fs * own), (2, own))
    gains_new = (gains_grad,) + owner_update(norm_gains, gains_grad, gains_moment, gains_average, step_size)
    new = (qkv_new, mix_new, inner_new, down_new, gains_new)
    return (layer_out, frames_grad) + tuple(n[kind] for kind in range(4) for n in new)


def solution(mesh):
    rows = P(("dp", "fsdp"), None, None)
    weight = P(None, "fsdp", None)
    gains = P(None, "fsdp")
    weights = (weight,) * 4 + (gains,)
    return jax.shard_map(
        per_device,
        mesh=mesh,
        in_specs=(rows, rows, P()) + weights * 3,
        out_specs=(rows, rows) + weights * 4,
        check_vma=False,
    )
```

```python
import functools
import math

import jax
import jax.numpy as jnp
from jax import lax
from jax.experimental import pallas as pl
from jax.experimental.pallas import tpu as pltpu
from jax.sharding import PartitionSpec as P

HEADS = 16
Z = 4
MESH = pl.DeviceIdType.MESH
ANY = pl.BlockSpec(memory_space=pl.ANY)
BF = jnp.bfloat16
F32 = jnp.float32

norm_eps = 1e-05
momentum_rate = 0.5
average_rate = 0.5
step_rate = 0.05
VMEM_BYTES = 60 * 1024 * 1024


def nn(a, b):
    return lax.dot_general(a, b, (((1,), (0,)), ((), ())), preferred_element_type=F32)


def nt(a, b):
    return lax.dot_general(a, b, (((1,), (1,)), ((), ())), preferred_element_type=F32)


def tn(a, b):
    return lax.dot_general(a, b, (((0,), (0,)), ((), ())), preferred_element_type=F32)


def scale_rows(values):
    square = jnp.mean(values * values, axis=-1, keepdims=True) + norm_eps
    inverse = lax.rsqrt(square)
    return inverse * (1.5 - 0.5 * square * inverse * inverse)


def norm_back(grad_in, normed, gain_row, inverse):
    scaled = grad_in * gain_row
    return inverse * (scaled - normed * jnp.mean(scaled * normed, axis=-1, keepdims=True))


def owner_update(weight, gradient, moment, average, step_size):
    moment_new = momentum_rate * moment + gradient
    weight_new = weight - step_size * (gradient + momentum_rate * moment_new)
    average_new = average_rate * average + (1.0 - average_rate) * weight_new
    return (moment_new, average_new, weight_new)


PAIRS = ((0, 0), (0, 1), (0, 2), (1, 0), (1, 1), (1, 2), (1, 3))
SPANS = ((0, range(0, 3)), (1, range(3, 7)))
CHUNK = 128
STEP = 256


def total_of(values):
    return functools.reduce(jnp.add, values)


def remote_copy(src, dst, send_sem, recv_sem, peer):
    return pltpu.make_async_remote_copy(
        src_ref=src, dst_ref=dst, send_sem=send_sem, recv_sem=recv_sem, device_id=peer, device_id_type=MESH
    )


def head_ones(lanes, head_size):
    row = lax.broadcasted_iota(jnp.int32, (lanes, lanes), 0) // head_size
    column = lax.broadcasted_iota(jnp.int32, (lanes, lanes), 1) // head_size
    return (row == column).astype(BF)


def per_head(left, right, ones):
    rows = left[0].shape[0]
    products = [(left[p] * right[n]).astype(BF) for p, n in PAIRS]
    sums = nn(jnp.concatenate(products, axis=0), ones)
    return [sums[m * rows : (m + 1) * rows] for m in range(len(PAIRS))]


def head_probs(scores, span, allowed, scale):
    s = [jnp.where(allowed, scores[m] * scale, -1e30) if PAIRS[m][1] < 2 else scores[m] * scale for m in span]
    top = functools.reduce(jnp.maximum, s)
    e = [jnp.exp(value - top) for value in s]
    e = [jnp.where(allowed, value, 0.0) if PAIRS[m][1] < 2 else value for m, value in zip(span, e)]
    inverse = 1.0 / total_of(e)
    return [value * inverse for value in e]


def forward_kernel(
    X, groups, head_size, frames, carried, cot, gains_own, qkv_weight, mix_weight, inner_weight, down_weight,
    attn, inner, down, gains_out, inputs_out, rows_out, mixed_out, edge_out, hres_out, b_rows, c_rows,
    attn_wide, inner_wide, down_wide, attn_own, inner_own, down_own,
    gains, inputs, rows_in, mixed, before, hres, b, proj, mix, edge_send, edge_recv,
    send_up, recv_up, send_down, recv_down, send_x, recv_x, send_y, recv_y, send_c, recv_c, send_r, recv_r,
    send_g, recv_g, send_e, recv_e, send_b, recv_b, send_q, recv_q, local_sem, out_sem, wide_sem,
):
    dp, fs = lax.axis_index("dp"), lax.axis_index("fsdp")
    F = Z * X
    y, core = dp // 2, dp % 2
    z, x = fs // X, fs % X
    me = dp * F + fs
    devices = 4 * F
    count = frames.shape[1]
    core_peer = (y * 2 + 1 - core, fs)
    y_peer = ((1 - y) * 2 + core, fs)
    up_peer = (dp, lax.rem(z + 1, Z) * X + x)
    down_peer = (dp, lax.rem(z + Z - 1, Z) * X + x)
    before_me = ((me - 1 + devices) % devices // F, (me - 1 + devices) % devices % F)
    after_me = ((me + 1) % devices // F, (me + 1) % devices % F)

    def z_peer(k):
        return (dp, lax.rem(z + k, Z) * X + x)

    def x_peer(i):
        return (dp, z * X + lax.rem(x + i, X))

    UNITS = unit_list(groups, inner_own.shape[1], down_own.shape[1])

    width = frames.shape[2]

    def wide(slot):
        return (attn_wide.at[slot] if slot < groups + 1 else (inner_wide, down_wide)[slot - groups - 1])

    def fetch(slot, src, condition=None):
        copy = pltpu.make_async_copy(src, wide(slot), wide_sem.at[slot])
        if condition is None:
            copy.start()
        else:
            pl.when(condition)(copy.start)

    def columns_of(weight, part, block):
        return weight.at[:, :, pl.ds(pl.multiple_of(part * width + block * STEP, STEP), STEP)]

    def fetch_all():
        for n in range(groups - 1):
            fetch(n, columns_of(qkv_weight, jnp.minimum(dp, 2), n), dp < 3)
            fetch(n, columns_of(mix_weight, 0, n), dp == 3)
        fetch(groups - 1, columns_of(qkv_weight, core, groups - 1))
        fetch(groups, columns_of(qkv_weight, 2, groups - 1), core == 0)
        fetch(groups, columns_of(mix_weight, 0, groups - 1), core == 1)
        half, hidden = width // 2, inner_own.shape[1]
        fetch(groups + 1, inner_weight.at[y, :, pl.ds(pl.multiple_of(core * hidden, 128), hidden)])
        fetch(groups + 2, down_weight.at[y, :, pl.ds(pl.multiple_of(core * half, 128), half)])

    def take(slot):
        pltpu.make_async_copy(wide(slot), wide(slot), wide_sem.at[slot]).wait()
        if slot < groups + 1:
            attn_own[slot] = attn_wide[slot].astype(BF)
        elif slot == groups + 1:
            inner_own[...] = inner_wide[...].astype(BF)
        else:
            down_own[...] = down_wide[...].astype(BF)

    def own(u):
        kind, n, columns = UNITS[u][:3]
        if kind in ("quarter", "low", "high"):
            return attn_own.at[n if kind != "high" else n + 1]
        return (down_own if kind == "down" else inner_own).at[:, columns]

    def part_of(u, core_index, plane):
        kind = UNITS[u][0]
        if kind == "quarter":
            return plane * 2 + core_index
        return 2 + core_index if kind == "high" else core_index

    def whole(u, part):
        kind, n, columns = UNITS[u][:3]
        if kind == "down":
            return down.at[part, :, columns]
        if kind == "inner":
            return inner.at[part, :, columns]
        return attn.at[n, part]

    def place(u, source, part=None):
        kind, n, columns = UNITS[u][:3]
        part = part_of(u, core, y) if part is None else part
        if kind == "down":
            R = down_own.shape[0]
            return down.at[part, pl.ds(source * R, R), columns]
        if kind == "inner":
            R = inner_own.shape[0]
            return inner.at[part, pl.ds(source * R, R), columns]
        R = attn_own.shape[2]
        return attn.at[n, part, :, pl.ds(source * R, R), :]

    fetch_all()
    barrier = pltpu.get_barrier_semaphore()
    peers = [z_peer(k) for k in range(1, Z)] + [x_peer(i) for i in range(1, X)]
    peers += [core_peer, y_peer, before_me, after_me]
    for peer in peers:
        pl.semaphore_signal(barrier, inc=1, device_id=peer, device_id_type=MESH)
    pl.semaphore_wait(barrier, len(peers))

    sent, local = [], []

    def send(condition, make):
        remote_copy(*make()).start()
        sent.append((condition, make))

    def wait_send(condition, make):
        def action():
            remote_copy(*make()).wait_send()

        if condition is None:
            action()
        else:
            pl.when(condition())(action)

    def wait_recv(dst, recv_sem, send_sem):
        remote_copy(dst, dst, send_sem, recv_sem, core_peer).wait_recv()

    def store(src, dst):
        copy = pltpu.make_async_copy(src, dst, out_sem.at[len(local)])
        copy.start()
        local.append(copy)

    def spread(u, row, mine, condition):
        def src():
            return own(u) if mine else place(u, row() * X + x)

        for i in range(1, X):
            send(
                condition,
                lambda i=i: (
                    src(), place(u, row() * X + x), send_x.at[u, row(), i], recv_x.at[u, row(), i], x_peer(i)
                ),
            )
        to_plane(u, lambda: row() * X + x, src, condition)

    def to_plane(u, source, src, condition):
        if UNITS[u][0] == "quarter":
            send(
                condition,
                lambda: (src(), place(u, source()), send_y.at[u, source()], recv_y.at[u, source()], y_peer),
            )

    def crossed(u):
        return UNITS[u][3]

    def block(u, row):
        kind, n, columns = UNITS[u][:3]
        array, R = (down, down_own.shape[0]) if kind == "down" else (inner, inner_own.shape[0])
        return array.at[core, pl.ds(row * X * R, X * R), columns]

    def send_along(u, src, dst):
        def below_top():
            return z < Z - 1

        def above_bottom():
            return z > 0

        def upward():
            return (src(), dst(), send_up.at[u, 1], recv_up.at[u, 1], up_peer)

        def downward():
            return (src(), dst(), send_down.at[u, 1], recv_down.at[u, 1], down_peer)

        pl.when(below_top())(lambda: send(below_top, upward))
        pl.when(above_bottom())(lambda: send(above_bottom, downward))

    def start_unit(u):
        for slot in slots_of[u]:
            take(slot)
        if not crossed(u):
            send_along(u, lambda: own(u), lambda: place(u, fs))
        spread(u, lambda: z, True, None)
        store(own(u), place(u, fs))

    def turn(u):
        for i in range(1, X):
            column = lax.rem(x - i + X, X)
            wait_recv(place(u, z * X + column), recv_x.at[u, z, i], send_x.at[u, z, i])
        local[own_store[u]].wait()
        send_along(u, lambda: block(u, z), lambda: block(u, z))

    def hop(u, k):
        def side(reached, row, further, send_sem, recv_sem, peer):
            def here():
                return block(u, row()) if crossed(u) else place(u, row() * X + x)

            def both():
                return reached() & further()

            def action():
                wait_recv(here(), recv_sem.at[u, k], send_sem.at[u, k])
                if k < Z - 1:
                    pl.when(further())(
                        lambda: send(
                            both, lambda: (here(), here(), send_sem.at[u, k + 1], recv_sem.at[u, k + 1], peer)
                        )
                    )
                if not crossed(u):
                    spread(u, row, False, reached)

            pl.when(reached())(action)

        side(lambda: z >= k, lambda: z - k, lambda: z < Z - 1, send_up, recv_up, up_peer)
        side(lambda: z + k < Z, lambda: z + k, lambda: z > 0, send_down, recv_down, down_peer)

    def arrivals(u):
        for row in range(0 if crossed(u) else Z):
            for i in range(1, X):
                column = lax.rem(x - i + X, X)
                source = row * X + column
                wait_recv(place(u, source), recv_x.at[u, row, i], send_x.at[u, row, i])
                to_plane(u, lambda source=source: source, lambda source=source: place(u, source), None)
        if not crossed(u):
            local[own_store[u]].wait()
        mine = whole(u, part_of(u, core, y))
        send(None, lambda: (mine, mine, send_c.at[u], recv_c.at[u], core_peer))

    def relay(u):
        if UNITS[u][0] != "quarter":
            return
        part = (1 - y) * 2 + core
        for source in range(F):
            wait_recv(place(u, source, part), recv_y.at[u, source], send_y.at[u, source])
        theirs = whole(u, part)
        send(None, lambda: (theirs, theirs, send_r.at[u], recv_r.at[u], core_peer))

    def complete(u):
        wait_recv(whole(u, part_of(u, 1 - core, y)), recv_c.at[u], send_c.at[u])
        if UNITS[u][0] == "quarter":
            wait_recv(whole(u, (1 - y) * 2 + 1 - core), recv_r.at[u], send_r.at[u])

    scale = 1.0 / math.sqrt(head_size)

    def gather_gains():
        keep = pltpu.make_async_copy(gains_own, gains.at[fs], local_sem.at[0])
        keep.start()
        for k in range(1, Z):
            send(None, lambda k=k: (gains_own, gains.at[fs], send_g.at[0, k], recv_g.at[0, k], z_peer(k)))
        for i in range(1, X):
            send(None, lambda i=i: (gains_own, gains.at[fs], send_g.at[i, 0], recv_g.at[i, 0], x_peer(i)))
        keep.wait()

    def chunk_source(k, i):
        return lax.rem(z - k + Z, Z) * X + lax.rem(x - i + X, X)

    def pass_gains():
        for k in range(1, Z):
            here = gains.at[chunk_source(k, 0)]
            wait_recv(here, recv_g.at[0, k], send_g.at[0, k])
            for i in range(1, X):
                send(
                    None,
                    lambda here=here, i=i, k=k: (here, here, send_g.at[i, k], recv_g.at[i, k], x_peer(i)),
                )

    def take_gains():
        for k in range(Z):
            for i in range(1, X):
                wait_recv(gains.at[chunk_source(k, i)], recv_g.at[i, k], send_g.at[i, k])
        total = gains[0]
        for source in range(1, F):
            total = total + gains[source]
        gains_out[...] = total

    def norm_rows():
        def chunk(c, carry):
            rows = pl.ds(pl.multiple_of(c * CHUNK, CHUNK), CHUNK)
            for p in range(2):
                value = frames[p, rows, :].astype(F32)
                inputs[p, rows, :] = (value * scale_rows(value) * gains_out[0:1, :]).astype(BF)
            return carry

        lax.fori_loop(0, count // CHUNK, chunk, 0)
        store(inputs, inputs_out)

    def heads(m):
        columns = slice(m * STEP, (m + 1) * STEP)
        load = pltpu.make_async_copy(attn.at[m, pl.ds(0, 3)], proj, local_sem.at[0])
        load.start()
        load.wait()
        for t in (1, 2, 0):
            for p in range(2):
                rows_in[t, p, :, columns] = nn(inputs[p], proj[t, p]).astype(BF)
                if t > 0:
                    tail = rows_in[t, p, count - 16 :, columns].astype(F32)
                    row = 2 * (t - 1) + p
                    edge_send[m, row : row + 1, :] = tail[15:16, :]
            if t == 2:
                to_after = remote_copy(edge_send.at[m], edge_recv.at[m], send_e.at[m], recv_e.at[m], after_me)
                pl.when(me < devices - 1)(to_after.start)
        pl.when(me > 0)(to_after.wait_recv)
        first = lax.broadcasted_iota(jnp.int32, (count, STEP), 0) == 0
        for t in range(2):
            for p in range(2):
                n = 2 * t + p
                shifted = pltpu.roll(rows_in[1 + t, p, :, columns].astype(F32), 1, 0)
                before[n] = jnp.where(first, edge_recv[m, n : n + 1, :], shifted)
        ones = head_ones(STEP, head_size)

        def chunk(c, carry):
            rows = pl.ds(pl.multiple_of(c * CHUNK, CHUNK), CHUNK)
            allowed = jnp.broadcast_to(carried[rows, :], (CHUNK, STEP)) > 0.5
            queries, here_k, here_v = (
                [rows_in[t, p, rows, columns].astype(F32) for p in range(2)] for t in range(3)
            )
            keys = [before[p, rows, :] for p in range(2)] + here_k
            values = [before[2 + p, rows, :] for p in range(2)] + here_v
            scores = per_head(queries, keys, ones)
            for p, span in SPANS:
                probs = head_probs(scores, span, allowed, scale)
                terms = [pr.astype(BF).astype(F32) * values[PAIRS[n][1]] for n, pr in zip(span, probs)]
                mixed[p, rows, columns] = total_of(terms).astype(BF)
            return carry

        lax.fori_loop(0, count // CHUNK, chunk, 0)

    def load_mix():
        return pltpu.make_async_copy(attn.at[:, 3], mix, local_sem.at[1])

    def finish_rows():
        load_mix().wait()
        for turn in range(2):
            p = 1 - y if turn == 0 else y
            for m in range(groups):
                columns = slice(m * STEP, (m + 1) * STEP)
                hres[p, :, columns] = frames[p, :, columns].astype(F32) + nn(mixed[p], mix[m, p])

            def chunk(c, carry):
                rows = pl.ds(pl.multiple_of(c * CHUNK, CHUNK), CHUNK)
                value = hres[p, rows, :]
                b[turn, rows, :] = (value * scale_rows(value) * gains_out[1:2, :]).astype(BF)
                return carry

            lax.fori_loop(0, count // CHUNK, chunk, 0)
            if turn == 0:
                send(None, lambda: (b.at[0], b_rows.at[1], send_b, recv_b, y_peer))
            else:
                store(b.at[1], b_rows.at[0])
        store(hres, hres_out)

    @pl.when(me == 0)
    def _():
        edge_recv[...] = jnp.zeros_like(edge_recv)

    slots_of = [
        [n] if kind in ("quarter", "low") else [n + 1] if kind == "high" else [] for kind, n, *_ in UNITS
    ]
    slots_of[[u[0] for u in UNITS].index("inner")] = [groups + 1]
    slots_of[[u[0] for u in UNITS].index("down")] = [groups + 2]
    own_store = {}
    last_of = {kind_n[1]: u for u, kind_n in enumerate(UNITS) if kind_n[0] in ("quarter", "low", "high")}
    last_plane = max(u for u, kind_n in enumerate(UNITS) if kind_n[0] == "quarter")
    store(cot.at[y], c_rows.at[0])
    gather_gains()
    starts = [unit[4] for unit in UNITS]
    for tick in range(max(starts) + Z + 2):
        def aged(age):
            return [u for u, begun in enumerate(starts) if tick - begun == age]

        for u in aged(0):
            own_store[u] = len(local)
            start_unit(u)
        for u in aged(1):
            if crossed(u):
                turn(u)
        for k in range(1, Z):
            for u in aged(k):
                if not crossed(u):
                    hop(u, k)
            for u in aged(k + 1):
                if crossed(u):
                    hop(u, k)
        if tick == 1:
            pass_gains()
        if tick == 2:
            take_gains()
            norm_rows()
        for u in aged(Z):
            arrivals(u)
            if u == last_plane:
                send(None, lambda: (cot.at[1 - y], c_rows.at[1], send_q, recv_q, y_peer))
        for u in aged(Z + 1):
            relay(u)
            complete(u)
            for m in range(groups):
                if last_of[m] == u:
                    if m == groups - 1:
                        load_mix().start()
                    heads(m)
                    if m == groups - 1:
                        store(rows_in, rows_out)
                        store(mixed, mixed_out)
                        store(edge_recv, edge_out)
                        finish_rows()
    wait_recv(b_rows.at[1], recv_b, send_b)
    wait_recv(c_rows.at[1], recv_q, send_q)
    for condition, make in sent:
        wait_send(condition, make)
    for n, copy in enumerate(local):
        if n not in own_store.values():
            copy.wait()

    @pl.when(me < devices - 1)
    def _():
        for m in range(groups):
            remote_copy(edge_send.at[m], edge_recv.at[m], send_e.at[m], recv_e.at[m], after_me).wait_send()


def unit_list(groups, inner_width, down_width):
    units = [("quarter", n, None, False, n) for n in range(groups - 1)]
    units += [("low", groups - 1, None, False, groups - 1), ("high", groups - 1, None, False, groups)]
    start = groups + 1
    for kind, tiles, turns in (("down", down_width // 128, 2), ("inner", inner_width // 128, 6)):
        over_x = tiles // 4 if kind == "down" else -(-tiles // 4)
        at = 0
        for turn in range(turns):
            for crossed, all_tiles in ((False, tiles - over_x), (True, over_x)):
                lo, hi = all_tiles * turn // turns, all_tiles * (turn + 1) // turns
                if hi > lo:
                    units.append((kind, 0, slice(128 * at, 128 * (at + hi - lo)), crossed, start))
                    at += hi - lo
            start += 1
    return units


def forward(
    frames, carried, cot, gains_own, qkv_weight, mix_weight, inner_weight, down_weight, head_size, fsdp_count
):
    X = fsdp_count // Z
    _, count, width = frames.shape
    R, R2 = qkv_weight.shape[1], down_weight.shape[1]
    hidden, half = inner_weight.shape[2] // 2, width // 2
    groups = width // STEP
    units = len(unit_list(groups, hidden, half))
    dma, vmem = pltpu.SemaphoreType.DMA, pltpu.VMEM
    whole = pl.BlockSpec(memory_space=pltpu.VMEM)
    act = jax.ShapeDtypeStruct((2, count, width), BF)
    return pl.pallas_call(
        functools.partial(forward_kernel, X, groups, head_size),
        out_shape=(
            jax.ShapeDtypeStruct((groups, 4, 2, R * fsdp_count, STEP), BF),
            jax.ShapeDtypeStruct((2, R * fsdp_count, hidden), BF),
            jax.ShapeDtypeStruct((2, R2 * fsdp_count, half), BF),
            jax.ShapeDtypeStruct(gains_own.shape, F32),
            act,
            jax.ShapeDtypeStruct((3, 2, count, width), BF),
            act,
            jax.ShapeDtypeStruct((groups, 8, STEP), F32),
            jax.ShapeDtypeStruct((2, count, width), F32),
            act,
            act,
        ),
        in_specs=[whole] * 4 + [ANY] * 4,
        out_specs=(ANY,) * 3 + (whole,) + (ANY,) * 7,
        scratch_shapes=[
            vmem((groups + 1, 2, R, STEP), F32), vmem((R, hidden), F32), vmem((R2, half), F32),
            vmem((groups + 1, 2, R, STEP), BF), vmem((R, hidden), BF), vmem((R2, half), BF),
            vmem((fsdp_count,) + gains_own.shape, F32),
            vmem((2, count, width), BF), vmem((3, 2, count, width), BF), vmem((2, count, width), BF),
            vmem((4, count, STEP), F32), vmem((2, count, width), F32), vmem((2, count, width), BF),
            vmem((3, 2, width, STEP), BF), vmem((groups, 2, width, STEP), BF),
            vmem((groups, 8, STEP), F32), vmem((groups, 8, STEP), F32),
            dma((units, Z)), dma((units, Z)), dma((units, Z)), dma((units, Z)),
            dma((units, Z, X)), dma((units, Z, X)), dma((groups, fsdp_count)), dma((groups, fsdp_count)),
            dma((units,)), dma((units,)), dma((groups,)), dma((groups,)),
            dma((X, Z)), dma((X, Z)), dma((groups,)), dma((groups,)), dma, dma, dma, dma,
            dma((2,)), dma((units + 8,)), dma((groups + 3,)),
        ],
        compiler_params=pltpu.CompilerParams(
            vmem_limit_bytes=VMEM_BYTES, collective_id=0, has_side_effects=True
        ),
        name="attention_forward",
    )(frames, carried, cot, gains_own, qkv_weight, mix_weight, inner_weight, down_weight)


def feed_forward_kernel(
    X, J, b, c, inner, down, out_mine, back_mine, out_theirs, back_recv, inner_all, down_columns, down_sum,
    out, back, down_here, down_there, down_from_core, down_stage, down_column, down_from_x, mine, other, from_core, summed, from_x, column, from_z, final, staged,
    s1, r1, s2, r2, s3, r3, s5, r5, s6, r6, s7, r7, local_sem,
    s_stage, s_own, sdx, rdx, s_column,
):
    j = pl.program_id(0)
    half = down.shape[2]
    rows_here = out_mine.shape[0]
    R, step = final.shape[1:]
    dp, fs = lax.axis_index("dp"), lax.axis_index("fsdp")
    y, core = dp // 2, dp % 2
    z, x = fs // X, fs % X
    core_peer = (y * 2 + 1 - core, fs)
    y_peer = ((1 - y) * 2 + core, fs)

    def z_peer(k):
        return (dp, lax.rem(z + k, Z) * X + x)

    def x_peer(i):
        return (dp, z * X + lax.rem(x + i, X))

    def dp_peer(d):
        return (((y + d // 2) % 2) * 2 + (core + d % 2) % 2, fs)

    def to_core(n):
        return remote_copy(other.at[n % 2], from_core.at[n], s1.at[n % 2], r1.at[n], core_peer)

    def to_x(n, i):
        return remote_copy(
            summed.at[n % 2, :, lax.rem(x + i, X)], from_x.at[n, i - 1], s2.at[n % 2, i - 1], r2.at[n, i - 1], x_peer(i)
        )

    def to_z(n, k):
        return remote_copy(
            column.at[n % 2, lax.rem(z + k, Z)], from_z.at[n, k - 1], s3.at[n % 2, k - 1], r3.at[n, k - 1], z_peer(k)
        )

    def place(n, owner):
        return inner_all.at[owner, :, pl.ds(pl.multiple_of(n * step, step), step)]

    def share(n, d):
        return remote_copy(final.at[n], place(n, dp), s5.at[n, d - 1], r5.at[n, d - 1], dp_peer(d))

    def keep(n):
        return pltpu.make_async_copy(final.at[n], place(n, dp), local_sem.at[n])

    exchange = remote_copy(staged, back_recv, s6, r6, y_peer)

    R2 = down_column.shape[1]
    ends = [-(-(g + 1) * X * R2 // step) - 1 for g in range(Z)]

    def down_rows(g, column):
        return down_sum.at[pl.ds((g * X + column) * R2, R2), :]

    def down_store(n):
        return pltpu.make_async_copy(
            down_stage.at[n % 2], down_sum.at[pl.ds(pl.multiple_of(n * step, step), step), :], s_stage.at[n % 2]
        )

    def down_load(g):
        return pltpu.make_async_copy(down_rows(g, x), down_column.at[g], s_own.at[g])

    def down_to_x(g, i):
        return remote_copy(
            down_rows(g, lax.rem(x + i, X)), down_from_x.at[g, i - 1], sdx.at[g, i - 1], rdx.at[g, i - 1], x_peer(i)
        )

    def down_keep(g):
        return pltpu.make_async_copy(down_column.at[g], down_columns.at[g], s_column.at[g])

    def down_to_core(n):
        return remote_copy(down_there.at[n % 2], down_from_core.at[n], s7.at[n % 2], r7.at[n], core_peer)

    @pl.when(j == 0)
    def _():
        barrier = pltpu.get_barrier_semaphore()
        peers = [z_peer(k) for k in range(1, Z)] + [x_peer(i) for i in range(1, X)]
        peers += [dp_peer(d) for d in range(1, 4)]
        for peer in peers:
            pl.semaphore_signal(barrier, inc=1, device_id=peer, device_id_type=MESH)
        pl.semaphore_wait(barrier, len(peers))
        out[...] = jnp.zeros_like(out)
        back[...] = jnp.zeros_like(back)

    @pl.when((j >= 2) & (j < J + 2))
    def _():
        down_store(j - 2).wait()

    for g in range(Z):
        @pl.when(j == ends[g] + 2)
        def _():
            for i in range(1, X):
                down_to_x(g, i).start()
            down_load(g).start()

    @pl.when((j >= 1) & (j < J + 1))
    def _():
        n = j - 1
        to_core(n).wait_recv()

        @pl.when(n >= 2)
        def _():
            for i in range(1, X):
                to_x(n - 2, i).wait_send()

        down_to_core(n).wait_recv()
        down_stage[n % 2] = (down_here[n % 2].astype(F32) + down_from_core[n].astype(F32)).astype(BF)
        down_store(n).start()
        total = (mine[n % 2].astype(F32) + from_core[n].astype(F32)).astype(BF)
        summed[n % 2] = total.reshape(summed.shape[1:])
        for i in range(1, X):
            to_x(n, i).start()

    @pl.when((j >= 2) & (j < J + 2))
    def _():
        n = j - 2
        for i in range(1, X):
            to_x(n, i).wait_recv()

        @pl.when(n >= 2)
        def _():
            for k in range(1, Z):
                to_z(n - 2, k).wait_send()

        total = summed[n % 2, :, x].astype(F32)
        for i in range(1, X):
            total = total + from_x[n, i - 1].astype(F32)
        column[n % 2] = total.astype(BF)
        for k in range(1, Z):
            to_z(n, k).start()

    for g in range(Z):
        @pl.when(j == min(ends[g] + 4, J + 2))
        def _():
            down_load(g).wait()
            for i in range(1, X):
                down_to_x(g, i).wait_recv()
            total = down_column[g].astype(F32) + total_of([down_from_x[g, i].astype(F32) for i in range(X - 1)])
            down_column[g] = total.astype(BF)
            down_keep(g).start()

    @pl.when((j >= 3) & (j < J + 3))
    def _():
        n = j - 3
        for k in range(1, Z):
            to_z(n, k).wait_recv()
        total = column[n % 2, z].astype(F32)
        for k in range(1, Z):
            total = total + from_z[n, k - 1].astype(F32)
        final[n] = total.astype(BF)
        keep(n).start()
        for d in range(1, 4):
            share(n, d).start()

    @pl.when(j < J)
    def _():
        rows, cot = b[...], c[...]
        gate = nn(rows, inner[0])
        up = nn(rows, inner[1])
        squashed = jax.nn.sigmoid(gate)
        active = gate * squashed
        hidden = (active * up).astype(BF)
        hidden_grad = nt(cot[:, :half], down[0]) + nt(cot[:, half:], down[1])
        gate_grad = (hidden_grad * up * (squashed * (1.0 + gate * (1.0 - squashed)))).astype(BF)
        up_grad = (hidden_grad * active).astype(BF)
        back[...] += nt(gate_grad, inner[0]) + nt(up_grad, inner[1])

        @pl.when(j == J - 1)
        def _():
            staged[...] = back[rows_here:, :].astype(BF)
            exchange.start()

        gate_term = tn(rows, gate_grad).astype(BF)
        up_term = tn(rows, up_grad).astype(BF)

        @pl.when(j >= 2)
        def _():
            to_core(j - 2).wait_send()
            down_to_core(j - 2).wait_send()

        mine[j % 2] = jnp.where(core == 0, gate_term, up_term)
        other[j % 2] = jnp.where(core == 0, up_term, gate_term)
        to_core(j).start()
        down_term = tn(hidden, cot).astype(BF)
        down_here[j % 2] = jnp.where(core == 0, down_term[:, :half], down_term[:, half:])
        down_there[j % 2] = jnp.where(core == 0, down_term[:, half:], down_term[:, :half])
        down_to_core(j).start()
        for n in range(2):
            part = slice(n * half, (n + 1) * half)
            out[:, part] += nn(hidden, down[n])

    @pl.when(j == J - 1)
    def _():
        out_theirs[...] = out[rows_here:, :].astype(BF)
        out_mine[...] = out[:rows_here, :]
        back_mine[...] = back[:rows_here, :]

    @pl.when(j == J + 2)
    def _():
        for n in (J - 2, J - 1):
            to_core(n).wait_send()
            down_to_core(n).wait_send()
            for i in range(1, X):
                to_x(n, i).wait_send()
            for k in range(1, Z):
                to_z(n, k).wait_send()

        def finish(n, carry):
            keep(n).wait()
            for d in range(1, 4):
                share(n, d).wait()
            return carry

        lax.fori_loop(0, J, finish, 0)
        exchange.wait()
        for g in range(Z):
            down_keep(g).wait()
            for i in range(1, X):
                down_to_x(g, i).wait_send()


def feed_forward(b, c, inner, down, fsdp_count):
    rows, width = b.shape
    _, _, hidden = inner.shape
    half = down.shape[2]
    step = 256
    J = hidden // step
    X = fsdp_count // Z
    R, R2 = width // fsdp_count, hidden // fsdp_count
    whole = pl.BlockSpec((rows, width), lambda j: (0, 0), pipeline_mode=pl.Buffered(1))
    part = pl.BlockSpec((rows // 2, width), lambda j: (0, 0), pipeline_mode=pl.Buffered(1))
    inner_spec = pl.BlockSpec((2, width, step), lambda j: (0, 0, jnp.minimum(j, J - 1)))
    down_spec = pl.BlockSpec((2, step, half), lambda j: (0, jnp.minimum(j, J - 1), 0))
    dma, vmem = pltpu.SemaphoreType.DMA, pltpu.VMEM
    return pl.pallas_call(
        functools.partial(feed_forward_kernel, X, J),
        grid=(J + 3,),
        out_shape=(
            jax.ShapeDtypeStruct((rows // 2, width), F32),
            jax.ShapeDtypeStruct((rows // 2, width), F32),
            jax.ShapeDtypeStruct((rows // 2, width), BF),
            jax.ShapeDtypeStruct((rows // 2, width), BF),
            jax.ShapeDtypeStruct((4, R, hidden), BF),
            jax.ShapeDtypeStruct((Z, R2, half), BF),
            jax.ShapeDtypeStruct((hidden, half), BF),
        ),
        in_specs=[whole, whole, inner_spec, down_spec],
        out_specs=(part, part, part, ANY, ANY, ANY, ANY),
        scratch_shapes=[
            vmem((rows, width), F32), vmem((rows, width), F32),
            vmem((2, step, half), BF), vmem((2, step, half), BF), vmem((J, step, half), BF),
            vmem((2, step, half), BF), vmem((Z, R2, half), BF), vmem((Z, X - 1, R2, half), BF),
            vmem((2, width, step), BF), vmem((2, width, step), BF), vmem((J, width, step), BF),
            vmem((2, Z, X, R, step), BF), vmem((J, X - 1, Z, R, step), BF),
            vmem((2, Z, R, step), BF), vmem((J, Z - 1, R, step), BF),
            vmem((J, R, step), BF), vmem((rows // 2, width), BF),
            dma((2,)), dma((J,)), dma((2, X - 1)), dma((J, X - 1)), dma((2, Z - 1)), dma((J, Z - 1)),
            dma((J, 3)), dma((J, 3)), dma, dma, dma((2,)), dma((J,)), dma((J,)),
            dma((2,)), dma((Z,)), dma((Z, X - 1)), dma((Z, X - 1)), dma((Z,)),
        ],
        compiler_params=pltpu.CompilerParams(
            vmem_limit_bytes=VMEM_BYTES, collective_id=1, has_side_effects=True
        ),
        cost_estimate=pl.CostEstimate(flops=18 * rows * width * hidden, bytes_accessed=60 * 2**20, transcendentals=0),
        name="feed_forward",
    )(b, c, inner, down)


def total_of(values):
    return functools.reduce(jnp.add, values)


def attention_back_kernel(
    X, groups, head_size, carried, q, k, v, edge, mix, dhb, mixed, inputs, proj, gains, second_gain, frames_in, down_in, out_send,
    frames_grad, gains_sum, attn_all, down_all, out_recv,
    da, gain_terms, gain_from, mixed_grad, before, terms_before, terms_here, tails, grads, edge_send, edge_recv,
    mine, other, from_core, keep_y, send_y, from_y, summed, from_x, column, from_z, final, plane, from_plane, final_plane,
    down_mine, down_from_z, down_final,
    s_edge, r_edge, s1, r1, sy, ry, sxa, rxa, sxb, rxb, sz, rz, sf, rf, sp, rp, sc, rc, local_sem,
    s_out, r_out, sg, rg, frame_sem, sdz, rdz, sdf, rdf, down_sem, free,
):
    i = pl.program_id(0)
    frames, step = q.shape[2:]
    R, thin = final.shape[1:]
    subs = 2 * groups
    slots = from_core.shape[0]
    dp, fs = lax.axis_index("dp"), lax.axis_index("fsdp")
    F = Z * X
    y, core = dp // 2, dp % 2
    z, x = fs // X, fs % X
    me = dp * F + fs
    devices = 4 * F
    core_peer = (y * 2 + 1 - core, fs)
    y_peer = ((1 - y) * 2 + core, fs)
    before_me = ((me - 1 + devices) % devices // F, (me - 1 + devices) % devices % F)
    after_me = ((me + 1) % devices // F, (me + 1) % devices % F)

    def z_peer(n):
        return (dp, lax.rem(z + n, Z) * X + x)

    def x_peer(n):
        return (dp, z * X + lax.rem(x + n, X))

    def dp_peer(d):
        return (((y + d // 2) % 2) * 2 + (core + d % 2) % 2, fs)

    def to_before(n):
        return remote_copy(edge_send.at[n % 2], edge_recv.at[n], s_edge.at[n % 2], r_edge.at[n], before_me)

    def to_core(n):
        return remote_copy(other.at[n % 2], from_core.at[n % slots], s1.at[n % 2], r1.at[n % slots], core_peer)

    def to_y(n):
        return remote_copy(send_y.at[n % 2], from_y.at[n], sy.at[n % 2], ry.at[n], y_peer)

    def to_x_early(n, j):
        return remote_copy(
            summed.at[n % 3, pl.ds(1, 2), :, lax.rem(x + j, X)], from_x.at[n, j - 1, pl.ds(1, 2)],
            sxa.at[n % 3, j - 1], rxa.at[n, j - 1], x_peer(j),
        )

    def to_x_late(n, j):
        return remote_copy(
            summed.at[n % 3, 0, :, lax.rem(x + j, X)], from_x.at[n, j - 1, 0],
            sxb.at[n % 3, j - 1], rxb.at[n, j - 1], x_peer(j),
        )

    def to_z(n, j):
        return remote_copy(
            column.at[n % 2, :, lax.rem(z + j, Z)], from_z.at[n, j - 1], sz.at[n % 2, j - 1], rz.at[n, j - 1], z_peer(j)
        )

    def place(n, t):
        return attn_all.at[t, core, :, pl.ds(pl.multiple_of(n * thin, thin), thin)]

    def share(n, d):
        return remote_copy(final.at[n], place(n, y), sf.at[n, d - 1], rf.at[n, d - 1], dp_peer(d))

    def relay(n):
        return remote_copy(place(n, 1 - y), place(n, 1 - y), sf.at[n, 2], rf.at[n, 2], core_peer)

    def down_to_z(k):
        return remote_copy(
            down_in.at[lax.rem(z + k, Z)], down_from_z.at[k - 1], sdz.at[k - 1], rdz.at[k - 1], z_peer(k)
        )

    def down_share(d):
        return remote_copy(down_final, down_all.at[dp], sdf.at[d - 1], rdf.at[d - 1], dp_peer(d))

    def down_relay():
        part = down_all.at[(1 - y) * 2 + core]
        return remote_copy(part, part, sdf.at[2], rdf.at[2], core_peer)

    def to_plane(n):
        return remote_copy(plane.at[n], from_plane.at[n], sp.at[n], rp.at[n], y_peer)

    def share_core(n, t):
        return remote_copy(final_plane.at[n, t], place(n, 2 + t), sc.at[n, t], rc.at[n, t], core_peer)

    def keep(n, t):
        src = final.at[n] if t == 0 else final_plane.at[n, t - 1]
        return pltpu.make_async_copy(src, place(n, y if t == 0 else 1 + t), local_sem.at[n, t])

    def load_frames(g):
        dst = grads.at[g] if g < 3 else mixed_grad
        return pltpu.make_async_copy(frames_in.at[:, :, pl.ds(g * step, step)], dst, frame_sem.at[g])

    def gain_copy(level, n):
        peer = (core_peer, y_peer, x_peer(n + 1), z_peer(n + 1))[level]
        return remote_copy(gain_terms.at[level], gain_from.at[level, n], sg.at[level, n], rg.at[level, n], peer)

    down_load = pltpu.make_async_copy(down_in.at[z], down_mine, down_sem.at[0])
    down_keep = pltpu.make_async_copy(down_final, down_all.at[dp], down_sem.at[1])
    out_copy = remote_copy(out_send, out_recv, s_out, r_out, y_peer)

    @pl.when(i == 0)
    def _():
        barrier = pltpu.get_barrier_semaphore()
        peers = [z_peer(n) for n in range(1, Z)] + [x_peer(n) for n in range(1, X)]
        peers += [dp_peer(d) for d in range(1, 4)] + [before_me, after_me]
        for peer in peers:
            pl.semaphore_signal(barrier, inc=1, device_id=peer, device_id_type=MESH)
        pl.semaphore_wait(barrier, len(peers))
        out_copy.start()
        for k in range(1, Z):
            down_to_z(k).start()
        down_load.start()
        da[...] = jnp.zeros_like(da)

        @pl.when(me == devices - 1)
        def _():
            edge_recv[...] = jnp.zeros_like(edge_recv)

    def active(first):
        return (i >= first) & (i < first + subs)

    @pl.when(active(2))
    def _():
        n = i - 2
        to_core(n).wait_recv()

        @pl.when(n >= 2)
        def _():
            to_y(n - 2).wait_send()

        @pl.when(n >= 3)
        def _():
            for j in range(1, X):
                to_x_early(n - 3, j).wait_send()

        def both(t):
            return (mine[n % 2, t].astype(F32) + from_core[n % slots, t].astype(F32)).astype(BF)

        send_y[n % 2] = both(1 - y)
        to_y(n).start()
        for t in range(2):
            summed[n % 3, 1 + t] = both(2 + t).reshape(summed.shape[2:])
        for j in range(1, X):
            to_x_early(n, j).start()
        keep_y[n % 2] = both(y)

        @pl.when(n < subs - slots)
        def _():
            pl.semaphore_signal(free, inc=1, device_id=core_peer, device_id_type=MESH)

    @pl.when(active(3))
    def _():
        n = i - 3
        to_y(n).wait_recv()

        @pl.when(n >= 3)
        def _():
            for j in range(1, X):
                to_x_late(n - 3, j).wait_send()

        total = (keep_y[n % 2].astype(F32) + from_y[n].astype(F32)).astype(BF)
        summed[n % 3, 0] = total.reshape(summed.shape[2:])
        for j in range(1, X):
            to_x_late(n, j).start()

    @pl.when(active(4))
    def _():
        n = i - 4
        for j in range(1, X):
            to_x_early(n, j).wait_recv()
            to_x_late(n, j).wait_recv()

        @pl.when(n >= 2)
        def _():
            for j in range(1, Z):
                to_z(n - 2, j).wait_send()

        total = summed[n % 3, :, :, x].astype(F32) + total_of([from_x[n, j].astype(F32) for j in range(X - 1)])
        column[n % 2] = total.astype(BF)
        for j in range(1, Z):
            to_z(n, j).start()

    @pl.when(active(5))
    def _():
        n = i - 5
        for j in range(1, Z):
            to_z(n, j).wait_recv()
        total = column[n % 2, :, z].astype(F32) + total_of([from_z[n, j].astype(F32) for j in range(Z - 1)])
        total = total.astype(BF)
        final[n] = total[0]
        plane[n] = total[1:]
        to_plane(n).start()
        keep(n, 0).start()
        for d in range(1, 3):
            share(n, d).start()

    @pl.when(active(6))
    def _():
        n = i - 6
        to_plane(n).wait_recv()
        share(n, 2).wait_recv()
        relay(n).start()
        final_plane[n] = (plane[n].astype(F32) + from_plane[n].astype(F32)).astype(BF)
        for t in range(2):
            keep(n, t + 1).start()
            share_core(n, t).start()

    @pl.when(i == 4)
    def _():
        down_load.wait()
        for k in range(1, Z):
            down_to_z(k).wait_recv()
        total = down_mine[...].astype(F32) + total_of([down_from_z[k].astype(F32) for k in range(Z - 1)])
        down_final[...] = total.astype(BF)
        down_keep.start()
        for d in range(1, 3):
            down_share(d).start()

    @pl.when(i == 6)
    def _():
        down_share(2).wait_recv()
        down_relay().start()

    @pl.when((i < subs) & (i % 2 == 0))
    def _():
        m = i // 2
        slot = m % 2
        ones = head_ones(step, head_size)
        scale = 1.0 / math.sqrt(head_size)
        first = lax.broadcasted_iota(jnp.int32, (frames, step), 0) == 0
        last = lax.broadcasted_iota(jnp.int32, (frames, step), 0) == frames - 1
        for p in range(2):
            mixed_grad[p] = total_of(
                [nt(dhb[p, :, g * step : (g + 1) * step], mix[g, 0, p]) for g in range(groups)]
            ).astype(BF)
            before[p] = jnp.where(first, edge[0, p : p + 1, :], pltpu.roll(k[0, p].astype(F32), 1, 0))
            before[2 + p] = jnp.where(first, edge[0, 2 + p : 3 + p, :], pltpu.roll(v[0, p].astype(F32), 1, 0))

        def chunk(c, carry):
            rows = pl.ds(pl.multiple_of(c * CHUNK, CHUNK), CHUNK)
            allowed = jnp.broadcast_to(carried[rows, :], (CHUNK, step)) > 0.5
            queries = [q[0, p, rows, :].astype(F32) for p in range(2)]
            cots = [mixed_grad[p, rows, :].astype(F32) for p in range(2)]
            keys = [before[p, rows, :] for p in range(2)] + [k[0, p, rows, :].astype(F32) for p in range(2)]
            values = [before[2 + p, rows, :] for p in range(2)] + [v[0, p, rows, :].astype(F32) for p in range(2)]

            scores = per_head(queries, keys, ones)
            dprobs = per_head(cots, values, ones)
            key_grads, value_grads = [[] for _ in range(4)], [[] for _ in range(4)]
            for p, span in SPANS:
                probs = head_probs(scores, span, allowed, scale)
                mean = total_of([pr * dprobs[m] for m, pr in zip(span, probs)])
                query_grad = []
                for m, pr in zip(span, probs):
                    n = PAIRS[m][1]
                    ds = (pr * (dprobs[m] - mean)).astype(BF).astype(F32) * scale
                    query_grad.append(ds * keys[n])
                    key_grads[n].append(ds * queries[p])
                    value_grads[n].append(pr.astype(BF).astype(F32) * cots[p])
                grads[0, p, rows, :] = total_of(query_grad).astype(BF)
            for p in range(2):
                terms_before[p, rows, :] = total_of(key_grads[p])
                terms_before[2 + p, rows, :] = total_of(value_grads[p])
                terms_here[p, rows, :] = total_of(key_grads[2 + p])
                terms_here[2 + p, rows, :] = total_of(value_grads[2 + p])
            return carry

        lax.fori_loop(0, frames // CHUNK, chunk, 0)

        @pl.when((m >= 2) & (me > 0))
        def _():
            to_before(m - 2).wait_send()

        for row in range(4):
            edge_send[slot, row : row + 1, :] = terms_before[row, 0:1, :]

        @pl.when(me > 0)
        def _():
            to_before(m).start()

        for row in range(4):
            total = terms_here[row] + jnp.where(last, 0.0, pltpu.roll(terms_before[row], frames - 1, 0))
            grads[1 + row // 2, row % 2] = total.astype(BF)
            tails[row] = total[frames - 16 :, :]

    @pl.when((i < subs) & (i % 2 == 1))
    def _():
        m = i // 2

        @pl.when(me < devices - 1)
        def _():
            to_before(m).wait_recv()

        bottom = lax.broadcasted_iota(jnp.int32, (16, step), 0) == 15
        for row in range(4):
            fixed = tails[row] + jnp.where(bottom, edge_recv[m, row : row + 1, :], 0.0)
            grads[1 + row // 2, row % 2, frames - 16 :, :] = fixed.astype(BF)

        @pl.when(m >= 1)
        def _():
            for h in range(2):
                to_core(2 * m - 2 + h).wait_send()

        for t in range(4):
            pair = []
            for p in range(2):
                if t < 3:
                    pair.append(tn(inputs[p], grads[t, p]).astype(BF))
                else:
                    pair.append(tn(mixed[p], dhb[p, :, pl.ds(pl.multiple_of(m * step, step), step)]).astype(BF))
            here = jnp.where(core == 0, pair[0], pair[1])
            there = jnp.where(core == 0, pair[1], pair[0])
            for h in range(2):
                mine[h, t] = here[:, h * thin : (h + 1) * thin]
                other[h, t] = there[:, h * thin : (h + 1) * thin]

        @pl.when(m >= slots // 2)
        def _():
            pl.semaphore_wait(free, 2)

        for h in range(2):
            to_core(2 * m + h).start()
        for p in range(2):
            da[p] += total_of([nt(grads[t, p], proj[0, t, p]) for t in range(3)])

        @pl.when(m == groups - 1)
        def _():
            for g in range(groups):
                load_frames(g).start()

    @pl.when(i == subs)
    def _():
        for g in range(groups):
            load_frames(g).wait()

        def chunk(c, term):
            rows = pl.ds(pl.multiple_of(c * CHUNK, CHUNK), CHUNK)
            for p in range(2):
                pieces = [grads[g, p, rows, :] if g < 3 else mixed_grad[p, rows, :] for g in range(groups)]
                value = jnp.concatenate(pieces, axis=1).astype(F32)
                inverse = scale_rows(value)
                normed = value * inverse
                grad = da[p, rows, :]
                term = term + jnp.sum(grad * normed, axis=0, keepdims=True)
                total = dhb[p, rows, :].astype(F32) + norm_back(grad, normed, gains[0:1, :], inverse)
                frames_grad[p, rows, :] = total.astype(BF)
            return term

        term = lax.fori_loop(0, frames // CHUNK, chunk, jnp.zeros((1, da.shape[2]), F32))
        gain_terms[0] = second_gain[...]
        gain_terms[0, 0:1, :] = term
        gain_copy(0, 0).start()

    for level in range(1, 4):
        @pl.when(i == subs + level)
        def _():
            count = X - 1 if level == 3 else 1
            total = gain_terms[level - 1]
            for n in range(count):
                gain_copy(level - 1, n).wait()
                total = total + gain_from[level - 1, n]
            gain_terms[level] = total
            for n in range(Z - 1 if level == 3 else X - 1 if level == 2 else 1):
                gain_copy(level, n).start()

    @pl.when(i == subs + 4)
    def _():
        total = gain_terms[3]
        for n in range(Z - 1):
            gain_copy(3, n).wait()
            total = total + gain_from[3, n]
        gains_sum[...] = total

    @pl.when(i == subs + 5)
    def _():
        @pl.when(me > 0)
        def _():
            for n in (groups - 2, groups - 1):
                to_before(n).wait_send()

        for n in (subs - 3, subs - 2, subs - 1):
            for j in range(1, X):
                to_x_early(n, j).wait_send()
                to_x_late(n, j).wait_send()

        for n in (subs - 2, subs - 1):
            to_core(n).wait_send()
            to_y(n).wait_send()
            for j in range(1, Z):
                to_z(n, j).wait_send()

        def finish(n, carry):
            to_plane(n).wait_send()
            keep(n, 0).wait()
            share(n, 1).wait()
            share(n, 2).wait_send()
            relay(n).wait()
            for t in range(2):
                keep(n, t + 1).wait()
                share_core(n, t).wait()
            return carry

        lax.fori_loop(0, subs, finish, 0)
        out_copy.wait()
        for k in range(1, Z):
            down_to_z(k).wait_send()
        down_keep.wait()
        down_share(1).wait()
        down_share(2).wait_send()
        down_relay().wait()


def attention_back(
    carried, qkv_rows, edge, attn, dhb, mixed, inputs, gains, second_gain, frames_in, down_in, out_send, head_size, fsdp_count
):
    _, frames, width = dhb.shape
    step = STEP
    groups = width // step
    X = fsdp_count // Z
    R = width // fsdp_count

    def early(i):
        return jnp.minimum(i // 2, groups - 1)

    rows = [pl.BlockSpec((1, 2, frames, step), lambda i, t=t: (t, 0, 0, early(i))) for t in range(3)]
    edge_spec = pl.BlockSpec((1, 8, step), lambda i: (early(i), 0, 0))
    mask = pl.BlockSpec((frames, 1), lambda i: (0, 0), pipeline_mode=pl.Buffered(1))
    whole = pl.BlockSpec((2, frames, width), lambda i: (0, 0, 0), pipeline_mode=pl.Buffered(1))
    mix_spec = pl.BlockSpec((groups, 1, 2, step, step), lambda i: (0, 3, 0, early(i), 0))
    proj_spec = pl.BlockSpec((1, 3, 2, width, step), lambda i: (jnp.clip((i - 1) // 2, 0, groups - 1), 0, 0, 0, 0))
    line = pl.BlockSpec((8, width), lambda i: (0, 0), pipeline_mode=pl.Buffered(1))
    dma, vmem = pltpu.SemaphoreType.DMA, pltpu.VMEM
    thin = step // 2
    n, slots, peers = 2 * groups, 4, max(X, Z) - 1
    return pl.pallas_call(
        functools.partial(attention_back_kernel, X, groups, head_size),
        grid=(n + 6,),
        out_shape=(
            jax.ShapeDtypeStruct((2, frames, width), BF),
            jax.ShapeDtypeStruct((8, width), F32),
            jax.ShapeDtypeStruct((4, 2, R, width), BF),
            jax.ShapeDtypeStruct((4,) + down_in.shape[1:], BF),
            jax.ShapeDtypeStruct(out_send.shape, BF),
        ),
        in_specs=[mask, *rows, edge_spec, mix_spec, whole, whole, whole, proj_spec, line, line, ANY, ANY, ANY],
        out_specs=(whole, line, ANY, ANY, ANY),
        scratch_shapes=[
            vmem((2, frames, width), F32), vmem((4, 8, width), F32), vmem((4, peers, 8, width), F32),
            vmem((2, frames, step), BF), vmem((4, frames, step), F32), vmem((4, frames, step), F32),
            vmem((4, frames, step), F32), vmem((4, 16, step), F32), vmem((3, 2, frames, step), BF),
            vmem((2, 8, step), F32), vmem((groups, 8, step), F32),
            vmem((2, 4, width, thin), BF), vmem((2, 4, width, thin), BF), vmem((slots, 4, width, thin), BF),
            vmem((2, width, thin), BF), vmem((2, width, thin), BF), vmem((n, width, thin), BF),
            vmem((3, 3, Z, X, R, thin), BF), vmem((n, X - 1, 3, Z, R, thin), BF),
            vmem((2, 3, Z, R, thin), BF), vmem((n, Z - 1, 3, R, thin), BF),
            vmem((n, R, thin), BF), vmem((n, 2, R, thin), BF), vmem((n, 2, R, thin), BF), vmem((n, 2, R, thin), BF),
            vmem(down_in.shape[1:], BF), vmem((Z - 1,) + down_in.shape[1:], BF), vmem(down_in.shape[1:], BF),
            dma((2,)), dma((groups,)), dma((2,)), dma((slots,)), dma((2,)), dma((n,)),
            dma((3, X - 1)), dma((n, X - 1)), dma((3, X - 1)), dma((n, X - 1)),
            dma((2, Z - 1)), dma((n, Z - 1)), dma((n, 3)), dma((n, 3)), dma((n,)), dma((n,)),
            dma((n, 2)), dma((n, 2)), dma((n, 3)),
            dma, dma, dma((4, peers)), dma((4, peers)), dma((groups,)),
            dma((Z - 1,)), dma((Z - 1,)), dma((3,)), dma((3,)), dma((2,)), pltpu.SemaphoreType.REGULAR,
        ],
        compiler_params=pltpu.CompilerParams(vmem_limit_bytes=63 * 2**20, collective_id=2, has_side_effects=True),
        name="attention_back",
    )(
        carried, qkv_rows, qkv_rows, qkv_rows, edge, attn, dhb, mixed, inputs, attn,
        gains, second_gain, frames_in, down_in, out_send,
    )


def update_kernel(step_size, share, weight, moment, average, grad_out, moment_out, average_out, weight_out):
    gradient = share[...].reshape(weight.shape).astype(F32)
    moment_new, average_new, weight_new = owner_update(
        weight[...], gradient, moment[...], average[...], step_size
    )
    grad_out[...] = gradient
    moment_out[...] = moment_new
    average_out[...] = average_new
    weight_out[...] = weight_new


def update(shares, share_block, share_at, grid, block, at, weight, moment, average, step_size, name):
    share_spec = pl.BlockSpec(share_block, share_at)
    spec = pl.BlockSpec(block, at)
    return pl.pallas_call(
        functools.partial(update_kernel, step_size),
        grid=grid,
        out_shape=(jax.ShapeDtypeStruct(weight.shape, F32),) * 4,
        in_specs=[share_spec, spec, spec, spec],
        out_specs=(spec,) * 4,
        compiler_params=pltpu.CompilerParams(vmem_limit_bytes=VMEM_BYTES),
        name=name,
    )(shares, weight, moment, average)


def per_device(
    frames, cotangent, segment_ids,
    qkv_weight, mix_weight, inner_weight, down_weight, norm_gains,
    qkv_moment, mix_moment, inner_moment, down_moment, gains_moment,
    qkv_average, mix_average, inner_average, down_average, gains_average,
):
    frame_count, positions, width = frames.shape
    head_size = width // HEADS
    hidden = inner_weight.shape[2] // 2
    dp_count, fsdp_count = lax.axis_size("dp"), lax.axis_size("fsdp")
    X = fsdp_count // Z
    devices = dp_count * fsdp_count
    total_frames = frame_count * devices
    dp, fs = lax.axis_index("dp"), lax.axis_index("fsdp")
    y, core = dp // 2, dp % 2
    z, x = fs // X, fs % X
    axes = ("dp", "fsdp")

    device = dp * fsdp_count + fs
    padded_ids = jnp.concatenate([jnp.full((1,), -1, jnp.int32), segment_ids])
    window = lax.dynamic_slice_in_dim(padded_ids, device * frame_count, frame_count + 1)
    carried = (window[1:] == window[:-1]).astype(F32)[:, None]

    half_width = width // 2
    own_gains = norm_gains.astype(BF).astype(F32)
    gains_own = lax.dynamic_update_slice(jnp.zeros((8, width), F32), own_gains, (0, fs * own_gains.shape[1]))
    frames_by = frames.transpose(1, 0, 2)
    cot = cotangent.transpose(1, 0, 2)
    attn, inner, down, gains, a, qkv_rows, mixed, edge, hres, b_rows, c_rows = forward(
        frames_by, carried, cot, gains_own, qkv_weight, mix_weight, inner_weight, down_weight, head_size, fsdp_count
    )
    r2 = scale_rows(hres)
    n2 = hres * r2
    b_rows = b_rows.reshape(2 * frame_count, width)
    c_rows = c_rows.reshape(2 * frame_count, width)
    out, back, out_there, back_there, inner_shares, down_columns, _ = feed_forward(b_rows, c_rows, inner, down, fsdp_count)

    def by_position(mine, theirs):
        return jnp.where(y == 0, jnp.stack([mine, theirs]), jnp.stack([theirs, mine]))

    db = by_position(back, back_there.astype(F32))

    e2 = jnp.sum(db * n2, axis=(0, 1))
    dh = cot.astype(F32) + norm_back(db, n2, gains[1], r2)
    dhb = dh.astype(BF)
    second_gain = jnp.zeros((8, width), F32).at[1].set(e2)
    frames_grad, gains_sum, attn_shares, down_shares, out_here = attention_back(
        carried, qkv_rows, edge, attn, dhb, mixed, a, gains, second_gain, frames_by, down_columns, out_there, head_size, fsdp_count
    )
    frames_grad = frames_grad.transpose(1, 0, 2)
    layer_out = (hres + by_position(out, out_here.astype(F32))).astype(BF).transpose(1, 0, 2)

    step_size = step_rate / math.sqrt(total_frames)
    R, R2 = qkv_weight.shape[1], down_weight.shape[1]
    cut = min(R, 64)
    qkv_new = update(
        attn_shares, (1, 1, R, width), lambda p, t: (t, p, 0, 0), (2, 3), (1, R, width), lambda p, t: (p, 0, t),
        qkv_weight, qkv_moment, qkv_average, step_size, "update_qkv",
    )
    mix_new = update(
        attn_shares, (1, 1, R, width), lambda p: (3, p, 0, 0), (2,), (1, R, width), lambda p: (p, 0, 0),
        mix_weight, mix_moment, mix_average, step_size, "update_mix",
    )
    inner_new = update(
        inner_shares, (1, cut, hidden), lambda p, c, r: (2 * p + c, r, 0), (2, 2, R // cut),
        (1, cut, hidden), lambda p, c, r: (p, r, c), inner_weight, inner_moment, inner_average, step_size, "update_inner",
    )
    down_new = update(
        down_shares, (1, R2, half_width), lambda p, c: (2 * p + c, 0, 0), (2, 2),
        (1, R2, half_width), lambda p, c: (p, 0, c), down_weight, down_moment, down_average, step_size, "update_down",
    )
    own = norm_gains.shape[1]
    gains_grad = lax.dynamic_slice(gains_sum, (0, fs * own), (2, own))
    gains_new = (gains_grad,) + owner_update(norm_gains, gains_grad, gains_moment, gains_average, step_size)
    new = (qkv_new, mix_new, inner_new, down_new, gains_new)
    return (layer_out, frames_grad) + tuple(n[kind] for kind in range(4) for n in new)


def solution(mesh):
    rows = P(("dp", "fsdp"), None, None)
    weight = P(None, "fsdp", None)
    gains = P(None, "fsdp")
    weights = (weight,) * 4 + (gains,)
    return jax.shard_map(
        per_device,
        mesh=mesh,
        in_specs=(rows, rows, P()) + weights * 3,
        out_specs=(rows, rows) + weights * 4,
        check_vma=False,
    )
```

```python
import functools
import math

import jax
import jax.numpy as jnp
from jax import lax
from jax.experimental import pallas as pl
from jax.experimental.pallas import tpu as pltpu
from jax.sharding import PartitionSpec as P

HEADS = 16
Z = 4
MESH = pl.DeviceIdType.MESH
ANY = pl.BlockSpec(memory_space=pl.ANY)
BF = jnp.bfloat16
F32 = jnp.float32

norm_eps = 1e-05
momentum_rate = 0.5
average_rate = 0.5
step_rate = 0.05
VMEM_BYTES = 60 * 1024 * 1024


def nn(a, b):
    return lax.dot_general(a, b, (((1,), (0,)), ((), ())), preferred_element_type=F32)


def nt(a, b):
    return lax.dot_general(a, b, (((1,), (1,)), ((), ())), preferred_element_type=F32)


def tn(a, b):
    return lax.dot_general(a, b, (((0,), (0,)), ((), ())), preferred_element_type=F32)


def scale_rows(values):
    square = jnp.mean(values * values, axis=-1, keepdims=True) + norm_eps
    inverse = lax.rsqrt(square)
    return inverse * (1.5 - 0.5 * square * inverse * inverse)


def norm_back(grad_in, normed, gain_row, inverse):
    scaled = grad_in * gain_row
    return inverse * (scaled - normed * jnp.mean(scaled * normed, axis=-1, keepdims=True))


def owner_update(weight, gradient, moment, average, step_size):
    moment_new = momentum_rate * moment + gradient
    weight_new = weight - step_size * (gradient + momentum_rate * moment_new)
    average_new = average_rate * average + (1.0 - average_rate) * weight_new
    return (moment_new, average_new, weight_new)


PAIRS = ((0, 0), (0, 1), (0, 2), (1, 0), (1, 1), (1, 2), (1, 3))
SPANS = ((0, range(0, 3)), (1, range(3, 7)))
CHUNK = 128
STEP = 256


def total_of(values):
    return functools.reduce(jnp.add, values)


def remote_copy(src, dst, send_sem, recv_sem, peer):
    return pltpu.make_async_remote_copy(
        src_ref=src, dst_ref=dst, send_sem=send_sem, recv_sem=recv_sem, device_id=peer, device_id_type=MESH
    )


def head_ones(lanes, head_size):
    row = lax.broadcasted_iota(jnp.int32, (lanes, lanes), 0) // head_size
    column = lax.broadcasted_iota(jnp.int32, (lanes, lanes), 1) // head_size
    return (row == column).astype(BF)


def per_head(left, right, ones):
    rows = left[0].shape[0]
    products = [(left[p] * right[n]).astype(BF) for p, n in PAIRS]
    sums = nn(jnp.concatenate(products, axis=0), ones)
    return [sums[m * rows : (m + 1) * rows] for m in range(len(PAIRS))]


def head_probs(scores, span, allowed, scale):
    s = [jnp.where(allowed, scores[m] * scale, -1e30) if PAIRS[m][1] < 2 else scores[m] * scale for m in span]
    top = functools.reduce(jnp.maximum, s)
    e = [jnp.exp(value - top) for value in s]
    e = [jnp.where(allowed, value, 0.0) if PAIRS[m][1] < 2 else value for m, value in zip(span, e)]
    inverse = 1.0 / total_of(e)
    return [value * inverse for value in e]


def forward_kernel(
    X, groups, head_size, frames, carried, cot, gains_own, qkv_weight, mix_weight, inner_weight, down_weight,
    attn, inner, down, gains_out, inputs_out, rows_out, mixed_out, edge_out, hres_out, b_rows, c_rows,
    attn_wide, inner_wide, down_wide, attn_own, inner_own, down_own,
    gains, inputs, rows_in, mixed, before, hres, b, proj, mix, edge_send, edge_recv,
    send_up, recv_up, send_down, recv_down, send_x, recv_x, send_y, recv_y, send_c, recv_c, send_r, recv_r,
    send_g, recv_g, send_e, recv_e, send_b, recv_b, send_q, recv_q, local_sem, out_sem, wide_sem,
):
    dp, fs = lax.axis_index("dp"), lax.axis_index("fsdp")
    F = Z * X
    y, core = dp // 2, dp % 2
    z, x = fs // X, fs % X
    me = dp * F + fs
    devices = 4 * F
    count = frames.shape[1]
    core_peer = (y * 2 + 1 - core, fs)
    y_peer = ((1 - y) * 2 + core, fs)
    up_peer = (dp, lax.rem(z + 1, Z) * X + x)
    down_peer = (dp, lax.rem(z + Z - 1, Z) * X + x)
    before_me = ((me - 1 + devices) % devices // F, (me - 1 + devices) % devices % F)
    after_me = ((me + 1) % devices // F, (me + 1) % devices % F)

    def z_peer(k):
        return (dp, lax.rem(z + k, Z) * X + x)

    def x_peer(i):
        return (dp, z * X + lax.rem(x + i, X))

    UNITS = unit_list(groups, inner_own.shape[1], down_own.shape[1])

    width = frames.shape[2]

    def wide(slot):
        return (attn_wide.at[slot] if slot < groups + 1 else (inner_wide, down_wide)[slot - groups - 1])

    def fetch(slot, src, condition=None):
        copy = pltpu.make_async_copy(src, wide(slot), wide_sem.at[slot])
        if condition is None:
            copy.start()
        else:
            pl.when(condition)(copy.start)

    def columns_of(weight, part, block):
        return weight.at[:, :, pl.ds(pl.multiple_of(part * width + block * STEP, STEP), STEP)]

    def fetch_all():
        for n in range(groups - 1):
            fetch(n, columns_of(qkv_weight, jnp.minimum(dp, 2), n), dp < 3)
            fetch(n, columns_of(mix_weight, 0, n), dp == 3)
        fetch(groups - 1, columns_of(qkv_weight, core, groups - 1))
        fetch(groups, columns_of(qkv_weight, 2, groups - 1), core == 0)
        fetch(groups, columns_of(mix_weight, 0, groups - 1), core == 1)
        half, hidden = width // 2, inner_own.shape[1]
        fetch(groups + 1, inner_weight.at[y, :, pl.ds(pl.multiple_of(core * hidden, 128), hidden)])
        fetch(groups + 2, down_weight.at[y, :, pl.ds(pl.multiple_of(core * half, 128), half)])

    def take(slot):
        pltpu.make_async_copy(wide(slot), wide(slot), wide_sem.at[slot]).wait()
        if slot < groups + 1:
            attn_own[slot] = attn_wide[slot].astype(BF)
        elif slot == groups + 1:
            inner_own[...] = inner_wide[...].astype(BF)
        else:
            down_own[...] = down_wide[...].astype(BF)

    def own(u):
        kind, n, columns = UNITS[u][:3]
        if kind in ("quarter", "low", "high"):
            return attn_own.at[n if kind != "high" else n + 1]
        return (down_own if kind == "down" else inner_own).at[:, columns]

    def part_of(u, core_index, plane):
        kind = UNITS[u][0]
        if kind == "quarter":
            return plane * 2 + core_index
        return 2 + core_index if kind == "high" else core_index

    def whole(u, part):
        kind, n, columns = UNITS[u][:3]
        if kind == "down":
            return down.at[part, :, columns]
        if kind == "inner":
            return inner.at[part, :, columns]
        return attn.at[n, part]

    def place(u, source, part=None):
        kind, n, columns = UNITS[u][:3]
        part = part_of(u, core, y) if part is None else part
        if kind == "down":
            R = down_own.shape[0]
            return down.at[part, pl.ds(source * R, R), columns]
        if kind == "inner":
            R = inner_own.shape[0]
            return inner.at[part, pl.ds(source * R, R), columns]
        R = attn_own.shape[2]
        return attn.at[n, part, :, pl.ds(source * R, R), :]

    fetch_all()
    barrier = pltpu.get_barrier_semaphore()
    peers = [z_peer(k) for k in range(1, Z)] + [x_peer(i) for i in range(1, X)]
    peers += [core_peer, y_peer, before_me, after_me]
    for peer in peers:
        pl.semaphore_signal(barrier, inc=1, device_id=peer, device_id_type=MESH)
    pl.semaphore_wait(barrier, len(peers))

    sent, local = [], []

    def send(condition, make):
        remote_copy(*make()).start()
        sent.append((condition, make))

    def wait_send(condition, make):
        def action():
            remote_copy(*make()).wait_send()

        if condition is None:
            action()
        else:
            pl.when(condition())(action)

    def wait_recv(dst, recv_sem, send_sem):
        remote_copy(dst, dst, send_sem, recv_sem, core_peer).wait_recv()

    def store(src, dst):
        copy = pltpu.make_async_copy(src, dst, out_sem.at[len(local)])
        copy.start()
        local.append(copy)

    def spread(u, row, mine, condition):
        def src():
            return own(u) if mine else place(u, row() * X + x)

        for i in range(1, X):
            send(
                condition,
                lambda i=i: (
                    src(), place(u, row() * X + x), send_x.at[u, row(), i], recv_x.at[u, row(), i], x_peer(i)
                ),
            )
        to_plane(u, lambda: row() * X + x, src, condition)

    def to_plane(u, source, src, condition):
        if UNITS[u][0] == "quarter":
            send(
                condition,
                lambda: (src(), place(u, source()), send_y.at[u, source()], recv_y.at[u, source()], y_peer),
            )

    def crossed(u):
        return UNITS[u][3]

    def block(u, row):
        kind, n, columns = UNITS[u][:3]
        array, R = (down, down_own.shape[0]) if kind == "down" else (inner, inner_own.shape[0])
        return array.at[core, pl.ds(row * X * R, X * R), columns]

    def send_along(u, src, dst):
        def below_top():
            return z < Z - 1

        def above_bottom():
            return z > 0

        def upward():
            return (src(), dst(), send_up.at[u, 1], recv_up.at[u, 1], up_peer)

        def downward():
            return (src(), dst(), send_down.at[u, 1], recv_down.at[u, 1], down_peer)

        pl.when(below_top())(lambda: send(below_top, upward))
        pl.when(above_bottom())(lambda: send(above_bottom, downward))

    def start_unit(u):
        for slot in slots_of[u]:
            take(slot)
        if not crossed(u):
            send_along(u, lambda: own(u), lambda: place(u, fs))
        spread(u, lambda: z, True, None)
        store(own(u), place(u, fs))

    def turn(u):
        for i in range(1, X):
            column = lax.rem(x - i + X, X)
            wait_recv(place(u, z * X + column), recv_x.at[u, z, i], send_x.at[u, z, i])
        local[own_store[u]].wait()
        send_along(u, lambda: block(u, z), lambda: block(u, z))

    def hop(u, k):
        def side(reached, row, further, send_sem, recv_sem, peer):
            def here():
                return block(u, row()) if crossed(u) else place(u, row() * X + x)

            def both():
                return reached() & further()

            def action():
                wait_recv(here(), recv_sem.at[u, k], send_sem.at[u, k])
                if k < Z - 1:
                    pl.when(further())(
                        lambda: send(
                            both, lambda: (here(), here(), send_sem.at[u, k + 1], recv_sem.at[u, k + 1], peer)
                        )
                    )
                if not crossed(u):
                    spread(u, row, False, reached)

            pl.when(reached())(action)

        side(lambda: z >= k, lambda: z - k, lambda: z < Z - 1, send_up, recv_up, up_peer)
        side(lambda: z + k < Z, lambda: z + k, lambda: z > 0, send_down, recv_down, down_peer)

    def arrivals(u):
        for row in range(0 if crossed(u) else Z):
            for i in range(1, X):
                column = lax.rem(x - i + X, X)
                source = row * X + column
                wait_recv(place(u, source), recv_x.at[u, row, i], send_x.at[u, row, i])
                to_plane(u, lambda source=source: source, lambda source=source: place(u, source), None)
        if not crossed(u):
            local[own_store[u]].wait()
        mine = whole(u, part_of(u, core, y))
        send(None, lambda: (mine, mine, send_c.at[u], recv_c.at[u], core_peer))

    def relay(u):
        if UNITS[u][0] != "quarter":
            return
        part = (1 - y) * 2 + core
        for source in range(F):
            wait_recv(place(u, source, part), recv_y.at[u, source], send_y.at[u, source])
        theirs = whole(u, part)
        send(None, lambda: (theirs, theirs, send_r.at[u], recv_r.at[u], core_peer))

    def complete(u):
        wait_recv(whole(u, part_of(u, 1 - core, y)), recv_c.at[u], send_c.at[u])
        if UNITS[u][0] == "quarter":
            wait_recv(whole(u, (1 - y) * 2 + 1 - core), recv_r.at[u], send_r.at[u])

    scale = 1.0 / math.sqrt(head_size)

    def gather_gains():
        keep = pltpu.make_async_copy(gains_own, gains.at[fs], local_sem.at[0])
        keep.start()
        for k in range(1, Z):
            send(None, lambda k=k: (gains_own, gains.at[fs], send_g.at[0, k], recv_g.at[0, k], z_peer(k)))
        for i in range(1, X):
            send(None, lambda i=i: (gains_own, gains.at[fs], send_g.at[i, 0], recv_g.at[i, 0], x_peer(i)))
        keep.wait()

    def chunk_source(k, i):
        return lax.rem(z - k + Z, Z) * X + lax.rem(x - i + X, X)

    def pass_gains():
        for k in range(1, Z):
            here = gains.at[chunk_source(k, 0)]
            wait_recv(here, recv_g.at[0, k], send_g.at[0, k])
            for i in range(1, X):
                send(
                    None,
                    lambda here=here, i=i, k=k: (here, here, send_g.at[i, k], recv_g.at[i, k], x_peer(i)),
                )

    def take_gains():
        for k in range(Z):
            for i in range(1, X):
                wait_recv(gains.at[chunk_source(k, i)], recv_g.at[i, k], send_g.at[i, k])
        total = gains[0]
        for source in range(1, F):
            total = total + gains[source]
        gains_out[...] = total

    def norm_rows():
        def chunk(c, carry):
            rows = pl.ds(pl.multiple_of(c * CHUNK, CHUNK), CHUNK)
            for p in range(2):
                value = frames[p, rows, :].astype(F32)
                inputs[p, rows, :] = (value * scale_rows(value) * gains_out[0:1, :]).astype(BF)
            return carry

        lax.fori_loop(0, count // CHUNK, chunk, 0)
        store(inputs, inputs_out)

    def heads(m):
        columns = slice(m * STEP, (m + 1) * STEP)
        load = pltpu.make_async_copy(attn.at[m, pl.ds(0, 3)], proj, local_sem.at[0])
        load.start()
        load.wait()
        for t in (1, 2, 0):
            for p in range(2):
                rows_in[t, p, :, columns] = nn(inputs[p], proj[t, p]).astype(BF)
                if t > 0:
                    tail = rows_in[t, p, count - 16 :, columns].astype(F32)
                    row = 2 * (t - 1) + p
                    edge_send[m, row : row + 1, :] = tail[15:16, :]
            if t == 2:
                to_after = remote_copy(edge_send.at[m], edge_recv.at[m], send_e.at[m], recv_e.at[m], after_me)
                pl.when(me < devices - 1)(to_after.start)
        pl.when(me > 0)(to_after.wait_recv)
        first = lax.broadcasted_iota(jnp.int32, (count, STEP), 0) == 0
        for t in range(2):
            for p in range(2):
                n = 2 * t + p
                shifted = pltpu.roll(rows_in[1 + t, p, :, columns].astype(F32), 1, 0)
                before[n] = jnp.where(first, edge_recv[m, n : n + 1, :], shifted)
        ones = head_ones(STEP, head_size)

        def chunk(c, carry):
            rows = pl.ds(pl.multiple_of(c * CHUNK, CHUNK), CHUNK)
            allowed = jnp.broadcast_to(carried[rows, :], (CHUNK, STEP)) > 0.5
            queries, here_k, here_v = (
                [rows_in[t, p, rows, columns].astype(F32) for p in range(2)] for t in range(3)
            )
            keys = [before[p, rows, :] for p in range(2)] + here_k
            values = [before[2 + p, rows, :] for p in range(2)] + here_v
            scores = per_head(queries, keys, ones)
            for p, span in SPANS:
                probs = head_probs(scores, span, allowed, scale)
                terms = [pr.astype(BF).astype(F32) * values[PAIRS[n][1]] for n, pr in zip(span, probs)]
                mixed[p, rows, columns] = total_of(terms).astype(BF)
            return carry

        lax.fori_loop(0, count // CHUNK, chunk, 0)

    def load_mix():
        return pltpu.make_async_copy(attn.at[:, 3], mix, local_sem.at[1])

    def finish_rows():
        load_mix().wait()
        for turn in range(2):
            p = 1 - y if turn == 0 else y
            for m in range(groups):
                columns = slice(m * STEP, (m + 1) * STEP)
                hres[p, :, columns] = frames[p, :, columns].astype(F32) + nn(mixed[p], mix[m, p])

            def chunk(c, carry):
                rows = pl.ds(pl.multiple_of(c * CHUNK, CHUNK), CHUNK)
                value = hres[p, rows, :]
                b[turn, rows, :] = (value * scale_rows(value) * gains_out[1:2, :]).astype(BF)
                return carry

            lax.fori_loop(0, count // CHUNK, chunk, 0)
            if turn == 0:
                send(None, lambda: (b.at[0], b_rows.at[1], send_b, recv_b, y_peer))
            else:
                store(b.at[1], b_rows.at[0])
        store(hres, hres_out)

    @pl.when(me == 0)
    def _():
        edge_recv[...] = jnp.zeros_like(edge_recv)

    slots_of = [
        [n] if kind in ("quarter", "low") else [n + 1] if kind == "high" else [] for kind, n, *_ in UNITS
    ]
    slots_of[[u[0] for u in UNITS].index("inner")] = [groups + 1]
    slots_of[[u[0] for u in UNITS].index("down")] = [groups + 2]
    own_store = {}
    last_of = {kind_n[1]: u for u, kind_n in enumerate(UNITS) if kind_n[0] in ("quarter", "low", "high")}
    last_plane = max(u for u, kind_n in enumerate(UNITS) if kind_n[0] == "quarter")
    store(cot.at[y], c_rows.at[0])
    gather_gains()
    starts = [unit[4] for unit in UNITS]
    for tick in range(max(starts) + Z + 2):
        def aged(age):
            return [u for u, begun in enumerate(starts) if tick - begun == age]

        for u in aged(0):
            own_store[u] = len(local)
            start_unit(u)
        for u in aged(1):
            if crossed(u):
                turn(u)
        for k in range(1, Z):
            for u in aged(k):
                if not crossed(u):
                    hop(u, k)
            for u in aged(k + 1):
                if crossed(u):
                    hop(u, k)
        if tick == 1:
            pass_gains()
        if tick == 2:
            take_gains()
            norm_rows()
        for u in aged(Z):
            arrivals(u)
            if u == last_plane:
                send(None, lambda: (cot.at[1 - y], c_rows.at[1], send_q, recv_q, y_peer))
        for u in aged(Z + 1):
            relay(u)
            complete(u)
            for m in range(groups):
                if last_of[m] == u:
                    if m == groups - 1:
                        load_mix().start()
                    heads(m)
                    if m == groups - 1:
                        store(rows_in, rows_out)
                        store(mixed, mixed_out)
                        store(edge_recv, edge_out)
                        finish_rows()
    wait_recv(b_rows.at[1], recv_b, send_b)
    wait_recv(c_rows.at[1], recv_q, send_q)
    for condition, make in sent:
        wait_send(condition, make)
    for n, copy in enumerate(local):
        if n not in own_store.values():
            copy.wait()

    @pl.when(me < devices - 1)
    def _():
        for m in range(groups):
            remote_copy(edge_send.at[m], edge_recv.at[m], send_e.at[m], recv_e.at[m], after_me).wait_send()


def unit_list(groups, inner_width, down_width):
    units = [("quarter", n, None, False, n) for n in range(groups - 1)]
    units += [("low", groups - 1, None, False, groups - 1), ("high", groups - 1, None, False, groups)]
    start = groups + 1
    for kind, tiles, turns in (("down", down_width // 128, 2), ("inner", inner_width // 128, 6)):
        over_x = tiles // 4 if kind == "down" else -(-tiles // 4)
        at = 0
        for turn in range(turns):
            for crossed, all_tiles in ((False, tiles - over_x), (True, over_x)):
                lo, hi = all_tiles * turn // turns, all_tiles * (turn + 1) // turns
                if hi > lo:
                    units.append((kind, 0, slice(128 * at, 128 * (at + hi - lo)), crossed, start))
                    at += hi - lo
            start += 1
    return units


def forward(
    frames, carried, cot, gains_own, qkv_weight, mix_weight, inner_weight, down_weight, head_size, fsdp_count
):
    X = fsdp_count // Z
    _, count, width = frames.shape
    R, R2 = qkv_weight.shape[1], down_weight.shape[1]
    hidden, half = inner_weight.shape[2] // 2, width // 2
    groups = width // STEP
    units = len(unit_list(groups, hidden, half))
    dma, vmem = pltpu.SemaphoreType.DMA, pltpu.VMEM
    whole = pl.BlockSpec(memory_space=pltpu.VMEM)
    act = jax.ShapeDtypeStruct((2, count, width), BF)
    return pl.pallas_call(
        functools.partial(forward_kernel, X, groups, head_size),
        out_shape=(
            jax.ShapeDtypeStruct((groups, 4, 2, R * fsdp_count, STEP), BF),
            jax.ShapeDtypeStruct((2, R * fsdp_count, hidden), BF),
            jax.ShapeDtypeStruct((2, R2 * fsdp_count, half), BF),
            jax.ShapeDtypeStruct(gains_own.shape, F32),
            act,
            jax.ShapeDtypeStruct((3, 2, count, width), BF),
            act,
            jax.ShapeDtypeStruct((groups, 8, STEP), F32),
            jax.ShapeDtypeStruct((2, count, width), F32),
            act,
            act,
        ),
        in_specs=[whole] * 4 + [ANY] * 4,
        out_specs=(ANY,) * 3 + (whole,) + (ANY,) * 7,
        scratch_shapes=[
            vmem((groups + 1, 2, R, STEP), F32), vmem((R, hidden), F32), vmem((R2, half), F32),
            vmem((groups + 1, 2, R, STEP), BF), vmem((R, hidden), BF), vmem((R2, half), BF),
            vmem((fsdp_count,) + gains_own.shape, F32),
            vmem((2, count, width), BF), vmem((3, 2, count, width), BF), vmem((2, count, width), BF),
            vmem((4, count, STEP), F32), vmem((2, count, width), F32), vmem((2, count, width), BF),
            vmem((3, 2, width, STEP), BF), vmem((groups, 2, width, STEP), BF),
            vmem((groups, 8, STEP), F32), vmem((groups, 8, STEP), F32),
            dma((units, Z)), dma((units, Z)), dma((units, Z)), dma((units, Z)),
            dma((units, Z, X)), dma((units, Z, X)), dma((groups, fsdp_count)), dma((groups, fsdp_count)),
            dma((units,)), dma((units,)), dma((groups,)), dma((groups,)),
            dma((X, Z)), dma((X, Z)), dma((groups,)), dma((groups,)), dma, dma, dma, dma,
            dma((2,)), dma((units + 8,)), dma((groups + 3,)),
        ],
        compiler_params=pltpu.CompilerParams(
            vmem_limit_bytes=VMEM_BYTES, collective_id=0, has_side_effects=True
        ),
        name="attention_forward",
    )(frames, carried, cot, gains_own, qkv_weight, mix_weight, inner_weight, down_weight)


def feed_forward_kernel(
    X, J, b, c, inner, down, out_mine, back_mine, out_theirs, back_recv, inner_all, down_columns, down_sum,
    out, back, acts, down_here, down_there, down_from_core, down_stage, down_column, down_from_x, mine, other, from_core, summed, from_x, column, from_z, final, staged,
    s1, r1, s2, r2, s3, r3, s5, r5, s6, r6, s7, r7, local_sem,
    s_stage, s_own, sdx, rdx, s_column,
):
    j = pl.program_id(0)
    half = down.shape[2]
    rows_here = out_mine.shape[0]
    R, step = final.shape[1:]
    dp, fs = lax.axis_index("dp"), lax.axis_index("fsdp")
    y, core = dp // 2, dp % 2
    z, x = fs // X, fs % X
    core_peer = (y * 2 + 1 - core, fs)
    y_peer = ((1 - y) * 2 + core, fs)

    def z_peer(k):
        return (dp, lax.rem(z + k, Z) * X + x)

    def x_peer(i):
        return (dp, z * X + lax.rem(x + i, X))

    def dp_peer(d):
        return (((y + d // 2) % 2) * 2 + (core + d % 2) % 2, fs)

    def to_core(n):
        return remote_copy(other.at[n % 2], from_core.at[n], s1.at[n % 2], r1.at[n], core_peer)

    def to_x(n, i):
        return remote_copy(
            summed.at[n % 2, :, lax.rem(x + i, X)], from_x.at[n, i - 1], s2.at[n % 2, i - 1], r2.at[n, i - 1], x_peer(i)
        )

    def to_z(n, k):
        return remote_copy(
            column.at[n % 2, lax.rem(z + k, Z)], from_z.at[n, k - 1], s3.at[n % 2, k - 1], r3.at[n, k - 1], z_peer(k)
        )

    def place(n, owner):
        return inner_all.at[owner, :, pl.ds(pl.multiple_of(n * step, step), step)]

    def share(n, d):
        return remote_copy(final.at[n], place(n, dp), s5.at[n, d - 1], r5.at[n, d - 1], dp_peer(d))

    def keep(n):
        return pltpu.make_async_copy(final.at[n], place(n, dp), local_sem.at[n])

    exchange = remote_copy(staged, back_recv, s6, r6, y_peer)

    R2 = down_column.shape[1]
    ends = [-(-(g + 1) * X * R2 // step) - 1 for g in range(Z)]

    def down_rows(g, column):
        return down_sum.at[pl.ds((g * X + column) * R2, R2), :]

    def down_store(n):
        return pltpu.make_async_copy(
            down_stage.at[n % 2], down_sum.at[pl.ds(pl.multiple_of(n * step, step), step), :], s_stage.at[n % 2]
        )

    def down_load(g):
        return pltpu.make_async_copy(down_rows(g, x), down_column.at[g], s_own.at[g])

    def down_to_x(g, i):
        return remote_copy(
            down_rows(g, lax.rem(x + i, X)), down_from_x.at[g, i - 1], sdx.at[g, i - 1], rdx.at[g, i - 1], x_peer(i)
        )

    def down_keep(g):
        return pltpu.make_async_copy(down_column.at[g], down_columns.at[g], s_column.at[g])

    def down_to_core(n):
        return remote_copy(down_there.at[n % 2], down_from_core.at[n], s7.at[n % 2], r7.at[n], core_peer)

    @pl.when(j == 0)
    def _():
        barrier = pltpu.get_barrier_semaphore()
        peers = [z_peer(k) for k in range(1, Z)] + [x_peer(i) for i in range(1, X)]
        peers += [dp_peer(d) for d in range(1, 4)]
        for peer in peers:
            pl.semaphore_signal(barrier, inc=1, device_id=peer, device_id_type=MESH)
        pl.semaphore_wait(barrier, len(peers))
        out[...] = jnp.zeros_like(out)
        back[...] = jnp.zeros_like(back)

    @pl.when(j < J)
    def _():
        rows, cot = b[...], c[...]
        gate = nn(rows, inner[0])
        up = nn(rows, inner[1])
        squashed = jax.nn.sigmoid(gate)
        active = gate * squashed
        hidden = (active * up).astype(BF)
        hidden_grad = nt(cot[:, :half], down[0]) + nt(cot[:, half:], down[1])
        gate_grad = (hidden_grad * up * (squashed * (1.0 + gate * (1.0 - squashed)))).astype(BF)
        up_grad = (hidden_grad * active).astype(BF)
        acts[0] = hidden
        acts[1] = gate_grad
        acts[2] = up_grad

    @pl.when((j >= 2) & (j < J + 2))
    def _():
        down_store(j - 2).wait()

    for g in range(Z):
        @pl.when(j == ends[g] + 2)
        def _():
            for i in range(1, X):
                down_to_x(g, i).start()
            down_load(g).start()

    @pl.when((j >= 1) & (j < J + 1))
    def _():
        n = j - 1
        to_core(n).wait_recv()

        @pl.when(n >= 2)
        def _():
            for i in range(1, X):
                to_x(n - 2, i).wait_send()

        down_to_core(n).wait_recv()
        down_stage[n % 2] = (down_here[n % 2].astype(F32) + down_from_core[n].astype(F32)).astype(BF)
        down_store(n).start()
        total = (mine[n % 2].astype(F32) + from_core[n].astype(F32)).astype(BF)
        summed[n % 2] = total.reshape(summed.shape[1:])
        for i in range(1, X):
            to_x(n, i).start()

    @pl.when((j >= 2) & (j < J + 2))
    def _():
        n = j - 2
        for i in range(1, X):
            to_x(n, i).wait_recv()

        @pl.when(n >= 2)
        def _():
            for k in range(1, Z):
                to_z(n - 2, k).wait_send()

        total = summed[n % 2, :, x].astype(F32)
        for i in range(1, X):
            total = total + from_x[n, i - 1].astype(F32)
        column[n % 2] = total.astype(BF)
        for k in range(1, Z):
            to_z(n, k).start()

    for g in range(Z):
        @pl.when(j == min(ends[g] + 4, J + 2))
        def _():
            down_load(g).wait()
            for i in range(1, X):
                down_to_x(g, i).wait_recv()
            total = down_column[g].astype(F32) + total_of([down_from_x[g, i].astype(F32) for i in range(X - 1)])
            down_column[g] = total.astype(BF)
            down_keep(g).start()

    @pl.when((j >= 3) & (j < J + 3))
    def _():
        n = j - 3
        for k in range(1, Z):
            to_z(n, k).wait_recv()
        total = column[n % 2, z].astype(F32)
        for k in range(1, Z):
            total = total + from_z[n, k - 1].astype(F32)
        final[n] = total.astype(BF)
        keep(n).start()
        for d in range(1, 4):
            share(n, d).start()

    @pl.when(j < J)
    def _():
        rows, cot = b[...], c[...]
        hidden, gate_grad, up_grad = (acts[n] for n in range(3))
        gate_term = tn(rows, gate_grad).astype(BF)
        up_term = tn(rows, up_grad).astype(BF)

        @pl.when(j >= 2)
        def _():
            to_core(j - 2).wait_send()
            down_to_core(j - 2).wait_send()

        mine[j % 2] = jnp.where(core == 0, gate_term, up_term)
        other[j % 2] = jnp.where(core == 0, up_term, gate_term)
        to_core(j).start()
        down_term = tn(hidden, cot).astype(BF)
        down_here[j % 2] = jnp.where(core == 0, down_term[:, :half], down_term[:, half:])
        down_there[j % 2] = jnp.where(core == 0, down_term[:, half:], down_term[:, :half])
        down_to_core(j).start()
        for n in range(2):
            part = slice(n * half, (n + 1) * half)
            out[:, part] += nn(hidden, down[n])
        back[...] += nt(gate_grad, inner[0]) + nt(up_grad, inner[1])

    @pl.when(j == J - 1)
    def _():
        staged[...] = back[rows_here:, :].astype(BF)
        exchange.start()
        out_theirs[...] = out[rows_here:, :].astype(BF)
        out_mine[...] = out[:rows_here, :]
        back_mine[...] = back[:rows_here, :]

    @pl.when(j == J + 2)
    def _():
        for n in (J - 2, J - 1):
            to_core(n).wait_send()
            down_to_core(n).wait_send()
            for i in range(1, X):
                to_x(n, i).wait_send()
            for k in range(1, Z):
                to_z(n, k).wait_send()

        def finish(n, carry):
            keep(n).wait()
            for d in range(1, 4):
                share(n, d).wait()
            return carry

        lax.fori_loop(0, J, finish, 0)
        exchange.wait()
        for g in range(Z):
            down_keep(g).wait()
            for i in range(1, X):
                down_to_x(g, i).wait_send()


def feed_forward(b, c, inner, down, fsdp_count):
    rows, width = b.shape
    _, _, hidden = inner.shape
    half = down.shape[2]
    step = 256
    J = hidden // step
    X = fsdp_count // Z
    R, R2 = width // fsdp_count, hidden // fsdp_count
    whole = pl.BlockSpec((rows, width), lambda j: (0, 0), pipeline_mode=pl.Buffered(1))
    part = pl.BlockSpec((rows // 2, width), lambda j: (0, 0), pipeline_mode=pl.Buffered(1))
    inner_spec = pl.BlockSpec((2, width, step), lambda j: (0, 0, jnp.minimum(j, J - 1)))
    down_spec = pl.BlockSpec((2, step, half), lambda j: (0, jnp.minimum(j, J - 1), 0))
    dma, vmem = pltpu.SemaphoreType.DMA, pltpu.VMEM
    return pl.pallas_call(
        functools.partial(feed_forward_kernel, X, J),
        grid=(J + 3,),
        out_shape=(
            jax.ShapeDtypeStruct((rows // 2, width), F32),
            jax.ShapeDtypeStruct((rows // 2, width), F32),
            jax.ShapeDtypeStruct((rows // 2, width), BF),
            jax.ShapeDtypeStruct((rows // 2, width), BF),
            jax.ShapeDtypeStruct((4, R, hidden), BF),
            jax.ShapeDtypeStruct((Z, R2, half), BF),
            jax.ShapeDtypeStruct((hidden, half), BF),
        ),
        in_specs=[whole, whole, inner_spec, down_spec],
        out_specs=(part, part, part, ANY, ANY, ANY, ANY),
        scratch_shapes=[
            vmem((rows, width), F32), vmem((rows, width), F32), vmem((3, rows, step), BF),
            vmem((2, step, half), BF), vmem((2, step, half), BF), vmem((J, step, half), BF),
            vmem((2, step, half), BF), vmem((Z, R2, half), BF), vmem((Z, X - 1, R2, half), BF),
            vmem((2, width, step), BF), vmem((2, width, step), BF), vmem((J, width, step), BF),
            vmem((2, Z, X, R, step), BF), vmem((J, X - 1, Z, R, step), BF),
            vmem((2, Z, R, step), BF), vmem((J, Z - 1, R, step), BF),
            vmem((J, R, step), BF), vmem((rows // 2, width), BF),
            dma((2,)), dma((J,)), dma((2, X - 1)), dma((J, X - 1)), dma((2, Z - 1)), dma((J, Z - 1)),
            dma((J, 3)), dma((J, 3)), dma, dma, dma((2,)), dma((J,)), dma((J,)),
            dma((2,)), dma((Z,)), dma((Z, X - 1)), dma((Z, X - 1)), dma((Z,)),
        ],
        compiler_params=pltpu.CompilerParams(
            vmem_limit_bytes=VMEM_BYTES, collective_id=1, has_side_effects=True
        ),
        cost_estimate=pl.CostEstimate(flops=18 * rows * width * hidden, bytes_accessed=60 * 2**20, transcendentals=0),
        name="feed_forward",
    )(b, c, inner, down)


def total_of(values):
    return functools.reduce(jnp.add, values)


def attention_back_kernel(
    X, groups, head_size, carried, q, k, v, edge, mix, dhb, mixed, inputs, proj, gains, second_gain, frames_in, down_in, out_send,
    frames_grad, gains_sum, attn_all, down_all, out_recv,
    da, gain_terms, gain_from, mixed_grad, before, terms_before, terms_here, tails, grads, edge_send, edge_recv,
    mine, other, from_core, keep_y, send_y, from_y, summed, from_x, column, from_z, final, plane, from_plane, final_plane,
    down_mine, down_from_z, down_final,
    s_edge, r_edge, s1, r1, sy, ry, sxa, rxa, sxb, rxb, sz, rz, sf, rf, sp, rp, sc, rc, local_sem,
    s_out, r_out, sg, rg, frame_sem, sdz, rdz, sdf, rdf, down_sem, free,
):
    i = pl.program_id(0)
    frames, step = q.shape[2:]
    R, thin = final.shape[1:]
    subs = 2 * groups
    slots = from_core.shape[0]
    dp, fs = lax.axis_index("dp"), lax.axis_index("fsdp")
    F = Z * X
    y, core = dp // 2, dp % 2
    z, x = fs // X, fs % X
    me = dp * F + fs
    devices = 4 * F
    core_peer = (y * 2 + 1 - core, fs)
    y_peer = ((1 - y) * 2 + core, fs)
    before_me = ((me - 1 + devices) % devices // F, (me - 1 + devices) % devices % F)
    after_me = ((me + 1) % devices // F, (me + 1) % devices % F)

    def z_peer(n):
        return (dp, lax.rem(z + n, Z) * X + x)

    def x_peer(n):
        return (dp, z * X + lax.rem(x + n, X))

    def dp_peer(d):
        return (((y + d // 2) % 2) * 2 + (core + d % 2) % 2, fs)

    def to_before(n):
        return remote_copy(edge_send.at[n % 2], edge_recv.at[n], s_edge.at[n % 2], r_edge.at[n], before_me)

    def to_core(n):
        return remote_copy(other.at[n % 2], from_core.at[n % slots], s1.at[n % 2], r1.at[n % slots], core_peer)

    def to_y(n):
        return remote_copy(send_y.at[n % 2], from_y.at[n], sy.at[n % 2], ry.at[n], y_peer)

    def to_x_early(n, j):
        return remote_copy(
            summed.at[n % 3, pl.ds(1, 2), :, lax.rem(x + j, X)], from_x.at[n, j - 1, pl.ds(1, 2)],
            sxa.at[n % 3, j - 1], rxa.at[n, j - 1], x_peer(j),
        )

    def to_x_late(n, j):
        return remote_copy(
            summed.at[n % 3, 0, :, lax.rem(x + j, X)], from_x.at[n, j - 1, 0],
            sxb.at[n % 3, j - 1], rxb.at[n, j - 1], x_peer(j),
        )

    def to_z(n, j):
        return remote_copy(
            column.at[n % 2, :, lax.rem(z + j, Z)], from_z.at[n, j - 1], sz.at[n % 2, j - 1], rz.at[n, j - 1], z_peer(j)
        )

    def place(n, t):
        return attn_all.at[t, core, :, pl.ds(pl.multiple_of(n * thin, thin), thin)]

    def share(n, d):
        return remote_copy(final.at[n], place(n, y), sf.at[n, d - 1], rf.at[n, d - 1], dp_peer(d))

    def relay(n):
        return remote_copy(place(n, 1 - y), place(n, 1 - y), sf.at[n, 2], rf.at[n, 2], core_peer)

    def down_to_z(k):
        return remote_copy(
            down_in.at[lax.rem(z + k, Z)], down_from_z.at[k - 1], sdz.at[k - 1], rdz.at[k - 1], z_peer(k)
        )

    def down_share(d):
        return remote_copy(down_final, down_all.at[dp], sdf.at[d - 1], rdf.at[d - 1], dp_peer(d))

    def down_relay():
        part = down_all.at[(1 - y) * 2 + core]
        return remote_copy(part, part, sdf.at[2], rdf.at[2], core_peer)

    def to_plane(n):
        return remote_copy(plane.at[n], from_plane.at[n], sp.at[n], rp.at[n], y_peer)

    def share_core(n, t):
        return remote_copy(final_plane.at[n, t], place(n, 2 + t), sc.at[n, t], rc.at[n, t], core_peer)

    def keep(n, t):
        src = final.at[n] if t == 0 else final_plane.at[n, t - 1]
        return pltpu.make_async_copy(src, place(n, y if t == 0 else 1 + t), local_sem.at[n, t])

    def load_frames(g):
        dst = grads.at[g] if g < 3 else mixed_grad
        return pltpu.make_async_copy(frames_in.at[:, :, pl.ds(g * step, step)], dst, frame_sem.at[g])

    def gain_copy(level, n):
        peer = (core_peer, y_peer, x_peer(n + 1), z_peer(n + 1))[level]
        return remote_copy(gain_terms.at[level], gain_from.at[level, n], sg.at[level, n], rg.at[level, n], peer)

    down_load = pltpu.make_async_copy(down_in.at[z], down_mine, down_sem.at[0])
    down_keep = pltpu.make_async_copy(down_final, down_all.at[dp], down_sem.at[1])
    out_copy = remote_copy(out_send, out_recv, s_out, r_out, y_peer)

    @pl.when(i == 0)
    def _():
        barrier = pltpu.get_barrier_semaphore()
        peers = [z_peer(n) for n in range(1, Z)] + [x_peer(n) for n in range(1, X)]
        peers += [dp_peer(d) for d in range(1, 4)] + [before_me, after_me]
        for peer in peers:
            pl.semaphore_signal(barrier, inc=1, device_id=peer, device_id_type=MESH)
        pl.semaphore_wait(barrier, len(peers))
        out_copy.start()
        for k in range(1, Z):
            down_to_z(k).start()
        down_load.start()
        da[...] = jnp.zeros_like(da)

        @pl.when(me == devices - 1)
        def _():
            edge_recv[...] = jnp.zeros_like(edge_recv)

    def active(first):
        return (i >= first) & (i < first + subs)

    @pl.when(active(2))
    def _():
        n = i - 2
        to_core(n).wait_recv()

        @pl.when(n >= 2)
        def _():
            to_y(n - 2).wait_send()

        @pl.when(n >= 3)
        def _():
            for j in range(1, X):
                to_x_early(n - 3, j).wait_send()

        def both(t):
            return (mine[n % 2, t].astype(F32) + from_core[n % slots, t].astype(F32)).astype(BF)

        send_y[n % 2] = both(1 - y)
        to_y(n).start()
        for t in range(2):
            summed[n % 3, 1 + t] = both(2 + t).reshape(summed.shape[2:])
        for j in range(1, X):
            to_x_early(n, j).start()
        keep_y[n % 2] = both(y)

        @pl.when(n < subs - slots)
        def _():
            pl.semaphore_signal(free, inc=1, device_id=core_peer, device_id_type=MESH)

    @pl.when(active(3))
    def _():
        n = i - 3
        to_y(n).wait_recv()

        @pl.when(n >= 3)
        def _():
            for j in range(1, X):
                to_x_late(n - 3, j).wait_send()

        total = (keep_y[n % 2].astype(F32) + from_y[n].astype(F32)).astype(BF)
        summed[n % 3, 0] = total.reshape(summed.shape[2:])
        for j in range(1, X):
            to_x_late(n, j).start()

    @pl.when(active(4))
    def _():
        n = i - 4
        for j in range(1, X):
            to_x_early(n, j).wait_recv()
            to_x_late(n, j).wait_recv()

        @pl.when(n >= 2)
        def _():
            for j in range(1, Z):
                to_z(n - 2, j).wait_send()

        total = summed[n % 3, :, :, x].astype(F32) + total_of([from_x[n, j].astype(F32) for j in range(X - 1)])
        column[n % 2] = total.astype(BF)
        for j in range(1, Z):
            to_z(n, j).start()

    @pl.when(active(5))
    def _():
        n = i - 5
        for j in range(1, Z):
            to_z(n, j).wait_recv()
        total = column[n % 2, :, z].astype(F32) + total_of([from_z[n, j].astype(F32) for j in range(Z - 1)])
        total = total.astype(BF)
        final[n] = total[0]
        plane[n] = total[1:]
        to_plane(n).start()
        keep(n, 0).start()
        for d in range(1, 3):
            share(n, d).start()

    @pl.when(active(6))
    def _():
        n = i - 6
        to_plane(n).wait_recv()
        share(n, 2).wait_recv()
        relay(n).start()
        final_plane[n] = (plane[n].astype(F32) + from_plane[n].astype(F32)).astype(BF)
        for t in range(2):
            keep(n, t + 1).start()
            share_core(n, t).start()

    @pl.when(i == 4)
    def _():
        down_load.wait()
        for k in range(1, Z):
            down_to_z(k).wait_recv()
        total = down_mine[...].astype(F32) + total_of([down_from_z[k].astype(F32) for k in range(Z - 1)])
        down_final[...] = total.astype(BF)
        down_keep.start()
        for d in range(1, 3):
            down_share(d).start()

    @pl.when(i == 6)
    def _():
        down_share(2).wait_recv()
        down_relay().start()

    @pl.when((i < subs) & (i % 2 == 0))
    def _():
        m = i // 2
        slot = m % 2
        ones = head_ones(step, head_size)
        scale = 1.0 / math.sqrt(head_size)
        first = lax.broadcasted_iota(jnp.int32, (frames, step), 0) == 0
        last = lax.broadcasted_iota(jnp.int32, (frames, step), 0) == frames - 1
        for p in range(2):
            mixed_grad[p] = total_of(
                [nt(dhb[p, :, g * step : (g + 1) * step], mix[g, 0, p]) for g in range(groups)]
            ).astype(BF)
            before[p] = jnp.where(first, edge[0, p : p + 1, :], pltpu.roll(k[0, p].astype(F32), 1, 0))
            before[2 + p] = jnp.where(first, edge[0, 2 + p : 3 + p, :], pltpu.roll(v[0, p].astype(F32), 1, 0))

        def chunk(c, carry):
            rows = pl.ds(pl.multiple_of(c * CHUNK, CHUNK), CHUNK)
            allowed = jnp.broadcast_to(carried[rows, :], (CHUNK, step)) > 0.5
            queries = [q[0, p, rows, :].astype(F32) for p in range(2)]
            cots = [mixed_grad[p, rows, :].astype(F32) for p in range(2)]
            keys = [before[p, rows, :] for p in range(2)] + [k[0, p, rows, :].astype(F32) for p in range(2)]
            values = [before[2 + p, rows, :] for p in range(2)] + [v[0, p, rows, :].astype(F32) for p in range(2)]

            scores = per_head(queries, keys, ones)
            dprobs = per_head(cots, values, ones)
            key_grads, value_grads = [[] for _ in range(4)], [[] for _ in range(4)]
            for p, span in SPANS:
                probs = head_probs(scores, span, allowed, scale)
                mean = total_of([pr * dprobs[m] for m, pr in zip(span, probs)])
                query_grad = []
                for m, pr in zip(span, probs):
                    n = PAIRS[m][1]
                    ds = (pr * (dprobs[m] - mean)).astype(BF).astype(F32) * scale
                    query_grad.append(ds * keys[n])
                    key_grads[n].append(ds * queries[p])
                    value_grads[n].append(pr.astype(BF).astype(F32) * cots[p])
                grads[0, p, rows, :] = total_of(query_grad).astype(BF)
            for p in range(2):
                terms_before[p, rows, :] = total_of(key_grads[p])
                terms_before[2 + p, rows, :] = total_of(value_grads[p])
                terms_here[p, rows, :] = total_of(key_grads[2 + p])
                terms_here[2 + p, rows, :] = total_of(value_grads[2 + p])
            return carry

        lax.fori_loop(0, frames // CHUNK, chunk, 0)

        @pl.when((m >= 2) & (me > 0))
        def _():
            to_before(m - 2).wait_send()

        for row in range(4):
            edge_send[slot, row : row + 1, :] = terms_before[row, 0:1, :]

        @pl.when(me > 0)
        def _():
            to_before(m).start()

        for row in range(4):
            total = terms_here[row] + jnp.where(last, 0.0, pltpu.roll(terms_before[row], frames - 1, 0))
            grads[1 + row // 2, row % 2] = total.astype(BF)
            tails[row] = total[frames - 16 :, :]

    @pl.when((i < subs) & (i % 2 == 1))
    def _():
        m = i // 2

        @pl.when(me < devices - 1)
        def _():
            to_before(m).wait_recv()

        bottom = lax.broadcasted_iota(jnp.int32, (16, step), 0) == 15
        for row in range(4):
            fixed = tails[row] + jnp.where(bottom, edge_recv[m, row : row + 1, :], 0.0)
            grads[1 + row // 2, row % 2, frames - 16 :, :] = fixed.astype(BF)

        @pl.when(m >= 1)
        def _():
            for h in range(2):
                to_core(2 * m - 2 + h).wait_send()

        for t in range(4):
            pair = []
            for p in range(2):
                if t < 3:
                    pair.append(tn(inputs[p], grads[t, p]).astype(BF))
                else:
                    pair.append(tn(mixed[p], dhb[p, :, pl.ds(pl.multiple_of(m * step, step), step)]).astype(BF))
            here = jnp.where(core == 0, pair[0], pair[1])
            there = jnp.where(core == 0, pair[1], pair[0])
            for h in range(2):
                mine[h, t] = here[:, h * thin : (h + 1) * thin]
                other[h, t] = there[:, h * thin : (h + 1) * thin]

        @pl.when(m >= slots // 2)
        def _():
            pl.semaphore_wait(free, 2)

        for h in range(2):
            to_core(2 * m + h).start()
        for p in range(2):
            da[p] += total_of([nt(grads[t, p], proj[0, t, p]) for t in range(3)])

        @pl.when(m == groups - 1)
        def _():
            for g in range(groups):
                load_frames(g).start()

    @pl.when(i == subs)
    def _():
        for g in range(groups):
            load_frames(g).wait()

        def chunk(c, term):
            rows = pl.ds(pl.multiple_of(c * CHUNK, CHUNK), CHUNK)
            for p in range(2):
                pieces = [grads[g, p, rows, :] if g < 3 else mixed_grad[p, rows, :] for g in range(groups)]
                value = jnp.concatenate(pieces, axis=1).astype(F32)
                inverse = scale_rows(value)
                normed = value * inverse
                grad = da[p, rows, :]
                term = term + jnp.sum(grad * normed, axis=0, keepdims=True)
                total = dhb[p, rows, :].astype(F32) + norm_back(grad, normed, gains[0:1, :], inverse)
                frames_grad[p, rows, :] = total.astype(BF)
            return term

        term = lax.fori_loop(0, frames // CHUNK, chunk, jnp.zeros((1, da.shape[2]), F32))
        gain_terms[0] = second_gain[...]
        gain_terms[0, 0:1, :] = term
        gain_copy(0, 0).start()

    for level in range(1, 4):
        @pl.when(i == subs + level)
        def _():
            count = X - 1 if level == 3 else 1
            total = gain_terms[level - 1]
            for n in range(count):
                gain_copy(level - 1, n).wait()
                total = total + gain_from[level - 1, n]
            gain_terms[level] = total
            for n in range(Z - 1 if level == 3 else X - 1 if level == 2 else 1):
                gain_copy(level, n).start()

    @pl.when(i == subs + 4)
    def _():
        total = gain_terms[3]
        for n in range(Z - 1):
            gain_copy(3, n).wait()
            total = total + gain_from[3, n]
        gains_sum[...] = total

    @pl.when(i == subs + 5)
    def _():
        @pl.when(me > 0)
        def _():
            for n in (groups - 2, groups - 1):
                to_before(n).wait_send()

        for n in (subs - 3, subs - 2, subs - 1):
            for j in range(1, X):
                to_x_early(n, j).wait_send()
                to_x_late(n, j).wait_send()

        for n in (subs - 2, subs - 1):
            to_core(n).wait_send()
            to_y(n).wait_send()
            for j in range(1, Z):
                to_z(n, j).wait_send()

        def finish(n, carry):
            to_plane(n).wait_send()
            keep(n, 0).wait()
            share(n, 1).wait()
            share(n, 2).wait_send()
            relay(n).wait()
            for t in range(2):
                keep(n, t + 1).wait()
                share_core(n, t).wait()
            return carry

        lax.fori_loop(0, subs, finish, 0)
        out_copy.wait()
        for k in range(1, Z):
            down_to_z(k).wait_send()
        down_keep.wait()
        down_share(1).wait()
        down_share(2).wait_send()
        down_relay().wait()


def attention_back(
    carried, qkv_rows, edge, attn, dhb, mixed, inputs, gains, second_gain, frames_in, down_in, out_send, head_size, fsdp_count
):
    _, frames, width = dhb.shape
    step = STEP
    groups = width // step
    X = fsdp_count // Z
    R = width // fsdp_count

    def early(i):
        return jnp.minimum(i // 2, groups - 1)

    rows = [pl.BlockSpec((1, 2, frames, step), lambda i, t=t: (t, 0, 0, early(i))) for t in range(3)]
    edge_spec = pl.BlockSpec((1, 8, step), lambda i: (early(i), 0, 0))
    mask = pl.BlockSpec((frames, 1), lambda i: (0, 0), pipeline_mode=pl.Buffered(1))
    whole = pl.BlockSpec((2, frames, width), lambda i: (0, 0, 0), pipeline_mode=pl.Buffered(1))
    mix_spec = pl.BlockSpec((groups, 1, 2, step, step), lambda i: (0, 3, 0, early(i), 0))
    proj_spec = pl.BlockSpec((1, 3, 2, width, step), lambda i: (jnp.clip((i - 1) // 2, 0, groups - 1), 0, 0, 0, 0))
    line = pl.BlockSpec((8, width), lambda i: (0, 0), pipeline_mode=pl.Buffered(1))
    dma, vmem = pltpu.SemaphoreType.DMA, pltpu.VMEM
    thin = step // 2
    n, slots, peers = 2 * groups, 4, max(X, Z) - 1
    return pl.pallas_call(
        functools.partial(attention_back_kernel, X, groups, head_size),
        grid=(n + 6,),
        out_shape=(
            jax.ShapeDtypeStruct((2, frames, width), BF),
            jax.ShapeDtypeStruct((8, width), F32),
            jax.ShapeDtypeStruct((4, 2, R, width), BF),
            jax.ShapeDtypeStruct((4,) + down_in.shape[1:], BF),
            jax.ShapeDtypeStruct(out_send.shape, BF),
        ),
        in_specs=[mask, *rows, edge_spec, mix_spec, whole, whole, whole, proj_spec, line, line, ANY, ANY, ANY],
        out_specs=(whole, line, ANY, ANY, ANY),
        scratch_shapes=[
            vmem((2, frames, width), F32), vmem((4, 8, width), F32), vmem((4, peers, 8, width), F32),
            vmem((2, frames, step), BF), vmem((4, frames, step), F32), vmem((4, frames, step), F32),
            vmem((4, frames, step), F32), vmem((4, 16, step), F32), vmem((3, 2, frames, step), BF),
            vmem((2, 8, step), F32), vmem((groups, 8, step), F32),
            vmem((2, 4, width, thin), BF), vmem((2, 4, width, thin), BF), vmem((slots, 4, width, thin), BF),
            vmem((2, width, thin), BF), vmem((2, width, thin), BF), vmem((n, width, thin), BF),
            vmem((3, 3, Z, X, R, thin), BF), vmem((n, X - 1, 3, Z, R, thin), BF),
            vmem((2, 3, Z, R, thin), BF), vmem((n, Z - 1, 3, R, thin), BF),
            vmem((n, R, thin), BF), vmem((n, 2, R, thin), BF), vmem((n, 2, R, thin), BF), vmem((n, 2, R, thin), BF),
            vmem(down_in.shape[1:], BF), vmem((Z - 1,) + down_in.shape[1:], BF), vmem(down_in.shape[1:], BF),
            dma((2,)), dma((groups,)), dma((2,)), dma((slots,)), dma((2,)), dma((n,)),
            dma((3, X - 1)), dma((n, X - 1)), dma((3, X - 1)), dma((n, X - 1)),
            dma((2, Z - 1)), dma((n, Z - 1)), dma((n, 3)), dma((n, 3)), dma((n,)), dma((n,)),
            dma((n, 2)), dma((n, 2)), dma((n, 3)),
            dma, dma, dma((4, peers)), dma((4, peers)), dma((groups,)),
            dma((Z - 1,)), dma((Z - 1,)), dma((3,)), dma((3,)), dma((2,)), pltpu.SemaphoreType.REGULAR,
        ],
        compiler_params=pltpu.CompilerParams(vmem_limit_bytes=63 * 2**20, collective_id=2, has_side_effects=True),
        name="attention_back",
    )(
        carried, qkv_rows, qkv_rows, qkv_rows, edge, attn, dhb, mixed, inputs, attn,
        gains, second_gain, frames_in, down_in, out_send,
    )


def update_kernel(step_size, share, weight, moment, average, grad_out, moment_out, average_out, weight_out):
    gradient = share[...].reshape(weight.shape).astype(F32)
    moment_new, average_new, weight_new = owner_update(
        weight[...], gradient, moment[...], average[...], step_size
    )
    grad_out[...] = gradient
    moment_out[...] = moment_new
    average_out[...] = average_new
    weight_out[...] = weight_new


def update(shares, share_block, share_at, grid, block, at, weight, moment, average, step_size, name):
    share_spec = pl.BlockSpec(share_block, share_at)
    spec = pl.BlockSpec(block, at)
    return pl.pallas_call(
        functools.partial(update_kernel, step_size),
        grid=grid,
        out_shape=(jax.ShapeDtypeStruct(weight.shape, F32),) * 4,
        in_specs=[share_spec, spec, spec, spec],
        out_specs=(spec,) * 4,
        compiler_params=pltpu.CompilerParams(vmem_limit_bytes=VMEM_BYTES),
        name=name,
    )(shares, weight, moment, average)


def per_device(
    frames, cotangent, segment_ids,
    qkv_weight, mix_weight, inner_weight, down_weight, norm_gains,
    qkv_moment, mix_moment, inner_moment, down_moment, gains_moment,
    qkv_average, mix_average, inner_average, down_average, gains_average,
):
    frame_count, positions, width = frames.shape
    head_size = width // HEADS
    hidden = inner_weight.shape[2] // 2
    dp_count, fsdp_count = lax.axis_size("dp"), lax.axis_size("fsdp")
    X = fsdp_count // Z
    devices = dp_count * fsdp_count
    total_frames = frame_count * devices
    dp, fs = lax.axis_index("dp"), lax.axis_index("fsdp")
    y, core = dp // 2, dp % 2
    z, x = fs // X, fs % X
    axes = ("dp", "fsdp")

    device = dp * fsdp_count + fs
    padded_ids = jnp.concatenate([jnp.full((1,), -1, jnp.int32), segment_ids])
    window = lax.dynamic_slice_in_dim(padded_ids, device * frame_count, frame_count + 1)
    carried = (window[1:] == window[:-1]).astype(F32)[:, None]

    half_width = width // 2
    own_gains = norm_gains.astype(BF).astype(F32)
    gains_own = lax.dynamic_update_slice(jnp.zeros((8, width), F32), own_gains, (0, fs * own_gains.shape[1]))
    frames_by = frames.transpose(1, 0, 2)
    cot = cotangent.transpose(1, 0, 2)
    attn, inner, down, gains, a, qkv_rows, mixed, edge, hres, b_rows, c_rows = forward(
        frames_by, carried, cot, gains_own, qkv_weight, mix_weight, inner_weight, down_weight, head_size, fsdp_count
    )
    r2 = scale_rows(hres)
    n2 = hres * r2
    b_rows = b_rows.reshape(2 * frame_count, width)
    c_rows = c_rows.reshape(2 * frame_count, width)
    out, back, out_there, back_there, inner_shares, down_columns, _ = feed_forward(b_rows, c_rows, inner, down, fsdp_count)

    def by_position(mine, theirs):
        return jnp.where(y == 0, jnp.stack([mine, theirs]), jnp.stack([theirs, mine]))

    db = by_position(back, back_there.astype(F32))

    e2 = jnp.sum(db * n2, axis=(0, 1))
    dh = cot.astype(F32) + norm_back(db, n2, gains[1], r2)
    dhb = dh.astype(BF)
    second_gain = jnp.zeros((8, width), F32).at[1].set(e2)
    frames_grad, gains_sum, attn_shares, down_shares, out_here = attention_back(
        carried, qkv_rows, edge, attn, dhb, mixed, a, gains, second_gain, frames_by, down_columns, out_there, head_size, fsdp_count
    )
    frames_grad = frames_grad.transpose(1, 0, 2)
    layer_out = (hres + by_position(out, out_here.astype(F32))).astype(BF).transpose(1, 0, 2)

    step_size = step_rate / math.sqrt(total_frames)
    R, R2 = qkv_weight.shape[1], down_weight.shape[1]
    cut = min(R, 64)
    qkv_new = update(
        attn_shares, (1, 1, R, width), lambda p, t: (t, p, 0, 0), (2, 3), (1, R, width), lambda p, t: (p, 0, t),
        qkv_weight, qkv_moment, qkv_average, step_size, "update_qkv",
    )
    mix_new = update(
        attn_shares, (1, 1, R, width), lambda p: (3, p, 0, 0), (2,), (1, R, width), lambda p: (p, 0, 0),
        mix_weight, mix_moment, mix_average, step_size, "update_mix",
    )
    inner_new = update(
        inner_shares, (1, cut, hidden), lambda p, c, r: (2 * p + c, r, 0), (2, 2, R // cut),
        (1, cut, hidden), lambda p, c, r: (p, r, c), inner_weight, inner_moment, inner_average, step_size, "update_inner",
    )
    down_new = update(
        down_shares, (1, R2, half_width), lambda p, c: (2 * p + c, 0, 0), (2, 2),
        (1, R2, half_width), lambda p, c: (p, 0, c), down_weight, down_moment, down_average, step_size, "update_down",
    )
    own = norm_gains.shape[1]
    gains_grad = lax.dynamic_slice(gains_sum, (0, fs * own), (2, own))
    gains_new = (gains_grad,) + owner_update(norm_gains, gains_grad, gains_moment, gains_average, step_size)
    new = (qkv_new, mix_new, inner_new, down_new, gains_new)
    return (layer_out, frames_grad) + tuple(n[kind] for kind in range(4) for n in new)


def solution(mesh):
    rows = P(("dp", "fsdp"), None, None)
    weight = P(None, "fsdp", None)
    gains = P(None, "fsdp")
    weights = (weight,) * 4 + (gains,)
    return jax.shard_map(
        per_device,
        mesh=mesh,
        in_specs=(rows, rows, P()) + weights * 3,
        out_specs=(rows, rows) + weights * 4,
        check_vma=False,
    )
```

```python
import functools
import math

import jax
import jax.numpy as jnp
from jax import lax
from jax.experimental import pallas as pl
from jax.experimental.pallas import tpu as pltpu
from jax.sharding import PartitionSpec as P

HEADS = 16
Z = 4
MESH = pl.DeviceIdType.MESH
ANY = pl.BlockSpec(memory_space=pl.ANY)
BF = jnp.bfloat16
F32 = jnp.float32

norm_eps = 1e-05
momentum_rate = 0.5
average_rate = 0.5
step_rate = 0.05
VMEM_BYTES = 60 * 1024 * 1024


def nn(a, b):
    return lax.dot_general(a, b, (((1,), (0,)), ((), ())), preferred_element_type=F32)


def nt(a, b):
    return lax.dot_general(a, b, (((1,), (1,)), ((), ())), preferred_element_type=F32)


def tn(a, b):
    return lax.dot_general(a, b, (((0,), (0,)), ((), ())), preferred_element_type=F32)


def scale_rows(values):
    square = jnp.mean(values * values, axis=-1, keepdims=True) + norm_eps
    inverse = lax.rsqrt(square)
    return inverse * (1.5 - 0.5 * square * inverse * inverse)


def norm_back(grad_in, normed, gain_row, inverse):
    scaled = grad_in * gain_row
    return inverse * (scaled - normed * jnp.mean(scaled * normed, axis=-1, keepdims=True))


def owner_update(weight, gradient, moment, average, step_size):
    moment_new = momentum_rate * moment + gradient
    weight_new = weight - step_size * (gradient + momentum_rate * moment_new)
    average_new = average_rate * average + (1.0 - average_rate) * weight_new
    return (moment_new, average_new, weight_new)


PAIRS = ((0, 0), (0, 1), (0, 2), (1, 0), (1, 1), (1, 2), (1, 3))
SPANS = ((0, range(0, 3)), (1, range(3, 7)))
CHUNK = 128
STEP = 256


def total_of(values):
    return functools.reduce(jnp.add, values)


def remote_copy(src, dst, send_sem, recv_sem, peer):
    return pltpu.make_async_remote_copy(
        src_ref=src, dst_ref=dst, send_sem=send_sem, recv_sem=recv_sem, device_id=peer, device_id_type=MESH
    )


def head_ones(lanes, head_size):
    row = lax.broadcasted_iota(jnp.int32, (lanes, lanes), 0) // head_size
    column = lax.broadcasted_iota(jnp.int32, (lanes, lanes), 1) // head_size
    return (row == column).astype(BF)


def per_head(left, right, ones):
    rows = left[0].shape[0]
    products = [(left[p] * right[n]).astype(BF) for p, n in PAIRS]
    sums = nn(jnp.concatenate(products, axis=0), ones)
    return [sums[m * rows : (m + 1) * rows] for m in range(len(PAIRS))]


def head_probs(scores, span, allowed, scale):
    s = [jnp.where(allowed, scores[m] * scale, -1e30) if PAIRS[m][1] < 2 else scores[m] * scale for m in span]
    top = functools.reduce(jnp.maximum, s)
    e = [jnp.exp(value - top) for value in s]
    e = [jnp.where(allowed, value, 0.0) if PAIRS[m][1] < 2 else value for m, value in zip(span, e)]
    inverse = 1.0 / total_of(e)
    return [value * inverse for value in e]


def forward_kernel(
    X, groups, head_size, frames, carried, cot, gains_own, qkv_weight, mix_weight, inner_weight, down_weight,
    attn, inner, down, gains_out, inputs_out, rows_out, mixed_out, edge_out, hres_out, b_rows, c_rows,
    attn_wide, inner_wide, down_wide, attn_own, inner_own, down_own,
    gains, inputs, rows_in, mixed, before, hres, b, proj, mix, edge_send, edge_recv,
    send_up, recv_up, send_down, recv_down, send_x, recv_x, send_y, recv_y, send_c, recv_c, send_r, recv_r,
    send_g, recv_g, send_e, recv_e, send_b, recv_b, send_q, recv_q, local_sem, out_sem, wide_sem,
):
    dp, fs = lax.axis_index("dp"), lax.axis_index("fsdp")
    F = Z * X
    y, core = dp // 2, dp % 2
    z, x = fs // X, fs % X
    me = dp * F + fs
    devices = 4 * F
    count = frames.shape[1]
    core_peer = (y * 2 + 1 - core, fs)
    y_peer = ((1 - y) * 2 + core, fs)
    up_peer = (dp, lax.rem(z + 1, Z) * X + x)
    down_peer = (dp, lax.rem(z + Z - 1, Z) * X + x)
    before_me = ((me - 1 + devices) % devices // F, (me - 1 + devices) % devices % F)
    after_me = ((me + 1) % devices // F, (me + 1) % devices % F)

    def z_peer(k):
        return (dp, lax.rem(z + k, Z) * X + x)

    def x_peer(i):
        return (dp, z * X + lax.rem(x + i, X))

    UNITS = unit_list(groups, inner_own.shape[1], down_own.shape[1])

    width = frames.shape[2]

    def wide(slot):
        return (attn_wide.at[slot] if slot < groups + 1 else (inner_wide, down_wide)[slot - groups - 1])

    def fetch(slot, src, condition=None):
        copy = pltpu.make_async_copy(src, wide(slot), wide_sem.at[slot])
        if condition is None:
            copy.start()
        else:
            pl.when(condition)(copy.start)

    def columns_of(weight, part, block):
        return weight.at[:, :, pl.ds(pl.multiple_of(part * width + block * STEP, STEP), STEP)]

    def fetch_all():
        for n in range(groups - 1):
            fetch(n, columns_of(qkv_weight, jnp.minimum(dp, 2), n), dp < 3)
            fetch(n, columns_of(mix_weight, 0, n), dp == 3)
        fetch(groups - 1, columns_of(qkv_weight, core, groups - 1))
        fetch(groups, columns_of(qkv_weight, 2, groups - 1), core == 0)
        fetch(groups, columns_of(mix_weight, 0, groups - 1), core == 1)
        half, hidden = width // 2, inner_own.shape[1]
        fetch(groups + 1, inner_weight.at[y, :, pl.ds(pl.multiple_of(core * hidden, 128), hidden)])
        fetch(groups + 2, down_weight.at[y, :, pl.ds(pl.multiple_of(core * half, 128), half)])

    def take(slot):
        pltpu.make_async_copy(wide(slot), wide(slot), wide_sem.at[slot]).wait()
        if slot < groups + 1:
            attn_own[slot] = attn_wide[slot].astype(BF)
        elif slot == groups + 1:
            inner_own[...] = inner_wide[...].astype(BF)
        else:
            down_own[...] = down_wide[...].astype(BF)

    def own(u):
        kind, n, columns = UNITS[u][:3]
        if kind in ("quarter", "low", "high"):
            return attn_own.at[n if kind != "high" else n + 1]
        return (down_own if kind == "down" else inner_own).at[:, columns]

    def part_of(u, core_index, plane):
        kind = UNITS[u][0]
        if kind == "quarter":
            return plane * 2 + core_index
        return 2 + core_index if kind == "high" else core_index

    def whole(u, part):
        kind, n, columns = UNITS[u][:3]
        if kind == "down":
            return down.at[part, :, columns]
        if kind == "inner":
            return inner.at[part, :, columns]
        return attn.at[n, part]

    def place(u, source, part=None):
        kind, n, columns = UNITS[u][:3]
        part = part_of(u, core, y) if part is None else part
        if kind == "down":
            R = down_own.shape[0]
            return down.at[part, pl.ds(source * R, R), columns]
        if kind == "inner":
            R = inner_own.shape[0]
            return inner.at[part, pl.ds(source * R, R), columns]
        R = attn_own.shape[2]
        return attn.at[n, part, :, pl.ds(source * R, R), :]

    fetch_all()
    barrier = pltpu.get_barrier_semaphore()
    peers = [z_peer(k) for k in range(1, Z)] + [x_peer(i) for i in range(1, X)]
    peers += [core_peer, y_peer, before_me, after_me]
    for peer in peers:
        pl.semaphore_signal(barrier, inc=1, device_id=peer, device_id_type=MESH)
    pl.semaphore_wait(barrier, len(peers))

    sent, local = [], []

    def send(condition, make):
        remote_copy(*make()).start()
        sent.append((condition, make))

    def wait_send(condition, make):
        def action():
            remote_copy(*make()).wait_send()

        if condition is None:
            action()
        else:
            pl.when(condition())(action)

    def wait_recv(dst, recv_sem, send_sem):
        remote_copy(dst, dst, send_sem, recv_sem, core_peer).wait_recv()

    def store(src, dst):
        copy = pltpu.make_async_copy(src, dst, out_sem.at[len(local)])
        copy.start()
        local.append(copy)

    def spread(u, row, mine, condition):
        def src():
            return own(u) if mine else place(u, row() * X + x)

        for i in range(1, X):
            send(
                condition,
                lambda i=i: (
                    src(), place(u, row() * X + x), send_x.at[u, row(), i], recv_x.at[u, row(), i], x_peer(i)
                ),
            )
        to_plane(u, lambda: row() * X + x, src, condition)

    def to_plane(u, source, src, condition):
        if UNITS[u][0] == "quarter":
            send(
                condition,
                lambda: (src(), place(u, source()), send_y.at[u, source()], recv_y.at[u, source()], y_peer),
            )

    def crossed(u):
        return UNITS[u][3]

    def block(u, row):
        kind, n, columns = UNITS[u][:3]
        array, R = (down, down_own.shape[0]) if kind == "down" else (inner, inner_own.shape[0])
        return array.at[core, pl.ds(row * X * R, X * R), columns]

    def send_along(u, src, dst):
        def below_top():
            return z < Z - 1

        def above_bottom():
            return z > 0

        def upward():
            return (src(), dst(), send_up.at[u, 1], recv_up.at[u, 1], up_peer)

        def downward():
            return (src(), dst(), send_down.at[u, 1], recv_down.at[u, 1], down_peer)

        pl.when(below_top())(lambda: send(below_top, upward))
        pl.when(above_bottom())(lambda: send(above_bottom, downward))

    def start_unit(u):
        for slot in slots_of[u]:
            take(slot)
        if not crossed(u):
            send_along(u, lambda: own(u), lambda: place(u, fs))
        spread(u, lambda: z, True, None)
        store(own(u), place(u, fs))

    def turn(u):
        for i in range(1, X):
            column = lax.rem(x - i + X, X)
            wait_recv(place(u, z * X + column), recv_x.at[u, z, i], send_x.at[u, z, i])
        local[own_store[u]].wait()
        send_along(u, lambda: block(u, z), lambda: block(u, z))

    def hop(u, k):
        def side(reached, row, further, send_sem, recv_sem, peer):
            def here():
                return block(u, row()) if crossed(u) else place(u, row() * X + x)

            def both():
                return reached() & further()

            def action():
                wait_recv(here(), recv_sem.at[u, k], send_sem.at[u, k])
                if k < Z - 1:
                    pl.when(further())(
                        lambda: send(
                            both, lambda: (here(), here(), send_sem.at[u, k + 1], recv_sem.at[u, k + 1], peer)
                        )
                    )
                if not crossed(u):
                    spread(u, row, False, reached)

            pl.when(reached())(action)

        side(lambda: z >= k, lambda: z - k, lambda: z < Z - 1, send_up, recv_up, up_peer)
        side(lambda: z + k < Z, lambda: z + k, lambda: z > 0, send_down, recv_down, down_peer)

    def arrivals(u):
        for row in range(0 if crossed(u) else Z):
            for i in range(1, X):
                column = lax.rem(x - i + X, X)
                source = row * X + column
                wait_recv(place(u, source), recv_x.at[u, row, i], send_x.at[u, row, i])
                to_plane(u, lambda source=source: source, lambda source=source: place(u, source), None)
        if not crossed(u):
            local[own_store[u]].wait()
        mine = whole(u, part_of(u, core, y))
        send(None, lambda: (mine, mine, send_c.at[u], recv_c.at[u], core_peer))

    def relay(u):
        if UNITS[u][0] != "quarter":
            return
        part = (1 - y) * 2 + core
        for source in range(F):
            wait_recv(place(u, source, part), recv_y.at[u, source], send_y.at[u, source])
        theirs = whole(u, part)
        send(None, lambda: (theirs, theirs, send_r.at[u], recv_r.at[u], core_peer))

    def complete(u):
        wait_recv(whole(u, part_of(u, 1 - core, y)), recv_c.at[u], send_c.at[u])
        if UNITS[u][0] == "quarter":
            wait_recv(whole(u, (1 - y) * 2 + 1 - core), recv_r.at[u], send_r.at[u])

    scale = 1.0 / math.sqrt(head_size)

    def gather_gains():
        keep = pltpu.make_async_copy(gains_own, gains.at[fs], local_sem.at[0])
        keep.start()
        for k in range(1, Z):
            send(None, lambda k=k: (gains_own, gains.at[fs], send_g.at[0, k], recv_g.at[0, k], z_peer(k)))
        for i in range(1, X):
            send(None, lambda i=i: (gains_own, gains.at[fs], send_g.at[i, 0], recv_g.at[i, 0], x_peer(i)))
        keep.wait()

    def chunk_source(k, i):
        return lax.rem(z - k + Z, Z) * X + lax.rem(x - i + X, X)

    def pass_gains():
        for k in range(1, Z):
            here = gains.at[chunk_source(k, 0)]
            wait_recv(here, recv_g.at[0, k], send_g.at[0, k])
            for i in range(1, X):
                send(
                    None,
                    lambda here=here, i=i, k=k: (here, here, send_g.at[i, k], recv_g.at[i, k], x_peer(i)),
                )

    def take_gains():
        for k in range(Z):
            for i in range(1, X):
                wait_recv(gains.at[chunk_source(k, i)], recv_g.at[i, k], send_g.at[i, k])
        total = gains[0]
        for source in range(1, F):
            total = total + gains[source]
        gains_out[...] = total

    def norm_rows():
        def chunk(c, carry):
            rows = pl.ds(pl.multiple_of(c * CHUNK, CHUNK), CHUNK)
            for p in range(2):
                value = frames[p, rows, :].astype(F32)
                inputs[p, rows, :] = (value * scale_rows(value) * gains_out[0:1, :]).astype(BF)
            return carry

        lax.fori_loop(0, count // CHUNK, chunk, 0)
        store(inputs, inputs_out)

    def heads(m):
        columns = slice(m * STEP, (m + 1) * STEP)
        load = pltpu.make_async_copy(attn.at[m, pl.ds(0, 3)], proj, local_sem.at[0])
        load.start()
        load.wait()
        for t in (1, 2, 0):
            for p in range(2):
                rows_in[t, p, :, columns] = nn(inputs[p], proj[t, p]).astype(BF)
                if t > 0:
                    tail = rows_in[t, p, count - 16 :, columns].astype(F32)
                    row = 2 * (t - 1) + p
                    edge_send[m, row : row + 1, :] = tail[15:16, :]
            if t == 2:
                to_after = remote_copy(edge_send.at[m], edge_recv.at[m], send_e.at[m], recv_e.at[m], after_me)
                pl.when(me < devices - 1)(to_after.start)
        pl.when(me > 0)(to_after.wait_recv)
        first = lax.broadcasted_iota(jnp.int32, (count, STEP), 0) == 0
        for t in range(2):
            for p in range(2):
                n = 2 * t + p
                shifted = pltpu.roll(rows_in[1 + t, p, :, columns].astype(F32), 1, 0)
                before[n] = jnp.where(first, edge_recv[m, n : n + 1, :], shifted)
        ones = head_ones(STEP, head_size)

        def chunk(c, carry):
            rows = pl.ds(pl.multiple_of(c * CHUNK, CHUNK), CHUNK)
            allowed = jnp.broadcast_to(carried[rows, :], (CHUNK, STEP)) > 0.5
            queries, here_k, here_v = (
                [rows_in[t, p, rows, columns].astype(F32) for p in range(2)] for t in range(3)
            )
            keys = [before[p, rows, :] for p in range(2)] + here_k
            values = [before[2 + p, rows, :] for p in range(2)] + here_v
            scores = per_head(queries, keys, ones)
            for p, span in SPANS:
                probs = head_probs(scores, span, allowed, scale)
                terms = [pr.astype(BF).astype(F32) * values[PAIRS[n][1]] for n, pr in zip(span, probs)]
                mixed[p, rows, columns] = total_of(terms).astype(BF)
            return carry

        lax.fori_loop(0, count // CHUNK, chunk, 0)

    def load_mix():
        return pltpu.make_async_copy(attn.at[:, 3], mix, local_sem.at[1])

    def finish_rows():
        load_mix().wait()
        for turn in range(2):
            p = 1 - y if turn == 0 else y
            for m in range(groups):
                columns = slice(m * STEP, (m + 1) * STEP)
                hres[p, :, columns] = frames[p, :, columns].astype(F32) + nn(mixed[p], mix[m, p])

            def chunk(c, carry):
                rows = pl.ds(pl.multiple_of(c * CHUNK, CHUNK), CHUNK)
                value = hres[p, rows, :]
                b[turn, rows, :] = (value * scale_rows(value) * gains_out[1:2, :]).astype(BF)
                return carry

            lax.fori_loop(0, count // CHUNK, chunk, 0)
            if turn == 0:
                send(None, lambda: (b.at[0], b_rows.at[1], send_b, recv_b, y_peer))
            else:
                store(b.at[1], b_rows.at[0])
        store(hres, hres_out)

    @pl.when(me == 0)
    def _():
        edge_recv[...] = jnp.zeros_like(edge_recv)

    slots_of = [
        [n] if kind in ("quarter", "low") else [n + 1] if kind == "high" else [] for kind, n, *_ in UNITS
    ]
    slots_of[[u[0] for u in UNITS].index("inner")] = [groups + 1]
    slots_of[[u[0] for u in UNITS].index("down")] = [groups + 2]
    own_store = {}
    last_of = {kind_n[1]: u for u, kind_n in enumerate(UNITS) if kind_n[0] in ("quarter", "low", "high")}
    last_plane = max(u for u, kind_n in enumerate(UNITS) if kind_n[0] == "quarter")
    store(cot.at[y], c_rows.at[0])
    gather_gains()
    for tick in range(len(UNITS) + Z + 2):
        if tick < len(UNITS):
            own_store[tick] = len(local)
            start_unit(tick)
        if 0 <= tick - 1 < len(UNITS) and crossed(tick - 1):
            turn(tick - 1)
        for k in range(1, Z):
            u = tick - k
            if 0 <= u < len(UNITS) and not crossed(u):
                hop(u, k)
            u = tick - k - 1
            if 0 <= u < len(UNITS) and crossed(u):
                hop(u, k)
        if tick == 1:
            pass_gains()
        if tick == 2:
            take_gains()
            norm_rows()
        u = tick - Z
        if 0 <= u < len(UNITS):
            arrivals(u)
            if u == last_plane:
                send(None, lambda: (cot.at[1 - y], c_rows.at[1], send_q, recv_q, y_peer))
        u = tick - Z - 1
        if 0 <= u < len(UNITS):
            relay(u)
            complete(u)
            for m in range(groups):
                if last_of[m] == u:
                    if m == groups - 1:
                        load_mix().start()
                    heads(m)
                    if m == groups - 1:
                        store(rows_in, rows_out)
                        store(mixed, mixed_out)
                        store(edge_recv, edge_out)
                        finish_rows()
    wait_recv(b_rows.at[1], recv_b, send_b)
    wait_recv(c_rows.at[1], recv_q, send_q)
    for condition, make in sent:
        wait_send(condition, make)
    for n, copy in enumerate(local):
        if n not in own_store.values():
            copy.wait()

    @pl.when(me < devices - 1)
    def _():
        for m in range(groups):
            remote_copy(edge_send.at[m], edge_recv.at[m], send_e.at[m], recv_e.at[m], after_me).wait_send()


def unit_list(groups, inner_width, down_width):
    units = [("quarter", n, None, False) for n in range(groups - 1)]
    units += [("low", groups - 1, None, False), ("high", groups - 1, None, False)]
    units += [("down", 0, slice(0, down_width // 2), True), ("down", 0, slice(down_width // 2, down_width), False)]
    tiles = inner_width // 128
    cuts = [128 * (tiles * n // 4) for n in range(5)]
    return units + [("inner", 0, slice(lo, hi), n == 1) for n, (lo, hi) in enumerate(zip(cuts, cuts[1:]))]


def forward(
    frames, carried, cot, gains_own, qkv_weight, mix_weight, inner_weight, down_weight, head_size, fsdp_count
):
    X = fsdp_count // Z
    _, count, width = frames.shape
    R, R2 = qkv_weight.shape[1], down_weight.shape[1]
    hidden, half = inner_weight.shape[2] // 2, width // 2
    groups = width // STEP
    units = len(unit_list(groups, hidden, half))
    dma, vmem = pltpu.SemaphoreType.DMA, pltpu.VMEM
    whole = pl.BlockSpec(memory_space=pltpu.VMEM)
    act = jax.ShapeDtypeStruct((2, count, width), BF)
    return pl.pallas_call(
        functools.partial(forward_kernel, X, groups, head_size),
        out_shape=(
            jax.ShapeDtypeStruct((groups, 4, 2, R * fsdp_count, STEP), BF),
            jax.ShapeDtypeStruct((2, R * fsdp_count, hidden), BF),
            jax.ShapeDtypeStruct((2, R2 * fsdp_count, half), BF),
            jax.ShapeDtypeStruct(gains_own.shape, F32),
            act,
            jax.ShapeDtypeStruct((3, 2, count, width), BF),
            act,
            jax.ShapeDtypeStruct((groups, 8, STEP), F32),
            jax.ShapeDtypeStruct((2, count, width), F32),
            act,
            act,
        ),
        in_specs=[whole] * 4 + [ANY] * 4,
        out_specs=(ANY,) * 3 + (whole,) + (ANY,) * 7,
        scratch_shapes=[
            vmem((groups + 1, 2, R, STEP), F32), vmem((R, hidden), F32), vmem((R2, half), F32),
            vmem((groups + 1, 2, R, STEP), BF), vmem((R, hidden), BF), vmem((R2, half), BF),
            vmem((fsdp_count,) + gains_own.shape, F32),
            vmem((2, count, width), BF), vmem((3, 2, count, width), BF), vmem((2, count, width), BF),
            vmem((4, count, STEP), F32), vmem((2, count, width), F32), vmem((2, count, width), BF),
            vmem((3, 2, width, STEP), BF), vmem((groups, 2, width, STEP), BF),
            vmem((groups, 8, STEP), F32), vmem((groups, 8, STEP), F32),
            dma((units, Z)), dma((units, Z)), dma((units, Z)), dma((units, Z)),
            dma((units, Z, X)), dma((units, Z, X)), dma((groups, fsdp_count)), dma((groups, fsdp_count)),
            dma((units,)), dma((units,)), dma((groups,)), dma((groups,)),
            dma((X, Z)), dma((X, Z)), dma((groups,)), dma((groups,)), dma, dma, dma, dma,
            dma((2,)), dma((units + 8,)), dma((groups + 3,)),
        ],
        compiler_params=pltpu.CompilerParams(
            vmem_limit_bytes=VMEM_BYTES, collective_id=0, has_side_effects=True
        ),
        name="attention_forward",
    )(frames, carried, cot, gains_own, qkv_weight, mix_weight, inner_weight, down_weight)


def feed_forward_kernel(
    X, J, b, c, inner, down, out_mine, back_mine, out_theirs, back_recv, inner_all, down_columns, down_sum,
    out, back, acts, down_here, down_there, down_from_core, down_stage, down_column, down_from_x, mine, other, from_core, summed, from_x, column, from_z, final, staged,
    s1, r1, s2, r2, s3, r3, s5, r5, s6, r6, s7, r7, local_sem,
    s_stage, s_own, sdx, rdx, s_column,
):
    j = pl.program_id(0)
    half = down.shape[2]
    rows_here = out_mine.shape[0]
    R, step = final.shape[1:]
    dp, fs = lax.axis_index("dp"), lax.axis_index("fsdp")
    y, core = dp // 2, dp % 2
    z, x = fs // X, fs % X
    core_peer = (y * 2 + 1 - core, fs)
    y_peer = ((1 - y) * 2 + core, fs)

    def z_peer(k):
        return (dp, lax.rem(z + k, Z) * X + x)

    def x_peer(i):
        return (dp, z * X + lax.rem(x + i, X))

    def dp_peer(d):
        return (((y + d // 2) % 2) * 2 + (core + d % 2) % 2, fs)

    def to_core(n):
        return remote_copy(other.at[n % 2], from_core.at[n], s1.at[n % 2], r1.at[n], core_peer)

    def to_x(n, i):
        return remote_copy(
            summed.at[n % 2, :, lax.rem(x + i, X)], from_x.at[n, i - 1], s2.at[n % 2, i - 1], r2.at[n, i - 1], x_peer(i)
        )

    def to_z(n, k):
        return remote_copy(
            column.at[n % 2, lax.rem(z + k, Z)], from_z.at[n, k - 1], s3.at[n % 2, k - 1], r3.at[n, k - 1], z_peer(k)
        )

    def place(n, owner):
        return inner_all.at[owner, :, pl.ds(pl.multiple_of(n * step, step), step)]

    def share(n, d):
        return remote_copy(final.at[n], place(n, dp), s5.at[n, d - 1], r5.at[n, d - 1], dp_peer(d))

    def keep(n):
        return pltpu.make_async_copy(final.at[n], place(n, dp), local_sem.at[n])

    exchange = remote_copy(staged, back_recv, s6, r6, y_peer)

    R2 = down_column.shape[1]
    ends = [-(-(g + 1) * X * R2 // step) - 1 for g in range(Z)]

    def down_rows(g, column):
        return down_sum.at[pl.ds((g * X + column) * R2, R2), :]

    def down_store(n):
        return pltpu.make_async_copy(
            down_stage.at[n % 2], down_sum.at[pl.ds(pl.multiple_of(n * step, step), step), :], s_stage.at[n % 2]
        )

    def down_load(g):
        return pltpu.make_async_copy(down_rows(g, x), down_column.at[g], s_own.at[g])

    def down_to_x(g, i):
        return remote_copy(
            down_rows(g, lax.rem(x + i, X)), down_from_x.at[g, i - 1], sdx.at[g, i - 1], rdx.at[g, i - 1], x_peer(i)
        )

    def down_keep(g):
        return pltpu.make_async_copy(down_column.at[g], down_columns.at[g], s_column.at[g])

    def down_to_core(n):
        return remote_copy(down_there.at[n % 2], down_from_core.at[n], s7.at[n % 2], r7.at[n], core_peer)

    @pl.when(j == 0)
    def _():
        barrier = pltpu.get_barrier_semaphore()
        peers = [z_peer(k) for k in range(1, Z)] + [x_peer(i) for i in range(1, X)]
        peers += [dp_peer(d) for d in range(1, 4)]
        for peer in peers:
            pl.semaphore_signal(barrier, inc=1, device_id=peer, device_id_type=MESH)
        pl.semaphore_wait(barrier, len(peers))
        out[...] = jnp.zeros_like(out)
        back[...] = jnp.zeros_like(back)

    @pl.when(j < J)
    def _():
        rows, cot = b[...], c[...]
        gate = nn(rows, inner[0])
        up = nn(rows, inner[1])
        squashed = jax.nn.sigmoid(gate)
        active = gate * squashed
        hidden = (active * up).astype(BF)
        hidden_grad = nt(cot[:, :half], down[0]) + nt(cot[:, half:], down[1])
        gate_grad = (hidden_grad * up * (squashed * (1.0 + gate * (1.0 - squashed)))).astype(BF)
        up_grad = (hidden_grad * active).astype(BF)
        acts[0] = hidden
        acts[1] = gate_grad
        acts[2] = up_grad

    @pl.when((j >= 2) & (j < J + 2))
    def _():
        down_store(j - 2).wait()

    for g in range(Z):
        @pl.when(j == ends[g] + 2)
        def _():
            for i in range(1, X):
                down_to_x(g, i).start()
            down_load(g).start()

    @pl.when((j >= 1) & (j < J + 1))
    def _():
        n = j - 1
        to_core(n).wait_recv()

        @pl.when(n >= 2)
        def _():
            for i in range(1, X):
                to_x(n - 2, i).wait_send()

        down_to_core(n).wait_recv()
        down_stage[n % 2] = (down_here[n % 2].astype(F32) + down_from_core[n].astype(F32)).astype(BF)
        down_store(n).start()
        total = (mine[n % 2].astype(F32) + from_core[n].astype(F32)).astype(BF)
        summed[n % 2] = total.reshape(summed.shape[1:])
        for i in range(1, X):
            to_x(n, i).start()

    @pl.when((j >= 2) & (j < J + 2))
    def _():
        n = j - 2
        for i in range(1, X):
            to_x(n, i).wait_recv()

        @pl.when(n >= 2)
        def _():
            for k in range(1, Z):
                to_z(n - 2, k).wait_send()

        total = summed[n % 2, :, x].astype(F32)
        for i in range(1, X):
            total = total + from_x[n, i - 1].astype(F32)
        column[n % 2] = total.astype(BF)
        for k in range(1, Z):
            to_z(n, k).start()

    for g in range(Z):
        @pl.when(j == min(ends[g] + 4, J + 2))
        def _():
            down_load(g).wait()
            for i in range(1, X):
                down_to_x(g, i).wait_recv()
            total = down_column[g].astype(F32) + total_of([down_from_x[g, i].astype(F32) for i in range(X - 1)])
            down_column[g] = total.astype(BF)
            down_keep(g).start()

    @pl.when((j >= 3) & (j < J + 3))
    def _():
        n = j - 3
        for k in range(1, Z):
            to_z(n, k).wait_recv()
        total = column[n % 2, z].astype(F32)
        for k in range(1, Z):
            total = total + from_z[n, k - 1].astype(F32)
        final[n] = total.astype(BF)
        keep(n).start()
        for d in range(1, 4):
            share(n, d).start()

    @pl.when(j < J)
    def _():
        rows, cot = b[...], c[...]
        hidden, gate_grad, up_grad = (acts[n] for n in range(3))
        gate_term = tn(rows, gate_grad).astype(BF)
        up_term = tn(rows, up_grad).astype(BF)

        @pl.when(j >= 2)
        def _():
            to_core(j - 2).wait_send()
            down_to_core(j - 2).wait_send()

        mine[j % 2] = jnp.where(core == 0, gate_term, up_term)
        other[j % 2] = jnp.where(core == 0, up_term, gate_term)
        to_core(j).start()
        down_term = tn(hidden, cot).astype(BF)
        down_here[j % 2] = jnp.where(core == 0, down_term[:, :half], down_term[:, half:])
        down_there[j % 2] = jnp.where(core == 0, down_term[:, half:], down_term[:, :half])
        down_to_core(j).start()
        for n in range(2):
            part = slice(n * half, (n + 1) * half)
            out[:, part] += nn(hidden, down[n])
        back[...] += nt(gate_grad, inner[0]) + nt(up_grad, inner[1])

    @pl.when(j == J - 1)
    def _():
        staged[...] = back[rows_here:, :].astype(BF)
        exchange.start()
        out_theirs[...] = out[rows_here:, :].astype(BF)
        out_mine[...] = out[:rows_here, :]
        back_mine[...] = back[:rows_here, :]

    @pl.when(j == J + 2)
    def _():
        for n in (J - 2, J - 1):
            to_core(n).wait_send()
            down_to_core(n).wait_send()
            for i in range(1, X):
                to_x(n, i).wait_send()
            for k in range(1, Z):
                to_z(n, k).wait_send()

        def finish(n, carry):
            keep(n).wait()
            for d in range(1, 4):
                share(n, d).wait()
            return carry

        lax.fori_loop(0, J, finish, 0)
        exchange.wait()
        for g in range(Z):
            down_keep(g).wait()
            for i in range(1, X):
                down_to_x(g, i).wait_send()


def feed_forward(b, c, inner, down, fsdp_count):
    rows, width = b.shape
    _, _, hidden = inner.shape
    half = down.shape[2]
    step = 256
    J = hidden // step
    X = fsdp_count // Z
    R, R2 = width // fsdp_count, hidden // fsdp_count
    whole = pl.BlockSpec((rows, width), lambda j: (0, 0), pipeline_mode=pl.Buffered(1))
    part = pl.BlockSpec((rows // 2, width), lambda j: (0, 0), pipeline_mode=pl.Buffered(1))
    inner_spec = pl.BlockSpec((2, width, step), lambda j: (0, 0, jnp.minimum(j, J - 1)))
    down_spec = pl.BlockSpec((2, step, half), lambda j: (0, jnp.minimum(j, J - 1), 0))
    dma, vmem = pltpu.SemaphoreType.DMA, pltpu.VMEM
    return pl.pallas_call(
        functools.partial(feed_forward_kernel, X, J),
        grid=(J + 3,),
        out_shape=(
            jax.ShapeDtypeStruct((rows // 2, width), F32),
            jax.ShapeDtypeStruct((rows // 2, width), F32),
            jax.ShapeDtypeStruct((rows // 2, width), BF),
            jax.ShapeDtypeStruct((rows // 2, width), BF),
            jax.ShapeDtypeStruct((4, R, hidden), BF),
            jax.ShapeDtypeStruct((Z, R2, half), BF),
            jax.ShapeDtypeStruct((hidden, half), BF),
        ),
        in_specs=[whole, whole, inner_spec, down_spec],
        out_specs=(part, part, part, ANY, ANY, ANY, ANY),
        scratch_shapes=[
            vmem((rows, width), F32), vmem((rows, width), F32), vmem((3, rows, step), BF),
            vmem((2, step, half), BF), vmem((2, step, half), BF), vmem((J, step, half), BF),
            vmem((2, step, half), BF), vmem((Z, R2, half), BF), vmem((Z, X - 1, R2, half), BF),
            vmem((2, width, step), BF), vmem((2, width, step), BF), vmem((J, width, step), BF),
            vmem((2, Z, X, R, step), BF), vmem((J, X - 1, Z, R, step), BF),
            vmem((2, Z, R, step), BF), vmem((J, Z - 1, R, step), BF),
            vmem((J, R, step), BF), vmem((rows // 2, width), BF),
            dma((2,)), dma((J,)), dma((2, X - 1)), dma((J, X - 1)), dma((2, Z - 1)), dma((J, Z - 1)),
            dma((J, 3)), dma((J, 3)), dma, dma, dma((2,)), dma((J,)), dma((J,)),
            dma((2,)), dma((Z,)), dma((Z, X - 1)), dma((Z, X - 1)), dma((Z,)),
        ],
        compiler_params=pltpu.CompilerParams(
            vmem_limit_bytes=VMEM_BYTES, collective_id=1, has_side_effects=True
        ),
        cost_estimate=pl.CostEstimate(flops=18 * rows * width * hidden, bytes_accessed=60 * 2**20, transcendentals=0),
        name="feed_forward",
    )(b, c, inner, down)


def total_of(values):
    return functools.reduce(jnp.add, values)


def attention_back_kernel(
    X, groups, head_size, carried, q, k, v, edge, mix, dhb, mixed, inputs, proj, gains, second_gain, frames_in, down_in, out_send,
    frames_grad, gains_sum, attn_all, down_all, out_recv,
    da, gain_terms, gain_from, mixed_grad, before, terms_before, terms_here, tails, grads, edge_send, edge_recv,
    mine, other, from_core, keep_y, send_y, from_y, summed, from_x, column, from_z, final, plane, from_plane, final_plane,
    down_mine, down_from_z, down_final,
    s_edge, r_edge, s1, r1, sy, ry, sxa, rxa, sxb, rxb, sz, rz, sf, rf, sp, rp, sc, rc, local_sem,
    s_out, r_out, sg, rg, frame_sem, sdz, rdz, sdf, rdf, down_sem, free,
):
    i = pl.program_id(0)
    frames, step = q.shape[2:]
    R, thin = final.shape[1:]
    subs = 2 * groups
    slots = from_core.shape[0]
    dp, fs = lax.axis_index("dp"), lax.axis_index("fsdp")
    F = Z * X
    y, core = dp // 2, dp % 2
    z, x = fs // X, fs % X
    me = dp * F + fs
    devices = 4 * F
    core_peer = (y * 2 + 1 - core, fs)
    y_peer = ((1 - y) * 2 + core, fs)
    before_me = ((me - 1 + devices) % devices // F, (me - 1 + devices) % devices % F)
    after_me = ((me + 1) % devices // F, (me + 1) % devices % F)

    def z_peer(n):
        return (dp, lax.rem(z + n, Z) * X + x)

    def x_peer(n):
        return (dp, z * X + lax.rem(x + n, X))

    def dp_peer(d):
        return (((y + d // 2) % 2) * 2 + (core + d % 2) % 2, fs)

    def to_before(n):
        return remote_copy(edge_send.at[n % 2], edge_recv.at[n], s_edge.at[n % 2], r_edge.at[n], before_me)

    def to_core(n):
        return remote_copy(other.at[n % 2], from_core.at[n % slots], s1.at[n % 2], r1.at[n % slots], core_peer)

    def to_y(n):
        return remote_copy(send_y.at[n % 2], from_y.at[n], sy.at[n % 2], ry.at[n], y_peer)

    def to_x_early(n, j):
        return remote_copy(
            summed.at[n % 3, pl.ds(1, 2), :, lax.rem(x + j, X)], from_x.at[n, j - 1, pl.ds(1, 2)],
            sxa.at[n % 3, j - 1], rxa.at[n, j - 1], x_peer(j),
        )

    def to_x_late(n, j):
        return remote_copy(
            summed.at[n % 3, 0, :, lax.rem(x + j, X)], from_x.at[n, j - 1, 0],
            sxb.at[n % 3, j - 1], rxb.at[n, j - 1], x_peer(j),
        )

    def to_z(n, j):
        return remote_copy(
            column.at[n % 2, :, lax.rem(z + j, Z)], from_z.at[n, j - 1], sz.at[n % 2, j - 1], rz.at[n, j - 1], z_peer(j)
        )

    def place(n, t):
        return attn_all.at[t, core, :, pl.ds(pl.multiple_of(n * thin, thin), thin)]

    def share(n, d):
        return remote_copy(final.at[n], place(n, y), sf.at[n, d - 1], rf.at[n, d - 1], dp_peer(d))

    def relay(n):
        return remote_copy(place(n, 1 - y), place(n, 1 - y), sf.at[n, 2], rf.at[n, 2], core_peer)

    def down_to_z(k):
        return remote_copy(
            down_in.at[lax.rem(z + k, Z)], down_from_z.at[k - 1], sdz.at[k - 1], rdz.at[k - 1], z_peer(k)
        )

    def down_share(d):
        return remote_copy(down_final, down_all.at[dp], sdf.at[d - 1], rdf.at[d - 1], dp_peer(d))

    def down_relay():
        part = down_all.at[(1 - y) * 2 + core]
        return remote_copy(part, part, sdf.at[2], rdf.at[2], core_peer)

    def to_plane(n):
        return remote_copy(plane.at[n], from_plane.at[n], sp.at[n], rp.at[n], y_peer)

    def share_core(n, t):
        return remote_copy(final_plane.at[n, t], place(n, 2 + t), sc.at[n, t], rc.at[n, t], core_peer)

    def keep(n, t):
        src = final.at[n] if t == 0 else final_plane.at[n, t - 1]
        return pltpu.make_async_copy(src, place(n, y if t == 0 else 1 + t), local_sem.at[n, t])

    def load_frames(g):
        dst = grads.at[g] if g < 3 else mixed_grad
        return pltpu.make_async_copy(frames_in.at[:, :, pl.ds(g * step, step)], dst, frame_sem.at[g])

    def gain_copy(level, n):
        peer = (core_peer, y_peer, x_peer(n + 1), z_peer(n + 1))[level]
        return remote_copy(gain_terms.at[level], gain_from.at[level, n], sg.at[level, n], rg.at[level, n], peer)

    down_load = pltpu.make_async_copy(down_in.at[z], down_mine, down_sem.at[0])
    down_keep = pltpu.make_async_copy(down_final, down_all.at[dp], down_sem.at[1])
    out_copy = remote_copy(out_send, out_recv, s_out, r_out, y_peer)

    @pl.when(i == 0)
    def _():
        barrier = pltpu.get_barrier_semaphore()
        peers = [z_peer(n) for n in range(1, Z)] + [x_peer(n) for n in range(1, X)]
        peers += [dp_peer(d) for d in range(1, 4)] + [before_me, after_me]
        for peer in peers:
            pl.semaphore_signal(barrier, inc=1, device_id=peer, device_id_type=MESH)
        pl.semaphore_wait(barrier, len(peers))
        out_copy.start()
        for k in range(1, Z):
            down_to_z(k).start()
        down_load.start()
        da[...] = jnp.zeros_like(da)

        @pl.when(me == devices - 1)
        def _():
            edge_recv[...] = jnp.zeros_like(edge_recv)

    def active(first):
        return (i >= first) & (i < first + subs)

    @pl.when(active(2))
    def _():
        n = i - 2
        to_core(n).wait_recv()

        @pl.when(n >= 2)
        def _():
            to_y(n - 2).wait_send()

        @pl.when(n >= 3)
        def _():
            for j in range(1, X):
                to_x_early(n - 3, j).wait_send()

        def both(t):
            return (mine[n % 2, t].astype(F32) + from_core[n % slots, t].astype(F32)).astype(BF)

        send_y[n % 2] = both(1 - y)
        to_y(n).start()
        for t in range(2):
            summed[n % 3, 1 + t] = both(2 + t).reshape(summed.shape[2:])
        for j in range(1, X):
            to_x_early(n, j).start()
        keep_y[n % 2] = both(y)

        @pl.when(n < subs - slots)
        def _():
            pl.semaphore_signal(free, inc=1, device_id=core_peer, device_id_type=MESH)

    @pl.when(active(3))
    def _():
        n = i - 3
        to_y(n).wait_recv()

        @pl.when(n >= 3)
        def _():
            for j in range(1, X):
                to_x_late(n - 3, j).wait_send()

        total = (keep_y[n % 2].astype(F32) + from_y[n].astype(F32)).astype(BF)
        summed[n % 3, 0] = total.reshape(summed.shape[2:])
        for j in range(1, X):
            to_x_late(n, j).start()

    @pl.when(active(4))
    def _():
        n = i - 4
        for j in range(1, X):
            to_x_early(n, j).wait_recv()
            to_x_late(n, j).wait_recv()

        @pl.when(n >= 2)
        def _():
            for j in range(1, Z):
                to_z(n - 2, j).wait_send()

        total = summed[n % 3, :, :, x].astype(F32) + total_of([from_x[n, j].astype(F32) for j in range(X - 1)])
        column[n % 2] = total.astype(BF)
        for j in range(1, Z):
            to_z(n, j).start()

    @pl.when(active(5))
    def _():
        n = i - 5
        for j in range(1, Z):
            to_z(n, j).wait_recv()
        total = column[n % 2, :, z].astype(F32) + total_of([from_z[n, j].astype(F32) for j in range(Z - 1)])
        total = total.astype(BF)
        final[n] = total[0]
        plane[n] = total[1:]
        to_plane(n).start()
        keep(n, 0).start()
        for d in range(1, 3):
            share(n, d).start()

    @pl.when(active(6))
    def _():
        n = i - 6
        to_plane(n).wait_recv()
        share(n, 2).wait_recv()
        relay(n).start()
        final_plane[n] = (plane[n].astype(F32) + from_plane[n].astype(F32)).astype(BF)
        for t in range(2):
            keep(n, t + 1).start()
            share_core(n, t).start()

    @pl.when(i == 4)
    def _():
        down_load.wait()
        for k in range(1, Z):
            down_to_z(k).wait_recv()
        total = down_mine[...].astype(F32) + total_of([down_from_z[k].astype(F32) for k in range(Z - 1)])
        down_final[...] = total.astype(BF)
        down_keep.start()
        for d in range(1, 3):
            down_share(d).start()

    @pl.when(i == 6)
    def _():
        down_share(2).wait_recv()
        down_relay().start()

    @pl.when((i < subs) & (i % 2 == 0))
    def _():
        m = i // 2
        slot = m % 2
        ones = head_ones(step, head_size)
        scale = 1.0 / math.sqrt(head_size)
        first = lax.broadcasted_iota(jnp.int32, (frames, step), 0) == 0
        last = lax.broadcasted_iota(jnp.int32, (frames, step), 0) == frames - 1
        for p in range(2):
            mixed_grad[p] = total_of(
                [nt(dhb[p, :, g * step : (g + 1) * step], mix[g, 0, p]) for g in range(groups)]
            ).astype(BF)
            before[p] = jnp.where(first, edge[0, p : p + 1, :], pltpu.roll(k[0, p].astype(F32), 1, 0))
            before[2 + p] = jnp.where(first, edge[0, 2 + p : 3 + p, :], pltpu.roll(v[0, p].astype(F32), 1, 0))

        def chunk(c, carry):
            rows = pl.ds(pl.multiple_of(c * CHUNK, CHUNK), CHUNK)
            allowed = jnp.broadcast_to(carried[rows, :], (CHUNK, step)) > 0.5
            queries = [q[0, p, rows, :].astype(F32) for p in range(2)]
            cots = [mixed_grad[p, rows, :].astype(F32) for p in range(2)]
            keys = [before[p, rows, :] for p in range(2)] + [k[0, p, rows, :].astype(F32) for p in range(2)]
            values = [before[2 + p, rows, :] for p in range(2)] + [v[0, p, rows, :].astype(F32) for p in range(2)]

            scores = per_head(queries, keys, ones)
            dprobs = per_head(cots, values, ones)
            key_grads, value_grads = [[] for _ in range(4)], [[] for _ in range(4)]
            for p, span in SPANS:
                probs = head_probs(scores, span, allowed, scale)
                mean = total_of([pr * dprobs[m] for m, pr in zip(span, probs)])
                query_grad = []
                for m, pr in zip(span, probs):
                    n = PAIRS[m][1]
                    ds = (pr * (dprobs[m] - mean)).astype(BF).astype(F32) * scale
                    query_grad.append(ds * keys[n])
                    key_grads[n].append(ds * queries[p])
                    value_grads[n].append(pr.astype(BF).astype(F32) * cots[p])
                grads[0, p, rows, :] = total_of(query_grad).astype(BF)
            for p in range(2):
                terms_before[p, rows, :] = total_of(key_grads[p])
                terms_before[2 + p, rows, :] = total_of(value_grads[p])
                terms_here[p, rows, :] = total_of(key_grads[2 + p])
                terms_here[2 + p, rows, :] = total_of(value_grads[2 + p])
            return carry

        lax.fori_loop(0, frames // CHUNK, chunk, 0)

        @pl.when((m >= 2) & (me > 0))
        def _():
            to_before(m - 2).wait_send()

        for row in range(4):
            edge_send[slot, row : row + 1, :] = terms_before[row, 0:1, :]

        @pl.when(me > 0)
        def _():
            to_before(m).start()

        for row in range(4):
            total = terms_here[row] + jnp.where(last, 0.0, pltpu.roll(terms_before[row], frames - 1, 0))
            grads[1 + row // 2, row % 2] = total.astype(BF)
            tails[row] = total[frames - 16 :, :]

    @pl.when((i < subs) & (i % 2 == 1))
    def _():
        m = i // 2

        @pl.when(me < devices - 1)
        def _():
            to_before(m).wait_recv()

        bottom = lax.broadcasted_iota(jnp.int32, (16, step), 0) == 15
        for row in range(4):
            fixed = tails[row] + jnp.where(bottom, edge_recv[m, row : row + 1, :], 0.0)
            grads[1 + row // 2, row % 2, frames - 16 :, :] = fixed.astype(BF)

        @pl.when(m >= 1)
        def _():
            for h in range(2):
                to_core(2 * m - 2 + h).wait_send()

        for t in range(4):
            pair = []
            for p in range(2):
                if t < 3:
                    pair.append(tn(inputs[p], grads[t, p]).astype(BF))
                else:
                    pair.append(tn(mixed[p], dhb[p, :, pl.ds(pl.multiple_of(m * step, step), step)]).astype(BF))
            here = jnp.where(core == 0, pair[0], pair[1])
            there = jnp.where(core == 0, pair[1], pair[0])
            for h in range(2):
                mine[h, t] = here[:, h * thin : (h + 1) * thin]
                other[h, t] = there[:, h * thin : (h + 1) * thin]

        @pl.when(m >= slots // 2)
        def _():
            pl.semaphore_wait(free, 2)

        for h in range(2):
            to_core(2 * m + h).start()
        for p in range(2):
            da[p] += total_of([nt(grads[t, p], proj[0, t, p]) for t in range(3)])

        @pl.when(m == groups - 1)
        def _():
            for g in range(groups):
                load_frames(g).start()

    @pl.when(i == subs)
    def _():
        for g in range(groups):
            load_frames(g).wait()

        def chunk(c, term):
            rows = pl.ds(pl.multiple_of(c * CHUNK, CHUNK), CHUNK)
            for p in range(2):
                pieces = [grads[g, p, rows, :] if g < 3 else mixed_grad[p, rows, :] for g in range(groups)]
                value = jnp.concatenate(pieces, axis=1).astype(F32)
                inverse = scale_rows(value)
                normed = value * inverse
                grad = da[p, rows, :]
                term = term + jnp.sum(grad * normed, axis=0, keepdims=True)
                total = dhb[p, rows, :].astype(F32) + norm_back(grad, normed, gains[0:1, :], inverse)
                frames_grad[p, rows, :] = total.astype(BF)
            return term

        term = lax.fori_loop(0, frames // CHUNK, chunk, jnp.zeros((1, da.shape[2]), F32))
        gain_terms[0] = second_gain[...]
        gain_terms[0, 0:1, :] = term
        gain_copy(0, 0).start()

    for level in range(1, 4):
        @pl.when(i == subs + level)
        def _():
            count = X - 1 if level == 3 else 1
            total = gain_terms[level - 1]
            for n in range(count):
                gain_copy(level - 1, n).wait()
                total = total + gain_from[level - 1, n]
            gain_terms[level] = total
            for n in range(Z - 1 if level == 3 else X - 1 if level == 2 else 1):
                gain_copy(level, n).start()

    @pl.when(i == subs + 4)
    def _():
        total = gain_terms[3]
        for n in range(Z - 1):
            gain_copy(3, n).wait()
            total = total + gain_from[3, n]
        gains_sum[...] = total

    @pl.when(i == subs + 5)
    def _():
        @pl.when(me > 0)
        def _():
            for n in (groups - 2, groups - 1):
                to_before(n).wait_send()

        for n in (subs - 3, subs - 2, subs - 1):
            for j in range(1, X):
                to_x_early(n, j).wait_send()
                to_x_late(n, j).wait_send()

        for n in (subs - 2, subs - 1):
            to_core(n).wait_send()
            to_y(n).wait_send()
            for j in range(1, Z):
                to_z(n, j).wait_send()

        def finish(n, carry):
            to_plane(n).wait_send()
            keep(n, 0).wait()
            share(n, 1).wait()
            share(n, 2).wait_send()
            relay(n).wait()
            for t in range(2):
                keep(n, t + 1).wait()
                share_core(n, t).wait()
            return carry

        lax.fori_loop(0, subs, finish, 0)
        out_copy.wait()
        for k in range(1, Z):
            down_to_z(k).wait_send()
        down_keep.wait()
        down_share(1).wait()
        down_share(2).wait_send()
        down_relay().wait()


def attention_back(
    carried, qkv_rows, edge, attn, dhb, mixed, inputs, gains, second_gain, frames_in, down_in, out_send, head_size, fsdp_count
):
    _, frames, width = dhb.shape
    step = STEP
    groups = width // step
    X = fsdp_count // Z
    R = width // fsdp_count

    def early(i):
        return jnp.minimum(i // 2, groups - 1)

    rows = [pl.BlockSpec((1, 2, frames, step), lambda i, t=t: (t, 0, 0, early(i))) for t in range(3)]
    edge_spec = pl.BlockSpec((1, 8, step), lambda i: (early(i), 0, 0))
    mask = pl.BlockSpec((frames, 1), lambda i: (0, 0), pipeline_mode=pl.Buffered(1))
    whole = pl.BlockSpec((2, frames, width), lambda i: (0, 0, 0), pipeline_mode=pl.Buffered(1))
    mix_spec = pl.BlockSpec((groups, 1, 2, step, step), lambda i: (0, 3, 0, early(i), 0))
    proj_spec = pl.BlockSpec((1, 3, 2, width, step), lambda i: (jnp.clip((i - 1) // 2, 0, groups - 1), 0, 0, 0, 0))
    line = pl.BlockSpec((8, width), lambda i: (0, 0), pipeline_mode=pl.Buffered(1))
    dma, vmem = pltpu.SemaphoreType.DMA, pltpu.VMEM
    thin = step // 2
    n, slots, peers = 2 * groups, 4, max(X, Z) - 1
    return pl.pallas_call(
        functools.partial(attention_back_kernel, X, groups, head_size),
        grid=(n + 6,),
        out_shape=(
            jax.ShapeDtypeStruct((2, frames, width), BF),
            jax.ShapeDtypeStruct((8, width), F32),
            jax.ShapeDtypeStruct((4, 2, R, width), BF),
            jax.ShapeDtypeStruct((4,) + down_in.shape[1:], BF),
            jax.ShapeDtypeStruct(out_send.shape, BF),
        ),
        in_specs=[mask, *rows, edge_spec, mix_spec, whole, whole, whole, proj_spec, line, line, ANY, ANY, ANY],
        out_specs=(whole, line, ANY, ANY, ANY),
        scratch_shapes=[
            vmem((2, frames, width), F32), vmem((4, 8, width), F32), vmem((4, peers, 8, width), F32),
            vmem((2, frames, step), BF), vmem((4, frames, step), F32), vmem((4, frames, step), F32),
            vmem((4, frames, step), F32), vmem((4, 16, step), F32), vmem((3, 2, frames, step), BF),
            vmem((2, 8, step), F32), vmem((groups, 8, step), F32),
            vmem((2, 4, width, thin), BF), vmem((2, 4, width, thin), BF), vmem((slots, 4, width, thin), BF),
            vmem((2, width, thin), BF), vmem((2, width, thin), BF), vmem((n, width, thin), BF),
            vmem((3, 3, Z, X, R, thin), BF), vmem((n, X - 1, 3, Z, R, thin), BF),
            vmem((2, 3, Z, R, thin), BF), vmem((n, Z - 1, 3, R, thin), BF),
            vmem((n, R, thin), BF), vmem((n, 2, R, thin), BF), vmem((n, 2, R, thin), BF), vmem((n, 2, R, thin), BF),
            vmem(down_in.shape[1:], BF), vmem((Z - 1,) + down_in.shape[1:], BF), vmem(down_in.shape[1:], BF),
            dma((2,)), dma((groups,)), dma((2,)), dma((slots,)), dma((2,)), dma((n,)),
            dma((3, X - 1)), dma((n, X - 1)), dma((3, X - 1)), dma((n, X - 1)),
            dma((2, Z - 1)), dma((n, Z - 1)), dma((n, 3)), dma((n, 3)), dma((n,)), dma((n,)),
            dma((n, 2)), dma((n, 2)), dma((n, 3)),
            dma, dma, dma((4, peers)), dma((4, peers)), dma((groups,)),
            dma((Z - 1,)), dma((Z - 1,)), dma((3,)), dma((3,)), dma((2,)), pltpu.SemaphoreType.REGULAR,
        ],
        compiler_params=pltpu.CompilerParams(vmem_limit_bytes=63 * 2**20, collective_id=2, has_side_effects=True),
        name="attention_back",
    )(
        carried, qkv_rows, qkv_rows, qkv_rows, edge, attn, dhb, mixed, inputs, attn,
        gains, second_gain, frames_in, down_in, out_send,
    )


def update_kernel(step_size, share, weight, moment, average, grad_out, moment_out, average_out, weight_out):
    gradient = share[...].reshape(weight.shape).astype(F32)
    moment_new, average_new, weight_new = owner_update(
        weight[...], gradient, moment[...], average[...], step_size
    )
    grad_out[...] = gradient
    moment_out[...] = moment_new
    average_out[...] = average_new
    weight_out[...] = weight_new


def update(shares, share_block, share_at, grid, block, at, weight, moment, average, step_size, name):
    share_spec = pl.BlockSpec(share_block, share_at)
    spec = pl.BlockSpec(block, at)
    return pl.pallas_call(
        functools.partial(update_kernel, step_size),
        grid=grid,
        out_shape=(jax.ShapeDtypeStruct(weight.shape, F32),) * 4,
        in_specs=[share_spec, spec, spec, spec],
        out_specs=(spec,) * 4,
        compiler_params=pltpu.CompilerParams(vmem_limit_bytes=VMEM_BYTES),
        name=name,
    )(shares, weight, moment, average)


def per_device(
    frames, cotangent, segment_ids,
    qkv_weight, mix_weight, inner_weight, down_weight, norm_gains,
    qkv_moment, mix_moment, inner_moment, down_moment, gains_moment,
    qkv_average, mix_average, inner_average, down_average, gains_average,
):
    frame_count, positions, width = frames.shape
    head_size = width // HEADS
    hidden = inner_weight.shape[2] // 2
    dp_count, fsdp_count = lax.axis_size("dp"), lax.axis_size("fsdp")
    X = fsdp_count // Z
    devices = dp_count * fsdp_count
    total_frames = frame_count * devices
    dp, fs = lax.axis_index("dp"), lax.axis_index("fsdp")
    y, core = dp // 2, dp % 2
    z, x = fs // X, fs % X
    axes = ("dp", "fsdp")

    device = dp * fsdp_count + fs
    padded_ids = jnp.concatenate([jnp.full((1,), -1, jnp.int32), segment_ids])
    window = lax.dynamic_slice_in_dim(padded_ids, device * frame_count, frame_count + 1)
    carried = (window[1:] == window[:-1]).astype(F32)[:, None]

    half_width = width // 2
    own_gains = norm_gains.astype(BF).astype(F32)
    gains_own = lax.dynamic_update_slice(jnp.zeros((8, width), F32), own_gains, (0, fs * own_gains.shape[1]))
    frames_by = frames.transpose(1, 0, 2)
    cot = cotangent.transpose(1, 0, 2)
    attn, inner, down, gains, a, qkv_rows, mixed, edge, hres, b_rows, c_rows = forward(
        frames_by, carried, cot, gains_own, qkv_weight, mix_weight, inner_weight, down_weight, head_size, fsdp_count
    )
    r2 = scale_rows(hres)
    n2 = hres * r2
    b_rows = b_rows.reshape(2 * frame_count, width)
    c_rows = c_rows.reshape(2 * frame_count, width)
    out, back, out_there, back_there, inner_shares, down_columns, _ = feed_forward(b_rows, c_rows, inner, down, fsdp_count)

    def by_position(mine, theirs):
        return jnp.where(y == 0, jnp.stack([mine, theirs]), jnp.stack([theirs, mine]))

    db = by_position(back, back_there.astype(F32))

    e2 = jnp.sum(db * n2, axis=(0, 1))
    dh = cot.astype(F32) + norm_back(db, n2, gains[1], r2)
    dhb = dh.astype(BF)
    second_gain = jnp.zeros((8, width), F32).at[1].set(e2)
    frames_grad, gains_sum, attn_shares, down_shares, out_here = attention_back(
        carried, qkv_rows, edge, attn, dhb, mixed, a, gains, second_gain, frames_by, down_columns, out_there, head_size, fsdp_count
    )
    frames_grad = frames_grad.transpose(1, 0, 2)
    layer_out = (hres + by_position(out, out_here.astype(F32))).astype(BF).transpose(1, 0, 2)

    step_size = step_rate / math.sqrt(total_frames)
    R, R2 = qkv_weight.shape[1], down_weight.shape[1]
    cut = min(R, 64)
    qkv_new = update(
        attn_shares, (1, 1, R, width), lambda p, t: (t, p, 0, 0), (2, 3), (1, R, width), lambda p, t: (p, 0, t),
        qkv_weight, qkv_moment, qkv_average, step_size, "update_qkv",
    )
    mix_new = update(
        attn_shares, (1, 1, R, width), lambda p: (3, p, 0, 0), (2,), (1, R, width), lambda p: (p, 0, 0),
        mix_weight, mix_moment, mix_average, step_size, "update_mix",
    )
    inner_new = update(
        inner_shares, (1, cut, hidden), lambda p, c, r: (2 * p + c, r, 0), (2, 2, R // cut),
        (1, cut, hidden), lambda p, c, r: (p, r, c), inner_weight, inner_moment, inner_average, step_size, "update_inner",
    )
    down_new = update(
        down_shares, (1, R2, half_width), lambda p, c: (2 * p + c, 0, 0), (2, 2),
        (1, R2, half_width), lambda p, c: (p, 0, c), down_weight, down_moment, down_average, step_size, "update_down",
    )
    own = norm_gains.shape[1]
    gains_grad = lax.dynamic_slice(gains_sum, (0, fs * own), (2, own))
    gains_new = (gains_grad,) + owner_update(norm_gains, gains_grad, gains_moment, gains_average, step_size)
    new = (qkv_new, mix_new, inner_new, down_new, gains_new)
    return (layer_out, frames_grad) + tuple(n[kind] for kind in range(4) for n in new)


def solution(mesh):
    rows = P(("dp", "fsdp"), None, None)
    weight = P(None, "fsdp", None)
    gains = P(None, "fsdp")
    weights = (weight,) * 4 + (gains,)
    return jax.shard_map(
        per_device,
        mesh=mesh,
        in_specs=(rows, rows, P()) + weights * 3,
        out_specs=(rows, rows) + weights * 4,
        check_vma=False,
    )
```

```python
import functools
import math

import jax
import jax.numpy as jnp
from jax import lax
from jax.experimental import pallas as pl
from jax.experimental.pallas import tpu as pltpu
from jax.sharding import PartitionSpec as P

HEADS = 16
Z = 4
MESH = pl.DeviceIdType.MESH
ANY = pl.BlockSpec(memory_space=pl.ANY)
BF = jnp.bfloat16
F32 = jnp.float32

norm_eps = 1e-05
momentum_rate = 0.5
average_rate = 0.5
step_rate = 0.05
VMEM_BYTES = 60 * 1024 * 1024


def nn(a, b):
    return lax.dot_general(a, b, (((1,), (0,)), ((), ())), preferred_element_type=F32)


def nt(a, b):
    return lax.dot_general(a, b, (((1,), (1,)), ((), ())), preferred_element_type=F32)


def tn(a, b):
    return lax.dot_general(a, b, (((0,), (0,)), ((), ())), preferred_element_type=F32)


def scale_rows(values):
    square = jnp.mean(values * values, axis=-1, keepdims=True) + norm_eps
    inverse = lax.rsqrt(square)
    return inverse * (1.5 - 0.5 * square * inverse * inverse)


def norm_back(grad_in, normed, gain_row, inverse):
    scaled = grad_in * gain_row
    return inverse * (scaled - normed * jnp.mean(scaled * normed, axis=-1, keepdims=True))


def owner_update(weight, gradient, moment, average, step_size):
    moment_new = momentum_rate * moment + gradient
    weight_new = weight - step_size * (gradient + momentum_rate * moment_new)
    average_new = average_rate * average + (1.0 - average_rate) * weight_new
    return (moment_new, average_new, weight_new)


PAIRS = ((0, 0), (0, 1), (0, 2), (1, 0), (1, 1), (1, 2), (1, 3))
SPANS = ((0, range(0, 3)), (1, range(3, 7)))
CHUNK = 128
STEP = 256


def total_of(values):
    return functools.reduce(jnp.add, values)


def remote_copy(src, dst, send_sem, recv_sem, peer):
    return pltpu.make_async_remote_copy(
        src_ref=src, dst_ref=dst, send_sem=send_sem, recv_sem=recv_sem, device_id=peer, device_id_type=MESH
    )


def head_ones(lanes, head_size):
    row = lax.broadcasted_iota(jnp.int32, (lanes, lanes), 0) // head_size
    column = lax.broadcasted_iota(jnp.int32, (lanes, lanes), 1) // head_size
    return (row == column).astype(BF)


def per_head(left, right, ones):
    rows = left[0].shape[0]
    products = [(left[p] * right[n]).astype(BF) for p, n in PAIRS]
    sums = nn(jnp.concatenate(products, axis=0), ones)
    return [sums[m * rows : (m + 1) * rows] for m in range(len(PAIRS))]


def head_probs(scores, span, allowed, scale):
    s = [jnp.where(allowed, scores[m] * scale, -1e30) if PAIRS[m][1] < 2 else scores[m] * scale for m in span]
    top = functools.reduce(jnp.maximum, s)
    e = [jnp.exp(value - top) for value in s]
    e = [jnp.where(allowed, value, 0.0) if PAIRS[m][1] < 2 else value for m, value in zip(span, e)]
    inverse = 1.0 / total_of(e)
    return [value * inverse for value in e]


def forward_kernel(
    X, groups, head_size, frames, carried, cot, gains_own, qkv_weight, mix_weight, inner_weight, down_weight,
    attn, inner, down, gains_out, inputs_out, rows_out, mixed_out, edge_out, hres_out, b_rows, c_rows,
    attn_wide, inner_wide, down_wide, attn_own, inner_own, down_own,
    gains, inputs, rows_in, mixed, before, hres, b, proj, mix, edge_send, edge_recv,
    send_up, recv_up, send_down, recv_down, send_x, recv_x, send_y, recv_y, send_c, recv_c, send_r, recv_r,
    send_g, recv_g, send_e, recv_e, send_b, recv_b, send_q, recv_q, local_sem, out_sem, wide_sem,
):
    dp, fs = lax.axis_index("dp"), lax.axis_index("fsdp")
    F = Z * X
    y, core = dp // 2, dp % 2
    z, x = fs // X, fs % X
    me = dp * F + fs
    devices = 4 * F
    count = frames.shape[1]
    core_peer = (y * 2 + 1 - core, fs)
    y_peer = ((1 - y) * 2 + core, fs)
    up_peer = (dp, lax.rem(z + 1, Z) * X + x)
    down_peer = (dp, lax.rem(z + Z - 1, Z) * X + x)
    before_me = ((me - 1 + devices) % devices // F, (me - 1 + devices) % devices % F)
    after_me = ((me + 1) % devices // F, (me + 1) % devices % F)

    def z_peer(k):
        return (dp, lax.rem(z + k, Z) * X + x)

    def x_peer(i):
        return (dp, z * X + lax.rem(x + i, X))

    UNITS = unit_list(groups, inner_own.shape[1], down_own.shape[1])

    width = frames.shape[2]

    def wide(slot):
        return (attn_wide.at[slot] if slot < groups + 1 else (inner_wide, down_wide)[slot - groups - 1])

    def fetch(slot, src, condition=None):
        copy = pltpu.make_async_copy(src, wide(slot), wide_sem.at[slot])
        if condition is None:
            copy.start()
        else:
            pl.when(condition)(copy.start)

    def columns_of(weight, part, block):
        return weight.at[:, :, pl.ds(pl.multiple_of(part * width + block * STEP, STEP), STEP)]

    def fetch_all():
        for n in range(groups - 1):
            fetch(n, columns_of(qkv_weight, jnp.minimum(dp, 2), n), dp < 3)
            fetch(n, columns_of(mix_weight, 0, n), dp == 3)
        fetch(groups - 1, columns_of(qkv_weight, core, groups - 1))
        fetch(groups, columns_of(qkv_weight, 2, groups - 1), core == 0)
        fetch(groups, columns_of(mix_weight, 0, groups - 1), core == 1)
        half, hidden = width // 2, inner_own.shape[1]
        fetch(groups + 1, inner_weight.at[y, :, pl.ds(pl.multiple_of(core * hidden, 128), hidden)])
        fetch(groups + 2, down_weight.at[y, :, pl.ds(pl.multiple_of(core * half, 128), half)])

    def take(slot):
        pltpu.make_async_copy(wide(slot), wide(slot), wide_sem.at[slot]).wait()
        if slot < groups + 1:
            attn_own[slot] = attn_wide[slot].astype(BF)
        elif slot == groups + 1:
            inner_own[...] = inner_wide[...].astype(BF)
        else:
            down_own[...] = down_wide[...].astype(BF)

    def own(u):
        kind, n, columns = UNITS[u][:3]
        if kind in ("quarter", "low", "high"):
            return attn_own.at[n if kind != "high" else n + 1]
        return (down_own if kind == "down" else inner_own).at[:, columns]

    def part_of(u, core_index, plane):
        kind = UNITS[u][0]
        if kind == "quarter":
            return plane * 2 + core_index
        return 2 + core_index if kind == "high" else core_index

    def whole(u, part):
        kind, n, columns = UNITS[u][:3]
        if kind == "down":
            return down.at[part, :, columns]
        if kind == "inner":
            return inner.at[part, :, columns]
        return attn.at[n, part]

    def place(u, source, part=None):
        kind, n, columns = UNITS[u][:3]
        part = part_of(u, core, y) if part is None else part
        if kind == "down":
            R = down_own.shape[0]
            return down.at[part, pl.ds(source * R, R), columns]
        if kind == "inner":
            R = inner_own.shape[0]
            return inner.at[part, pl.ds(source * R, R), columns]
        R = attn_own.shape[2]
        return attn.at[n, part, :, pl.ds(source * R, R), :]

    fetch_all()
    barrier = pltpu.get_barrier_semaphore()
    peers = [z_peer(k) for k in range(1, Z)] + [x_peer(i) for i in range(1, X)]
    peers += [core_peer, y_peer, before_me, after_me]
    for peer in peers:
        pl.semaphore_signal(barrier, inc=1, device_id=peer, device_id_type=MESH)
    pl.semaphore_wait(barrier, len(peers))

    sent, local = [], []

    def send(condition, make):
        remote_copy(*make()).start()
        sent.append((condition, make))

    def wait_send(condition, make):
        def action():
            remote_copy(*make()).wait_send()

        if condition is None:
            action()
        else:
            pl.when(condition())(action)

    def wait_recv(dst, recv_sem, send_sem):
        remote_copy(dst, dst, send_sem, recv_sem, core_peer).wait_recv()

    def store(src, dst):
        copy = pltpu.make_async_copy(src, dst, out_sem.at[len(local)])
        copy.start()
        local.append(copy)

    def spread(u, row, mine, condition):
        def src():
            return own(u) if mine else place(u, row() * X + x)

        for i in range(1, X):
            send(
                condition,
                lambda i=i: (
                    src(), place(u, row() * X + x), send_x.at[u, row(), i], recv_x.at[u, row(), i], x_peer(i)
                ),
            )
        to_plane(u, lambda: row() * X + x, src, condition)

    def to_plane(u, source, src, condition):
        if UNITS[u][0] == "quarter":
            send(
                condition,
                lambda: (src(), place(u, source()), send_y.at[u, source()], recv_y.at[u, source()], y_peer),
            )

    def crossed(u):
        return UNITS[u][3]

    def block(u, row):
        kind, n, columns = UNITS[u][:3]
        array, R = (down, down_own.shape[0]) if kind == "down" else (inner, inner_own.shape[0])
        return array.at[core, pl.ds(row * X * R, X * R), columns]

    def send_along(u, src, dst):
        def below_top():
            return z < Z - 1

        def above_bottom():
            return z > 0

        def upward():
            return (src(), dst(), send_up.at[u, 1], recv_up.at[u, 1], up_peer)

        def downward():
            return (src(), dst(), send_down.at[u, 1], recv_down.at[u, 1], down_peer)

        pl.when(below_top())(lambda: send(below_top, upward))
        pl.when(above_bottom())(lambda: send(above_bottom, downward))

    def start_unit(u):
        for slot in slots_of[u]:
            take(slot)
        if not crossed(u):
            send_along(u, lambda: own(u), lambda: place(u, fs))
        spread(u, lambda: z, True, None)
        store(own(u), place(u, fs))

    def turn(u):
        for i in range(1, X):
            column = lax.rem(x - i + X, X)
            wait_recv(place(u, z * X + column), recv_x.at[u, z, i], send_x.at[u, z, i])
        local[own_store[u]].wait()
        send_along(u, lambda: block(u, z), lambda: block(u, z))

    def hop(u, k):
        def side(reached, row, further, send_sem, recv_sem, peer):
            def here():
                return block(u, row()) if crossed(u) else place(u, row() * X + x)

            def both():
                return reached() & further()

            def action():
                wait_recv(here(), recv_sem.at[u, k], send_sem.at[u, k])
                if k < Z - 1:
                    pl.when(further())(
                        lambda: send(
                            both, lambda: (here(), here(), send_sem.at[u, k + 1], recv_sem.at[u, k + 1], peer)
                        )
                    )
                if not crossed(u):
                    spread(u, row, False, reached)

            pl.when(reached())(action)

        side(lambda: z >= k, lambda: z - k, lambda: z < Z - 1, send_up, recv_up, up_peer)
        side(lambda: z + k < Z, lambda: z + k, lambda: z > 0, send_down, recv_down, down_peer)

    def arrivals(u):
        for row in range(0 if crossed(u) else Z):
            for i in range(1, X):
                column = lax.rem(x - i + X, X)
                source = row * X + column
                wait_recv(place(u, source), recv_x.at[u, row, i], send_x.at[u, row, i])
                to_plane(u, lambda source=source: source, lambda source=source: place(u, source), None)
        if not crossed(u):
            local[own_store[u]].wait()
        mine = whole(u, part_of(u, core, y))
        send(None, lambda: (mine, mine, send_c.at[u], recv_c.at[u], core_peer))

    def relay(u):
        if UNITS[u][0] != "quarter":
            return
        part = (1 - y) * 2 + core
        for source in range(F):
            wait_recv(place(u, source, part), recv_y.at[u, source], send_y.at[u, source])
        theirs = whole(u, part)
        send(None, lambda: (theirs, theirs, send_r.at[u], recv_r.at[u], core_peer))

    def complete(u):
        wait_recv(whole(u, part_of(u, 1 - core, y)), recv_c.at[u], send_c.at[u])
        if UNITS[u][0] == "quarter":
            wait_recv(whole(u, (1 - y) * 2 + 1 - core), recv_r.at[u], send_r.at[u])

    scale = 1.0 / math.sqrt(head_size)

    def gather_gains():
        keep = pltpu.make_async_copy(gains_own, gains.at[fs], local_sem.at[0])
        keep.start()
        for k in range(1, Z):
            send(None, lambda k=k: (gains_own, gains.at[fs], send_g.at[0, k], recv_g.at[0, k], z_peer(k)))
        for i in range(1, X):
            send(None, lambda i=i: (gains_own, gains.at[fs], send_g.at[i, 0], recv_g.at[i, 0], x_peer(i)))
        keep.wait()

    def chunk_source(k, i):
        return lax.rem(z - k + Z, Z) * X + lax.rem(x - i + X, X)

    def pass_gains():
        for k in range(1, Z):
            here = gains.at[chunk_source(k, 0)]
            wait_recv(here, recv_g.at[0, k], send_g.at[0, k])
            for i in range(1, X):
                send(
                    None,
                    lambda here=here, i=i, k=k: (here, here, send_g.at[i, k], recv_g.at[i, k], x_peer(i)),
                )

    def take_gains():
        for k in range(Z):
            for i in range(1, X):
                wait_recv(gains.at[chunk_source(k, i)], recv_g.at[i, k], send_g.at[i, k])
        total = gains[0]
        for source in range(1, F):
            total = total + gains[source]
        gains_out[...] = total

    def norm_rows():
        def chunk(c, carry):
            rows = pl.ds(pl.multiple_of(c * CHUNK, CHUNK), CHUNK)
            for p in range(2):
                value = frames[p, rows, :].astype(F32)
                inputs[p, rows, :] = (value * scale_rows(value) * gains_out[0:1, :]).astype(BF)
            return carry

        lax.fori_loop(0, count // CHUNK, chunk, 0)
        store(inputs, inputs_out)

    def heads(m):
        columns = slice(m * STEP, (m + 1) * STEP)
        load = pltpu.make_async_copy(attn.at[m, pl.ds(0, 3)], proj, local_sem.at[0])
        load.start()
        load.wait()
        for t in (1, 2, 0):
            for p in range(2):
                rows_in[t, p, :, columns] = nn(inputs[p], proj[t, p]).astype(BF)
                if t > 0:
                    tail = rows_in[t, p, count - 16 :, columns].astype(F32)
                    row = 2 * (t - 1) + p
                    edge_send[m, row : row + 1, :] = tail[15:16, :]
            if t == 2:
                to_after = remote_copy(edge_send.at[m], edge_recv.at[m], send_e.at[m], recv_e.at[m], after_me)
                pl.when(me < devices - 1)(to_after.start)
        pl.when(me > 0)(to_after.wait_recv)
        first = lax.broadcasted_iota(jnp.int32, (count, STEP), 0) == 0
        for t in range(2):
            for p in range(2):
                n = 2 * t + p
                shifted = pltpu.roll(rows_in[1 + t, p, :, columns].astype(F32), 1, 0)
                before[n] = jnp.where(first, edge_recv[m, n : n + 1, :], shifted)
        ones = head_ones(STEP, head_size)

        def chunk(c, carry):
            rows = pl.ds(pl.multiple_of(c * CHUNK, CHUNK), CHUNK)
            allowed = jnp.broadcast_to(carried[rows, :], (CHUNK, STEP)) > 0.5
            queries, here_k, here_v = (
                [rows_in[t, p, rows, columns].astype(F32) for p in range(2)] for t in range(3)
            )
            keys = [before[p, rows, :] for p in range(2)] + here_k
            values = [before[2 + p, rows, :] for p in range(2)] + here_v
            scores = per_head(queries, keys, ones)
            for p, span in SPANS:
                probs = head_probs(scores, span, allowed, scale)
                terms = [pr.astype(BF).astype(F32) * values[PAIRS[n][1]] for n, pr in zip(span, probs)]
                mixed[p, rows, columns] = total_of(terms).astype(BF)
            return carry

        lax.fori_loop(0, count // CHUNK, chunk, 0)

    def load_mix():
        return pltpu.make_async_copy(attn.at[:, 3], mix, local_sem.at[1])

    def finish_rows():
        load_mix().wait()
        for turn in range(2):
            p = 1 - y if turn == 0 else y
            for m in range(groups):
                columns = slice(m * STEP, (m + 1) * STEP)
                hres[p, :, columns] = frames[p, :, columns].astype(F32) + nn(mixed[p], mix[m, p])

            def chunk(c, carry):
                rows = pl.ds(pl.multiple_of(c * CHUNK, CHUNK), CHUNK)
                value = hres[p, rows, :]
                b[turn, rows, :] = (value * scale_rows(value) * gains_out[1:2, :]).astype(BF)
                return carry

            lax.fori_loop(0, count // CHUNK, chunk, 0)
            if turn == 0:
                send(None, lambda: (b.at[0], b_rows.at[1], send_b, recv_b, y_peer))
            else:
                store(b.at[1], b_rows.at[0])
        store(hres, hres_out)

    @pl.when(me == 0)
    def _():
        edge_recv[...] = jnp.zeros_like(edge_recv)

    slots_of = [
        [n] if kind in ("quarter", "low") else [n + 1] if kind == "high" else [] for kind, n, *_ in UNITS
    ]
    slots_of[[u[0] for u in UNITS].index("inner")] = [groups + 1]
    slots_of[[u[0] for u in UNITS].index("down")] = [groups + 2]
    own_store = {}
    last_of = {kind_n[1]: u for u, kind_n in enumerate(UNITS) if kind_n[0] in ("quarter", "low", "high")}
    last_plane = max(u for u, kind_n in enumerate(UNITS) if kind_n[0] == "quarter")
    store(cot.at[y], c_rows.at[0])
    gather_gains()
    for tick in range(len(UNITS) + Z + 2):
        if tick < len(UNITS):
            own_store[tick] = len(local)
            start_unit(tick)
        if 0 <= tick - 1 < len(UNITS) and crossed(tick - 1):
            turn(tick - 1)
        for k in range(1, Z):
            u = tick - k
            if 0 <= u < len(UNITS) and not crossed(u):
                hop(u, k)
            u = tick - k - 1
            if 0 <= u < len(UNITS) and crossed(u):
                hop(u, k)
        if tick == 1:
            pass_gains()
        if tick == 2:
            take_gains()
            norm_rows()
        u = tick - Z
        if 0 <= u < len(UNITS):
            arrivals(u)
            if u == last_plane:
                send(None, lambda: (cot.at[1 - y], c_rows.at[1], send_q, recv_q, y_peer))
        u = tick - Z - 1
        if 0 <= u < len(UNITS):
            relay(u)
            complete(u)
            for m in range(groups):
                if last_of[m] == u:
                    if m == groups - 1:
                        load_mix().start()
                    heads(m)
                    if m == groups - 1:
                        store(rows_in, rows_out)
                        store(mixed, mixed_out)
                        store(edge_recv, edge_out)
                        finish_rows()
    wait_recv(b_rows.at[1], recv_b, send_b)
    wait_recv(c_rows.at[1], recv_q, send_q)
    for condition, make in sent:
        wait_send(condition, make)
    for n, copy in enumerate(local):
        if n not in own_store.values():
            copy.wait()

    @pl.when(me < devices - 1)
    def _():
        for m in range(groups):
            remote_copy(edge_send.at[m], edge_recv.at[m], send_e.at[m], recv_e.at[m], after_me).wait_send()


def unit_list(groups, inner_width, down_width):
    units = [("quarter", n, None, False) for n in range(groups - 1)]
    units += [("low", groups - 1, None, False), ("high", groups - 1, None, False)]
    units += [("down", 0, slice(0, down_width // 2), True), ("down", 0, slice(down_width // 2, down_width), False)]
    tiles = inner_width // 128
    cuts = [128 * (tiles * n // 4) for n in range(5)]
    return units + [("inner", 0, slice(lo, hi), n == 1) for n, (lo, hi) in enumerate(zip(cuts, cuts[1:]))]


def forward(
    frames, carried, cot, gains_own, qkv_weight, mix_weight, inner_weight, down_weight, head_size, fsdp_count
):
    X = fsdp_count // Z
    _, count, width = frames.shape
    R, R2 = qkv_weight.shape[1], down_weight.shape[1]
    hidden, half = inner_weight.shape[2] // 2, width // 2
    groups = width // STEP
    units = len(unit_list(groups, hidden, half))
    dma, vmem = pltpu.SemaphoreType.DMA, pltpu.VMEM
    whole = pl.BlockSpec(memory_space=pltpu.VMEM)
    act = jax.ShapeDtypeStruct((2, count, width), BF)
    return pl.pallas_call(
        functools.partial(forward_kernel, X, groups, head_size),
        out_shape=(
            jax.ShapeDtypeStruct((groups, 4, 2, R * fsdp_count, STEP), BF),
            jax.ShapeDtypeStruct((2, R * fsdp_count, hidden), BF),
            jax.ShapeDtypeStruct((2, R2 * fsdp_count, half), BF),
            jax.ShapeDtypeStruct(gains_own.shape, F32),
            act,
            jax.ShapeDtypeStruct((3, 2, count, width), BF),
            act,
            jax.ShapeDtypeStruct((groups, 8, STEP), F32),
            jax.ShapeDtypeStruct((2, count, width), F32),
            act,
            act,
        ),
        in_specs=[whole] * 4 + [ANY] * 4,
        out_specs=(ANY,) * 3 + (whole,) + (ANY,) * 7,
        scratch_shapes=[
            vmem((groups + 1, 2, R, STEP), F32), vmem((R, hidden), F32), vmem((R2, half), F32),
            vmem((groups + 1, 2, R, STEP), BF), vmem((R, hidden), BF), vmem((R2, half), BF),
            vmem((fsdp_count,) + gains_own.shape, F32),
            vmem((2, count, width), BF), vmem((3, 2, count, width), BF), vmem((2, count, width), BF),
            vmem((4, count, STEP), F32), vmem((2, count, width), F32), vmem((2, count, width), BF),
            vmem((3, 2, width, STEP), BF), vmem((groups, 2, width, STEP), BF),
            vmem((groups, 8, STEP), F32), vmem((groups, 8, STEP), F32),
            dma((units, Z)), dma((units, Z)), dma((units, Z)), dma((units, Z)),
            dma((units, Z, X)), dma((units, Z, X)), dma((groups, fsdp_count)), dma((groups, fsdp_count)),
            dma((units,)), dma((units,)), dma((groups,)), dma((groups,)),
            dma((X, Z)), dma((X, Z)), dma((groups,)), dma((groups,)), dma, dma, dma, dma,
            dma((2,)), dma((units + 8,)), dma((groups + 3,)),
        ],
        compiler_params=pltpu.CompilerParams(
            vmem_limit_bytes=VMEM_BYTES, collective_id=0, has_side_effects=True
        ),
        name="attention_forward",
    )(frames, carried, cot, gains_own, qkv_weight, mix_weight, inner_weight, down_weight)


def feed_forward_kernel(
    X, J, b, c, inner, down, out_mine, back_mine, out_theirs, back_recv, inner_all, down_columns, down_sum,
    out, back, acts, down_here, down_there, down_from_core, down_stage, down_column, down_from_x, mine, other, from_core, summed, from_x, column, from_z, final, staged,
    s1, r1, s2, r2, s3, r3, s5, r5, s6, r6, s7, r7, local_sem,
    s_stage, s_own, sdx, rdx, s_column,
):
    j = pl.program_id(0)
    half = down.shape[2]
    rows_here = out_mine.shape[0]
    R, step = final.shape[1:]
    dp, fs = lax.axis_index("dp"), lax.axis_index("fsdp")
    y, core = dp // 2, dp % 2
    z, x = fs // X, fs % X
    core_peer = (y * 2 + 1 - core, fs)
    y_peer = ((1 - y) * 2 + core, fs)

    def z_peer(k):
        return (dp, lax.rem(z + k, Z) * X + x)

    def x_peer(i):
        return (dp, z * X + lax.rem(x + i, X))

    def dp_peer(d):
        return (((y + d // 2) % 2) * 2 + (core + d % 2) % 2, fs)

    def to_core(n):
        return remote_copy(other.at[n % 2], from_core.at[n], s1.at[n % 2], r1.at[n], core_peer)

    def to_x(n, i):
        return remote_copy(
            summed.at[n % 2, :, lax.rem(x + i, X)], from_x.at[n, i - 1], s2.at[n % 2, i - 1], r2.at[n, i - 1], x_peer(i)
        )

    def to_z(n, k):
        return remote_copy(
            column.at[n % 2, lax.rem(z + k, Z)], from_z.at[n, k - 1], s3.at[n % 2, k - 1], r3.at[n, k - 1], z_peer(k)
        )

    def place(n, owner):
        return inner_all.at[owner, :, pl.ds(pl.multiple_of(n * step, step), step)]

    def share(n, d):
        return remote_copy(final.at[n], place(n, dp), s5.at[n, d - 1], r5.at[n, d - 1], dp_peer(d))

    def keep(n):
        return pltpu.make_async_copy(final.at[n], place(n, dp), local_sem.at[n])

    exchange = remote_copy(staged, back_recv, s6, r6, y_peer)

    R2 = down_column.shape[1]
    ends = [-(-(g + 1) * X * R2 // step) - 1 for g in range(Z)]

    def down_rows(g, column):
        return down_sum.at[pl.ds((g * X + column) * R2, R2), :]

    def down_store(n):
        return pltpu.make_async_copy(
            down_stage.at[n % 2], down_sum.at[pl.ds(pl.multiple_of(n * step, step), step), :], s_stage.at[n % 2]
        )

    def down_load(g):
        return pltpu.make_async_copy(down_rows(g, x), down_column.at[g], s_own.at[g])

    def down_to_x(g, i):
        return remote_copy(
            down_rows(g, lax.rem(x + i, X)), down_from_x.at[g, i - 1], sdx.at[g, i - 1], rdx.at[g, i - 1], x_peer(i)
        )

    def down_keep(g):
        return pltpu.make_async_copy(down_column.at[g], down_columns.at[g], s_column.at[g])

    def down_to_core(n):
        return remote_copy(down_there.at[n % 2], down_from_core.at[n], s7.at[n % 2], r7.at[n], core_peer)

    @pl.when(j == 0)
    def _():
        barrier = pltpu.get_barrier_semaphore()
        peers = [z_peer(k) for k in range(1, Z)] + [x_peer(i) for i in range(1, X)]
        peers += [dp_peer(d) for d in range(1, 4)]
        for peer in peers:
            pl.semaphore_signal(barrier, inc=1, device_id=peer, device_id_type=MESH)
        pl.semaphore_wait(barrier, len(peers))
        out[...] = jnp.zeros_like(out)
        back[...] = jnp.zeros_like(back)

    @pl.when(j < J)
    def _():
        rows, cot = b[...], c[...]
        gate = nn(rows, inner[0])
        up = nn(rows, inner[1])
        squashed = jax.nn.sigmoid(gate)
        active = gate * squashed
        hidden = (active * up).astype(BF)
        hidden_grad = nt(cot[:, :half], down[0]) + nt(cot[:, half:], down[1])
        gate_grad = (hidden_grad * up * (squashed * (1.0 + gate * (1.0 - squashed)))).astype(BF)
        up_grad = (hidden_grad * active).astype(BF)
        acts[0] = hidden
        acts[1] = gate_grad
        acts[2] = up_grad

    @pl.when((j >= 2) & (j < J + 2))
    def _():
        down_store(j - 2).wait()

    for g in range(Z):
        @pl.when(j == ends[g] + 2)
        def _():
            for i in range(1, X):
                down_to_x(g, i).start()
            down_load(g).start()

    @pl.when((j >= 1) & (j < J + 1))
    def _():
        n = j - 1
        to_core(n).wait_recv()

        @pl.when(n >= 2)
        def _():
            for i in range(1, X):
                to_x(n - 2, i).wait_send()

        down_to_core(n).wait_recv()
        down_stage[n % 2] = (down_here[n % 2].astype(F32) + down_from_core[n].astype(F32)).astype(BF)
        down_store(n).start()
        total = (mine[n % 2].astype(F32) + from_core[n].astype(F32)).astype(BF)
        summed[n % 2] = total.reshape(summed.shape[1:])
        for i in range(1, X):
            to_x(n, i).start()

    @pl.when((j >= 2) & (j < J + 2))
    def _():
        n = j - 2
        for i in range(1, X):
            to_x(n, i).wait_recv()

        @pl.when(n >= 2)
        def _():
            for k in range(1, Z):
                to_z(n - 2, k).wait_send()

        total = summed[n % 2, :, x].astype(F32)
        for i in range(1, X):
            total = total + from_x[n, i - 1].astype(F32)
        column[n % 2] = total.astype(BF)
        for k in range(1, Z):
            to_z(n, k).start()

    for g in range(Z):
        @pl.when(j == min(ends[g] + 4, J + 2))
        def _():
            down_load(g).wait()
            for i in range(1, X):
                down_to_x(g, i).wait_recv()
            total = down_column[g].astype(F32) + total_of([down_from_x[g, i].astype(F32) for i in range(X - 1)])
            down_column[g] = total.astype(BF)
            down_keep(g).start()

    @pl.when((j >= 3) & (j < J + 3))
    def _():
        n = j - 3
        for k in range(1, Z):
            to_z(n, k).wait_recv()
        total = column[n % 2, z].astype(F32)
        for k in range(1, Z):
            total = total + from_z[n, k - 1].astype(F32)
        final[n] = total.astype(BF)
        keep(n).start()
        for d in range(1, 4):
            share(n, d).start()

    @pl.when(j < J)
    def _():
        rows, cot = b[...], c[...]
        hidden, gate_grad, up_grad = (acts[n] for n in range(3))
        gate_term = tn(rows, gate_grad).astype(BF)
        up_term = tn(rows, up_grad).astype(BF)

        @pl.when(j >= 2)
        def _():
            to_core(j - 2).wait_send()
            down_to_core(j - 2).wait_send()

        mine[j % 2] = jnp.where(core == 0, gate_term, up_term)
        other[j % 2] = jnp.where(core == 0, up_term, gate_term)
        to_core(j).start()
        down_term = tn(hidden, cot).astype(BF)
        down_here[j % 2] = jnp.where(core == 0, down_term[:, :half], down_term[:, half:])
        down_there[j % 2] = jnp.where(core == 0, down_term[:, half:], down_term[:, :half])
        down_to_core(j).start()
        for n in range(2):
            part = slice(n * half, (n + 1) * half)
            out[:, part] += nn(hidden, down[n])
        back[...] += nt(gate_grad, inner[0]) + nt(up_grad, inner[1])

    @pl.when(j == J - 1)
    def _():
        staged[...] = back[rows_here:, :].astype(BF)
        exchange.start()
        out_theirs[...] = out[rows_here:, :].astype(BF)
        out_mine[...] = out[:rows_here, :]
        back_mine[...] = back[:rows_here, :]

    @pl.when(j == J + 2)
    def _():
        for n in (J - 2, J - 1):
            to_core(n).wait_send()
            down_to_core(n).wait_send()
            for i in range(1, X):
                to_x(n, i).wait_send()
            for k in range(1, Z):
                to_z(n, k).wait_send()

        def finish(n, carry):
            keep(n).wait()
            for d in range(1, 4):
                share(n, d).wait()
            return carry

        lax.fori_loop(0, J, finish, 0)
        exchange.wait()
        for g in range(Z):
            down_keep(g).wait()
            for i in range(1, X):
                down_to_x(g, i).wait_send()


def feed_forward(b, c, inner, down, fsdp_count):
    rows, width = b.shape
    _, _, hidden = inner.shape
    half = down.shape[2]
    step = 256
    J = hidden // step
    X = fsdp_count // Z
    R, R2 = width // fsdp_count, hidden // fsdp_count
    whole = pl.BlockSpec((rows, width), lambda j: (0, 0), pipeline_mode=pl.Buffered(1))
    part = pl.BlockSpec((rows // 2, width), lambda j: (0, 0), pipeline_mode=pl.Buffered(1))
    inner_spec = pl.BlockSpec((2, width, step), lambda j: (0, 0, jnp.minimum(j, J - 1)))
    down_spec = pl.BlockSpec((2, step, half), lambda j: (0, jnp.minimum(j, J - 1), 0))
    dma, vmem = pltpu.SemaphoreType.DMA, pltpu.VMEM
    return pl.pallas_call(
        functools.partial(feed_forward_kernel, X, J),
        grid=(J + 3,),
        out_shape=(
            jax.ShapeDtypeStruct((rows // 2, width), F32),
            jax.ShapeDtypeStruct((rows // 2, width), F32),
            jax.ShapeDtypeStruct((rows // 2, width), BF),
            jax.ShapeDtypeStruct((rows // 2, width), BF),
            jax.ShapeDtypeStruct((4, R, hidden), BF),
            jax.ShapeDtypeStruct((Z, R2, half), BF),
            jax.ShapeDtypeStruct((hidden, half), BF),
        ),
        in_specs=[whole, whole, inner_spec, down_spec],
        out_specs=(part, part, part, ANY, ANY, ANY, ANY),
        scratch_shapes=[
            vmem((rows, width), F32), vmem((rows, width), F32), vmem((3, rows, step), BF),
            vmem((2, step, half), BF), vmem((2, step, half), BF), vmem((J, step, half), BF),
            vmem((2, step, half), BF), vmem((Z, R2, half), BF), vmem((Z, X - 1, R2, half), BF),
            vmem((2, width, step), BF), vmem((2, width, step), BF), vmem((J, width, step), BF),
            vmem((2, Z, X, R, step), BF), vmem((J, X - 1, Z, R, step), BF),
            vmem((2, Z, R, step), BF), vmem((J, Z - 1, R, step), BF),
            vmem((J, R, step), BF), vmem((rows // 2, width), BF),
            dma((2,)), dma((J,)), dma((2, X - 1)), dma((J, X - 1)), dma((2, Z - 1)), dma((J, Z - 1)),
            dma((J, 3)), dma((J, 3)), dma, dma, dma((2,)), dma((J,)), dma((J,)),
            dma((2,)), dma((Z,)), dma((Z, X - 1)), dma((Z, X - 1)), dma((Z,)),
        ],
        compiler_params=pltpu.CompilerParams(
            vmem_limit_bytes=VMEM_BYTES, collective_id=1, has_side_effects=True
        ),
        cost_estimate=pl.CostEstimate(flops=18 * rows * width * hidden, bytes_accessed=60 * 2**20, transcendentals=0),
        name="feed_forward",
    )(b, c, inner, down)


def total_of(values):
    return functools.reduce(jnp.add, values)


def attention_back_kernel(
    X, groups, head_size, carried, q, k, v, edge, mix, dhb, mixed, inputs, proj, gains, second_gain, frames_in, down_in, out_send,
    frames_grad, gains_sum, attn_all, down_all, out_recv,
    da, gain_terms, gain_from, mixed_grad, before, terms_before, terms_here, tails, grads, edge_send, edge_recv,
    mine, other, from_core, keep_y, send_y, from_y, summed, from_x, column, from_z, final, plane, from_plane, final_plane,
    down_mine, down_from_z, down_final,
    s_edge, r_edge, s1, r1, sy, ry, sxa, rxa, sxb, rxb, sz, rz, sf, rf, sp, rp, sc, rc, local_sem,
    s_out, r_out, sg, rg, frame_sem, sdz, rdz, sdf, rdf, down_sem, free,
):
    i = pl.program_id(0)
    frames, step = q.shape[2:]
    R, thin = final.shape[1:]
    subs = 2 * groups
    slots = from_core.shape[0]
    dp, fs = lax.axis_index("dp"), lax.axis_index("fsdp")
    F = Z * X
    y, core = dp // 2, dp % 2
    z, x = fs // X, fs % X
    me = dp * F + fs
    devices = 4 * F
    core_peer = (y * 2 + 1 - core, fs)
    y_peer = ((1 - y) * 2 + core, fs)
    before_me = ((me - 1 + devices) % devices // F, (me - 1 + devices) % devices % F)
    after_me = ((me + 1) % devices // F, (me + 1) % devices % F)

    def z_peer(n):
        return (dp, lax.rem(z + n, Z) * X + x)

    def x_peer(n):
        return (dp, z * X + lax.rem(x + n, X))

    def dp_peer(d):
        return (((y + d // 2) % 2) * 2 + (core + d % 2) % 2, fs)

    def to_before(n):
        return remote_copy(edge_send.at[n % 2], edge_recv.at[n], s_edge.at[n % 2], r_edge.at[n], before_me)

    def to_core(n):
        return remote_copy(other.at[n % 2], from_core.at[n % slots], s1.at[n % 2], r1.at[n % slots], core_peer)

    def to_y(n):
        return remote_copy(send_y.at[n % 2], from_y.at[n], sy.at[n % 2], ry.at[n], y_peer)

    def to_x_early(n, j):
        return remote_copy(
            summed.at[n % 3, pl.ds(1, 2), :, lax.rem(x + j, X)], from_x.at[n, j - 1, pl.ds(1, 2)],
            sxa.at[n % 3, j - 1], rxa.at[n, j - 1], x_peer(j),
        )

    def to_x_late(n, j):
        return remote_copy(
            summed.at[n % 3, 0, :, lax.rem(x + j, X)], from_x.at[n, j - 1, 0],
            sxb.at[n % 3, j - 1], rxb.at[n, j - 1], x_peer(j),
        )

    def to_z(n, j):
        return remote_copy(
            column.at[n % 2, :, lax.rem(z + j, Z)], from_z.at[n, j - 1], sz.at[n % 2, j - 1], rz.at[n, j - 1], z_peer(j)
        )

    def place(n, t):
        return attn_all.at[t, core, :, pl.ds(pl.multiple_of(n * thin, thin), thin)]

    def share(n, d):
        return remote_copy(final.at[n], place(n, y), sf.at[n, d - 1], rf.at[n, d - 1], dp_peer(d))

    def relay(n):
        return remote_copy(place(n, 1 - y), place(n, 1 - y), sf.at[n, 2], rf.at[n, 2], core_peer)

    def down_to_z(k):
        return remote_copy(
            down_in.at[lax.rem(z + k, Z)], down_from_z.at[k - 1], sdz.at[k - 1], rdz.at[k - 1], z_peer(k)
        )

    def down_share(d):
        return remote_copy(down_final, down_all.at[dp], sdf.at[d - 1], rdf.at[d - 1], dp_peer(d))

    def down_relay():
        part = down_all.at[(1 - y) * 2 + core]
        return remote_copy(part, part, sdf.at[2], rdf.at[2], core_peer)

    def to_plane(n):
        return remote_copy(plane.at[n], from_plane.at[n], sp.at[n], rp.at[n], y_peer)

    def share_core(n, t):
        return remote_copy(final_plane.at[n, t], place(n, 2 + t), sc.at[n, t], rc.at[n, t], core_peer)

    def keep(n, t):
        src = final.at[n] if t == 0 else final_plane.at[n, t - 1]
        return pltpu.make_async_copy(src, place(n, y if t == 0 else 1 + t), local_sem.at[n, t])

    def load_frames(g):
        dst = grads.at[g] if g < 3 else mixed_grad
        return pltpu.make_async_copy(frames_in.at[:, :, pl.ds(g * step, step)], dst, frame_sem.at[g])

    def gain_copy(level, n):
        peer = (core_peer, y_peer, x_peer(n + 1), z_peer(n + 1))[level]
        return remote_copy(gain_terms.at[level], gain_from.at[level, n], sg.at[level, n], rg.at[level, n], peer)

    down_load = pltpu.make_async_copy(down_in.at[z], down_mine, down_sem.at[0])
    down_keep = pltpu.make_async_copy(down_final, down_all.at[dp], down_sem.at[1])
    out_copy = remote_copy(out_send, out_recv, s_out, r_out, y_peer)

    @pl.when(i == 0)
    def _():
        barrier = pltpu.get_barrier_semaphore()
        peers = [z_peer(n) for n in range(1, Z)] + [x_peer(n) for n in range(1, X)]
        peers += [dp_peer(d) for d in range(1, 4)] + [before_me, after_me]
        for peer in peers:
            pl.semaphore_signal(barrier, inc=1, device_id=peer, device_id_type=MESH)
        pl.semaphore_wait(barrier, len(peers))
        out_copy.start()
        for k in range(1, Z):
            down_to_z(k).start()
        down_load.start()
        da[...] = jnp.zeros_like(da)

        @pl.when(me == devices - 1)
        def _():
            edge_recv[...] = jnp.zeros_like(edge_recv)

    @pl.when((i < subs) & (i % 2 == 0))
    def _():
        m = i // 2
        slot = m % 2
        ones = head_ones(step, head_size)
        scale = 1.0 / math.sqrt(head_size)
        first = lax.broadcasted_iota(jnp.int32, (frames, step), 0) == 0
        last = lax.broadcasted_iota(jnp.int32, (frames, step), 0) == frames - 1
        for p in range(2):
            mixed_grad[p] = total_of(
                [nt(dhb[p, :, g * step : (g + 1) * step], mix[g, 0, p]) for g in range(groups)]
            ).astype(BF)
            before[p] = jnp.where(first, edge[0, p : p + 1, :], pltpu.roll(k[0, p].astype(F32), 1, 0))
            before[2 + p] = jnp.where(first, edge[0, 2 + p : 3 + p, :], pltpu.roll(v[0, p].astype(F32), 1, 0))

        def chunk(c, carry):
            rows = pl.ds(pl.multiple_of(c * CHUNK, CHUNK), CHUNK)
            allowed = jnp.broadcast_to(carried[rows, :], (CHUNK, step)) > 0.5
            queries = [q[0, p, rows, :].astype(F32) for p in range(2)]
            cots = [mixed_grad[p, rows, :].astype(F32) for p in range(2)]
            keys = [before[p, rows, :] for p in range(2)] + [k[0, p, rows, :].astype(F32) for p in range(2)]
            values = [before[2 + p, rows, :] for p in range(2)] + [v[0, p, rows, :].astype(F32) for p in range(2)]

            scores = per_head(queries, keys, ones)
            dprobs = per_head(cots, values, ones)
            key_grads, value_grads = [[] for _ in range(4)], [[] for _ in range(4)]
            for p, span in SPANS:
                probs = head_probs(scores, span, allowed, scale)
                mean = total_of([pr * dprobs[m] for m, pr in zip(span, probs)])
                query_grad = []
                for m, pr in zip(span, probs):
                    n = PAIRS[m][1]
                    ds = (pr * (dprobs[m] - mean)).astype(BF).astype(F32) * scale
                    query_grad.append(ds * keys[n])
                    key_grads[n].append(ds * queries[p])
                    value_grads[n].append(pr.astype(BF).astype(F32) * cots[p])
                grads[0, p, rows, :] = total_of(query_grad).astype(BF)
            for p in range(2):
                terms_before[p, rows, :] = total_of(key_grads[p])
                terms_before[2 + p, rows, :] = total_of(value_grads[p])
                terms_here[p, rows, :] = total_of(key_grads[2 + p])
                terms_here[2 + p, rows, :] = total_of(value_grads[2 + p])
            return carry

        lax.fori_loop(0, frames // CHUNK, chunk, 0)

        @pl.when((m >= 2) & (me > 0))
        def _():
            to_before(m - 2).wait_send()

        for row in range(4):
            edge_send[slot, row : row + 1, :] = terms_before[row, 0:1, :]

        @pl.when(me > 0)
        def _():
            to_before(m).start()

        for row in range(4):
            total = terms_here[row] + jnp.where(last, 0.0, pltpu.roll(terms_before[row], frames - 1, 0))
            grads[1 + row // 2, row % 2] = total.astype(BF)
            tails[row] = total[frames - 16 :, :]

    def active(first):
        return (i >= first) & (i < first + subs)

    @pl.when(active(2))
    def _():
        n = i - 2
        to_core(n).wait_recv()

        @pl.when(n >= 2)
        def _():
            to_y(n - 2).wait_send()

        @pl.when(n >= 3)
        def _():
            for j in range(1, X):
                to_x_early(n - 3, j).wait_send()

        def both(t):
            return (mine[n % 2, t].astype(F32) + from_core[n % slots, t].astype(F32)).astype(BF)

        send_y[n % 2] = both(1 - y)
        to_y(n).start()
        for t in range(2):
            summed[n % 3, 1 + t] = both(2 + t).reshape(summed.shape[2:])
        for j in range(1, X):
            to_x_early(n, j).start()
        keep_y[n % 2] = both(y)

        @pl.when(n < subs - slots)
        def _():
            pl.semaphore_signal(free, inc=1, device_id=core_peer, device_id_type=MESH)

    @pl.when(active(3))
    def _():
        n = i - 3
        to_y(n).wait_recv()

        @pl.when(n >= 3)
        def _():
            for j in range(1, X):
                to_x_late(n - 3, j).wait_send()

        total = (keep_y[n % 2].astype(F32) + from_y[n].astype(F32)).astype(BF)
        summed[n % 3, 0] = total.reshape(summed.shape[2:])
        for j in range(1, X):
            to_x_late(n, j).start()

    @pl.when(active(4))
    def _():
        n = i - 4
        for j in range(1, X):
            to_x_early(n, j).wait_recv()
            to_x_late(n, j).wait_recv()

        @pl.when(n >= 2)
        def _():
            for j in range(1, Z):
                to_z(n - 2, j).wait_send()

        total = summed[n % 3, :, :, x].astype(F32) + total_of([from_x[n, j].astype(F32) for j in range(X - 1)])
        column[n % 2] = total.astype(BF)
        for j in range(1, Z):
            to_z(n, j).start()

    @pl.when(active(5))
    def _():
        n = i - 5
        for j in range(1, Z):
            to_z(n, j).wait_recv()
        total = column[n % 2, :, z].astype(F32) + total_of([from_z[n, j].astype(F32) for j in range(Z - 1)])
        total = total.astype(BF)
        final[n] = total[0]
        plane[n] = total[1:]
        to_plane(n).start()
        keep(n, 0).start()
        for d in range(1, 3):
            share(n, d).start()

    @pl.when(active(6))
    def _():
        n = i - 6
        to_plane(n).wait_recv()
        share(n, 2).wait_recv()
        relay(n).start()
        final_plane[n] = (plane[n].astype(F32) + from_plane[n].astype(F32)).astype(BF)
        for t in range(2):
            keep(n, t + 1).start()
            share_core(n, t).start()

    @pl.when(i == 4)
    def _():
        down_load.wait()
        for k in range(1, Z):
            down_to_z(k).wait_recv()
        total = down_mine[...].astype(F32) + total_of([down_from_z[k].astype(F32) for k in range(Z - 1)])
        down_final[...] = total.astype(BF)
        down_keep.start()
        for d in range(1, 3):
            down_share(d).start()

    @pl.when(i == 6)
    def _():
        down_share(2).wait_recv()
        down_relay().start()

    @pl.when((i < subs) & (i % 2 == 1))
    def _():
        m = i // 2

        @pl.when(me < devices - 1)
        def _():
            to_before(m).wait_recv()

        bottom = lax.broadcasted_iota(jnp.int32, (16, step), 0) == 15
        for row in range(4):
            fixed = tails[row] + jnp.where(bottom, edge_recv[m, row : row + 1, :], 0.0)
            grads[1 + row // 2, row % 2, frames - 16 :, :] = fixed.astype(BF)

        @pl.when(m >= 1)
        def _():
            for h in range(2):
                to_core(2 * m - 2 + h).wait_send()

        for t in range(4):
            pair = []
            for p in range(2):
                if t < 3:
                    pair.append(tn(inputs[p], grads[t, p]).astype(BF))
                else:
                    pair.append(tn(mixed[p], dhb[p, :, pl.ds(pl.multiple_of(m * step, step), step)]).astype(BF))
            here = jnp.where(core == 0, pair[0], pair[1])
            there = jnp.where(core == 0, pair[1], pair[0])
            for h in range(2):
                mine[h, t] = here[:, h * thin : (h + 1) * thin]
                other[h, t] = there[:, h * thin : (h + 1) * thin]

        @pl.when(m >= slots // 2)
        def _():
            pl.semaphore_wait(free, 2)

        for h in range(2):
            to_core(2 * m + h).start()
        for p in range(2):
            da[p] += total_of([nt(grads[t, p], proj[0, t, p]) for t in range(3)])

        @pl.when(m == groups - 1)
        def _():
            for g in range(groups):
                load_frames(g).start()

    @pl.when(i == subs)
    def _():
        for g in range(groups):
            load_frames(g).wait()

        def chunk(c, term):
            rows = pl.ds(pl.multiple_of(c * CHUNK, CHUNK), CHUNK)
            for p in range(2):
                pieces = [grads[g, p, rows, :] if g < 3 else mixed_grad[p, rows, :] for g in range(groups)]
                value = jnp.concatenate(pieces, axis=1).astype(F32)
                inverse = scale_rows(value)
                normed = value * inverse
                grad = da[p, rows, :]
                term = term + jnp.sum(grad * normed, axis=0, keepdims=True)
                total = dhb[p, rows, :].astype(F32) + norm_back(grad, normed, gains[0:1, :], inverse)
                frames_grad[p, rows, :] = total.astype(BF)
            return term

        term = lax.fori_loop(0, frames // CHUNK, chunk, jnp.zeros((1, da.shape[2]), F32))
        gain_terms[0] = second_gain[...]
        gain_terms[0, 0:1, :] = term
        gain_copy(0, 0).start()

    for level in range(1, 4):
        @pl.when(i == subs + level)
        def _():
            count = X - 1 if level == 3 else 1
            total = gain_terms[level - 1]
            for n in range(count):
                gain_copy(level - 1, n).wait()
                total = total + gain_from[level - 1, n]
            gain_terms[level] = total
            for n in range(Z - 1 if level == 3 else X - 1 if level == 2 else 1):
                gain_copy(level, n).start()

    @pl.when(i == subs + 4)
    def _():
        total = gain_terms[3]
        for n in range(Z - 1):
            gain_copy(3, n).wait()
            total = total + gain_from[3, n]
        gains_sum[...] = total

    @pl.when(i == subs + 5)
    def _():
        @pl.when(me > 0)
        def _():
            for n in (groups - 2, groups - 1):
                to_before(n).wait_send()

        for n in (subs - 3, subs - 2, subs - 1):
            for j in range(1, X):
                to_x_early(n, j).wait_send()
                to_x_late(n, j).wait_send()

        for n in (subs - 2, subs - 1):
            to_core(n).wait_send()
            to_y(n).wait_send()
            for j in range(1, Z):
                to_z(n, j).wait_send()

        def finish(n, carry):
            to_plane(n).wait_send()
            keep(n, 0).wait()
            share(n, 1).wait()
            share(n, 2).wait_send()
            relay(n).wait()
            for t in range(2):
                keep(n, t + 1).wait()
                share_core(n, t).wait()
            return carry

        lax.fori_loop(0, subs, finish, 0)
        out_copy.wait()
        for k in range(1, Z):
            down_to_z(k).wait_send()
        down_keep.wait()
        down_share(1).wait()
        down_share(2).wait_send()
        down_relay().wait()


def attention_back(
    carried, qkv_rows, edge, attn, dhb, mixed, inputs, gains, second_gain, frames_in, down_in, out_send, head_size, fsdp_count
):
    _, frames, width = dhb.shape
    step = STEP
    groups = width // step
    X = fsdp_count // Z
    R = width // fsdp_count

    def early(i):
        return jnp.minimum(i // 2, groups - 1)

    rows = [pl.BlockSpec((1, 2, frames, step), lambda i, t=t: (t, 0, 0, early(i))) for t in range(3)]
    edge_spec = pl.BlockSpec((1, 8, step), lambda i: (early(i), 0, 0))
    mask = pl.BlockSpec((frames, 1), lambda i: (0, 0), pipeline_mode=pl.Buffered(1))
    whole = pl.BlockSpec((2, frames, width), lambda i: (0, 0, 0), pipeline_mode=pl.Buffered(1))
    mix_spec = pl.BlockSpec((groups, 1, 2, step, step), lambda i: (0, 3, 0, early(i), 0))
    proj_spec = pl.BlockSpec((1, 3, 2, width, step), lambda i: (jnp.clip((i - 1) // 2, 0, groups - 1), 0, 0, 0, 0))
    line = pl.BlockSpec((8, width), lambda i: (0, 0), pipeline_mode=pl.Buffered(1))
    dma, vmem = pltpu.SemaphoreType.DMA, pltpu.VMEM
    thin = step // 2
    n, slots, peers = 2 * groups, 4, max(X, Z) - 1
    return pl.pallas_call(
        functools.partial(attention_back_kernel, X, groups, head_size),
        grid=(n + 6,),
        out_shape=(
            jax.ShapeDtypeStruct((2, frames, width), BF),
            jax.ShapeDtypeStruct((8, width), F32),
            jax.ShapeDtypeStruct((4, 2, R, width), BF),
            jax.ShapeDtypeStruct((4,) + down_in.shape[1:], BF),
            jax.ShapeDtypeStruct(out_send.shape, BF),
        ),
        in_specs=[mask, *rows, edge_spec, mix_spec, whole, whole, whole, proj_spec, line, line, ANY, ANY, ANY],
        out_specs=(whole, line, ANY, ANY, ANY),
        scratch_shapes=[
            vmem((2, frames, width), F32), vmem((4, 8, width), F32), vmem((4, peers, 8, width), F32),
            vmem((2, frames, step), BF), vmem((4, frames, step), F32), vmem((4, frames, step), F32),
            vmem((4, frames, step), F32), vmem((4, 16, step), F32), vmem((3, 2, frames, step), BF),
            vmem((2, 8, step), F32), vmem((groups, 8, step), F32),
            vmem((2, 4, width, thin), BF), vmem((2, 4, width, thin), BF), vmem((slots, 4, width, thin), BF),
            vmem((2, width, thin), BF), vmem((2, width, thin), BF), vmem((n, width, thin), BF),
            vmem((3, 3, Z, X, R, thin), BF), vmem((n, X - 1, 3, Z, R, thin), BF),
            vmem((2, 3, Z, R, thin), BF), vmem((n, Z - 1, 3, R, thin), BF),
            vmem((n, R, thin), BF), vmem((n, 2, R, thin), BF), vmem((n, 2, R, thin), BF), vmem((n, 2, R, thin), BF),
            vmem(down_in.shape[1:], BF), vmem((Z - 1,) + down_in.shape[1:], BF), vmem(down_in.shape[1:], BF),
            dma((2,)), dma((groups,)), dma((2,)), dma((slots,)), dma((2,)), dma((n,)),
            dma((3, X - 1)), dma((n, X - 1)), dma((3, X - 1)), dma((n, X - 1)),
            dma((2, Z - 1)), dma((n, Z - 1)), dma((n, 3)), dma((n, 3)), dma((n,)), dma((n,)),
            dma((n, 2)), dma((n, 2)), dma((n, 3)),
            dma, dma, dma((4, peers)), dma((4, peers)), dma((groups,)),
            dma((Z - 1,)), dma((Z - 1,)), dma((3,)), dma((3,)), dma((2,)), pltpu.SemaphoreType.REGULAR,
        ],
        compiler_params=pltpu.CompilerParams(vmem_limit_bytes=63 * 2**20, collective_id=2, has_side_effects=True),
        name="attention_back",
    )(
        carried, qkv_rows, qkv_rows, qkv_rows, edge, attn, dhb, mixed, inputs, attn,
        gains, second_gain, frames_in, down_in, out_send,
    )


def update_kernel(step_size, share, weight, moment, average, grad_out, moment_out, average_out, weight_out):
    gradient = share[...].reshape(weight.shape).astype(F32)
    moment_new, average_new, weight_new = owner_update(
        weight[...], gradient, moment[...], average[...], step_size
    )
    grad_out[...] = gradient
    moment_out[...] = moment_new
    average_out[...] = average_new
    weight_out[...] = weight_new


def update(shares, share_block, share_at, grid, block, at, weight, moment, average, step_size, name):
    share_spec = pl.BlockSpec(share_block, share_at)
    spec = pl.BlockSpec(block, at)
    return pl.pallas_call(
        functools.partial(update_kernel, step_size),
        grid=grid,
        out_shape=(jax.ShapeDtypeStruct(weight.shape, F32),) * 4,
        in_specs=[share_spec, spec, spec, spec],
        out_specs=(spec,) * 4,
        compiler_params=pltpu.CompilerParams(vmem_limit_bytes=VMEM_BYTES),
        name=name,
    )(shares, weight, moment, average)


def per_device(
    frames, cotangent, segment_ids,
    qkv_weight, mix_weight, inner_weight, down_weight, norm_gains,
    qkv_moment, mix_moment, inner_moment, down_moment, gains_moment,
    qkv_average, mix_average, inner_average, down_average, gains_average,
):
    frame_count, positions, width = frames.shape
    head_size = width // HEADS
    hidden = inner_weight.shape[2] // 2
    dp_count, fsdp_count = lax.axis_size("dp"), lax.axis_size("fsdp")
    X = fsdp_count // Z
    devices = dp_count * fsdp_count
    total_frames = frame_count * devices
    dp, fs = lax.axis_index("dp"), lax.axis_index("fsdp")
    y, core = dp // 2, dp % 2
    z, x = fs // X, fs % X
    axes = ("dp", "fsdp")

    device = dp * fsdp_count + fs
    padded_ids = jnp.concatenate([jnp.full((1,), -1, jnp.int32), segment_ids])
    window = lax.dynamic_slice_in_dim(padded_ids, device * frame_count, frame_count + 1)
    carried = (window[1:] == window[:-1]).astype(F32)[:, None]

    half_width = width // 2
    own_gains = norm_gains.astype(BF).astype(F32)
    gains_own = lax.dynamic_update_slice(jnp.zeros((8, width), F32), own_gains, (0, fs * own_gains.shape[1]))
    frames_by = frames.transpose(1, 0, 2)
    cot = cotangent.transpose(1, 0, 2)
    attn, inner, down, gains, a, qkv_rows, mixed, edge, hres, b_rows, c_rows = forward(
        frames_by, carried, cot, gains_own, qkv_weight, mix_weight, inner_weight, down_weight, head_size, fsdp_count
    )
    r2 = scale_rows(hres)
    n2 = hres * r2
    b_rows = b_rows.reshape(2 * frame_count, width)
    c_rows = c_rows.reshape(2 * frame_count, width)
    out, back, out_there, back_there, inner_shares, down_columns, _ = feed_forward(b_rows, c_rows, inner, down, fsdp_count)

    def by_position(mine, theirs):
        return jnp.where(y == 0, jnp.stack([mine, theirs]), jnp.stack([theirs, mine]))

    db = by_position(back, back_there.astype(F32))

    e2 = jnp.sum(db * n2, axis=(0, 1))
    dh = cot.astype(F32) + norm_back(db, n2, gains[1], r2)
    dhb = dh.astype(BF)
    second_gain = jnp.zeros((8, width), F32).at[1].set(e2)
    frames_grad, gains_sum, attn_shares, down_shares, out_here = attention_back(
        carried, qkv_rows, edge, attn, dhb, mixed, a, gains, second_gain, frames_by, down_columns, out_there, head_size, fsdp_count
    )
    frames_grad = frames_grad.transpose(1, 0, 2)
    layer_out = (hres + by_position(out, out_here.astype(F32))).astype(BF).transpose(1, 0, 2)

    step_size = step_rate / math.sqrt(total_frames)
    R, R2 = qkv_weight.shape[1], down_weight.shape[1]
    cut = min(R, 64)
    qkv_new = update(
        attn_shares, (1, 1, R, width), lambda p, t: (t, p, 0, 0), (2, 3), (1, R, width), lambda p, t: (p, 0, t),
        qkv_weight, qkv_moment, qkv_average, step_size, "update_qkv",
    )
    mix_new = update(
        attn_shares, (1, 1, R, width), lambda p: (3, p, 0, 0), (2,), (1, R, width), lambda p: (p, 0, 0),
        mix_weight, mix_moment, mix_average, step_size, "update_mix",
    )
    inner_new = update(
        inner_shares, (1, cut, hidden), lambda p, c, r: (2 * p + c, r, 0), (2, 2, R // cut),
        (1, cut, hidden), lambda p, c, r: (p, r, c), inner_weight, inner_moment, inner_average, step_size, "update_inner",
    )
    down_new = update(
        down_shares, (1, R2, half_width), lambda p, c: (2 * p + c, 0, 0), (2, 2),
        (1, R2, half_width), lambda p, c: (p, 0, c), down_weight, down_moment, down_average, step_size, "update_down",
    )
    own = norm_gains.shape[1]
    gains_grad = lax.dynamic_slice(gains_sum, (0, fs * own), (2, own))
    gains_new = (gains_grad,) + owner_update(norm_gains, gains_grad, gains_moment, gains_average, step_size)
    new = (qkv_new, mix_new, inner_new, down_new, gains_new)
    return (layer_out, frames_grad) + tuple(n[kind] for kind in range(4) for n in new)


def solution(mesh):
    rows = P(("dp", "fsdp"), None, None)
    weight = P(None, "fsdp", None)
    gains = P(None, "fsdp")
    weights = (weight,) * 4 + (gains,)
    return jax.shard_map(
        per_device,
        mesh=mesh,
        in_specs=(rows, rows, P()) + weights * 3,
        out_specs=(rows, rows) + weights * 4,
        check_vma=False,
    )
```
